32 devices in a mesh: dp: 8 (over y, x, core), blk: 4 (over z).
Axes of the slice: x: 2, y: 2, z: 4, core: 2. Of those that a mesh axis runs over, the one named last changes fastest.
Arguments:
- block_input: bfloat16 [8, 1024, 2048], P('dp', 'blk'), may hold values from -8 to 8
- out_cotangent: bfloat16 [8, 1024, 2048], P('dp', 'blk'), may hold values from -6 to 6
- row_lengths: int32 [8], P('dp'), may hold values from 256 to 1024, as said below
- rope_positions: int32 [8, 1024], P('dp', 'blk'), may hold values from 0 to 2046, as said below
- gain_attention: float32 [2048], replicated, may hold values from 0.25 to 1.75
- gain_feedforward: float32 [2048], replicated, may hold values from 0.25 to 1.75
- base_attention: bfloat16 [6, 2048, 512], P(None, None, 'dp'), may hold values from -0.125 to 0.125
- base_output: bfloat16 [4, 2048, 512], P(None, None, 'dp'), may hold values from -0.125 to 0.125
- base_feedforward: bfloat16 [2, 2048, 5632], P(None, None, 'dp'), may hold values from -0.125 to 0.125
- base_down: bfloat16 [5632, 2048], P(None, 'dp'), may hold values from -0.078125 to 0.078125
- rank_in_attention: bfloat16 [3, 2048, 16], replicated, may hold values from -0.125 to 0.125
- rank_out_attention: bfloat16 [6, 16, 512], replicated, may hold values from -0.75 to 0.75
- magnitude_attention: float32 [6, 512], replicated, may hold values from 0.8 to 2
- rank_in_output: bfloat16 [2048, 16], replicated, may hold values from -0.125 to 0.125
- rank_out_output: bfloat16 [4, 16, 512], replicated, may hold values from -0.75 to 0.75
- magnitude_output: float32 [4, 512], replicated, may hold values from 3 to 12
- rank_in_feedforward: bfloat16 [2, 2048, 16], replicated, may hold values from -0.125 to 0.125
- rank_out_feedforward: bfloat16 [2, 16, 5632], replicated, may hold values from -0.75 to 0.75
- magnitude_feedforward: float32 [2, 5632], replicated, may hold values from 0.7 to 2
- rank_in_down: bfloat16 [5632, 16], replicated, may hold values from -0.078125 to 0.078125
- rank_out_down: bfloat16 [16, 2048], replicated, may hold values from -0.75 to 0.75
- magnitude_down: float32 [2048], replicated, may hold values from 0.8 to 2.5
Outputs:
- block_output: bfloat16 [8, 1024, 2048], P('dp', 'blk')
- input_grad: bfloat16 [8, 1024, 2048], P('dp', 'blk')
- grad_rank_in_attention: float32 [3, 2048, 16], replicated
- grad_rank_out_attention: float32 [6, 16, 512], replicated
- grad_magnitude_attention: float32 [6, 512], replicated
- grad_rank_in_output: float32 [2048, 16], replicated
- grad_rank_out_output: float32 [4, 16, 512], replicated
- grad_magnitude_output: float32 [4, 512], replicated
- grad_rank_in_feedforward: float32 [2, 2048, 16], replicated
- grad_rank_out_feedforward: float32 [2, 16, 5632], replicated
- grad_magnitude_feedforward: float32 [2, 5632], replicated
- grad_rank_in_down: float32 [5632, 16], replicated
- grad_rank_out_down: float32 [16, 2048], replicated
- grad_magnitude_down: float32 [2048], replicated
The draws below stay inside these ranges and needn't reach their ends.
Inputs may be any that keep to these rules, and one draw needn't show every extreme that they name: Row r holds row_lengths[r] real tokens followed by padding; some row is 1024 tokens long. `rope_positions`: each row's positions start at 0 and rise by 1 or 2 from one token to the next; some row rises by 2 at every token.
All inputs are finite; a program needn't handle non-finite values.
Results may differ from the reference program's by a relative error of at most 0.019.
Values may be sent and summed in bfloat16 or wider, within the bound.
No kernel may reach another device: no remote copies, remote signals or barrier semaphores. Data moves between devices by JAX's collectives and lax.ppermute only.
A program may use at most 704 MiB of HBM per device.

```python
import math
import jax
import jax.numpy as jnp
from jax import lax

D = 2048
KV_HEADS = 4
HEAD = 128
FF = 5632
RANK = 16
GROUP = 4
KVW = 512
PAD = 1024
ROWS = 8


def draw_block_input(key, part):
    key_noise, key_scale = jax.random.split(key, 2)
    noise = jax.random.normal(key_noise, (ROWS, PAD, D), jnp.float32)
    scales = jnp.exp(jax.random.uniform(key_scale, (ROWS, PAD, 1), jnp.float32, math.log(0.5), math.log(2.0)))
    values = scales * noise
    return jnp.clip(values, -8.0, 8.0).astype(jnp.bfloat16)


def draw_row_lengths(key, part):
    key_one, key_two, key_full = jax.random.split(key, 3)
    shortest = PAD // 4
    span_size = PAD - shortest + 1
    drawn = jnp.minimum(jax.random.randint(key_one, (ROWS,), 0, span_size), jax.random.randint(key_two, (ROWS,), 0, span_size))
    full_row = jax.random.randint(key_full, (), 0, ROWS)
    return jnp.where(jnp.arange(ROWS) == full_row, PAD, shortest + drawn).astype(jnp.int32)


def draw_rope_positions(key, part):
    key_steps, key_row = jax.random.split(key)
    steps_drawn = jax.random.randint(key_steps, (ROWS, PAD), 1, 3)
    wide_row = jax.random.randint(key_row, (), 0, ROWS)
    steps_drawn = jnp.where((jnp.arange(ROWS) == wide_row)[:, None], 2, steps_drawn)
    return (jnp.cumsum(steps_drawn, axis=1) - steps_drawn[:, :1]).astype(jnp.int32)


def level_of(stream_key, shape, pieces, low, top_value):
    def one(dim, parts):
        steps = jax.random.uniform(jax.random.fold_in(jax.random.fold_in(stream_key, 6), dim), (parts,), jnp.float32, low / len(pieces), top_value / len(pieces))
        return jnp.repeat(jnp.exp(steps), shape[dim] // parts).reshape((-1,) + (1,) * (len(shape) - dim - 1))

    level = one(*pieces[0])
    for cut in pieces[1:]:
        level = level * one(*cut)
    return level


def scatter_about(own_key, shape, scale, bound, cuts=(), held_as=jnp.bfloat16):
    level = level_of(own_key, shape, cuts, -0.22, 0.18) if cuts else 1.0
    values = jax.random.normal(own_key, shape, jnp.float32) * scale * level
    return jnp.minimum(jnp.maximum(values, -bound), bound).astype(held_as)


def setup_inputs(seed: int = 0) -> dict:
    keys = jax.random.split(jax.random.key(seed), 23)
    return {
        "block_input": draw_block_input(jax.random.fold_in(keys[22], 71), 0),
        "out_cotangent": scatter_about(keys[1], (ROWS, PAD, D), 1.0, 6.0, ((0, 8), (1, 4))),
        "row_lengths": draw_row_lengths(jax.random.fold_in(keys[22], 71), 0),
        "rope_positions": draw_rope_positions(jax.random.fold_in(keys[22], 71), 0),
        "gain_attention": jnp.clip(1.0 + 0.15 * jax.random.normal(keys[4], (D,), jnp.float32), 0.25, 1.75),
        "gain_feedforward": jnp.clip(1.0 + 0.15 * jax.random.normal(keys[5], (D,), jnp.float32), 0.25, 1.75),
        "base_attention": scatter_about(keys[6], (GROUP + 2, D, KVW), D ** -0.5, 0.125, ((2, 8),)),
        "base_output": scatter_about(keys[7], (GROUP, D, KVW), D ** -0.5, 0.125, ((2, 8),)),
        "base_feedforward": scatter_about(keys[8], (2, D, FF), D ** -0.5, 0.125, ((2, 8),)),
        "base_down": scatter_about(keys[9], (FF, D), FF ** -0.5, 0.078125, ((1, 8),)),
        "rank_in_attention": scatter_about(keys[10], (3, D, RANK), D ** -0.5, 0.125),
        "rank_out_attention": scatter_about(keys[11], (GROUP + 2, RANK, KVW), (4 * RANK) ** -0.5, 0.75),
        "magnitude_attention": jnp.clip(jnp.exp(jax.random.uniform(keys[12], (GROUP + 2, KVW), jnp.float32, math.log(0.8), math.log(2.0))), 0.8, 2.0),
        "rank_in_output": scatter_about(keys[13], (D, RANK), D ** -0.5, 0.125),
        "rank_out_output": scatter_about(keys[14], (GROUP, RANK, KVW), (4 * RANK) ** -0.5, 0.75),
        "magnitude_output": jnp.clip(jnp.exp(jax.random.uniform(keys[15], (GROUP, KVW), jnp.float32, math.log(3.0), math.log(12.0))), 3.0, 12.0),
        "rank_in_feedforward": scatter_about(keys[16], (2, D, RANK), D ** -0.5, 0.125),
        "rank_out_feedforward": scatter_about(keys[17], (2, RANK, FF), (4 * RANK) ** -0.5, 0.75),
        "magnitude_feedforward": jnp.clip(jnp.exp(jax.random.uniform(keys[18], (2, FF), jnp.float32, math.log(0.7), math.log(2.0))), 0.7, 2.0),
        "rank_in_down": scatter_about(keys[19], (FF, RANK), FF ** -0.5, 0.078125),
        "rank_out_down": scatter_about(keys[20], (RANK, D), (4 * RANK) ** -0.5, 0.75),
        "magnitude_down": jnp.clip(jnp.exp(jax.random.uniform(keys[21], (D,), jnp.float32, math.log(0.8), math.log(2.5))), 0.8, 2.5),
    }


@jax.custom_vjp
def low(v):
    return lax.optimization_barrier(v.astype(jnp.bfloat16)).astype(jnp.float32)

@jax.custom_vjp
def low_back(v):
    return v

def low_keep(v):
    return (low(v), None)

def low_pass(kept, grad):
    return (grad,)

def back_keep(v):
    return (v, None)

def back_low(kept, grad):
    return (low(grad),)
low.defvjp(low_keep, low_pass)
low_back.defvjp(back_keep, back_low)
alpha_value = 32.0
rms_eps = 1e-05
rope_base = 10000.0
masked_score = -1e+30
highest = lax.Precision.HIGHEST

def matmul(left, right):
    return jnp.dot(left, right, precision=highest)

def rms_scaled(values, gain_row):
    return values * lax.rsqrt(lax.optimization_barrier(jnp.mean(values * values, axis=-1, keepdims=True)) + rms_eps) * gain_row

def rotate(values, cosine_table, sine_table):
    half_size = values.shape[-1] // 2
    turned = jnp.concatenate([-values[..., half_size:], values[..., :half_size]], axis=-1)
    return values * cosine_table + turned * sine_table

def rope_tables(positions_row, head_size):
    frequency = rope_base ** (-(jnp.arange(head_size // 2, dtype=jnp.float32) * 2.0) / head_size)
    angles = positions_row.astype(jnp.float32)[:, None] * frequency[None, :]
    angles = jnp.concatenate([angles, angles], axis=-1)
    return (jnp.cos(angles), jnp.sin(angles))

def side_by_side(blocks_in):
    return jnp.transpose(blocks_in, (1, 0, 2)).reshape(blocks_in.shape[1], -1)

def dora(inputs, weights, rank_in, rank_out, magnitude):
    merged = weights + alpha_value / RANK * matmul(rank_in, rank_out)
    column_norm = jnp.sqrt(lax.optimization_barrier(jnp.sum(merged * merged, axis=0)))
    base_value = low_back(matmul(inputs, weights))
    small_part = low_back(matmul(inputs, rank_in))
    return (base_value + alpha_value / RANK * matmul(small_part, rank_out)) * (magnitude / column_norm)

def attend(queries, keys_rotated, values, seq_length):
    block_size = min(512, PAD)
    block_count = PAD // block_size
    key_pos = jnp.arange(PAD, dtype=jnp.int32)
    score_scale = HEAD ** (-0.5)

    def one_block(block_inputs):
        query_part, query_first = block_inputs
        scores = low_back(jnp.einsum('tajd,sjd->ajts', query_part, keys_rotated, precision=highest) * score_scale)
        query_pos = query_first + jnp.arange(block_size, dtype=jnp.int32)
        allowed = (key_pos[None, :] <= query_pos[:, None]) & (key_pos[None, :] < seq_length)
        scores = jnp.where(allowed[None, None], scores, masked_score)
        row_max = lax.optimization_barrier(jnp.max(scores, axis=-1, keepdims=True))
        exp_terms = jnp.exp(scores - row_max)
        softmax_probs = low(exp_terms / lax.optimization_barrier(jnp.sum(exp_terms, axis=-1, keepdims=True)))
        return jnp.einsum('ajts,sjd->tajd', softmax_probs, values, precision=highest)
    query_blocks = queries.reshape((block_count, block_size) + queries.shape[1:])
    query_firsts = jnp.arange(block_count, dtype=jnp.int32) * block_size
    return lax.map(jax.checkpoint(one_block), (query_blocks, query_firsts)).reshape(PAD, -1)

def layer(adapters, row_values, consts, cosine_table, sine_table, seq_length):
    rank_in_attention, rank_out_attention, magnitude_attention, rank_in_output, rank_out_output, magnitude_output, rank_in_feedforward, rank_out_feedforward, magnitude_feedforward, rank_in_down, rank_out_down, magnitude_down = adapters
    gain_attention, gain_feedforward, base_attention, base_output, base_feedforward, base_down = consts
    normed = low(rms_scaled(row_values, gain_attention))
    query_raw = dora(normed, side_by_side(base_attention[:GROUP]), rank_in_attention[0], side_by_side(rank_out_attention[:GROUP]), magnitude_attention[:GROUP].reshape(-1))
    key_raw = dora(normed, base_attention[GROUP], rank_in_attention[1], rank_out_attention[GROUP], magnitude_attention[GROUP])
    value_raw = dora(normed, base_attention[GROUP + 1], rank_in_attention[2], rank_out_attention[GROUP + 1], magnitude_attention[GROUP + 1])
    queries = low(rotate(query_raw.reshape(PAD, GROUP, KV_HEADS, HEAD), cosine_table[:, None, None, :], sine_table[:, None, None, :]))
    keys_rotated = low(rotate(key_raw.reshape(PAD, KV_HEADS, HEAD), cosine_table[:, None, :], sine_table[:, None, :]))
    values = low(value_raw.reshape(PAD, KV_HEADS, HEAD))
    mixed_heads = low(low_back(attend(queries, keys_rotated, values, seq_length)))
    residual = row_values + dora(mixed_heads, side_by_side(base_output), rank_in_output, side_by_side(rank_out_output), magnitude_output.reshape(-1))
    normed_feed = low(rms_scaled(residual, gain_feedforward))
    gate_value = dora(normed_feed, base_feedforward[0], rank_in_feedforward[0], rank_out_feedforward[0], magnitude_feedforward[0])
    up_value = dora(normed_feed, base_feedforward[1], rank_in_feedforward[1], rank_out_feedforward[1], magnitude_feedforward[1])
    hidden = low(jax.nn.silu(gate_value) * up_value)
    return residual + dora(hidden, base_down, rank_in_down, rank_out_down, magnitude_down)

def reference(block_input, out_cotangent, row_lengths, rope_positions, gain_attention, gain_feedforward, base_attention, base_output, base_feedforward, base_down, rank_in_attention, rank_out_attention, magnitude_attention, rank_in_output, rank_out_output, magnitude_output, rank_in_feedforward, rank_out_feedforward, magnitude_feedforward, rank_in_down, rank_out_down, magnitude_down):
    params = tuple((array_in.astype(jnp.float32) for array_in in (rank_in_attention, rank_out_attention, magnitude_attention, rank_in_output, rank_out_output, magnitude_output, rank_in_feedforward, rank_out_feedforward, magnitude_feedforward, rank_in_down, rank_out_down, magnitude_down)))
    consts = tuple((array_in.astype(jnp.float32) for array_in in (gain_attention, gain_feedforward, base_attention, base_output, base_feedforward, base_down)))
    token_pos = jnp.arange(PAD, dtype=jnp.int32)

    def row_step(totals, row_inputs):
        row_values, row_grad, seq_length, row_positions = row_inputs
        cosine_table, sine_table = rope_tables(row_positions, HEAD)

        def forward(adapters, values_in):
            return layer(adapters, values_in, consts, cosine_table, sine_table, seq_length)
        result, pullback = jax.vjp(forward, params, row_values.astype(jnp.float32))
        valid_rows = (token_pos < seq_length).astype(jnp.float32)[:, None]
        grad_params, grad_values = pullback(row_grad.astype(jnp.float32) * valid_rows)
        totals = jax.tree.map(lambda summed, update: summed + update, totals, grad_params)
        return (totals, (result.astype(jnp.bfloat16), grad_values.astype(jnp.bfloat16)))
    zero_grads = jax.tree.map(jnp.zeros_like, params)
    totals, (outputs, grads_in) = lax.scan(row_step, zero_grads, (block_input, out_cotangent, row_lengths, rope_positions))
    return (outputs, grads_in, totals[0], totals[1], totals[2], totals[3], totals[4], totals[5], totals[6], totals[7], totals[8], totals[9], totals[10], totals[11])
```

```python
import functools

import jax
import jax.numpy as jnp
from jax import lax
from jax.experimental import pallas as pl
from jax.experimental.pallas import tpu as pltpu
from jax.sharding import PartitionSpec as P

D = 2048
KV_HEADS = 4
HEAD = 128
FF = 5632
RANK = 16
GROUP = 4
KVW = 512

factor = 32.0 / RANK
rms_eps = 1e-05
rope_base = 10000.0
masked_score = -1e30
log2_e = 1.4426950408889634
score_scale = HEAD ** (-0.5)
f32 = jnp.float32
bf16 = jnp.bfloat16


def dot_nt(left, right):
    return lax.dot_general(left, right, (((1,), (1,)), ((), ())), preferred_element_type=f32)


def dot_nn(left, right):
    return lax.dot_general(left, right, (((1,), (0,)), ((), ())), preferred_element_type=f32)


def dot_tn(left, right):
    return lax.dot_general(left, right, (((0,), (0,)), ((), ())), preferred_element_type=f32)


def fold_kernel(weight_ref, rank_in_ref, rank_out_ref, mag_ref, out_ref, norm_ref, proj_ref, merged_ref, *, chunk):
    inputs, columns = weight_ref.shape[1], weight_ref.shape[2]
    row = lax.broadcasted_iota(jnp.int32, (columns, columns), 0)
    col = lax.broadcasted_iota(jnp.int32, (columns, columns), 1)
    eye = jnp.where(row == col, 1.0, 0.0).astype(bf16)

    def merge(index, total):
        part = pl.ds(pl.multiple_of(index * chunk, chunk), chunk)
        merged = dot_nt(eye, weight_ref[0, part, :]) + dot_nt(rank_out_ref[0], rank_in_ref[0, part, :])
        merged_ref[:, part] = merged
        return total + jnp.sum(merged * merged, axis=1, keepdims=True)

    total = lax.fori_loop(0, inputs // chunk, merge, jnp.zeros((columns, 1), f32))
    norm = jnp.sqrt(total)
    norm_ref[0] = norm
    scale = mag_ref[0] / norm

    def finish(index, proj):
        part = pl.ds(pl.multiple_of(index * chunk, chunk), chunk)
        folded = (merged_ref[:, part] * scale).astype(bf16)
        out_ref[0, :, part] = folded
        return proj + dot_nn(folded, rank_in_ref[0, part, :])

    proj_ref[0] = lax.fori_loop(0, inputs // chunk, finish, jnp.zeros((columns, RANK), f32))


def fold(weights, rank_in, rank_out, magnitude, rank_of, name):
    members, inputs, columns = weights.shape
    doubled = (factor * rank_out.astype(f32)).astype(bf16).transpose(0, 2, 1)
    return pl.pallas_call(
        functools.partial(fold_kernel, chunk=256),
        out_shape=(
            jax.ShapeDtypeStruct((members, columns, inputs), bf16),
            jax.ShapeDtypeStruct((members, columns, 1), f32),
            jax.ShapeDtypeStruct((members, columns, RANK), f32),
        ),
        grid=(members,),
        in_specs=[
            pl.BlockSpec((1, inputs, columns), lambda b: (b, 0, 0)),
            pl.BlockSpec((1, inputs, RANK), lambda b: (rank_of(b), 0, 0)),
            pl.BlockSpec((1, columns, RANK), lambda b: (b, 0, 0)),
            pl.BlockSpec((1, columns, 1), lambda b: (b, 0, 0)),
        ],
        out_specs=(
            pl.BlockSpec((1, columns, inputs), lambda b: (b, 0, 0)),
            pl.BlockSpec((1, columns, 1), lambda b: (b, 0, 0)),
            pl.BlockSpec((1, columns, RANK), lambda b: (b, 0, 0)),
        ),
        scratch_shapes=[pltpu.VMEM((columns, inputs), f32)],
        compiler_params=pltpu.CompilerParams(vmem_limit_bytes=48 << 20),
        name=name,
    )(weights, rank_in, doubled, magnitude[:, :, None])


def rope_kernel(x_ref, weight_ref, cos_ref, sin_ref, out_ref, *, plain_from):
    raw = dot_nt(x_ref[...], weight_ref[0])
    roped = pl.program_id(0) < plain_from
    for head in range(KVW // HEAD):
        part = raw[:, head * HEAD : (head + 1) * HEAD]
        turned = part * cos_ref[...] + pltpu.roll(part, HEAD // 2, 1) * sin_ref[...]
        out_ref[:, head * HEAD : (head + 1) * HEAD] = jnp.where(roped, turned, part).astype(bf16)


def project_rope(inputs, weights, cosine, sine, plain_from, name):
    tokens = inputs.shape[0]
    blocks = weights.shape[0]
    return pl.pallas_call(
        functools.partial(rope_kernel, plain_from=plain_from),
        out_shape=jax.ShapeDtypeStruct((tokens, blocks * KVW), bf16),
        grid=(blocks,),
        in_specs=[
            pl.BlockSpec((tokens, D), lambda b: (0, 0)),
            pl.BlockSpec((1, KVW, D), lambda b: (b, 0, 0)),
            pl.BlockSpec((tokens, HEAD), lambda b: (0, 0)),
            pl.BlockSpec((tokens, HEAD), lambda b: (0, 0)),
        ],
        out_specs=pl.BlockSpec((tokens, KVW), lambda b: (0, b)),
        compiler_params=pltpu.CompilerParams(vmem_limit_bytes=32 << 20),
        name=name,
    )(inputs, weights, cosine, sine)


def lane_block(start, head):
    return pl.ds(pl.multiple_of(start + head * HEAD, HEAD), HEAD)


def masked_scores(keys, queries, key_first, length, causal):
    tokens, lanes = keys.shape[0], queries.shape[0]
    scores = dot_nt(keys, queries)
    key_pos = key_first + lax.broadcasted_iota(jnp.int32, (tokens, 1), 0)
    scores = scores + jnp.where(key_pos < length, 0.0, masked_score)
    if causal:
        key_index = lax.broadcasted_iota(jnp.int32, (tokens, lanes), 0)
        token_index = lax.broadcasted_iota(jnp.int32, (tokens, lanes), 1) & (tokens - 1)
        scores = jnp.where(key_index <= token_index, scores, masked_score)
    return scores


def attend_kernel(scalar_ref, query_ref, *refs, steps):
    kv_refs = refs[:steps]
    mixed_ref, lse_ref, stacked_ref, max_ref, sum_ref, accum_ref = refs[steps:]
    head = pl.program_id(0)
    tokens = query_ref.shape[0]
    block_index, length = scalar_ref[0], scalar_ref[1]
    scale = score_scale * log2_e
    for group in range(GROUP):
        stacked_ref[group * tokens : (group + 1) * tokens, :] = query_ref[:, lane_block(group * KVW, head)]

    for distance in range(steps):

        def step(distance=distance):
            keys = kv_refs[distance][:, lane_block(0, head)]
            values = kv_refs[distance][:, lane_block(KVW, head)]
            key_first = (block_index - distance) * tokens
            scores = masked_scores(keys, stacked_ref[...], key_first, length, distance == 0)
            block_max = jnp.max(scores, axis=0, keepdims=True)
            new_max = block_max if distance == 0 else jnp.maximum(max_ref[...], block_max)
            terms = jnp.exp2((scores - new_max) * scale)
            added = jnp.sum(terms, axis=0, keepdims=True)
            product = dot_tn(values, terms.astype(bf16))
            if distance == 0:
                sum_ref[...] = added
                accum_ref[...] = product
            else:
                fade = jnp.exp2((max_ref[...] - new_max) * scale)
                sum_ref[...] = sum_ref[...] * fade + added
                accum_ref[...] = accum_ref[...] * fade + product
            max_ref[...] = new_max

        if distance == 0:
            step()
        else:
            pl.when(block_index >= distance)(step)
    mixed = accum_ref[...] / sum_ref[...]
    for group in range(GROUP):
        part = mixed[:, group * tokens : (group + 1) * tokens]
        mixed_ref[:, lane_block(group * KVW, head)] = part.T.astype(bf16)
    lse_ref[0] = max_ref[...] * scale + jnp.log(sum_ref[...]) * log2_e


def attend(scalars, queries, kv_blocks):
    tokens = queries.shape[0]
    steps = len(kv_blocks)
    lanes = GROUP * tokens
    whole = lambda *shape: pl.BlockSpec(shape, lambda j, s: (0,) * len(shape))
    return pl.pallas_call(
        functools.partial(attend_kernel, steps=steps),
        out_shape=(
            jax.ShapeDtypeStruct((tokens, D), bf16),
            jax.ShapeDtypeStruct((KV_HEADS, 1, lanes), f32),
        ),
        grid_spec=pltpu.PrefetchScalarGridSpec(
            num_scalar_prefetch=1,
            grid=(KV_HEADS,),
            in_specs=[whole(tokens, D)] + [whole(tokens, 2 * KVW)] * steps,
            out_specs=(whole(tokens, D), pl.BlockSpec((1, 1, lanes), lambda j, s: (j, 0, 0))),
            scratch_shapes=[
                pltpu.VMEM((lanes, HEAD), bf16),
                pltpu.VMEM((1, lanes), f32),
                pltpu.VMEM((1, lanes), f32),
                pltpu.VMEM((HEAD, lanes), f32),
            ],
        ),
        compiler_params=pltpu.CompilerParams(vmem_limit_bytes=48 << 20),
        name="attend",
    )(scalars, queries, *kv_blocks)


def attend_back_kernel(scalar_ref, query_ref, grad_ref, lse_ref, delta_ref, kv_ref, *refs, distance, chained):
    if chained:
        sent_ref, before_ref, grad_query_ref, grad_kv_ref, stacked_ref, stacked_grad_ref = refs
    else:
        grad_query_ref, grad_kv_ref, stacked_ref, stacked_grad_ref = refs
    head = pl.program_id(0)
    tokens = query_ref.shape[0]
    block_index, length = scalar_ref[0], scalar_ref[1]
    active = (block_index >= distance) & (block_index * tokens < length)
    key_lanes, value_lanes = lane_block(0, head), lane_block(KVW, head)

    @pl.when(active)
    def _():
        for group in range(GROUP):
            rows = slice(group * tokens, (group + 1) * tokens)
            stacked_ref[rows, :] = query_ref[:, lane_block(group * KVW, head)]
            stacked_grad_ref[rows, :] = grad_ref[:, lane_block(group * KVW, head)]
        keys = kv_ref[:, key_lanes]
        values = kv_ref[:, value_lanes]
        key_first = (block_index - distance) * tokens
        scores = masked_scores(keys, stacked_ref[...], key_first, length, distance == 0)
        probs = jnp.exp2(scores * (score_scale * log2_e) - lse_ref[0])
        grad_probs = dot_nt(values, stacked_grad_ref[...])
        grad_scores = (probs * (grad_probs - delta_ref[0])).astype(bf16)
        grad_values = dot_nn(probs.astype(bf16), stacked_grad_ref[...])
        grad_keys = dot_nn(grad_scores, stacked_ref[...]) * score_scale
        grad_queries = dot_tn(grad_scores, keys) * score_scale
        for group in range(GROUP):
            lanes = lane_block(group * KVW, head)
            part = grad_queries[group * tokens : (group + 1) * tokens, :]
            if chained:
                part = part + before_ref[:, lanes]
            grad_query_ref[:, lanes] = part
        if chained:
            grad_keys = grad_keys + sent_ref[:, key_lanes].astype(f32)
            grad_values = grad_values + sent_ref[:, value_lanes].astype(f32)
        grad_kv_ref[:, key_lanes] = grad_keys.astype(grad_kv_ref.dtype)
        grad_kv_ref[:, value_lanes] = grad_values.astype(grad_kv_ref.dtype)

    @pl.when(jnp.logical_not(active))
    def _():
        for group in range(GROUP):
            lanes = lane_block(group * KVW, head)
            if chained:
                grad_query_ref[:, lanes] = before_ref[:, lanes]
            else:
                grad_query_ref[:, lanes] = jnp.zeros((tokens, HEAD), f32)
        for lanes in (key_lanes, value_lanes):
            if chained:
                grad_kv_ref[:, lanes] = sent_ref[:, lanes].astype(grad_kv_ref.dtype)
            else:
                grad_kv_ref[:, lanes] = jnp.zeros((tokens, HEAD), grad_kv_ref.dtype)


def attend_back(scalars, queries, grad_mixed, lse, delta, kv_block, sent, before, distance):
    tokens = queries.shape[0]
    lanes = GROUP * tokens
    whole = lambda *shape: pl.BlockSpec(shape, lambda j, s: (0,) * len(shape))
    row = pl.BlockSpec((1, 1, lanes), lambda j, s: (j, 0, 0))
    chained = before is not None
    operands = [scalars, queries, grad_mixed, lse, delta, kv_block]
    specs = [whole(tokens, D), whole(tokens, D), row, row, whole(tokens, 2 * KVW)]
    if chained:
        operands += [sent, before]
        specs += [whole(tokens, 2 * KVW), whole(tokens, D)]
    return pl.pallas_call(
        functools.partial(attend_back_kernel, distance=distance, chained=chained),
        out_shape=(
            jax.ShapeDtypeStruct((tokens, D), f32),
            jax.ShapeDtypeStruct((tokens, 2 * KVW), f32 if distance == 0 else bf16),
        ),
        grid_spec=pltpu.PrefetchScalarGridSpec(
            num_scalar_prefetch=1,
            grid=(KV_HEADS,),
            in_specs=specs,
            out_specs=(whole(tokens, D), whole(tokens, 2 * KVW)),
            scratch_shapes=[pltpu.VMEM((lanes, HEAD), bf16), pltpu.VMEM((lanes, HEAD), bf16)],
        ),
        input_output_aliases={7: 0} if chained else {},
        compiler_params=pltpu.CompilerParams(vmem_limit_bytes=48 << 20),
        name=f"attend_back_{distance}",
    )(*operands)


def rms_parts(values, gain):
    inverse = lax.rsqrt(jnp.mean(values * values, axis=-1, keepdims=True) + rms_eps)
    return (values * inverse * gain).astype(bf16), inverse


def rms_back(values, inverse, gain, grad):
    scaled = grad * gain
    return inverse * (scaled - values * (inverse * inverse * jnp.mean(scaled * values, axis=-1, keepdims=True)))


class Links:
    def __init__(self, devices):
        self.devices = devices
        self.chips = devices // 2
        self.index = lax.axis_index("dp")
        self.core = self.index % 2
        self.square = self.chips == 4

    def swap(self, value, bits):
        return lax.ppermute(value, "dp", [(i, i ^ bits) for i in range(self.devices)])

    def split_swap(self, value, even_bits, odd_bits):
        return lax.ppermute(
            value, "dp", [(i, i ^ (odd_bits if i % 2 else even_bits)) for i in range(self.devices)]
        )

    def chip_gather(self, value):
        if not self.square:
            return [value] + [self.swap(value, 2 * r) for r in range(1, self.chips)]
        side = self.swap(value, 2)
        other = self.swap(value, 4)
        across = self.split_swap(jnp.where(self.core == 0, other, side), 2, 4)
        return [value, side, other, across]

    def chip_reduce(self, shares):
        add = lambda *parts: sum(part.astype(f32) for part in parts)
        if not self.square:
            return add(shares[0], *[self.swap(shares[r], 2 * r) for r in range(1, self.chips)])
        across = self.split_swap(shares[3], 2, 4)
        first = self.split_swap(jnp.where(self.core == 0, shares[1], shares[2]), 2, 4)
        late = jnp.where(self.core == 0, shares[2], shares[1])
        second = self.split_swap(add(late, across).astype(bf16), 4, 2)
        return add(shares[0], first, second)

    def gather(self, value):
        entries = [None] * self.devices
        for r, piece in enumerate(self.chip_gather(value)):
            entries[2 * r] = piece
            entries[2 * r + 1] = self.swap(piece, 1)
        return entries

    def gather_rows(self, value):
        groups, rows, width = value.shape
        whole = jnp.zeros((groups, self.devices, rows, width), value.dtype)
        for i, piece in enumerate(self.gather(value)):
            whole = lax.dynamic_update_slice(whole, piece[:, None], (0, self.index ^ i, 0, 0))
        return whole.reshape(groups, self.devices * rows, width)


def after(value, *others):
    return lax.optimization_barrier((value,) + others)[0]


def shards(
    block_input,
    out_cotangent,
    row_lengths,
    rope_positions,
    gain_attention,
    gain_feedforward,
    base_attention,
    base_output,
    base_feedforward,
    base_down,
    rank_in_attention,
    rank_out_attention,
    magnitude_attention,
    rank_in_output,
    rank_out_output,
    magnitude_output,
    rank_in_feedforward,
    rank_out_feedforward,
    magnitude_feedforward,
    rank_in_down,
    rank_out_down,
    magnitude_down,
    *,
    devices,
    blocks,
):
    links = Links(devices)
    index, core, chips = links.index, links.core, links.chips
    chip = index // 2
    block_index = lax.axis_index("blk")
    rows_in = block_input[0].astype(f32)
    tokens = rows_in.shape[0]
    length = row_lengths[0]
    token_pos = block_index * tokens + jnp.arange(tokens, dtype=jnp.int32)
    valid = (token_pos < length)[:, None]
    scalars = jnp.stack([block_index.astype(jnp.int32), length])

    frequency = rope_base ** (-(jnp.arange(HEAD // 2, dtype=f32) * 2.0) / HEAD)
    angles = rope_positions[0].astype(f32)[:, None] * frequency[None, :]
    cos_half, sin_half = jnp.cos(angles), jnp.sin(angles)
    cosine = jnp.concatenate([cos_half, cos_half], axis=-1)
    sine = jnp.concatenate([-sin_half, sin_half], axis=-1)

    def columns_of(value, width):
        return lax.dynamic_slice_in_dim(value, index * width, width, value.ndim - 1)

    attn_cols = base_attention.shape[2]
    out_cols = base_output.shape[2]
    feed_cols = base_feedforward.shape[2]
    down_cols = base_down.shape[1]
    attn_rank = columns_of(rank_out_attention, attn_cols)
    attn_mag = columns_of(magnitude_attention, attn_cols)
    kv_fold, kv_norm, kv_proj = fold(
        base_attention[GROUP:], rank_in_attention[1:], attn_rank[GROUP:], attn_mag[GROUP:], lambda b: b, "fold_kv"
    )
    q_fold, q_norm, q_proj = fold(
        base_attention[:GROUP], rank_in_attention[:1], attn_rank[:GROUP], attn_mag[:GROUP], lambda b: 0, "fold_q"
    )
    o_fold, o_norm, o_proj = fold(
        base_output,
        rank_in_output[None],
        columns_of(rank_out_output, out_cols),
        columns_of(magnitude_output, out_cols),
        lambda b: 0,
        "fold_o",
    )
    f_fold, f_norm, f_proj = fold(
        base_feedforward,
        rank_in_feedforward,
        columns_of(rank_out_feedforward, feed_cols),
        columns_of(magnitude_feedforward, feed_cols),
        lambda b: b,
        "fold_f",
    )
    d_fold, d_norm, d_proj = fold(
        base_down[None],
        rank_in_down[None],
        columns_of(rank_out_down, down_cols)[None],
        columns_of(magnitude_down, down_cols)[None],
        lambda b: 0,
        "fold_d",
    )

    kv_weights = links.gather_rows(kv_fold)
    q_weights = links.gather_rows(after(q_fold, kv_weights))
    o_weights = links.gather_rows(after(o_fold, q_weights)).reshape(D, D)

    feed_weights = jnp.zeros((2, 2, feed_cols, D), bf16)
    feed_weights = lax.dynamic_update_slice(feed_weights, f_fold[:, None], (0, core, 0, 0))
    feed_weights = lax.dynamic_update_slice(feed_weights, links.swap(f_fold, 1)[:, None], (0, 1 - core, 0, 0))
    feed_weights = feed_weights.reshape(2, 2 * feed_cols, D)
    chip_cols = 2 * feed_cols
    gate_weights, up_weights = feed_weights[0], feed_weights[1]

    d_source = after(d_fold[0], o_weights)
    down_weights = jnp.zeros((devices, down_cols, chip_cols), bf16)
    for r in range(chips):
        piece = lax.dynamic_slice_in_dim(d_source, (chip ^ r) * chip_cols, chip_cols, 1)
        if r:
            piece = links.swap(piece, 2 * r)
        down_weights = lax.dynamic_update_slice(down_weights, piece[None], (index ^ (2 * r), 0, 0))
        down_weights = lax.dynamic_update_slice(
            down_weights, links.swap(piece, 1)[None], (index ^ (2 * r + 1), 0, 0)
        )
    down_weights = down_weights.reshape(D, chip_cols)

    grad_out = jnp.where(valid, out_cotangent[0], jnp.zeros((), bf16))
    grad_blocks = links.chip_gather(after(grad_out, o_weights))

    normed, inverse_in = rms_parts(rows_in, gain_attention)
    kv_own = project_rope(normed, kv_weights, cosine, sine, 1, "project_kv")
    kv_blocks = [kv_own]
    for _ in range(1, blocks):
        kv_blocks.append(lax.ppermute(kv_blocks[-1], "blk", [(i, i + 1) for i in range(blocks - 1)]))
    queries = project_rope(normed, q_weights, cosine, sine, GROUP, "project_q")
    mixed, lse = attend(scalars, queries, kv_blocks)
    out_value = dot_nt(mixed, o_weights)
    residual = rows_in + out_value
    normed_feed, inverse_feed = rms_parts(residual, gain_feedforward)

    feed_blocks = links.chip_gather(normed_feed)
    shares_out, shares_grad = [], []
    hiddens, grad_gates, grad_ups = [], [], []
    gate_mag_sum = jnp.zeros((chip_cols,), f32)
    up_mag_sum = jnp.zeros((chip_cols,), f32)
    down_mag_sum = jnp.zeros((D,), f32)
    for r in range(chips):
        gate = dot_nt(feed_blocks[r], gate_weights)
        up = dot_nt(feed_blocks[r], up_weights)
        sigma = jax.nn.sigmoid(gate)
        hidden = (gate * sigma * up).astype(bf16)
        grad_hidden = dot_nn(grad_blocks[r], down_weights)
        grad_gate = grad_hidden * up * sigma * (1.0 + gate * (1.0 - sigma))
        grad_up = grad_hidden * gate * sigma
        gate_mag_sum = gate_mag_sum + jnp.sum(grad_gate * gate, axis=0)
        up_mag_sum = up_mag_sum + jnp.sum(grad_up * up, axis=0)
        grad_gate, grad_up = grad_gate.astype(bf16), grad_up.astype(bf16)
        shares_grad.append((dot_nn(grad_gate, gate_weights) + dot_nn(grad_up, up_weights)).astype(bf16))
        down_value = dot_nt(hidden, down_weights)
        down_mag_sum = down_mag_sum + jnp.sum(grad_blocks[r].astype(f32) * down_value, axis=0)
        shares_out.append(down_value.astype(bf16))
        hiddens.append(hidden)
        grad_gates.append(grad_gate)
        grad_ups.append(grad_up)
    grad_normed_feed = links.chip_reduce(shares_grad)
    grad_residual = grad_out.astype(f32) + rms_back(residual, inverse_feed, gain_feedforward, grad_normed_feed)
    block_out = (residual + links.chip_reduce(shares_out)).astype(bf16)[None]

    grad_residual_low = grad_residual.astype(bf16)
    grad_mixed = dot_nn(grad_residual_low, o_weights).astype(bf16)
    delta = jnp.sum(
        (grad_mixed.astype(f32) * mixed.astype(f32)).reshape(tokens, GROUP, KV_HEADS, HEAD), axis=-1
    )
    delta = delta.transpose(2, 1, 0).reshape(KV_HEADS, 1, GROUP * tokens)
    grad_queries, grad_kv = None, None
    for distance in reversed(range(blocks)):
        if grad_kv is not None:
            grad_kv = lax.ppermute(grad_kv, "blk", [(i + 1, i) for i in range(blocks - 1)])
        grad_queries, grad_kv = attend_back(
            scalars, queries, grad_mixed, lse, delta, kv_blocks[distance], grad_kv, grad_queries, distance
        )

    def rope_back(grads):
        heads = grads.reshape(tokens, -1, HEAD)
        return (heads * cosine[:, None] - jnp.roll(heads, HEAD // 2, axis=-1) * sine[:, None]).reshape(tokens, -1)

    grad_q_raw = rope_back(grad_queries)
    grad_k_raw = rope_back(grad_kv[:, :KVW])
    grad_v_raw = grad_kv[:, KVW:]
    q_flat = q_weights.reshape(GROUP * KVW, D)
    grad_q_low = grad_q_raw.astype(bf16)
    grad_kv_low = jnp.concatenate([grad_k_raw, grad_v_raw], axis=1).astype(bf16)
    grad_normed = dot_nn(grad_q_low, q_flat) + dot_nn(grad_kv_low, kv_weights.reshape(2 * KVW, D))
    input_grad = (grad_residual + rms_back(rows_in, inverse_in, gain_attention, grad_normed)).astype(bf16)[None]

    def all_columns(value):
        gathered = lax.all_gather(value, "dp", axis=0)
        return jnp.moveaxis(gathered, 0, -2).reshape(value.shape[:-1] + (-1,))

    def rows_first(norm, proj):
        return jnp.concatenate([norm, proj], axis=2).transpose(0, 2, 1)

    attn_aux = all_columns(
        jnp.concatenate([rows_first(q_norm, q_proj), rows_first(kv_norm, kv_proj), rows_first(o_norm, o_proj)])
    )
    feed_aux = rows_first(f_norm, f_proj)
    feed_other = links.swap(feed_aux, 1)
    feed_aux = jnp.where(
        core == 0,
        jnp.concatenate([feed_aux, feed_other], axis=2),
        jnp.concatenate([feed_other, feed_aux], axis=2),
    )
    down_norm = lax.all_gather(d_norm.reshape(-1), "dp", axis=0, tiled=True)

    def adapter(inputs, grads, weights, rank_in, rank_out, magnitude, norm, proj, mag_sum):
        small = dot_nn(inputs, rank_in).astype(bf16)
        scale = magnitude / norm
        grad_mag = mag_sum / magnitude
        turn = -(grad_mag / norm)
        wide = rank_out.astype(f32)
        grad_small = (factor * dot_nt(grads, (wide * scale).astype(bf16))).astype(bf16)
        grad_rank_out = factor * (dot_tn(small, grads) * scale + proj * turn)
        grad_rank_in = dot_tn(inputs, grad_small) + factor * lax.dot_general(
            weights, (wide * turn).astype(bf16), (((0,), (1,)), ((), ())), preferred_element_type=f32
        )
        return grad_rank_in, grad_rank_out, grad_mag

    def flat_blocks(value):
        return value.transpose(1, 0, 2).reshape(value.shape[1], -1)

    def block_form(value):
        return value.reshape(value.shape[0], -1, KVW).transpose(1, 0, 2)

    o_aux = flat_blocks(attn_aux[GROUP + 2 :])
    out_in, out_out, out_mag = adapter(
        mixed,
        grad_residual_low,
        o_weights,
        rank_in_output,
        flat_blocks(rank_out_output),
        magnitude_output.reshape(-1),
        o_aux[0],
        o_aux[1:],
        jnp.sum(grad_residual * out_value, axis=0),
    )

    feed_all = jnp.concatenate(feed_blocks)
    feed_ins, feed_outs, feed_mags = [], [], []
    for member, (grads, mag_sum) in enumerate(
        ((jnp.concatenate(grad_gates), gate_mag_sum), (jnp.concatenate(grad_ups), up_mag_sum))
    ):
        grad_in, grad_rank, grad_mag = adapter(
            feed_all,
            grads,
            feed_weights[member],
            rank_in_feedforward[member],
            lax.dynamic_slice_in_dim(rank_out_feedforward[member], chip * chip_cols, chip_cols, 1),
            lax.dynamic_slice_in_dim(magnitude_feedforward[member], chip * chip_cols, chip_cols, 0),
            feed_aux[member, 0],
            feed_aux[member, 1:],
            mag_sum,
        )
        feed_ins.append(grad_in)
        feed_outs.append(
            lax.dynamic_update_slice(jnp.zeros((RANK, FF), f32), grad_rank, (0, chip * chip_cols))
        )
        feed_mags.append(lax.dynamic_update_slice(jnp.zeros((FF,), f32), grad_mag, (chip * chip_cols,)))

    down_grad_mag = lax.psum(down_mag_sum / magnitude_down, ("dp", "blk"))
    hidden_all = jnp.concatenate(hiddens)
    grad_all = jnp.concatenate(grad_blocks)
    down_scale = magnitude_down / down_norm
    down_wide = rank_out_down.astype(f32)
    down_small = dot_nn(
        hidden_all, lax.dynamic_slice_in_dim(rank_in_down, chip * chip_cols, chip_cols, 0)
    ).astype(bf16)
    down_grad_small = (factor * dot_nt(grad_all, (down_wide * down_scale).astype(bf16))).astype(bf16)
    down_out = factor * dot_tn(down_small, grad_all) * down_scale
    down_in = lax.dynamic_update_slice(
        jnp.zeros((FF, RANK), f32), dot_tn(hidden_all, down_grad_small), (chip * chip_cols, 0)
    )
    own_turn = columns_of(-(down_grad_mag / down_norm), down_cols) * (1.0 / blocks)
    own_wide = columns_of(down_wide, down_cols)
    down_in = down_in + factor * lax.dot_general(
        d_fold[0], (own_wide * own_turn).astype(bf16), (((0,), (1,)), ((), ())), preferred_element_type=f32
    )
    own_out = factor * d_proj[0].T * own_turn
    down_out = down_out + lax.dynamic_update_slice(jnp.zeros((RANK, D), f32), own_out, (0, index * down_cols))

    def turned_back(low):
        heads = low.astype(f32).reshape(tokens, -1, HEAD)
        return (heads * cosine[:, None] - jnp.roll(heads, HEAD // 2, axis=-1) * sine[:, None]).reshape(tokens, -1)

    kv_wide = kv_weights.reshape(2, KVW, D)
    values_in = (
        (grad_q_raw, q_flat, 0, slice(0, GROUP), turned_back(queries)),
        (grad_k_raw, kv_wide[0], 1, slice(GROUP, GROUP + 1), turned_back(kv_own[:, :KVW])),
        (grad_v_raw, kv_wide[1], 2, slice(GROUP + 1, GROUP + 2), kv_own[:, KVW:].astype(f32)),
    )
    attn_ins, attn_outs, attn_mags = [], [], []
    for grads, weights, member, span, raw in values_in:
        aux = flat_blocks(attn_aux[span])
        grad_in, grad_rank, grad_mag = adapter(
            normed,
            grads.astype(bf16),
            weights,
            rank_in_attention[member],
            flat_blocks(rank_out_attention[span]),
            magnitude_attention[span].reshape(-1),
            aux[0],
            aux[1:],
            jnp.sum(grads * raw, axis=0),
        )
        attn_ins.append(grad_in)
        attn_outs.append(block_form(grad_rank))
        attn_mags.append(grad_mag.reshape(-1, KVW))

    early = lax.psum(
        (
            out_in,
            block_form(out_out),
            out_mag.reshape(-1, KVW),
            jnp.stack(feed_ins),
            jnp.stack(feed_outs),
            jnp.stack(feed_mags),
            down_in,
            down_out,
        ),
        ("dp", "blk"),
    )
    late = lax.psum(
        (jnp.stack(attn_ins), jnp.concatenate(attn_outs), jnp.concatenate(attn_mags)), ("dp", "blk")
    )
    return (block_out, input_grad) + tuple(late) + tuple(early) + (down_grad_mag,)


def solution(mesh):
    split_tokens = P("dp", "blk", None)
    placed = (
        split_tokens,
        split_tokens,
        P("dp"),
        P("dp", "blk"),
        P(),
        P(),
        P(None, None, "dp"),
        P(None, None, "dp"),
        P(None, None, "dp"),
        P(None, "dp"),
    ) + (P(),) * 12
    return jax.shard_map(
        functools.partial(shards, devices=mesh.shape["dp"], blocks=mesh.shape["blk"]),
        mesh=mesh,
        in_specs=placed,
        out_specs=(split_tokens, split_tokens) + (P(),) * 12,
        check_vma=False,
    )
```

```python
import functools

import jax
import jax.numpy as jnp
from jax import lax
from jax.experimental import pallas as pl
from jax.experimental.pallas import tpu as pltpu
from jax.sharding import PartitionSpec as P

D = 2048
KV_HEADS = 4
HEAD = 128
FF = 5632
RANK = 16
GROUP = 4
KVW = 512

EXT = 128
WIDE = D + EXT
SLOTS = 3
INV_AT = 48
PROJ_AT = 64
AUX = 32

factor = 32.0 / RANK
rms_eps = 1e-05
rope_base = 10000.0
masked_score = -1e30
log2_e = 1.4426950408889634
score_scale = HEAD ** (-0.5)
f32 = jnp.float32
bf16 = jnp.bfloat16


def dot_nt(left, right):
    return lax.dot_general(left, right, (((1,), (1,)), ((), ())), preferred_element_type=f32)


def dot_nn(left, right):
    return lax.dot_general(left, right, (((1,), (0,)), ((), ())), preferred_element_type=f32)


def dot_tn(left, right):
    return lax.dot_general(left, right, (((0,), (0,)), ((), ())), preferred_element_type=f32)


def limits(mebibytes):
    return pltpu.CompilerParams(vmem_limit_bytes=mebibytes << 20)


kernel_call = functools.partial(
    pl.pallas_call, cost_estimate=pl.CostEstimate(flops=0, transcendentals=0, bytes_accessed=0)
)


anywhere = pl.BlockSpec(memory_space=pltpu.HBM)
in_vmem = pl.BlockSpec(memory_space=pltpu.VMEM)
in_smem = pl.BlockSpec(memory_space=pltpu.SMEM)


def shape_of(shape, dtype=f32):
    return jax.ShapeDtypeStruct(shape, dtype)


def split_low(value):
    high = value.astype(bf16)
    return high, (value - high.astype(f32)).astype(bf16)


def iota(shape, dim):
    return lax.broadcasted_iota(jnp.int32, shape, dim)


def lanes_at(start):
    return pl.ds(pl.multiple_of(start, HEAD), HEAD)


def fold_kernel(weight_ref, rank_in_ref, rank_out_ref, mag_ref, out_ref, column_ref, *, first_slot, moving):
    slot = first_slot + (pl.program_id(0) if moving else 0)
    rows = weight_ref.shape[1]

    def placed_at(start):
        spot = iota((RANK, EXT), 1) == iota((RANK, EXT), 0) + start
        return jnp.where(spot, 1.0, 0.0).astype(bf16)

    @pl.when(pl.program_id(1) == 0)
    def _():
        column_ref[0] = dot_tn(rank_out_ref[0], placed_at(0))
        column_ref[1] = dot_tn(rank_out_ref[0], placed_at(RANK * slot))
        mags = jnp.broadcast_to(mag_ref[0], (8, mag_ref.shape[2]))
        one = jnp.where(iota((8, EXT), 0) == 0, 1.0, 0.0)
        column_ref[2] = lax.dot_general(
            mags, one, (((0,), (0,)), ((), ())), precision=lax.Precision.HIGHEST, preferred_element_type=f32
        )

    own = pl.ds(pl.multiple_of(pl.program_id(1) * rows, 16), rows)
    doubled = (factor * column_ref[0, own, :RANK]).astype(bf16)
    merged = weight_ref[0].astype(f32) + dot_nn(doubled, rank_in_ref[0])
    inverse = 1.0 / jnp.sqrt(jnp.sum(merged * merged, axis=1, keepdims=True))
    scale = column_ref[2, own, :1] * inverse
    folded = (merged * scale).astype(bf16)
    out_ref[0, :, :D] = folded
    ext = column_ref[1, own, :] * (factor * scale)
    for index, part in enumerate(split_low(dot_nt(folded, rank_in_ref[0]))):
        ext = ext + dot_nn(part, placed_at(PROJ_AT + RANK * index))
    lane = iota(ext.shape, 1)
    for index, part in enumerate(split_low(inverse)):
        ext = ext + jnp.where(lane == INV_AT + index, part.astype(f32), 0.0)
    out_ref[0, :, D:] = ext.astype(bf16)


def fold(weights, rank_in_t, rank_out, magnitude, rank_first, moving, name, first=0):
    members, columns = magnitude.shape
    pieces = 4 if columns % 64 == 0 and columns > 256 else 1
    rows = columns // pieces
    rank_block = (lambda b, c: (b + rank_first, 0, 0)) if moving else (lambda b, c: (rank_first, 0, 0))
    return kernel_call(
        functools.partial(fold_kernel, first_slot=rank_first, moving=moving),
        out_shape=shape_of((members, columns, WIDE), bf16),
        grid=(members, pieces),
        in_specs=[
            pl.BlockSpec((1, rows, D), lambda b, c: (b + first, c, 0)),
            pl.BlockSpec((1, RANK, D), rank_block),
            pl.BlockSpec((1, RANK, columns), lambda b, c: (b, 0, 0)),
            pl.BlockSpec((1, 1, columns), lambda b, c: (b, 0, 0)),
        ],
        out_specs=pl.BlockSpec((1, rows, WIDE), lambda b, c: (b, c, 0)),
        scratch_shapes=[pltpu.VMEM((3, columns, EXT), f32)],
        compiler_params=limits(32),
        name=name,
    )(weights, rank_in_t, rank_out, magnitude[:, None, :])


def fold_down_kernel(weight_ref, rank_in_ref, rank_out_ref, mag_ref, out_ref, proj_ref, merged_ref, *, chips):
    rows = weight_ref.shape[0] // chips
    total = 0.0
    doubled = (factor * rank_out_ref[...].astype(f32)).astype(bf16)
    for part in range(chips):
        span = slice(part * rows, (part + 1) * rows)
        merged = weight_ref[span, :].astype(f32) + dot_tn(rank_in_ref[:, span], doubled)
        merged_ref[span, :] = merged
        total = total + jnp.sum(merged * merged, axis=0, keepdims=True)
    inverse = 1.0 / jnp.sqrt(total)
    scale = mag_ref[...] * inverse
    high, low = split_low(inverse)
    row = iota((AUX - RANK, scale.shape[1]), 0)
    tail = jnp.where(row == 0, high.astype(f32), jnp.where(row == 1, low.astype(f32), 0.0))
    aux = jnp.concatenate([doubled.astype(f32) * scale, tail], axis=0).astype(bf16)
    proj = 0.0
    for part in range(chips):
        span = slice(part * rows, (part + 1) * rows)
        folded = (merged_ref[span, :] * scale).astype(bf16)
        out_ref[part, :rows, :] = folded
        out_ref[part, rows:, :] = aux
        proj = proj + dot_nn(rank_in_ref[:, span], folded)
    proj_ref[...] = proj


def fold_down(weights, rank_in_t, rank_out, magnitude, chips):
    inputs, columns = weights.shape
    return kernel_call(
        functools.partial(fold_down_kernel, chips=chips),
        out_shape=(shape_of((chips, inputs // chips + AUX, columns), bf16), shape_of((RANK, columns))),
        scratch_shapes=[pltpu.VMEM((inputs, columns), f32)],
        compiler_params=limits(32),
        name="fold_down",
    )(weights, rank_in_t, rank_out, magnitude[None])


def head_kernel(scalar_ref, first_ref, second_ref, input_ref, cos_ref, sin_ref, *refs, roped):
    before_refs, (weight_ref, out_ref, token_ref) = refs[:-3], refs[-3:]
    members, half = first_ref.shape[0], first_ref.shape[1]
    for member in range(members):
        for order, ref in ((scalar_ref[0], first_ref), (1 - scalar_ref[0], second_ref)):
            weight_ref[pl.ds(pl.multiple_of((2 * member + order) * half, half), half), :] = ref[member]
    wide = members * HEAD
    for index, ref in enumerate(before_refs):
        out_ref[:, pl.ds(pl.multiple_of(scalar_ref[2 + index] * wide, wide), wide)] = ref[...]
    raw = dot_nt(input_ref[...], weight_ref[:, :D])
    for member in range(members):
        part = raw[:, member * HEAD : (member + 1) * HEAD]
        if member < roped:
            part = part * cos_ref[...] + pltpu.roll(part, HEAD // 2, 1) * sin_ref[...]
        start = (scalar_ref[1] * wide if before_refs else 0) + member * HEAD
        out_ref[:, lanes_at(start)] = part.astype(bf16)
    token_ref[...] = jnp.zeros(token_ref.shape, f32)


def head_step(scalars, first, second, inputs, tables, roped, before, name):
    members, half, _ = first.shape
    tokens = inputs.shape[0]
    wide = members * HEAD
    return kernel_call(
        functools.partial(head_kernel, roped=roped),
        out_shape=(
            shape_of((wide, WIDE), bf16),
            shape_of((tokens, (1 + len(before)) * wide), bf16),
            shape_of((8, HEAD)),
        ),
        in_specs=[in_smem] + [in_vmem] * (5 + len(before)),
        out_specs=(in_vmem,) * 3,
        compiler_params=limits(24),
        name=name,
    )(scalars, first, second, inputs, *tables, *before)


def head_copies(weight_ref, head, out_ref, semaphores, first=0):
    devices, members, part = weight_ref.shape[:3]
    parts = devices // KV_HEADS
    copies = []
    for at in range(parts):
        for member in range(members):
            copies.append(
                pltpu.make_async_copy(
                    weight_ref.at[parts * head + at, member],
                    out_ref.at[pl.ds((parts * member + at) * part, part), :],
                    semaphores.at[first + len(copies)],
                )
            )
    return copies


def head_scratch(weights):
    each = weights.shape[0] // KV_HEADS * weights.shape[1]
    return [
        pltpu.VMEM((KV_HEADS, weights.shape[1] * HEAD, WIDE), bf16),
        pltpu.SemaphoreType.DMA((KV_HEADS * each,)),
    ]


def all_head_copies(weight_ref, out_ref, semaphores):
    each = weight_ref.shape[0] // KV_HEADS * weight_ref.shape[1]
    return [head_copies(weight_ref, head, out_ref.at[head], semaphores, head * each) for head in range(KV_HEADS)]


def next_head(copies, head):
    if head == 0:
        for copy in copies[0] + copies[1]:
            copy.start()
    elif head + 1 < len(copies):
        for copy in copies[head + 1]:
            copy.start()
    for copy in copies[head]:
        copy.wait()


def query_kernel(input_ref, cos_ref, sin_ref, weight_hbm, out_ref, weight_ref, semaphores):
    copies = all_head_copies(weight_hbm, weight_ref, semaphores)
    for head in range(KV_HEADS):
        next_head(copies, head)
        raw = dot_nt(input_ref[...], weight_ref[head, :, :D])
        for group in range(GROUP):
            part = raw[:, group * HEAD : (group + 1) * HEAD]
            part = part * cos_ref[...] + pltpu.roll(part, HEAD // 2, 1) * sin_ref[...]
            start = (head * GROUP + group) * HEAD
            out_ref[:, start : start + HEAD] = part.astype(bf16)


def query_project(inputs, tables, weights):
    return kernel_call(
        query_kernel,
        out_shape=shape_of((inputs.shape[0], D), bf16),
        in_specs=[in_vmem] * 3 + [anywhere],
        out_specs=in_vmem,
        scratch_shapes=head_scratch(weights),
        compiler_params=limits(24),
        name="query_project",
    )(inputs, *tables, weights)


def masked_scores(keys, queries, key_first, length, causal):
    tokens, lanes = keys.shape[0], queries.shape[0]
    scores = dot_nt(keys, queries)
    key_pos = key_first + iota((tokens, 1), 0)
    scores = scores + jnp.where(key_pos < length, 0.0, masked_score)
    if causal:
        allowed = iota((tokens, lanes), 0) <= (iota((tokens, lanes), 1) & (tokens - 1))
        scores = jnp.where(allowed, scores, masked_score)
    return scores


def attend_kernel(scalar_ref, query_ref, *refs, steps):
    kv_refs = refs[:steps]
    mixed_ref, lse_ref, stacked_ref, max_ref, sum_ref, accum_ref = refs[steps:]
    head = pl.program_id(0)
    tokens = query_ref.shape[0]
    block_index, length = scalar_ref[0], scalar_ref[1]
    scale = score_scale * log2_e
    for group in range(GROUP):
        stacked_ref[group * tokens : (group + 1) * tokens, :] = query_ref[:, group * HEAD : (group + 1) * HEAD]

    for distance in range(steps):

        def step(distance=distance):
            keys = kv_refs[distance][:, :HEAD]
            values = kv_refs[distance][:, HEAD:]
            key_first = (block_index - distance) * tokens
            scores = masked_scores(keys, stacked_ref[...], key_first, length, distance == 0)
            block_max = jnp.max(scores, axis=0, keepdims=True)
            new_max = block_max if distance == 0 else jnp.maximum(max_ref[...], block_max)
            terms = jnp.exp2((scores - new_max) * scale)
            added = jnp.sum(terms, axis=0, keepdims=True)
            product = dot_tn(values, terms.astype(bf16))
            if distance == 0:
                sum_ref[...] = added
                accum_ref[...] = product
            else:
                fade = jnp.exp2((max_ref[...] - new_max) * scale)
                sum_ref[...] = sum_ref[...] * fade + added
                accum_ref[...] = accum_ref[...] * fade + product
            max_ref[...] = new_max

        if distance == 0:
            step()
        else:
            pl.when(block_index >= distance)(step)
    mixed = accum_ref[...] / sum_ref[...]
    for group in range(GROUP):
        part = mixed[:, group * tokens : (group + 1) * tokens]
        mixed_ref[:, lanes_at(group * KVW + head * HEAD)] = part.T.astype(bf16)
    lse_ref[0] = max_ref[...] * scale + jnp.log(sum_ref[...]) * log2_e


def attend(scalars, queries, kv_blocks):
    tokens = queries.shape[0]
    steps = len(kv_blocks)
    lanes = GROUP * tokens
    return kernel_call(
        functools.partial(attend_kernel, steps=steps),
        out_shape=(shape_of((tokens, D), bf16), shape_of((KV_HEADS, 1, lanes))),
        grid_spec=pltpu.PrefetchScalarGridSpec(
            num_scalar_prefetch=1,
            grid=(KV_HEADS,),
            in_specs=[pl.BlockSpec((tokens, GROUP * HEAD), lambda j, s: (0, j))]
            + [pl.BlockSpec((tokens, 2 * HEAD), lambda j, s: (0, j))] * steps,
            out_specs=(
                pl.BlockSpec((tokens, D), lambda j, s: (0, 0)),
                pl.BlockSpec((1, 1, lanes), lambda j, s: (j, 0, 0)),
            ),
            scratch_shapes=[
                pltpu.VMEM((lanes, HEAD), bf16),
                pltpu.VMEM((1, lanes), f32),
                pltpu.VMEM((1, lanes), f32),
                pltpu.VMEM((HEAD, lanes), f32),
            ],
        ),
        compiler_params=limits(40),
        name="attend",
    )(scalars, queries, *kv_blocks)


def attend_back_kernel(scalar_ref, query_ref, grad_ref, lse_ref, delta_ref, kv_ref, *refs, distance, chained):
    if chained:
        before_ref, grad_query_ref, grad_kv_ref, stacked_ref, stacked_grad_ref = refs
    else:
        grad_query_ref, grad_kv_ref, stacked_ref, stacked_grad_ref = refs
    head = pl.program_id(0)
    tokens = query_ref.shape[0]
    block_index, length = scalar_ref[0], scalar_ref[1]
    active = (block_index >= distance) & (block_index * tokens < length)

    @pl.when(active)
    def _():
        for group in range(GROUP):
            rows = slice(group * tokens, (group + 1) * tokens)
            stacked_ref[rows, :] = query_ref[:, group * HEAD : (group + 1) * HEAD]
            stacked_grad_ref[rows, :] = grad_ref[:, lanes_at(group * KVW + head * HEAD)]
        keys = kv_ref[:, :HEAD]
        values = kv_ref[:, HEAD:]
        key_first = (block_index - distance) * tokens
        scores = masked_scores(keys, stacked_ref[...], key_first, length, distance == 0)
        probs = jnp.exp2(scores * (score_scale * log2_e) - lse_ref[0])
        grad_probs = dot_nt(values, stacked_grad_ref[...])
        grad_scores = (probs * (grad_probs - delta_ref[0])).astype(bf16)
        grad_values = dot_nn(probs.astype(bf16), stacked_grad_ref[...])
        grad_keys = dot_nn(grad_scores, stacked_ref[...]) * score_scale
        grad_queries = dot_tn(grad_scores, keys) * score_scale
        for group in range(GROUP):
            lanes = slice(group * HEAD, (group + 1) * HEAD)
            part = grad_queries[group * tokens : (group + 1) * tokens, :]
            if chained:
                part = part + before_ref[:, lanes]
            grad_query_ref[:, lanes] = part
        grad_kv_ref[:, :HEAD] = grad_keys.astype(grad_kv_ref.dtype)
        grad_kv_ref[:, HEAD:] = grad_values.astype(grad_kv_ref.dtype)

    @pl.when(jnp.logical_not(active))
    def _():
        grad_query_ref[...] = before_ref[...] if chained else jnp.zeros(grad_query_ref.shape, f32)
        grad_kv_ref[...] = jnp.zeros(grad_kv_ref.shape, grad_kv_ref.dtype)


def attend_back(scalars, queries, grad_mixed, lse, delta, kv_block, before, distance):
    tokens = queries.shape[0]
    lanes = GROUP * tokens
    row = pl.BlockSpec((1, 1, lanes), lambda j, s: (j, 0, 0))
    per_query = pl.BlockSpec((tokens, GROUP * HEAD), lambda j, s: (0, j))
    per_key = pl.BlockSpec((tokens, 2 * HEAD), lambda j, s: (0, j))
    chained = before is not None
    operands = [scalars, queries, grad_mixed, lse, delta, kv_block]
    specs = [per_query, pl.BlockSpec((tokens, D), lambda j, s: (0, 0)), row, row, per_key]
    if chained:
        operands += [before]
        specs += [per_query]
    return kernel_call(
        functools.partial(attend_back_kernel, distance=distance, chained=chained),
        out_shape=(shape_of((tokens, D)), shape_of((tokens, 2 * KVW), f32 if distance == 0 else bf16)),
        grid_spec=pltpu.PrefetchScalarGridSpec(
            num_scalar_prefetch=1,
            grid=(KV_HEADS,),
            in_specs=specs,
            out_specs=(per_query, per_key),
            scratch_shapes=[pltpu.VMEM((lanes, HEAD), bf16), pltpu.VMEM((lanes, HEAD), bf16)],
        ),
        input_output_aliases={6: 0} if chained else {},
        compiler_params=limits(40),
        name=f"attend_back_{distance}",
    )(*operands)


def rms_inverse(values):
    return lax.rsqrt(jnp.mean(values * values, axis=-1, keepdims=True) + rms_eps)


def rms_back(values, inverse, gain, grad):
    scaled = grad * gain
    return inverse * (scaled - values * (inverse * inverse * jnp.mean(scaled * values, axis=-1, keepdims=True)))


def output_kernel(mixed_ref, input_ref, gain_ref, weight_hbm, residual_ref, normed_ref, weight_ref, semaphores):
    copies = all_head_copies(weight_hbm, weight_ref, semaphores)
    for head in range(KV_HEADS):
        next_head(copies, head)
        value = dot_nt(mixed_ref[...], weight_ref[head, :, :D])
        for group in range(GROUP):
            start = group * KVW + head * HEAD
            lanes = slice(start, start + HEAD)
            residual_ref[:, lanes] = input_ref[:, lanes].astype(f32) + value[:, group * HEAD : (group + 1) * HEAD]
    values = residual_ref[...]
    normed_ref[...] = (values * rms_inverse(values) * gain_ref[...]).astype(bf16)


def output_project(mixed, weights, inputs, gain):
    tokens = mixed.shape[0]
    return kernel_call(
        output_kernel,
        out_shape=(shape_of((tokens, D)), shape_of((tokens, D), bf16)),
        in_specs=[in_vmem] * 3 + [anywhere],
        out_specs=(in_vmem,) * 2,
        scratch_shapes=head_scratch(weights),
        compiler_params=limits(28),
        name="output_project",
    )(mixed, inputs, gain[None], weights)


def feed_forward_kernel(normed_ref, own_ref, partner_ref, gate_ref, up_ref, weight_ref, semaphores, *, block):
    copies = []
    for half, ref in enumerate((own_ref, partner_ref)):
        for member in range(2):
            at = 2 * half + member
            copies.append(pltpu.make_async_copy(ref.at[member], weight_ref.at[at], semaphores.at[at]))
    copies[0].start()
    copies[1].start()
    for half in range(2):
        for member, out_ref in enumerate((gate_ref, up_ref)):
            at = 2 * half + member
            copies[at].wait()
            if at + 2 < 4:
                copies[at + 2].start()
            for start in range(0, normed_ref.shape[0], block):
                rows = slice(start, start + block)
                out_ref[half, rows, :] = dot_nt(normed_ref[rows, :], weight_ref[at, :, :D])


def feed_forward(normed, own, partner, block):
    tokens = normed.shape[0]
    columns = own.shape[1]
    return kernel_call(
        functools.partial(feed_forward_kernel, block=block),
        out_shape=(shape_of((2, tokens, columns)), shape_of((2, tokens, columns))),
        in_specs=[in_vmem, anywhere, anywhere],
        out_specs=(in_vmem,) * 2,
        scratch_shapes=[pltpu.VMEM((4, columns, WIDE), bf16), pltpu.SemaphoreType.DMA((4,))],
        compiler_params=limits(24),
        name="feed_forward",
    )(normed, own, partner)


def grad_copies(place_ref, grad_hbm, grad_ref, semaphores, chips, block, first):
    return [
        pltpu.make_async_copy(
            grad_hbm.at[0 if r is None else place_ref[1] ^ (2 * r)], grad_ref.at[pl.ds(turn * block, block), :], semaphores.at[first + turn]
        )
        for turn, r in enumerate(chips)
    ]


def feed_back_kernel(place_ref, grad_hbm, gate_ref, up_ref, own_ref, partner_ref, *refs, block, devices, chips):
    piece_refs, refs = refs[:devices], refs[devices:]
    share_refs, down_refs, refs = refs[: len(chips)], refs[len(chips) : 2 * len(chips)], refs[2 * len(chips) :]
    ext_ref, hidden_ref, grad_gate_ref, grad_up_ref, down_ext_ref, mag_ref, down_mag_ref = refs[:7]
    aux_ref, weight_ref, down_weight_ref, grad_ref, semaphores = refs[7:]
    core = place_ref[0]
    columns = own_ref.shape[1]
    width = piece_refs[0].shape[1]
    copies = grad_copies(place_ref, grad_hbm, grad_ref, semaphores, chips, block, devices + 2)
    for i, ref in enumerate(piece_refs):
        lanes = pl.ds(pl.multiple_of((place_ref[1] ^ i) * width, width), width)
        copies.append(pltpu.make_async_copy(ref, down_weight_ref.at[:, lanes], semaphores.at[i]))
    for copy in copies:
        copy.start()
    weight_copies = [
        pltpu.make_async_copy(ref, weight_ref.at[half], semaphores.at[devices + half])
        for half, ref in enumerate((own_ref, partner_ref))
    ]
    mag_ref[...] = jnp.zeros(mag_ref.shape, f32)
    down_mag_ref[...] = jnp.zeros(down_mag_ref.shape, f32)
    weight_copies[0].start()
    for copy in copies:
        copy.wait()
    weight_copies[1].start()
    aux_ref[...] = down_weight_ref[2 * columns :, :]

    def step(turn, carry):
        rows = pl.ds(pl.multiple_of(turn * block, block), block)
        grad = grad_ref[rows, :]
        down_ext_ref[rows, :] = dot_nt(grad, down_weight_ref[2 * columns :, :]).astype(bf16)
        share, down = None, None
        for half in range(2):
            order = core if half == 0 else 1 - core
            down_rows = pl.ds(pl.multiple_of(order * columns, 16), columns)
            gate, up = gate_ref[half, rows, :], up_ref[half, rows, :]
            grad_hidden = dot_nt(grad, down_weight_ref[down_rows, :])
            sigma = 1.0 / (1.0 + jnp.exp(-gate))
            silu = gate * sigma
            hidden = (silu * up).astype(bf16)
            grad_gate = grad_hidden * up * (sigma + silu * (1.0 - sigma))
            grad_up = grad_hidden * silu
            mag_ref[half : half + 1, :] += jnp.sum(grad_gate * gate, axis=0, keepdims=True)
            mag_ref[2 + half : 3 + half, :] += jnp.sum(grad_up * up, axis=0, keepdims=True)
            grad_gate, grad_up = grad_gate.astype(bf16), grad_up.astype(bf16)
            hidden_ref[half, rows, :] = hidden
            grad_gate_ref[half, rows, :] = grad_gate
            grad_up_ref[half, rows, :] = grad_up
            part = dot_nn(hidden, down_weight_ref[down_rows, :])
            down = part if down is None else down + part
            pl.when(turn == 0)(weight_copies[half].wait)
            part = dot_nn(grad_gate, weight_ref[half, 0]) + dot_nn(grad_up, weight_ref[half, 1])
            share = part if share is None else share + part
        ext_ref[rows, :] = share[:, D:].astype(bf16)
        for at in range(len(chips)):

            @pl.when((turn ^ core if len(chips) == 2 else turn) == at)
            def _(at=at):
                share_refs[at][...] = share[:, :D].astype(bf16)
                down_refs[at][...] = down.astype(bf16)

        down_mag_ref[0:1, :] += jnp.sum(grad.astype(f32) * down, axis=0, keepdims=True)
        return carry

    lax.fori_loop(0, len(chips), step, 0)


def feed_back(place, grads, chips, gate, up, own, partner, pieces, block):
    tokens = len(chips) * block
    columns = own.shape[1]
    devices = len(pieces)
    return kernel_call(
        functools.partial(feed_back_kernel, block=block, devices=devices, chips=chips),
        out_shape=(shape_of((block, D), bf16),) * (2 * len(chips))
        + (
            shape_of((tokens, EXT), bf16),
            shape_of((2, tokens, columns), bf16),
            shape_of((2, tokens, columns), bf16),
            shape_of((2, tokens, columns), bf16),
            shape_of((tokens, AUX), bf16),
            shape_of((4, columns)),
            shape_of((8, D)),
            shape_of((AUX, D), bf16),
        ),
        in_specs=[in_smem, anywhere, in_vmem, in_vmem] + [anywhere] * (2 + devices),
        out_specs=(in_vmem,) * (8 + 2 * len(chips)),
        scratch_shapes=[
            pltpu.VMEM((2, 2, columns, WIDE), bf16),
            pltpu.VMEM((2 * columns + AUX, D), bf16),
            pltpu.VMEM((tokens, D), bf16),
            pltpu.SemaphoreType.DMA((2 + devices + len(chips),)),
        ],
        compiler_params=limits(40),
        name="feed_back",
    )(place, grads, gate, up, own, partner, *pieces)


def feed_adapter_kernel(
    place_ref, normed_ref, grad_hbm, hidden_ref, grad_gate_ref, grad_up_ref, ext_ref, down_ext_ref, rank_in_ref,
    down_in_ref, in_ref, out_ref, down_rank_in_ref, down_out_ref, grad_ref, semaphores, *, chips, block,
):
    copies = grad_copies(place_ref, grad_hbm, grad_ref, semaphores, chips, block, 0)
    for copy in copies:
        copy.start()
    normed = normed_ref[...]
    small = dot_nt(rank_in_ref[...], normed).astype(bf16)
    in_ref[...] = dot_nn(ext_ref[...].T[: 2 * RANK], normed)
    down_small = 0.0
    grad_small = down_ext_ref[...].T[:RANK]
    for half in range(2):
        hidden = hidden_ref[half]
        out_ref[half, :RANK] = dot_nn(small[:RANK], grad_gate_ref[half])
        out_ref[half, RANK:] = dot_nn(small[RANK:], grad_up_ref[half])
        down_small = down_small + dot_nt(down_in_ref[half], hidden)
        down_rank_in_ref[half] = dot_nn(grad_small, hidden)
    for copy in copies:
        copy.wait()
    down_out_ref[...] = dot_nn(down_small.astype(bf16), grad_ref[...])


def feed_adapter(place, normed, grads, chips, hidden, grad_gate, grad_up, ext, down_ext, rank_in_t, down_in_t):
    columns = hidden.shape[2]
    return kernel_call(
        functools.partial(feed_adapter_kernel, chips=chips, block=normed.shape[0] // len(chips)),
        out_shape=(
            shape_of((2 * RANK, D)),
            shape_of((2, 2 * RANK, columns)),
            shape_of((2, RANK, columns)),
            shape_of((RANK, D)),
        ),
        in_specs=[in_smem, in_vmem, anywhere] + [in_vmem] * 7,
        out_specs=(in_vmem,) * 4,
        scratch_shapes=[pltpu.VMEM(normed.shape, bf16), pltpu.SemaphoreType.DMA((len(chips),))],
        compiler_params=limits(24),
        name="feed_adapter",
    )(place, normed, grads, hidden, grad_gate, grad_up, ext, down_ext, rank_in_t, down_in_t)


def adapter_columns(products, mag_raw, mag, weights, slot):
    ext = weights[:, D:].astype(f32).T
    inverse = ext[INV_AT : INV_AT + 1] + ext[INV_AT + 1 : INV_AT + 2]
    proj = ext[PROJ_AT : PROJ_AT + RANK] + ext[PROJ_AT + RANK : PROJ_AT + 2 * RANK]
    grad_mag = mag_raw / mag
    grad_out = factor * (products * (mag * inverse) - proj * (grad_mag * inverse))
    turned = ext[RANK * slot : RANK * (slot + 1)] * (-grad_mag / mag)
    return grad_mag, grad_out, dot_nn(turned.astype(bf16), weights[:, :D])


def finish_kernel(weight_ref, products_ref, mag_raw_ref, mag_ref, grad_mag_ref, grad_out_ref, grad_in_ref):
    for slot in range(2):
        grad_mag, grad_out, grad_in = adapter_columns(
            products_ref[slot * RANK : (slot + 1) * RANK],
            mag_raw_ref[slot : slot + 1],
            mag_ref[slot : slot + 1],
            weight_ref[slot],
            slot,
        )
        grad_mag_ref[slot : slot + 1] = grad_mag
        grad_out_ref[slot * RANK : (slot + 1) * RANK] = grad_out
        grad_in_ref[slot * RANK : (slot + 1) * RANK] = grad_in


def finish_columns(weights, products, mag_raw, mag):
    columns = weights.shape[1]
    return kernel_call(
        finish_kernel,
        out_shape=(shape_of((2, columns)), shape_of((2 * RANK, columns)), shape_of((2 * RANK, D))),
        compiler_params=limits(40),
        name="feed_finish",
    )(weights, products, mag_raw, mag)


def output_adapter_kernel(
    grad_ref, mag_raw_ref, mag_ref, mixed_ref, ext_ref, rank_in_ref, weight_hbm,
    grad_mag_ref, grad_out_ref, grad_in_ref, weight_ref, semaphores,
):
    copies = all_head_copies(weight_hbm, weight_ref, semaphores)
    small = dot_nt(rank_in_ref[...], mixed_ref[...]).astype(bf16)
    grad_in_total = dot_nn(ext_ref[...].T[:RANK], mixed_ref[...])
    wide = GROUP * HEAD
    for head in range(KV_HEADS):
        next_head(copies, head)
        lanes = slice(head * wide, (head + 1) * wide)
        place = slice(head * HEAD, (head + 1) * HEAD)
        mag = jnp.concatenate([mag_ref[group : group + 1, place] for group in range(GROUP)], axis=1)
        grad_mag, grad_out, grad_in = adapter_columns(
            dot_nn(small, grad_ref[:, lanes]), mag_raw_ref[:, lanes], mag, weight_ref[head], 0
        )
        for group in range(GROUP):
            own = slice(group * HEAD, (group + 1) * HEAD)
            at = slice(group * KVW + head * HEAD, group * KVW + (head + 1) * HEAD)
            grad_mag_ref[:, at] = grad_mag[:, own]
            grad_out_ref[:, at] = grad_out[:, own]
        grad_in_total = grad_in_total + grad_in
    grad_in_ref[...] = grad_in_total


def output_adapter(grads, mag_raw, mag, weights, mixed, ext, rank_in_t):
    return kernel_call(
        output_adapter_kernel,
        out_shape=(shape_of((1, D)), shape_of((RANK, D)), shape_of((RANK, D))),
        in_specs=[in_vmem] * 6 + [anywhere],
        out_specs=(in_vmem,) * 3,
        scratch_shapes=head_scratch(weights),
        compiler_params=limits(28),
        name="output_adapter",
    )(grads, mag_raw, mag, mixed, ext, rank_in_t, weights)


def residual_back_kernel(
    first_ref, second_ref, third_ref, residual_ref, gain_ref, cotangent_ref, input_ref, mixed_ref, weight_hbm,
    grad_ref, ordered_ref, mag_ref, ext_ref, grad_mixed_ref, delta_ref, weight_ref, semaphores, column_ref,
):
    tokens = residual_ref.shape[0]
    copies = all_head_copies(weight_hbm, weight_ref, semaphores)
    for head in range(KV_HEADS):
        for copy in copies[head]:
            copy.start()
    normed_grad = first_ref[...].astype(f32) + second_ref[...].astype(f32) + third_ref[...].astype(f32)
    values = residual_ref[...]
    grad_ref[...] = cotangent_ref[...].astype(f32) + rms_back(
        values, rms_inverse(values), gain_ref[...], normed_grad
    )
    wide = GROUP * HEAD
    total = None
    for head in range(KV_HEADS):
        for group in range(GROUP):
            start = group * KVW + head * HEAD
            lanes = slice(start, start + HEAD)
            own = slice(head * wide + group * HEAD, head * wide + (group + 1) * HEAD)
            grad = grad_ref[:, lanes]
            ordered_ref[:, own] = grad.astype(bf16)
            value = residual_ref[:, lanes] - input_ref[:, lanes].astype(f32)
            mag_ref[:, own] = jnp.sum(grad * value, axis=0, keepdims=True)
        for copy in copies[head]:
            copy.wait()
        part = dot_nn(ordered_ref[:, head * wide : (head + 1) * wide], weight_ref[head])
        total = part if total is None else total + part
    ext_ref[...] = total[:, D:].astype(bf16)
    grad_mixed_ref[...] = total[:, :D].astype(bf16)
    for head in range(KV_HEADS):
        for group in range(GROUP):
            start = group * KVW + head * HEAD
            lanes = slice(start, start + HEAD)
            both = grad_mixed_ref[:, lanes].astype(f32) * mixed_ref[:, lanes].astype(f32)
            column_ref[:, head * GROUP + group : head * GROUP + group + 1] = jnp.sum(both, axis=1, keepdims=True)
    rows = column_ref[...].T
    for head in range(KV_HEADS):
        for group in range(GROUP):
            at = head * GROUP + group
            delta_ref[head, :, group * tokens : (group + 1) * tokens] = rows[at : at + 1]


def residual_back(shares, residual, gain, cotangent, inputs, mixed, weights):
    tokens = residual.shape[0]
    lanes = GROUP * tokens
    return kernel_call(
        residual_back_kernel,
        out_shape=(
            shape_of((tokens, D)),
            shape_of((tokens, D), bf16),
            shape_of((1, D)),
            shape_of((tokens, EXT), bf16),
            shape_of((tokens, D), bf16),
            shape_of((KV_HEADS, 1, lanes)),
        ),
        in_specs=[in_vmem] * 8 + [anywhere],
        out_specs=(in_vmem,) * 6,
        scratch_shapes=head_scratch(weights) + [pltpu.VMEM((tokens, HEAD), f32)],
        compiler_params=limits(40),
        name="residual_back",
    )(*shares, residual, gain[None], cotangent, inputs, mixed, weights)


def turn_back(values, cosine, sine):
    return values * cosine - pltpu.roll(values, HEAD // 2, 1) * sine


def query_back_kernel(
    grad_ref, query_ref, cos_ref, sin_ref, normed_ref, rank_in_ref, mag_ref, weight_hbm,
    accum_ref, grad_in_ref, out_ref, grad_mag_ref, turned_ref, weight_ref, semaphores,
):
    copies = all_head_copies(weight_hbm, weight_ref, semaphores)
    wide = GROUP * HEAD
    small = dot_nt(rank_in_ref[...], normed_ref[...]).astype(bf16)
    total, grad_in_total = None, None
    for head in range(KV_HEADS):
        mags = []
        for group in range(GROUP):
            lanes = slice(head * wide + group * HEAD, head * wide + (group + 1) * HEAD)
            grad = turn_back(grad_ref[:, lanes], cos_ref[...], sin_ref[...])
            raw = turn_back(query_ref[:, lanes].astype(f32), cos_ref[...], sin_ref[...])
            mags.append(jnp.sum(grad * raw, axis=0, keepdims=True))
            turned_ref[:, lanes] = grad.astype(bf16)
        turned = turned_ref[:, head * wide : (head + 1) * wide]
        next_head(copies, head)
        part = dot_nn(turned, weight_ref[head])
        total = part if total is None else total + part
        place = slice(head * HEAD, (head + 1) * HEAD)
        mag = jnp.concatenate([mag_ref[group : group + 1, place] for group in range(GROUP)], axis=1)
        grad_mag, grad_out, grad_in = adapter_columns(
            dot_nn(small, turned), jnp.concatenate(mags, axis=1), mag, weight_ref[head], 0
        )
        grad_in_total = grad_in if grad_in_total is None else grad_in_total + grad_in
        for group in range(GROUP):
            own = slice(group * HEAD, (group + 1) * HEAD)
            at = slice(group * KVW + head * HEAD, group * KVW + (head + 1) * HEAD)
            grad_mag_ref[:, at] = grad_mag[:, own]
            out_ref[:, at] = grad_out[:, own]
    accum_ref[...] = total
    grad_in_ref[...] = grad_in_total + dot_nn(total[:, D:].astype(bf16).T[:RANK], normed_ref[...])


def query_back(grads, queries, weights, cosine, sine, normed, rank_in_t, mag):
    tokens = normed.shape[0]
    return kernel_call(
        query_back_kernel,
        out_shape=(
            shape_of((tokens, WIDE)),
            shape_of((RANK, D)),
            shape_of((RANK, D)),
            shape_of((1, D)),
        ),
        in_specs=[in_vmem] * 7 + [anywhere],
        out_specs=(in_vmem,) * 4,
        scratch_shapes=[pltpu.VMEM((tokens, D), bf16)] + head_scratch(weights),
        compiler_params=limits(40),
        name="query_back",
    )(grads, queries, cosine, sine, normed, rank_in_t, mag, weights)


def key_back_kernel(
    heads_ref, sent_ref, grad_ref, kv_ref, cos_ref, sin_ref, normed_ref, input_ref, gain_ref, residual_ref,
    before_ref, rank_in_ref, mag_ref, *refs,
):
    weight_refs = refs[:KV_HEADS]
    input_grad_ref, grad_in_ref, out_ref, grad_mag_ref, turned_ref = refs[KV_HEADS:]
    small = dot_nt(rank_in_ref[...], normed_ref[...]).astype(bf16)
    total = before_ref[...]
    near = 2 * HEAD
    grad_ins = [None, None]
    for slot in range(KV_HEADS):
        place = heads_ref[slot] * HEAD
        mags = []
        for part in range(2):
            lanes = lanes_at(2 * place + part * HEAD)
            grad = grad_ref[:, lanes] + sent_ref[:, lanes].astype(f32)
            raw = kv_ref[:, lanes].astype(f32)
            if part == 0:
                grad = turn_back(grad, cos_ref[...], sin_ref[...])
                raw = turn_back(raw, cos_ref[...], sin_ref[...])
            mags.append(jnp.sum(grad * raw, axis=0, keepdims=True))
            turned_ref[:, slot * near + part * HEAD : slot * near + (part + 1) * HEAD] = grad.astype(bf16)
        total = total + dot_nn(turned_ref[:, slot * near : (slot + 1) * near], weight_refs[slot][...])
        for part in range(2):
            lanes = slice(slot * near + part * HEAD, slot * near + (part + 1) * HEAD)
            grad_mag, grad_out, grad_in = adapter_columns(
                dot_nn(small[part * RANK : (part + 1) * RANK], turned_ref[:, lanes]),
                mags[part],
                mag_ref[part : part + 1, lanes_at(place)],
                weight_refs[slot][part * HEAD : (part + 1) * HEAD, :],
                1 + part,
            )
            grad_mag_ref[:, lanes_at(part * KVW + place)] = grad_mag
            out_ref[:, lanes_at(part * KVW + place)] = grad_out
            grad_ins[part] = grad_in if grad_ins[part] is None else grad_ins[part] + grad_in
    ext = total[:, D:].astype(bf16).T
    for part in range(2):
        rows = slice(part * RANK, (part + 1) * RANK)
        grad_in_ref[rows] = grad_ins[part] + dot_nn(ext[(1 + part) * RANK : (2 + part) * RANK], normed_ref[...])
    values = input_ref[...].astype(f32)
    back = rms_back(values, rms_inverse(values), gain_ref[...], total[:, :D])
    input_grad_ref[...] = (residual_ref[...] + back).astype(bf16)


def key_back(heads, sent, grads, kv, weights, cosine, sine, normed, inputs, gain, grad_residual, before, rank_in_t, mag):
    tokens = normed.shape[0]
    return kernel_call(
        key_back_kernel,
        out_shape=(
            shape_of((tokens, D), bf16),
            shape_of((2 * RANK, D)),
            shape_of((RANK, 2 * KVW)),
            shape_of((1, 2 * KVW)),
        ),
        in_specs=[in_smem] + [in_vmem] * (12 + KV_HEADS),
        out_specs=(in_vmem,) * 4,
        scratch_shapes=[pltpu.VMEM((tokens, 2 * KVW), bf16)],
        compiler_params=limits(40),
        name="key_back",
    )(
        heads, sent, grads, kv, cosine, sine, normed, inputs, gain[None], grad_residual,
        before, rank_in_t, mag, *weights,
    )


def cut_kernel(place_ref, value_ref, *out_refs):
    rows = out_refs[0].shape[0]
    for r, ref in enumerate(out_refs):
        ref[...] = value_ref[pl.ds(pl.multiple_of((place_ref[2] ^ r) * rows, rows), rows), :]


def cut_rows(place, value, chips):
    shape = shape_of((value.shape[0] // chips, value.shape[1]), value.dtype)
    return kernel_call(
        cut_kernel,
        out_shape=(shape,) * chips,
        in_specs=[in_smem, in_vmem],
        out_specs=(in_vmem,) * chips,
        name="cut_rows",
    )(place, value)


def join_kernel(place_ref, *refs):
    piece_refs, out_ref = refs[:-1], refs[-1]
    rows = piece_refs[0].shape[0]
    for r, ref in enumerate(piece_refs):
        out_ref[pl.ds(pl.multiple_of((place_ref[2] ^ r) * rows, rows), rows), :] = ref[...]


def join_rows(place, pieces):
    rows, lanes = pieces[0].shape
    return kernel_call(
        join_kernel,
        out_shape=shape_of((rows * len(pieces), lanes), pieces[0].dtype),
        in_specs=[in_smem] + [in_vmem] * len(pieces),
        out_specs=in_vmem,
        name="join_rows",
    )(place, *pieces)


class Order:
    def __init__(self):
        self.last = None

    def __call__(self, *values):
        if self.last is not None:
            values = lax.optimization_barrier(tuple(values) + (self.last,))[:-1]
        return values[0] if len(values) == 1 else values

    def mark(self, value):
        self.last = value
        return value

    def pin(self, *values):
        values = self(*values)
        self.last = values[0] if isinstance(values, (tuple, list)) else values
        return values


def after(value, *others):
    return lax.optimization_barrier((value,) + others)[0]


class Links:
    def __init__(self, devices, blocks):
        self.devices = devices
        self.blocks = blocks
        self.chips = devices // 2
        self.index = lax.axis_index("dp")
        self.core = self.index % 2
        self.chip = self.index // 2
        self.block = lax.axis_index("blk")
        self.square = self.chips == 4
        self.place = jnp.stack([self.core, self.index, self.chip]).astype(jnp.int32)

    def swap(self, value, bits):
        return lax.ppermute(value, "dp", [(i, i ^ bits) for i in range(self.devices)])

    def split_swap(self, value, even_bits, odd_bits):
        return lax.ppermute(
            value, "dp", [(i, i ^ (odd_bits if i % 2 else even_bits)) for i in range(self.devices)]
        )

    def row_swap(self, value, bits):
        return lax.ppermute(value, "blk", [(i, i ^ bits) for i in range(self.blocks)])

    def row_shift(self, value, distance):
        pairs = [(i, i + distance) for i in range(self.blocks) if 0 <= i + distance < self.blocks]
        return lax.ppermute(value, "blk", pairs)

    def sides(self, value):
        return self.swap(value, 2), self.swap(value, 4)

    def across(self, side, other):
        return self.split_swap(jnp.where(self.core == 0, other, side), 2, 4)

    def total(self, value, order):
        part = value.shape[1] // 2
        value = value.astype(bf16)
        cut = lambda core: lax.dynamic_slice_in_dim(value, core * part, part, 1)
        sent = self.swap(cut(1 - self.core), 1)
        kept = cut(self.core)
        yield
        sent = order(sent)
        value = (kept.astype(f32) + sent.astype(f32)).astype(bf16)
        cuts = cut_rows(self.place, value, self.chips)
        order.mark(cuts[0])
        sent = [self.swap(cuts[r], 2 * r) for r in range(1, self.chips)]
        yield
        sent = order(*sent)
        value = order.mark(sum([cuts[0].astype(f32)] + [part.astype(f32) for part in sent]).astype(bf16))
        bits = 1
        while bits < self.blocks:
            sent = self.row_swap(value, bits)
            yield
            sent = order(sent)
            value = order.mark((value.astype(f32) + sent.astype(f32)).astype(bf16))
            bits *= 2
        sent = [self.swap(value, 2 * r) for r in range(1, self.chips)]
        yield
        sent = order(*sent)
        value = order.mark(join_rows(self.place, [value, *sent]))
        sent = self.swap(value, 1)
        yield
        sent = order(sent)
        pair = lambda first, second: jnp.concatenate([first, second], axis=1)
        yield jnp.where(self.core == 0, pair(value, sent), pair(sent, value)).astype(f32)

    def small_total(self, value, order):
        for swap, count in ((self.swap, self.devices), (self.row_swap, self.blocks)):
            bits = 1
            while bits < count:
                sent = swap(value, bits)
                yield
                sent = order(sent)
                value = order.mark(value + sent)
                bits *= 2
        yield value


def shards(
    block_input,
    out_cotangent,
    row_lengths,
    rope_positions,
    gain_attention,
    gain_feedforward,
    base_attention,
    base_output,
    base_feedforward,
    base_down,
    rank_in_attention,
    rank_out_attention,
    magnitude_attention,
    rank_in_output,
    rank_out_output,
    magnitude_output,
    rank_in_feedforward,
    rank_out_feedforward,
    magnitude_feedforward,
    rank_in_down,
    rank_out_down,
    magnitude_down,
    *,
    devices,
    blocks,
):
    links = Links(devices, blocks)
    order = Order()
    mark = order.mark
    index, core, chip, chips = links.index, links.core, links.chip, links.chips
    place = links.place
    partner = lambda value: links.swap(value, 1)
    rows_in = block_input[0]
    tokens = rows_in.shape[0]
    length = row_lengths[0]
    token_pos = links.block * tokens + jnp.arange(tokens, dtype=jnp.int32)
    fast = links.square and base_attention.shape[2] * devices == KVW and blocks == 4
    heads = jnp.arange(KV_HEADS, dtype=jnp.int32)
    heads = chip ^ heads if fast else heads
    scalars = jnp.stack([links.block.astype(jnp.int32), length])

    def columns_of(value, width):
        return lax.dynamic_slice_in_dim(value, index * width, width, value.ndim - 1)

    attn_cols, out_cols = base_attention.shape[2], base_output.shape[2]
    feed_cols, down_cols = base_feedforward.shape[2], base_down.shape[1]
    chip_cols = 2 * feed_cols
    attn_rank = columns_of(rank_out_attention, attn_cols)
    attn_mag = columns_of(magnitude_attention, attn_cols)
    attn_base = base_attention.transpose(0, 2, 1)
    attn_in_t = rank_in_attention.transpose(0, 2, 1)
    out_in_t = rank_in_output.T
    feed_in_t = rank_in_feedforward.transpose(0, 2, 1)
    down_in_t = rank_in_down.T

    def fold_out():
        return fold(
            order(base_output).transpose(0, 2, 1),
            out_in_t[None],
            columns_of(rank_out_output, out_cols),
            columns_of(magnitude_output, out_cols),
            0,
            False,
            "fold_o",
        )

    def fold_feed():
        return fold(
            order(base_feedforward).transpose(0, 2, 1),
            feed_in_t,
            columns_of(rank_out_feedforward, feed_cols),
            columns_of(magnitude_feedforward, feed_cols),
            0,
            True,
            "fold_feed",
        )

    def folded_down():
        return fold_down(
            order(base_down),
            down_in_t,
            columns_of(rank_out_down, down_cols),
            columns_of(magnitude_down, down_cols),
            chips,
        )

    def norm_in():
        values = order(rows_in).astype(f32)
        return (values * rms_inverse(values) * gain_attention).astype(bf16)

    frequency = rope_base ** (-(jnp.arange(HEAD // 2, dtype=f32) * 2.0) / HEAD)
    angles = rope_positions[0].astype(f32)[:, None] * frequency[None, :]
    cos_half, sin_half = jnp.cos(angles), jnp.sin(angles)
    cosine = jnp.concatenate([cos_half, cos_half], axis=-1)
    sine = jnp.concatenate([-sin_half, sin_half], axis=-1)
    tables = (cosine, sine)

    wheres = [jnp.stack([core, chip ^ r, chip, chip ^ 1, chip ^ 2]).astype(jnp.int32) for r in range(KV_HEADS)]

    settle = order.pin

    def project(where, first, second, roped, name, before=()):
        first, second = order(first, second)
        weights, out, token = head_step(where, first, second, normed, tables, roped, before, name)
        mark(token)
        return weights, out

    def send_kv(kv_blocks):
        kv_blocks.append(links.row_shift(kv_blocks[-1], 1))

    kv_fold = mark(
        fold(attn_base, attn_in_t, attn_rank[GROUP:], attn_mag[GROUP:], 1, True, "fold_kv", first=GROUP)
    )
    down_cut = lambda r: lax.dynamic_index_in_dim(down_fold, chip ^ r, 0, keepdims=False)
    spread = lambda value: lax.all_gather(value, "dp", axis=0)
    grad_out = jnp.where((token_pos < length)[:, None], out_cotangent[0], jnp.zeros((), bf16))
    grad_own = grad_out[None]
    chip_in_t = lax.dynamic_slice_in_dim(down_in_t, chip * chip_cols, chip_cols, 1)
    halves_in_t = jnp.stack(
        [lax.dynamic_slice_in_dim(chip_in_t, at * feed_cols, feed_cols, 1) for at in (core, 1 - core)]
    )
    feed_mag = lax.dynamic_slice_in_dim(magnitude_feedforward, chip * chip_cols, chip_cols, 1)
    if fast:
        kv_side, kv_other = links.sides(kv_fold)
        kv_partner = partner(kv_fold)
        q_fold = mark(fold(order(attn_base), attn_in_t, attn_rank[:GROUP], attn_mag[:GROUP], 0, False, "fold_q"))
        q_weights = spread(q_fold)
        kv_side, kv_other, kv_partner = settle(kv_side, kv_other, kv_partner)
        kv_across = links.across(kv_side, kv_other)
        kv_side_p, kv_other_p = partner(kv_side), partner(kv_other)
        o_fold = mark(fold_out())
        o_weights = spread(after(o_fold, q_fold))
        normed = mark(norm_in())
        kv_made = [
            project(wheres[0], kv_fold, kv_partner, 1, "head_kv"),
            project(wheres[1], kv_side, kv_side_p, 1, "head_kv"),
            project(wheres[2], kv_other, kv_other_p, 1, "head_kv"),
        ]
        kv_across = settle(kv_across)
        kv_across_p = partner(kv_across)
        kv_made.append(project(wheres[3], kv_across, kv_across_p, 1, "head_kv", [out for _, out in kv_made]))
        kv_own = kv_made[-1][1]
        kv_blocks = [kv_own]
        send_kv(kv_blocks)
        grad_own, halves_in_t, feed_mag = settle(grad_own, halves_in_t, feed_mag)
        feed_own = mark(fold_feed())
        kv_blocks[1] = settle(kv_blocks[1])
        send_kv(kv_blocks)
        down_fold, down_proj = folded_down()
        mark(down_proj)
        down_0, down_c1, down_c2, down_c3 = settle(*[down_cut(r) for r in range(4)])
        grad_all = spread(order(grad_out))
        kv_blocks[2] = settle(kv_blocks[2])
        send_kv(kv_blocks)
        queries = mark(query_project(order(normed), tables, q_weights))
        kv_blocks[3] = settle(kv_blocks[3])
        down_1, down_2, down_3 = links.swap(down_c1, 2), links.swap(down_c2, 4), links.swap(down_c3, 6)
        mixed, lse = attend(scalars, order(queries), kv_blocks)
        mark(lse)
        down_1, down_2, down_3 = settle(down_1, down_2, down_3)
        down_pieces = [down_0, None, down_1, None, down_2, None, down_3, None]
        for at in range(0, 8, 2):
            down_pieces[at + 1] = partner(order(down_pieces[at]))
        feed_partner = partner(order(feed_own))

        def feed_late():
            down_pieces[1::2] = settle(*down_pieces[1::2])
    else:
        q_fold = fold(attn_base, attn_in_t, attn_rank[:GROUP], attn_mag[:GROUP], 0, False, "fold_q")
        q_weights, o_weights, normed = spread(q_fold), spread(fold_out()), norm_in()
        down_fold, down_proj = folded_down()
        feed_own = fold_feed()
        feed_partner = partner(feed_own)
        whole = lax.all_gather(kv_fold, "dp", axis=1, tiled=True).reshape(2, KV_HEADS, 2, HEAD // 2, WIDE)
        kv_made = []
        for j in range(KV_HEADS):
            before = [out for _, out in kv_made] if j == KV_HEADS - 1 else ()
            where = jnp.array([0, j, 0, 1, 2], jnp.int32)
            kv_made.append(project(where, whole[:, j, 0], whole[:, j, 1], 1, "head_kv", before))
        kv_own = kv_made[-1][1]
        kv_blocks = [kv_own]
        for _ in range(1, blocks):
            send_kv(kv_blocks)
        queries = query_project(normed, tables, q_weights)
        grad_all = spread(grad_out)
        mixed, lse = attend(scalars, queries, kv_blocks)
        down_pieces = []
        for r in range(chips):
            piece = links.swap(down_cut(r), 2 * r) if r else down_cut(r)
            down_pieces += [piece, partner(piece)]
    residual, normed_feed = output_project(order(mixed), o_weights, rows_in, gain_feedforward)
    mark(normed_feed)

    forward = lambda normed_group: settle(*feed_forward(order(normed_group), feed_own, feed_partner, tokens))
    aux = []

    def backward(members, kept):
        grads = grad_own if members == (None,) else grad_all
        made = feed_back(place, grads, members, *order(*kept), feed_own, feed_partner, down_pieces, tokens)
        mark(made[0])
        count = len(members)
        return made[:count], made[count : 2 * count], made[2 * count :]

    def adapters(members, normed_group, made):
        ext, hidden, grad_gate, grad_up, down_ext, mag_sum, down_mag, down_aux = made[2]
        parts = feed_adapter(
            place, order(normed_group), grad_own if members == (None,) else grad_all, members, hidden, grad_gate, grad_up, ext, down_ext,
            feed_in_t.reshape(2 * RANK, D), halves_in_t,
        )
        mark(parts[0])
        aux.append(down_aux)
        return tuple(parts) + (mag_sum, down_mag)

    if fast:
        side, other = links.sides(normed_feed)
        kept = forward(normed_feed)
        feed_late()
        own_made = backward((None,), kept)
        side, other = settle(side, other)
        crossed = links.across(side, other)
        near = settle(jnp.concatenate([side, other]))
        near_kept = forward(near)
        own_sums = adapters((None,), normed_feed, own_made)
        crossed = settle(crossed)
        far_kept = forward(crossed)
        far_made = backward((3,), far_kept)
        from_far = links.split_swap(far_made[0][0], 2, 4)
        near_made = backward((1, 2), near_kept)
        early_first = links.split_swap(near_made[0][0], 2, 4)
        from_far = settle(from_far)
        late_share = settle((near_made[0][1].astype(f32) + from_far.astype(f32)).astype(bf16))
        early_second = links.split_swap(late_share, 4, 2)
        down_mag_steps = links.small_total(own_made[2][6][:1] + near_made[2][6][:1] + far_made[2][6][:1], order)
        next(down_mag_steps)
        near_sums = adapters((1, 2), near, near_made)
        next(down_mag_steps)
        far_sums = adapters((3,), crossed, far_made)
        next(down_mag_steps)
        early_first = settle(early_first)
        all_sums = [own_sums, near_sums, far_sums]
        reduced = (own_made[0][0], early_first, early_second)
        shares_out = [own_made[1][0], *near_made[1], far_made[1][0]]
    else:
        all_sums, shares_grad, shares_out = [], [], []
        for r in range(chips):
            normed_group = links.swap(normed_feed, 2 * r) if r else normed_feed
            made = backward((r,), forward(normed_group))
            all_sums.append(adapters((r,), normed_group, made))
            shares_grad.append(made[0][0])
            shares_out.append(made[1][0])
        rest = sum(links.swap(shares_grad[r], 2 * r).astype(f32) for r in range(1, chips)).astype(bf16)
        reduced = (shares_grad[0], rest, jnp.zeros(rest.shape, bf16))
        down_mag_steps = links.small_total(sum(part[5][:1] for part in all_sums), order)
        next(down_mag_steps)
    feed_in, feed_products, down_in, down_products, feed_mag_raw, _ = (sum(parts) for parts in zip(*all_sums))

    finished = []
    for half, (weights, at) in enumerate(((feed_own, core), (feed_partner, 1 - core))):
        finished.append(
            finish_columns(
                weights,
                order(feed_products[half]),
                feed_mag_raw[half::2],
                lax.dynamic_slice_in_dim(feed_mag, at * feed_cols, feed_cols, 1),
            )
        )
        mark(finished[-1][0])
        next(down_mag_steps)
    reduced = settle(*reduced)
    grad_residual, grad_ordered, out_mag_raw, out_ext, grad_mixed, delta = residual_back(
        reduced, residual, gain_feedforward, grad_out, rows_in, mixed, o_weights
    )
    mark(delta)

    def pack_early(down_mag_total):
        grad_mag, grad_out_part, grad_in_part = zip(*finished)
        columns = [
            jnp.concatenate([part.astype(bf16) for part in parts])
            for parts in zip(grad_out_part, down_in, grad_mag)
        ]
        columns = jnp.where(core == 0, jnp.concatenate(columns, axis=1), jnp.concatenate(columns[::-1], axis=1))
        full = lax.dynamic_update_slice(jnp.zeros((64, 3 * D), bf16), columns, (0, chip * chip_cols))
        down_aux = aux[0]
        down_inverse = (down_aux[RANK].astype(f32) + down_aux[RANK + 1].astype(f32))[None]
        down_grad_mag = down_mag_total / magnitude_down[None]
        down_out = factor * down_products * (magnitude_down[None] * down_inverse)
        own_turn = columns_of(-down_grad_mag * down_inverse, down_cols) * (factor / blocks)
        down_out = lax.dynamic_update_slice(
            down_out, columns_of(down_out, down_cols) + down_proj * own_turn, (0, index * down_cols)
        )
        own_wide = (columns_of(rank_out_down.astype(f32), down_cols) * own_turn).astype(bf16)
        down_norm_in = lax.dot_general(
            own_wide, down_fold[:, :chip_cols], (((1,), (2,)), ((), ())), preferred_element_type=f32
        ).reshape(RANK, FF)
        down_full = (full[2 * RANK : 3 * RANK, :FF].astype(f32) + down_norm_in).astype(bf16)
        full = lax.dynamic_update_slice(full, down_full, (2 * RANK, 0))
        top = jnp.concatenate([(feed_in + sum(grad_in_part)).astype(bf16), down_out.astype(bf16)])
        return down_grad_mag, jnp.concatenate(
            [jnp.pad(top, ((0, 16), (0, 0)))] + [full[:, i * D : (i + 1) * D] for i in range(3)]
        )

    grad_queries, grad_kvs = None, []

    def keys_back(distance):
        grad_queries_next, grad_kv = attend_back(
            scalars, order(queries), grad_mixed, lse, delta, kv_blocks[distance], grad_queries, distance
        )
        mark(grad_kv)
        return grad_queries_next, grad_kv

    def pass_down(passed, grad_kv):
        passed = order(passed)
        passed = settle((passed.astype(f32) + grad_kv.astype(f32)).astype(bf16))
        return links.row_shift(passed, -1)

    grad_queries, grad_kv = keys_back(blocks - 1)
    passed = links.row_shift(grad_kv, -1)
    held = None
    for distance in reversed(range(1, blocks - 1)):
        grad_queries, grad_kv = keys_back(distance)
        if held is not None:
            passed = pass_down(passed, held)
        held = grad_kv
    grad_queries, grad_kv = keys_back(0)
    for down_mag_total in down_mag_steps:
        pass
    if fast:
        out_far = links.split_swap(order(shares_out[3]), 2, 4)
        out_first = links.split_swap(order(shares_out[1]), 2, 4)
    out_grad_mag, out_out, out_in = output_adapter(
        order(grad_ordered), out_mag_raw, magnitude_output, o_weights, mixed, out_ext, out_in_t
    )
    mark(out_in)
    passed = pass_down(passed, held)
    q_acc, q_in, q_out, q_grad_mag = query_back(
        order(grad_queries), queries, q_weights, cosine, sine, normed, attn_in_t[0], magnitude_attention[:GROUP]
    )
    mark(q_in)
    if fast:
        out_far, out_first = settle(out_far, out_first)
        out_late = settle((shares_out[2].astype(f32) + out_far.astype(f32)).astype(bf16))
        out_second = links.split_swap(out_late, 4, 2)
        out_parts = [shares_out[0], out_first, out_second]
    else:
        out_parts = [shares_out[0]] + [links.swap(shares_out[r], 2 * r) for r in range(1, chips)]
    down_grad_mag, early = pack_early(down_mag_total)
    early_steps = links.total(settle(early), order)
    next(early_steps)
    out_parts = settle(*out_parts)
    next(early_steps)
    next(early_steps)
    input_grad, kv_in, kv_out, kv_grad_mag = key_back(
        heads, order(passed), grad_kv, kv_own, [weights for weights, _ in kv_made], cosine, sine, normed, rows_in,
        gain_attention, grad_residual, q_acc, attn_in_t[1:].reshape(2 * RANK, D), magnitude_attention[GROUP:],
    )
    mark(kv_in)
    rows = lambda *parts: jnp.concatenate([part.astype(bf16) for part in parts])
    late = jnp.concatenate(
        [
            rows(q_in, kv_in, q_out),
            rows(out_in, out_out, out_grad_mag, jnp.zeros((31, D), bf16)),
            rows(
                kv_out[:, :KVW],
                kv_out[:, KVW:],
                q_grad_mag.reshape(-1, KVW),
                kv_grad_mag.reshape(-1, KVW),
                jnp.zeros((26, KVW), bf16),
            ),
        ],
        axis=1,
    )
    late_steps = links.total(settle(late), order)
    late = early = None
    while late is None:
        late = next(late_steps)
        if early is None:
            early = next(early_steps)
    while early is None:
        early = next(early_steps)

    block_out = (residual + sum(part.astype(f32) for part in out_parts)).astype(bf16)[None]
    feed_full = jnp.concatenate([early[64 * (1 + i) : 64 * (2 + i)] for i in range(3)], axis=1)[:, :FF]
    late_in, late_out = late[: 3 * RANK, :D], late[3 * RANK :, :D]
    mid, side = late[:, D : 2 * D], late[:, 2 * D :]
    return (
        block_out,
        input_grad[None],
        late_in.reshape(3, RANK, D).transpose(0, 2, 1),
        jnp.concatenate(
            [
                late_out.reshape(RANK, GROUP, KVW).transpose(1, 0, 2),
                jnp.stack([side[:RANK], side[RANK : 2 * RANK]]),
            ]
        ),
        side[2 * RANK : 2 * RANK + 6],
        mid[:RANK].T,
        mid[RANK : 2 * RANK].reshape(RANK, GROUP, KVW).transpose(1, 0, 2),
        mid[2 * RANK].reshape(GROUP, KVW),
        early[: 2 * RANK].reshape(2, RANK, D).transpose(0, 2, 1),
        feed_full[: 2 * RANK].reshape(2, RANK, FF),
        feed_full[3 * RANK : 3 * RANK + 2],
        feed_full[2 * RANK : 3 * RANK].T,
        early[2 * RANK : 3 * RANK],
        down_grad_mag[0],
    )


def solution(mesh):
    split_tokens = P("dp", "blk", None)
    placed = (
        split_tokens,
        split_tokens,
        P("dp"),
        P("dp", "blk"),
        P(),
        P(),
        P(None, None, "dp"),
        P(None, None, "dp"),
        P(None, None, "dp"),
        P(None, "dp"),
    ) + (P(),) * 12
    return jax.shard_map(
        functools.partial(shards, devices=mesh.shape["dp"], blocks=mesh.shape["blk"]),
        mesh=mesh,
        in_specs=placed,
        out_specs=(split_tokens, split_tokens) + (P(),) * 12,
        check_vma=False,
    )
```

```python
import functools

import jax
import jax.numpy as jnp
from jax import lax
from jax.experimental import pallas as pl
from jax.experimental.pallas import tpu as pltpu
from jax.sharding import PartitionSpec as P

D = 2048
KV_HEADS = 4
HEAD = 128
FF = 5632
RANK = 16
GROUP = 4
KVW = 512

EXT = 128
WIDE = D + EXT
SLOTS = 3
INV_AT = 48
PROJ_AT = 64
AUX = 32

factor = 32.0 / RANK
rms_eps = 1e-05
rope_base = 10000.0
masked_score = -1e30
log2_e = 1.4426950408889634
score_scale = HEAD ** (-0.5)
f32 = jnp.float32
bf16 = jnp.bfloat16


def dot_nt(left, right):
    return lax.dot_general(left, right, (((1,), (1,)), ((), ())), preferred_element_type=f32)


def dot_nn(left, right):
    return lax.dot_general(left, right, (((1,), (0,)), ((), ())), preferred_element_type=f32)


def dot_tn(left, right):
    return lax.dot_general(left, right, (((0,), (0,)), ((), ())), preferred_element_type=f32)


def limits(mebibytes):
    return pltpu.CompilerParams(vmem_limit_bytes=mebibytes << 20)


def kernel_call(*args, in_specs=None, **options):
    if in_specs is not None:
        options["in_specs"] = in_specs
    call = pl.pallas_call(
        *args, cost_estimate=pl.CostEstimate(flops=0, transcendentals=0, bytes_accessed=0), **options
    )
    if in_specs is None:
        return call
    keep = lambda value, spec: pltpu.with_memory_space_constraint(value, pltpu.HBM) if spec is anywhere else value
    return lambda *operands: call(*[keep(value, spec) for value, spec in zip(operands, in_specs)])


anywhere = pl.BlockSpec(memory_space=pltpu.HBM)
in_vmem = pl.BlockSpec(memory_space=pltpu.VMEM)
in_smem = pl.BlockSpec(memory_space=pltpu.SMEM)


def shape_of(shape, dtype=f32):
    return jax.ShapeDtypeStruct(shape, dtype)


def split_low(value):
    high = value.astype(bf16)
    return high, (value - high.astype(f32)).astype(bf16)


def iota(shape, dim):
    return lax.broadcasted_iota(jnp.int32, shape, dim)


def lanes_at(start):
    return pl.ds(pl.multiple_of(start, HEAD), HEAD)


def fold_kernel(weight_ref, rank_in_ref, rank_out_ref, mag_ref, out_ref, column_ref, *, first_slot, moving):
    slot = first_slot + (pl.program_id(0) if moving else 0)
    rows = weight_ref.shape[1]

    def placed_at(start):
        spot = iota((RANK, EXT), 1) == iota((RANK, EXT), 0) + start
        return jnp.where(spot, 1.0, 0.0).astype(bf16)

    @pl.when(pl.program_id(1) == 0)
    def _():
        column_ref[0] = dot_tn(rank_out_ref[0], placed_at(0))
        column_ref[1] = dot_tn(rank_out_ref[0], placed_at(RANK * slot))
        mags = jnp.broadcast_to(mag_ref[0], (8, mag_ref.shape[2]))
        one = jnp.where(iota((8, EXT), 0) == 0, 1.0, 0.0)
        column_ref[2] = lax.dot_general(
            mags, one, (((0,), (0,)), ((), ())), precision=lax.Precision.HIGHEST, preferred_element_type=f32
        )

    own = pl.ds(pl.multiple_of(pl.program_id(1) * rows, 16), rows)
    doubled = (factor * column_ref[0, own, :RANK]).astype(bf16)
    merged = weight_ref[0].astype(f32) + dot_nn(doubled, rank_in_ref[0])
    inverse = 1.0 / jnp.sqrt(jnp.sum(merged * merged, axis=1, keepdims=True))
    scale = column_ref[2, own, :1] * inverse
    folded = (merged * scale).astype(bf16)
    out_ref[0, :, :D] = folded
    ext = column_ref[1, own, :] * (factor * scale)
    for index, part in enumerate(split_low(dot_nt(folded, rank_in_ref[0]))):
        ext = ext + dot_nn(part, placed_at(PROJ_AT + RANK * index))
    lane = iota(ext.shape, 1)
    for index, part in enumerate(split_low(inverse)):
        ext = ext + jnp.where(lane == INV_AT + index, part.astype(f32), 0.0)
    out_ref[0, :, D:] = ext.astype(bf16)


def fold(weights, rank_in_t, rank_out, magnitude, rank_first, moving, name, first=0):
    members, columns = magnitude.shape
    pieces = 4 if columns % 64 == 0 and columns > 256 else 1
    rows = columns // pieces
    rank_block = (lambda b, c: (b + rank_first, 0, 0)) if moving else (lambda b, c: (rank_first, 0, 0))
    return kernel_call(
        functools.partial(fold_kernel, first_slot=rank_first, moving=moving),
        out_shape=shape_of((members, columns, WIDE), bf16),
        grid=(members, pieces),
        in_specs=[
            pl.BlockSpec((1, rows, D), lambda b, c: (b + first, c, 0)),
            pl.BlockSpec((1, RANK, D), rank_block),
            pl.BlockSpec((1, RANK, columns), lambda b, c: (b, 0, 0)),
            pl.BlockSpec((1, 1, columns), lambda b, c: (b, 0, 0)),
        ],
        out_specs=pl.BlockSpec((1, rows, WIDE), lambda b, c: (b, c, 0)),
        scratch_shapes=[pltpu.VMEM((3, columns, EXT), f32)],
        compiler_params=limits(32),
        name=name,
    )(weights, rank_in_t, rank_out, magnitude[:, None, :])


def fold_down_kernel(weight_ref, rank_in_ref, rank_out_ref, mag_ref, out_ref, proj_ref, merged_ref, *, chips):
    rows = weight_ref.shape[0] // chips
    total = 0.0
    doubled = (factor * rank_out_ref[...].astype(f32)).astype(bf16)
    for part in range(chips):
        span = slice(part * rows, (part + 1) * rows)
        merged = weight_ref[span, :].astype(f32) + dot_tn(rank_in_ref[:, span], doubled)
        merged_ref[span, :] = merged
        total = total + jnp.sum(merged * merged, axis=0, keepdims=True)
    inverse = 1.0 / jnp.sqrt(total)
    scale = mag_ref[...] * inverse
    high, low = split_low(inverse)
    row = iota((AUX - RANK, scale.shape[1]), 0)
    tail = jnp.where(row == 0, high.astype(f32), jnp.where(row == 1, low.astype(f32), 0.0))
    aux = jnp.concatenate([doubled.astype(f32) * scale, tail], axis=0).astype(bf16)
    proj = 0.0
    for part in range(chips):
        span = slice(part * rows, (part + 1) * rows)
        folded = (merged_ref[span, :] * scale).astype(bf16)
        out_ref[part, :rows, :] = folded
        out_ref[part, rows:, :] = aux
        proj = proj + dot_nn(rank_in_ref[:, span], folded)
    proj_ref[...] = proj


def fold_down(weights, rank_in_t, rank_out, magnitude, chips):
    inputs, columns = weights.shape
    return kernel_call(
        functools.partial(fold_down_kernel, chips=chips),
        out_shape=(shape_of((chips, inputs // chips + AUX, columns), bf16), shape_of((RANK, columns))),
        scratch_shapes=[pltpu.VMEM((inputs, columns), f32)],
        compiler_params=limits(32),
        name="fold_down",
    )(weights, rank_in_t, rank_out, magnitude[None])


def head_kernel(scalar_ref, first_ref, second_ref, input_ref, cos_ref, sin_ref, *refs, roped):
    before_refs, (weight_ref, out_ref, token_ref) = refs[:-3], refs[-3:]
    members, half = first_ref.shape[0], first_ref.shape[1]
    for member in range(members):
        for order, ref in ((scalar_ref[0], first_ref), (1 - scalar_ref[0], second_ref)):
            weight_ref[pl.ds(pl.multiple_of((2 * member + order) * half, half), half), :] = ref[member]
    wide = members * HEAD
    for index, ref in enumerate(before_refs):
        out_ref[:, pl.ds(pl.multiple_of(scalar_ref[2 + index] * wide, wide), wide)] = ref[...]
    raw = dot_nt(input_ref[...], weight_ref[:, :D])
    for member in range(members):
        part = raw[:, member * HEAD : (member + 1) * HEAD]
        if member < roped:
            part = part * cos_ref[...] + pltpu.roll(part, HEAD // 2, 1) * sin_ref[...]
        start = (scalar_ref[1] * wide if before_refs else 0) + member * HEAD
        out_ref[:, lanes_at(start)] = part.astype(bf16)
    token_ref[...] = jnp.zeros(token_ref.shape, f32)


def head_step(scalars, first, second, inputs, tables, roped, before, name):
    members, half, _ = first.shape
    tokens = inputs.shape[0]
    wide = members * HEAD
    return kernel_call(
        functools.partial(head_kernel, roped=roped),
        out_shape=(
            shape_of((wide, WIDE), bf16),
            shape_of((tokens, (1 + len(before)) * wide), bf16),
            shape_of((8, HEAD)),
        ),
        in_specs=[in_smem] + [in_vmem] * (5 + len(before)),
        out_specs=(in_vmem,) * 3,
        compiler_params=limits(24),
        name=name,
    )(scalars, first, second, inputs, *tables, *before)


def head_copies(weight_ref, head, out_ref, semaphores, first=0):
    devices, members, part = weight_ref.shape[:3]
    parts = devices // KV_HEADS
    copies = []
    for at in range(parts):
        for member in range(members):
            copies.append(
                pltpu.make_async_copy(
                    weight_ref.at[parts * head + at, member],
                    out_ref.at[pl.ds((parts * member + at) * part, part), :],
                    semaphores.at[first + len(copies)],
                )
            )
    return copies


def head_scratch(weights):
    each = weights.shape[0] // KV_HEADS * weights.shape[1]
    return [
        pltpu.VMEM((KV_HEADS, weights.shape[1] * HEAD, WIDE), bf16),
        pltpu.SemaphoreType.DMA((KV_HEADS * each,)),
    ]


def all_head_copies(weight_ref, out_ref, semaphores):
    each = weight_ref.shape[0] // KV_HEADS * weight_ref.shape[1]
    return [head_copies(weight_ref, head, out_ref.at[head], semaphores, head * each) for head in range(KV_HEADS)]


def next_head(copies, head):
    if head == 0:
        for copy in copies[0] + copies[1]:
            copy.start()
    elif head + 1 < len(copies):
        for copy in copies[head + 1]:
            copy.start()
    for copy in copies[head]:
        copy.wait()


def query_kernel(input_ref, cos_ref, sin_ref, weight_hbm, out_ref, weight_ref, semaphores):
    copies = all_head_copies(weight_hbm, weight_ref, semaphores)
    for head in range(KV_HEADS):
        next_head(copies, head)
        raw = dot_nt(input_ref[...], weight_ref[head, :, :D])
        for group in range(GROUP):
            part = raw[:, group * HEAD : (group + 1) * HEAD]
            part = part * cos_ref[...] + pltpu.roll(part, HEAD // 2, 1) * sin_ref[...]
            start = (head * GROUP + group) * HEAD
            out_ref[:, start : start + HEAD] = part.astype(bf16)


def query_project(inputs, tables, weights):
    return kernel_call(
        query_kernel,
        out_shape=shape_of((inputs.shape[0], D), bf16),
        in_specs=[in_vmem] * 3 + [anywhere],
        out_specs=in_vmem,
        scratch_shapes=head_scratch(weights),
        compiler_params=limits(24),
        name="query_project",
    )(inputs, *tables, weights)


def masked_scores(keys, queries, key_first, length, causal):
    tokens, lanes = keys.shape[0], queries.shape[0]
    scores = dot_nt(keys, queries)
    key_pos = key_first + iota((tokens, 1), 0)
    scores = scores + jnp.where(key_pos < length, 0.0, masked_score)
    if causal:
        allowed = iota((tokens, lanes), 0) <= (iota((tokens, lanes), 1) & (tokens - 1))
        scores = jnp.where(allowed, scores, masked_score)
    return scores


def attend_kernel(scalar_ref, query_ref, *refs, steps):
    kv_refs = refs[:steps]
    mixed_ref, lse_ref, stacked_ref, max_ref, sum_ref, accum_ref = refs[steps:]
    head = pl.program_id(0)
    tokens = query_ref.shape[0]
    block_index, length = scalar_ref[0], scalar_ref[1]
    scale = score_scale * log2_e
    for group in range(GROUP):
        stacked_ref[group * tokens : (group + 1) * tokens, :] = query_ref[:, group * HEAD : (group + 1) * HEAD]

    for distance in range(steps):

        def step(distance=distance):
            keys = kv_refs[distance][:, :HEAD]
            values = kv_refs[distance][:, HEAD:]
            key_first = (block_index - distance) * tokens
            scores = masked_scores(keys, stacked_ref[...], key_first, length, distance == 0)
            block_max = jnp.max(scores, axis=0, keepdims=True)
            new_max = block_max if distance == 0 else jnp.maximum(max_ref[...], block_max)
            terms = jnp.exp2((scores - new_max) * scale)
            added = jnp.sum(terms, axis=0, keepdims=True)
            product = dot_tn(values, terms.astype(bf16))
            if distance == 0:
                sum_ref[...] = added
                accum_ref[...] = product
            else:
                fade = jnp.exp2((max_ref[...] - new_max) * scale)
                sum_ref[...] = sum_ref[...] * fade + added
                accum_ref[...] = accum_ref[...] * fade + product
            max_ref[...] = new_max

        if distance == 0:
            step()
        else:
            pl.when(block_index >= distance)(step)
    mixed = accum_ref[...] / sum_ref[...]
    for group in range(GROUP):
        part = mixed[:, group * tokens : (group + 1) * tokens]
        mixed_ref[:, lanes_at(group * KVW + head * HEAD)] = part.T.astype(bf16)
    lse_ref[0] = max_ref[...] * scale + jnp.log(sum_ref[...]) * log2_e


def attend(scalars, queries, kv_blocks):
    tokens = queries.shape[0]
    steps = len(kv_blocks)
    lanes = GROUP * tokens
    return kernel_call(
        functools.partial(attend_kernel, steps=steps),
        out_shape=(shape_of((tokens, D), bf16), shape_of((KV_HEADS, 1, lanes))),
        grid_spec=pltpu.PrefetchScalarGridSpec(
            num_scalar_prefetch=1,
            grid=(KV_HEADS,),
            in_specs=[pl.BlockSpec((tokens, GROUP * HEAD), lambda j, s: (0, j))]
            + [pl.BlockSpec((tokens, 2 * HEAD), lambda j, s: (0, j))] * steps,
            out_specs=(
                pl.BlockSpec((tokens, D), lambda j, s: (0, 0)),
                pl.BlockSpec((1, 1, lanes), lambda j, s: (j, 0, 0)),
            ),
            scratch_shapes=[
                pltpu.VMEM((lanes, HEAD), bf16),
                pltpu.VMEM((1, lanes), f32),
                pltpu.VMEM((1, lanes), f32),
                pltpu.VMEM((HEAD, lanes), f32),
            ],
        ),
        compiler_params=limits(40),
        name="attend",
    )(scalars, queries, *kv_blocks)


def attend_back_kernel(scalar_ref, query_ref, grad_ref, lse_ref, delta_ref, kv_ref, *refs, distance, chained):
    if chained:
        before_ref, grad_query_ref, grad_kv_ref, stacked_ref, stacked_grad_ref = refs
    else:
        grad_query_ref, grad_kv_ref, stacked_ref, stacked_grad_ref = refs
    head = pl.program_id(0)
    tokens = query_ref.shape[0]
    block_index, length = scalar_ref[0], scalar_ref[1]
    active = (block_index >= distance) & (block_index * tokens < length)

    @pl.when(active)
    def _():
        for group in range(GROUP):
            rows = slice(group * tokens, (group + 1) * tokens)
            stacked_ref[rows, :] = query_ref[:, group * HEAD : (group + 1) * HEAD]
            stacked_grad_ref[rows, :] = grad_ref[:, lanes_at(group * KVW + head * HEAD)]
        keys = kv_ref[:, :HEAD]
        values = kv_ref[:, HEAD:]
        key_first = (block_index - distance) * tokens
        scores = masked_scores(keys, stacked_ref[...], key_first, length, distance == 0)
        probs = jnp.exp2(scores * (score_scale * log2_e) - lse_ref[0])
        grad_probs = dot_nt(values, stacked_grad_ref[...])
        grad_scores = (probs * (grad_probs - delta_ref[0])).astype(bf16)
        grad_values = dot_nn(probs.astype(bf16), stacked_grad_ref[...])
        grad_keys = dot_nn(grad_scores, stacked_ref[...]) * score_scale
        grad_queries = dot_tn(grad_scores, keys) * score_scale
        for group in range(GROUP):
            lanes = slice(group * HEAD, (group + 1) * HEAD)
            part = grad_queries[group * tokens : (group + 1) * tokens, :]
            if chained:
                part = part + before_ref[:, lanes]
            grad_query_ref[:, lanes] = part
        grad_kv_ref[:, :HEAD] = grad_keys.astype(grad_kv_ref.dtype)
        grad_kv_ref[:, HEAD:] = grad_values.astype(grad_kv_ref.dtype)

    @pl.when(jnp.logical_not(active))
    def _():
        grad_query_ref[...] = before_ref[...] if chained else jnp.zeros(grad_query_ref.shape, f32)
        grad_kv_ref[...] = jnp.zeros(grad_kv_ref.shape, grad_kv_ref.dtype)


def attend_back(scalars, queries, grad_mixed, lse, delta, kv_block, before, distance):
    tokens = queries.shape[0]
    lanes = GROUP * tokens
    row = pl.BlockSpec((1, 1, lanes), lambda j, s: (j, 0, 0))
    per_query = pl.BlockSpec((tokens, GROUP * HEAD), lambda j, s: (0, j))
    per_key = pl.BlockSpec((tokens, 2 * HEAD), lambda j, s: (0, j))
    chained = before is not None
    operands = [scalars, queries, grad_mixed, lse, delta, kv_block]
    specs = [per_query, pl.BlockSpec((tokens, D), lambda j, s: (0, 0)), row, row, per_key]
    if chained:
        operands += [before]
        specs += [per_query]
    return kernel_call(
        functools.partial(attend_back_kernel, distance=distance, chained=chained),
        out_shape=(shape_of((tokens, D)), shape_of((tokens, 2 * KVW), f32 if distance == 0 else bf16)),
        grid_spec=pltpu.PrefetchScalarGridSpec(
            num_scalar_prefetch=1,
            grid=(KV_HEADS,),
            in_specs=specs,
            out_specs=(per_query, per_key),
            scratch_shapes=[pltpu.VMEM((lanes, HEAD), bf16), pltpu.VMEM((lanes, HEAD), bf16)],
        ),
        input_output_aliases={6: 0} if chained else {},
        compiler_params=limits(40),
        name=f"attend_back_{distance}",
    )(*operands)


def rms_inverse(values):
    return lax.rsqrt(jnp.mean(values * values, axis=-1, keepdims=True) + rms_eps)


def rms_back(values, inverse, gain, grad):
    scaled = grad * gain
    return inverse * (scaled - values * (inverse * inverse * jnp.mean(scaled * values, axis=-1, keepdims=True)))


def output_kernel(mixed_ref, input_ref, gain_ref, weight_hbm, residual_ref, normed_ref, weight_ref, semaphores):
    copies = all_head_copies(weight_hbm, weight_ref, semaphores)
    for head in range(KV_HEADS):
        next_head(copies, head)
        value = dot_nt(mixed_ref[...], weight_ref[head, :, :D])
        for group in range(GROUP):
            start = group * KVW + head * HEAD
            lanes = slice(start, start + HEAD)
            residual_ref[:, lanes] = input_ref[:, lanes].astype(f32) + value[:, group * HEAD : (group + 1) * HEAD]
    values = residual_ref[...]
    normed_ref[...] = (values * rms_inverse(values) * gain_ref[...]).astype(bf16)


def output_project(mixed, weights, inputs, gain):
    tokens = mixed.shape[0]
    return kernel_call(
        output_kernel,
        out_shape=(shape_of((tokens, D)), shape_of((tokens, D), bf16)),
        in_specs=[in_vmem] * 3 + [anywhere],
        out_specs=(in_vmem,) * 2,
        scratch_shapes=head_scratch(weights),
        compiler_params=limits(28),
        name="output_project",
    )(mixed, inputs, gain[None], weights)


class Copies:
    def __init__(self, semaphores):
        self.semaphores = semaphores
        self.made = []

    def __call__(self, source, target):
        copy = pltpu.make_async_copy(source, target, self.semaphores.at[len(self.made)])
        self.made.append(copy)
        return copy

    def started(self, source, target):
        copy = self(source, target)
        copy.start()
        return copy


def feed_forward_kernel(normed_ref, own_ref, partner_ref, gate_hbm, up_hbm, weight_ref, value_ref, semaphores, *, block):
    copies = Copies(semaphores)
    pairs = [(half, member) for half in range(2) for member in range(2)]
    fetches = [
        copies((own_ref, partner_ref)[half].at[member], weight_ref.at[2 * half + member]) for half, member in pairs
    ]
    fetches[0].start()
    fetches[1].start()
    stores = []
    for half, member in pairs:
        at = 2 * half + member
        fetches[at].wait()
        if at + 2 < 4:
            fetches[at + 2].start()
        for start in range(0, normed_ref.shape[0], block):
            rows = slice(start, start + block)
            value_ref[at, rows, :] = dot_nt(normed_ref[rows, :], weight_ref[at, :, :D])
        stores.append(copies.started(value_ref.at[at], (gate_hbm, up_hbm)[member].at[half]))
    for store in stores:
        store.wait()


def feed_forward(normed, own, partner, block):
    tokens = normed.shape[0]
    columns = own.shape[1]
    return kernel_call(
        functools.partial(feed_forward_kernel, block=block),
        out_shape=(shape_of((2, tokens, columns)), shape_of((2, tokens, columns))),
        in_specs=[in_vmem, anywhere, anywhere],
        out_specs=(anywhere,) * 2,
        scratch_shapes=[
            pltpu.VMEM((4, columns, WIDE), bf16),
            pltpu.VMEM((4, tokens, columns), f32),
            pltpu.SemaphoreType.DMA((8,)),
        ],
        compiler_params=limits(28),
        name="feed_forward",
    )(normed, own, partner)


def grad_copies(copies, place_ref, grad_hbm, grad_ref, chips, block):
    return [
        copies(
            grad_hbm.at[0 if r is None else place_ref[1] ^ (2 * r)], grad_ref.at[pl.ds(turn * block, block), :]
        )
        for turn, r in enumerate(chips)
    ]


MAGS = 8


def feed_back_kernel(place_ref, grad_hbm, own_ref, partner_ref, *refs, block, devices, chips, fused):
    kept, refs = refs[: 2 - fused], refs[2 - fused :]
    piece_refs, refs = refs[:devices], refs[devices:]
    count = len(chips)
    share_hbm, down_hbm, refs = refs[:count], refs[count : 2 * count], refs[2 * count :]
    hidden_hbm, grad_gate_hbm, grad_up_hbm, ext_ref, mag_ref, aux_ref, refs = *refs[:6], refs[6:]
    weight_ref, down_weight_ref, grad_ref, share_ref, made_ref, value_ref, semaphores = refs
    core = place_ref[0]
    columns = own_ref.shape[1]
    width = piece_refs[0].shape[1]
    copies = Copies(semaphores)
    fetches = grad_copies(copies, place_ref, grad_hbm, grad_ref, chips, block)
    for i, ref in enumerate(piece_refs):
        lanes = pl.ds(pl.multiple_of((place_ref[1] ^ i) * width, width), width)
        fetches.append(copies(ref, down_weight_ref.at[:, lanes]))
    if not fused:
        fetches.append(copies(kept[0], value_ref.at[0]))
        fetches.append(copies(kept[1], value_ref.at[1]))
    weight_fetches = [copies(ref, weight_ref.at[half]) for half, ref in enumerate((own_ref, partner_ref))]
    if fused:
        weight_fetches[0].start()
    for fetch in fetches:
        fetch.start()
    mag_ref[...] = jnp.zeros(mag_ref.shape, f32)
    if fused:
        weight_fetches[0].wait()
        value_ref[0, 0] = dot_nt(kept[0][...], weight_ref[0, 0, :, :D])
        value_ref[1, 0] = dot_nt(kept[0][...], weight_ref[0, 1, :, :D])
    else:
        weight_fetches[0].start()
    for fetch in fetches:
        fetch.wait()
    weight_fetches[1].start()
    aux_ref[...] = down_weight_ref[2 * columns :, :]
    stores = []
    for turn in range(count):
        rows = slice(turn * block, (turn + 1) * block)
        grad = grad_ref[rows, :]
        share, down = None, None
        for half in range(2):
            order = core if half == 0 else 1 - core
            down_rows = pl.ds(pl.multiple_of(order * columns, 16), columns)
            if fused and half:
                weight_fetches[1].wait()
                value_ref[0, 1] = dot_nt(kept[0][...], weight_ref[1, 0, :, :D])
                value_ref[1, 1] = dot_nt(kept[0][...], weight_ref[1, 1, :, :D])
            gate, up = value_ref[0, half, rows, :], value_ref[1, half, rows, :]
            grad_hidden = dot_nt(grad, down_weight_ref[down_rows, :])
            sigma = 1.0 / (1.0 + jnp.exp(-gate))
            silu = gate * sigma
            hidden = (silu * up).astype(bf16)
            grad_gate = grad_hidden * up * (sigma + silu * (1.0 - sigma))
            grad_up = grad_hidden * silu
            mag_ref[half : half + 1, :columns] += jnp.sum(grad_gate * gate, axis=0, keepdims=True)
            mag_ref[2 + half : 3 + half, :columns] += jnp.sum(grad_up * up, axis=0, keepdims=True)
            grad_gate, grad_up = grad_gate.astype(bf16), grad_up.astype(bf16)
            for at, (value, ref) in enumerate(((hidden, hidden_hbm), (grad_gate, grad_gate_hbm), (grad_up, grad_up_hbm))):
                made_ref[at, half, rows, :] = value
                stores.append(copies.started(made_ref.at[at, half, rows, :], ref.at[half, rows, :]))
            part = dot_nn(hidden, down_weight_ref[down_rows, :])
            down = part if down is None else down + part
            if turn == 0 and not fused:
                weight_fetches[half].wait()
            part = dot_nn(grad_gate, weight_ref[half, 0]) + dot_nn(grad_up, weight_ref[half, 1])
            share = part if share is None else share + part
        share_ref[0, rows, :] = share[:, :D].astype(bf16)
        share_ref[1, rows, :] = down.astype(bf16)
        ext_ref[rows, :EXT] = share[:, D:].astype(bf16)
        small = dot_nt(grad, down_weight_ref[2 * columns :, :])
        ext_ref[rows, EXT : EXT + AUX] = small.astype(bf16)
        mag_ref[4:5, :] += jnp.sum(grad.astype(f32) * down, axis=0, keepdims=True)
    for at in range(count):
        turn = at ^ core if count == 2 else at
        rows = pl.ds(pl.multiple_of(turn * block, block), block)
        stores.append(copies.started(share_ref.at[0, rows, :], share_hbm[at]))
        stores.append(copies.started(share_ref.at[1, rows, :], down_hbm[at]))
    for store in stores:
        store.wait()


def feed_back(place, grads, chips, kept, own, partner, pieces, block):
    fused = int(len(kept) == 1)
    count = len(chips)
    tokens = count * block
    columns = own.shape[1]
    devices = len(pieces)
    return kernel_call(
        functools.partial(feed_back_kernel, block=block, devices=devices, chips=chips, fused=fused),
        out_shape=(shape_of((block, D), bf16),) * (2 * count)
        + (
            shape_of((2, tokens, columns), bf16),
            shape_of((2, tokens, columns), bf16),
            shape_of((2, tokens, columns), bf16),
            shape_of((tokens, 2 * EXT), bf16),
            shape_of((MAGS, D)),
            shape_of((AUX, D), bf16),
        ),
        in_specs=[in_smem] + [anywhere] * 3 + ([in_vmem] if fused else [anywhere] * 2) + [anywhere] * devices,
        out_specs=(anywhere,) * (3 + 2 * count) + (in_vmem,) * 3,
        scratch_shapes=[
            pltpu.VMEM((2, 2, columns, WIDE), bf16),
            pltpu.VMEM((2 * columns + AUX, D), bf16),
            pltpu.VMEM((tokens, D), bf16),
            pltpu.VMEM((2, tokens, D), bf16),
            pltpu.VMEM((3, 2, tokens, columns), bf16),
            pltpu.VMEM((2, 2, tokens, columns), f32),
            pltpu.SemaphoreType.DMA((4 + devices + 9 * count,)),
        ],
        compiler_params=limits(54),
        name="feed_back",
    )(place, grads, own, partner, *kept, *pieces)


def feed_adapter_kernel(
    place_ref, normed_ref, grad_hbm, hidden_hbm, grad_gate_hbm, grad_up_hbm, ext_ref, rank_in_ref, down_in_ref, *refs,
    chips, block, before,
):
    before_refs, refs = refs[: 4 * before], refs[4 * before :]
    in_ref, out_ref, down_rank_in_ref, down_out_ref, grad_ref, made_ref, semaphores = refs
    copies = Copies(semaphores)
    fetches = [
        copies.started(ref, made_ref.at[at]) for at, ref in enumerate((hidden_hbm, grad_gate_hbm, grad_up_hbm))
    ]
    for fetch in grad_copies(copies, place_ref, grad_hbm, grad_ref, chips, block):
        fetch.start()
        fetches.append(fetch)

    def put(ref, index, value, at):
        ref[index] = value + before_refs[at][index] if before else value

    normed = normed_ref[...]
    small = dot_nt(rank_in_ref[...], normed).astype(bf16)
    ext = ext_ref[...].T
    put(in_ref, ..., dot_nn(ext[: 2 * RANK], normed), 0)
    for fetch in fetches:
        fetch.wait()
    down_small = 0.0
    for half in range(2):
        put(out_ref, (half, slice(0, RANK)), dot_nn(small[:RANK], made_ref[1, half]), 1)
        put(out_ref, (half, slice(RANK, 2 * RANK)), dot_nn(small[RANK:], made_ref[2, half]), 1)
        down_small = down_small + dot_nt(down_in_ref[half], made_ref[0, half])
        put(down_rank_in_ref, half, dot_nn(ext[EXT : EXT + RANK], made_ref[0, half]), 2)
    put(down_out_ref, ..., dot_nn(down_small.astype(bf16), grad_ref[...]), 3)


def feed_adapter(place, normed, grads, chips, hidden, grad_gate, grad_up, ext, rank_in_t, down_in_t, before):
    columns = hidden.shape[2]
    return kernel_call(
        functools.partial(
            feed_adapter_kernel, chips=chips, block=normed.shape[0] // len(chips), before=int(before is not None)
        ),
        out_shape=(
            shape_of((2 * RANK, D)),
            shape_of((2, 2 * RANK, columns)),
            shape_of((2, RANK, columns)),
            shape_of((RANK, D)),
        ),
        in_specs=[in_smem, in_vmem] + [anywhere] * 4 + [in_vmem] * (3 + 4 * (before is not None)),
        out_specs=(in_vmem,) * 4,
        scratch_shapes=[
            pltpu.VMEM(normed.shape, bf16),
            pltpu.VMEM((3,) + hidden.shape, bf16),
            pltpu.SemaphoreType.DMA((3 + len(chips),)),
        ],
        compiler_params=limits(28),
        name="feed_adapter",
    )(place, normed, grads, hidden, grad_gate, grad_up, ext, rank_in_t, down_in_t, *(before or ()))


def adapter_columns(products, mag_raw, mag, weights, slot):
    ext = weights[:, D:].astype(f32).T
    inverse = ext[INV_AT : INV_AT + 1] + ext[INV_AT + 1 : INV_AT + 2]
    proj = ext[PROJ_AT : PROJ_AT + RANK] + ext[PROJ_AT + RANK : PROJ_AT + 2 * RANK]
    grad_mag = mag_raw / mag
    grad_out = factor * (products * (mag * inverse) - proj * (grad_mag * inverse))
    turned = ext[RANK * slot : RANK * (slot + 1)] * (-grad_mag / mag)
    return grad_mag, grad_out, dot_nn(turned.astype(bf16), weights[:, :D])


def finish_kernel(weight_ref, products_ref, mag_raw_ref, mag_ref, grad_mag_ref, grad_out_ref, grad_in_ref):
    for slot in range(2):
        grad_mag, grad_out, grad_in = adapter_columns(
            products_ref[slot * RANK : (slot + 1) * RANK],
            mag_raw_ref[slot : slot + 1],
            mag_ref[slot : slot + 1],
            weight_ref[slot],
            slot,
        )
        grad_mag_ref[slot : slot + 1] = grad_mag
        grad_out_ref[slot * RANK : (slot + 1) * RANK] = grad_out
        grad_in_ref[slot * RANK : (slot + 1) * RANK] = grad_in


def finish_columns(weights, products, mag_raw, mag):
    columns = weights.shape[1]
    return kernel_call(
        finish_kernel,
        out_shape=(shape_of((2, columns)), shape_of((2 * RANK, columns)), shape_of((2 * RANK, D))),
        compiler_params=limits(40),
        name="feed_finish",
    )(weights, products, mag_raw, mag)


def feed_pack_kernel(
    place_ref, own_hbm, partner_hbm, fold_hbm, products_ref, mag_raw_ref, mag_ref, in_ref, down_in_ref,
    down_products_ref, down_total_ref, down_mag_ref, down_aux_ref, down_proj_ref, down_rank_ref,
    out_ref, down_grad_ref, weight_ref, fold_ref, full_ref, semaphores, *, share,
):
    copies = Copies(semaphores)
    fold_fetch = copies(fold_hbm, fold_ref)
    fetches = [
        copies.started((own_hbm, partner_hbm)[half].at[slot], weight_ref.at[half, slot])
        for half in range(2)
        for slot in range(2)
    ]
    columns = own_hbm.shape[1]
    chips, rows = fold_ref.shape[0], 2 * columns
    core, index, chip = place_ref[0], place_ref[1], place_ref[2]
    width = fold_ref.shape[2]
    full_ref[...] = jnp.zeros(full_ref.shape, f32)
    down_grad_ref[...] = down_total_ref[...] / down_mag_ref[...]
    inverse = down_aux_ref[RANK : RANK + 1].astype(f32) + down_aux_ref[RANK + 1 : RANK + 2].astype(f32)
    down_out = factor * down_products_ref[...] * (down_mag_ref[...] * inverse)
    turn = down_grad_ref[...] * inverse * (-factor * share)
    full_ref[:1, :D] = turn
    full_ref[RANK : 2 * RANK, :D] = down_out
    own = pl.ds(pl.multiple_of(index * width, width), width)
    own_turn = full_ref[:1, own]
    full_ref[RANK : 2 * RANK, own] += down_proj_ref[...] * own_turn
    out_ref[2 * RANK : 3 * RANK] = full_ref[RANK : 2 * RANK, :D].astype(bf16)
    out_ref[3 * RANK : 4 * RANK] = jnp.zeros((RANK, D), bf16)
    own_wide = (down_rank_ref[:, own].astype(f32) * own_turn).astype(bf16)
    full_ref[: 2 * RANK, :D] = jnp.zeros((2 * RANK, D), f32)
    fetches[0].wait()
    fold_fetch.start()
    parts = []
    ins = [in_ref[slot * RANK : (slot + 1) * RANK] for slot in range(2)]
    for half in range(2):
        outs, mags = [], []
        for slot in range(2):
            at = 2 * half + slot
            if at:
                fetches[at].wait()
            grad_mag, grad_out, grad_in = adapter_columns(
                products_ref[half, slot * RANK : (slot + 1) * RANK],
                mag_raw_ref[half + 2 * slot : half + 2 * slot + 1, :columns],
                mag_ref[half, slot : slot + 1],
                weight_ref[half, slot],
                slot,
            )
            outs.append(grad_out)
            mags.append(grad_mag)
            ins[slot] = ins[slot] + grad_in
        row = iota((RANK, columns), 0)
        tail = jnp.where(row == 0, mags[0], jnp.where(row == 1, mags[1], 0.0))
        parts.append(jnp.concatenate([*outs, down_in_ref[half], tail], axis=0))
    first, second = jnp.where(core == 0, parts[0], parts[1]), jnp.where(core == 0, parts[1], parts[0])
    full_ref[:, pl.ds(pl.multiple_of(chip * rows, HEAD), rows)] = jnp.concatenate([first, second], axis=1)
    for slot in range(2):
        out_ref[slot * RANK : (slot + 1) * RANK] = ins[slot].astype(bf16)
    fold_fetch.wait()
    for part in range(chips):
        lanes = slice(part * rows, (part + 1) * rows)
        full_ref[2 * RANK : 3 * RANK, lanes] += dot_nt(own_wide, fold_ref[part, :rows])
    for part in range(3):
        out_ref[64 * (1 + part) : 64 * (2 + part)] = full_ref[:, part * D : (part + 1) * D].astype(bf16)


def feed_pack(place, own, partner, fold_down, *rest, share):
    return kernel_call(
        functools.partial(feed_pack_kernel, share=share),
        out_shape=(shape_of((256, D), bf16), shape_of((1, D))),
        in_specs=[in_smem] + [anywhere] * 3 + [in_vmem] * 11,
        out_specs=(in_vmem,) * 2,
        scratch_shapes=[
            pltpu.VMEM((2,) + own.shape, bf16),
            pltpu.VMEM(fold_down.shape, bf16),
            pltpu.VMEM((64, 3 * D), f32),
            pltpu.SemaphoreType.DMA((5,)),
        ],
        compiler_params=limits(40),
        name="feed_pack",
    )(place, own, partner, fold_down, *rest)


def output_adapter_kernel(
    grad_ref, mag_raw_ref, mag_ref, mixed_ref, ext_ref, rank_in_ref, weight_hbm,
    grad_mag_ref, grad_out_ref, grad_in_ref, weight_ref, semaphores,
):
    copies = all_head_copies(weight_hbm, weight_ref, semaphores)
    small = dot_nt(rank_in_ref[...], mixed_ref[...]).astype(bf16)
    grad_in_total = dot_nn(ext_ref[...].T[:RANK], mixed_ref[...])
    wide = GROUP * HEAD
    for head in range(KV_HEADS):
        next_head(copies, head)
        lanes = slice(head * wide, (head + 1) * wide)
        place = slice(head * HEAD, (head + 1) * HEAD)
        mag = jnp.concatenate([mag_ref[group : group + 1, place] for group in range(GROUP)], axis=1)
        grad_mag, grad_out, grad_in = adapter_columns(
            dot_nn(small, grad_ref[:, lanes]), mag_raw_ref[:, lanes], mag, weight_ref[head], 0
        )
        for group in range(GROUP):
            own = slice(group * HEAD, (group + 1) * HEAD)
            at = slice(group * KVW + head * HEAD, group * KVW + (head + 1) * HEAD)
            grad_mag_ref[:, at] = grad_mag[:, own]
            grad_out_ref[:, at] = grad_out[:, own]
        grad_in_total = grad_in_total + grad_in
    grad_in_ref[...] = grad_in_total


def output_adapter(grads, mag_raw, mag, weights, mixed, ext, rank_in_t):
    return kernel_call(
        output_adapter_kernel,
        out_shape=(shape_of((1, D)), shape_of((RANK, D)), shape_of((RANK, D))),
        in_specs=[in_vmem] * 6 + [anywhere],
        out_specs=(in_vmem,) * 3,
        scratch_shapes=head_scratch(weights),
        compiler_params=limits(28),
        name="output_adapter",
    )(grads, mag_raw, mag, mixed, ext, rank_in_t, weights)


def residual_back_kernel(
    first_ref, second_ref, third_ref, residual_ref, gain_ref, cotangent_ref, input_ref, mixed_ref, weight_hbm,
    grad_ref, ordered_ref, mag_ref, ext_ref, grad_mixed_ref, delta_ref, weight_ref, semaphores, column_ref,
):
    tokens = residual_ref.shape[0]
    copies = all_head_copies(weight_hbm, weight_ref, semaphores)
    for head in range(KV_HEADS):
        for copy in copies[head]:
            copy.start()
    normed_grad = first_ref[...].astype(f32) + second_ref[...].astype(f32) + third_ref[...].astype(f32)
    values = residual_ref[...]
    grad_ref[...] = cotangent_ref[...].astype(f32) + rms_back(
        values, rms_inverse(values), gain_ref[...], normed_grad
    )
    wide = GROUP * HEAD
    total = None
    for head in range(KV_HEADS):
        for group in range(GROUP):
            start = group * KVW + head * HEAD
            lanes = slice(start, start + HEAD)
            own = slice(head * wide + group * HEAD, head * wide + (group + 1) * HEAD)
            grad = grad_ref[:, lanes]
            ordered_ref[:, own] = grad.astype(bf16)
            value = residual_ref[:, lanes] - input_ref[:, lanes].astype(f32)
            mag_ref[:, own] = jnp.sum(grad * value, axis=0, keepdims=True)
        for copy in copies[head]:
            copy.wait()
        part = dot_nn(ordered_ref[:, head * wide : (head + 1) * wide], weight_ref[head])
        total = part if total is None else total + part
    ext_ref[...] = total[:, D:].astype(bf16)
    grad_mixed_ref[...] = total[:, :D].astype(bf16)
    for head in range(KV_HEADS):
        for group in range(GROUP):
            start = group * KVW + head * HEAD
            lanes = slice(start, start + HEAD)
            both = grad_mixed_ref[:, lanes].astype(f32) * mixed_ref[:, lanes].astype(f32)
            column_ref[:, head * GROUP + group : head * GROUP + group + 1] = jnp.sum(both, axis=1, keepdims=True)
    rows = column_ref[...].T
    for head in range(KV_HEADS):
        for group in range(GROUP):
            at = head * GROUP + group
            delta_ref[head, :, group * tokens : (group + 1) * tokens] = rows[at : at + 1]


def residual_back(shares, residual, gain, cotangent, inputs, mixed, weights):
    tokens = residual.shape[0]
    lanes = GROUP * tokens
    return kernel_call(
        residual_back_kernel,
        out_shape=(
            shape_of((tokens, D)),
            shape_of((tokens, D), bf16),
            shape_of((1, D)),
            shape_of((tokens, EXT), bf16),
            shape_of((tokens, D), bf16),
            shape_of((KV_HEADS, 1, lanes)),
        ),
        in_specs=[in_vmem] * 8 + [anywhere],
        out_specs=(in_vmem,) * 6,
        scratch_shapes=head_scratch(weights) + [pltpu.VMEM((tokens, HEAD), f32)],
        compiler_params=limits(40),
        name="residual_back",
    )(*shares, residual, gain[None], cotangent, inputs, mixed, weights)


def turn_back(values, cosine, sine):
    return values * cosine - pltpu.roll(values, HEAD // 2, 1) * sine


def query_back_kernel(
    grad_ref, query_ref, cos_ref, sin_ref, normed_ref, rank_in_ref, mag_ref, weight_hbm,
    accum_ref, grad_in_ref, out_ref, grad_mag_ref, turned_ref, weight_ref, semaphores,
):
    copies = all_head_copies(weight_hbm, weight_ref, semaphores)
    wide = GROUP * HEAD
    small = dot_nt(rank_in_ref[...], normed_ref[...]).astype(bf16)
    total, grad_in_total = None, None
    for head in range(KV_HEADS):
        mags = []
        for group in range(GROUP):
            lanes = slice(head * wide + group * HEAD, head * wide + (group + 1) * HEAD)
            grad = turn_back(grad_ref[:, lanes], cos_ref[...], sin_ref[...])
            raw = turn_back(query_ref[:, lanes].astype(f32), cos_ref[...], sin_ref[...])
            mags.append(jnp.sum(grad * raw, axis=0, keepdims=True))
            turned_ref[:, lanes] = grad.astype(bf16)
        turned = turned_ref[:, head * wide : (head + 1) * wide]
        next_head(copies, head)
        part = dot_nn(turned, weight_ref[head])
        total = part if total is None else total + part
        place = slice(head * HEAD, (head + 1) * HEAD)
        mag = jnp.concatenate([mag_ref[group : group + 1, place] for group in range(GROUP)], axis=1)
        grad_mag, grad_out, grad_in = adapter_columns(
            dot_nn(small, turned), jnp.concatenate(mags, axis=1), mag, weight_ref[head], 0
        )
        grad_in_total = grad_in if grad_in_total is None else grad_in_total + grad_in
        for group in range(GROUP):
            own = slice(group * HEAD, (group + 1) * HEAD)
            at = slice(group * KVW + head * HEAD, group * KVW + (head + 1) * HEAD)
            grad_mag_ref[:, at] = grad_mag[:, own]
            out_ref[:, at] = grad_out[:, own]
    accum_ref[...] = total
    grad_in_ref[...] = grad_in_total + dot_nn(total[:, D:].astype(bf16).T[:RANK], normed_ref[...])


def query_back(grads, queries, weights, cosine, sine, normed, rank_in_t, mag):
    tokens = normed.shape[0]
    return kernel_call(
        query_back_kernel,
        out_shape=(
            shape_of((tokens, WIDE)),
            shape_of((RANK, D)),
            shape_of((RANK, D)),
            shape_of((1, D)),
        ),
        in_specs=[in_vmem] * 7 + [anywhere],
        out_specs=(in_vmem,) * 4,
        scratch_shapes=[pltpu.VMEM((tokens, D), bf16)] + head_scratch(weights),
        compiler_params=limits(40),
        name="query_back",
    )(grads, queries, cosine, sine, normed, rank_in_t, mag, weights)


def key_back_kernel(
    heads_ref, sent_ref, grad_ref, kv_ref, cos_ref, sin_ref, normed_ref, input_ref, gain_ref, residual_hbm,
    before_hbm, rank_in_ref, mag_ref, *refs,
):
    weight_hbm = refs[:KV_HEADS]
    input_grad_ref, grad_in_ref, out_ref, grad_mag_ref, turned_ref = refs[KV_HEADS : KV_HEADS + 5]
    weight_refs, before_ref, residual_ref, semaphores = refs[KV_HEADS + 5 :]
    copies = Copies(semaphores)
    fetches = [copies.started(ref, weight_refs.at[slot]) for slot, ref in enumerate(weight_hbm)]
    before_fetch = copies.started(before_hbm, before_ref)
    residual_fetch = copies.started(residual_hbm, residual_ref)
    small = dot_nt(rank_in_ref[...], normed_ref[...]).astype(bf16)
    total = None
    near = 2 * HEAD
    grad_ins = [None, None]
    for slot in range(KV_HEADS):
        place = heads_ref[slot] * HEAD
        mags = []
        for part in range(2):
            lanes = lanes_at(2 * place + part * HEAD)
            grad = grad_ref[:, lanes] + sent_ref[:, lanes].astype(f32)
            raw = kv_ref[:, lanes].astype(f32)
            if part == 0:
                grad = turn_back(grad, cos_ref[...], sin_ref[...])
                raw = turn_back(raw, cos_ref[...], sin_ref[...])
            mags.append(jnp.sum(grad * raw, axis=0, keepdims=True))
            turned_ref[:, slot * near + part * HEAD : slot * near + (part + 1) * HEAD] = grad.astype(bf16)
        fetches[slot].wait()
        part = dot_nn(turned_ref[:, slot * near : (slot + 1) * near], weight_refs[slot])
        total = part if total is None else total + part
        for part in range(2):
            lanes = slice(slot * near + part * HEAD, slot * near + (part + 1) * HEAD)
            grad_mag, grad_out, grad_in = adapter_columns(
                dot_nn(small[part * RANK : (part + 1) * RANK], turned_ref[:, lanes]),
                mags[part],
                mag_ref[part : part + 1, lanes_at(place)],
                weight_refs[slot, part * HEAD : (part + 1) * HEAD, :],
                1 + part,
            )
            grad_mag_ref[:, lanes_at(part * KVW + place)] = grad_mag
            out_ref[:, lanes_at(part * KVW + place)] = grad_out
            grad_ins[part] = grad_in if grad_ins[part] is None else grad_ins[part] + grad_in
    before_fetch.wait()
    total = total + before_ref[...]
    residual_fetch.wait()
    ext = total[:, D:].astype(bf16).T
    for part in range(2):
        rows = slice(part * RANK, (part + 1) * RANK)
        grad_in_ref[rows] = grad_ins[part] + dot_nn(ext[(1 + part) * RANK : (2 + part) * RANK], normed_ref[...])
    values = input_ref[...].astype(f32)
    back = rms_back(values, rms_inverse(values), gain_ref[...], total[:, :D])
    input_grad_ref[...] = (residual_ref[...] + back).astype(bf16)


def key_back(heads, sent, grads, kv, weights, cosine, sine, normed, inputs, gain, grad_residual, before, rank_in_t, mag):
    tokens = normed.shape[0]
    return kernel_call(
        key_back_kernel,
        out_shape=(
            shape_of((tokens, D), bf16),
            shape_of((2 * RANK, D)),
            shape_of((RANK, 2 * KVW)),
            shape_of((1, 2 * KVW)),
        ),
        in_specs=[in_smem] + [in_vmem] * 8 + [anywhere] * 2 + [in_vmem] * 2 + [anywhere] * KV_HEADS,
        out_specs=(in_vmem,) * 4,
        scratch_shapes=[
            pltpu.VMEM((tokens, 2 * KVW), bf16),
            pltpu.VMEM((KV_HEADS, 2 * HEAD, WIDE), bf16),
            pltpu.VMEM((tokens, WIDE), f32),
            pltpu.VMEM((tokens, D), f32),
            pltpu.SemaphoreType.DMA((KV_HEADS + 2,)),
        ],
        compiler_params=limits(40),
        name="key_back",
    )(
        heads, sent, grads, kv, cosine, sine, normed, inputs, gain[None], grad_residual,
        before, rank_in_t, mag, *weights,
    )


def cut_kernel(place_ref, value_ref, *out_refs):
    rows = out_refs[0].shape[0]
    for r, ref in enumerate(out_refs):
        ref[...] = value_ref[pl.ds(pl.multiple_of((place_ref[2] ^ r) * rows, rows), rows), :]


def cut_rows(place, value, chips):
    shape = shape_of((value.shape[0] // chips, value.shape[1]), value.dtype)
    return kernel_call(
        cut_kernel,
        out_shape=(shape,) * chips,
        in_specs=[in_smem, in_vmem],
        out_specs=(in_vmem,) * chips,
        name="cut_rows",
    )(place, value)


def join_kernel(place_ref, *refs):
    piece_refs, out_ref = refs[:-1], refs[-1]
    rows = piece_refs[0].shape[0]
    for r, ref in enumerate(piece_refs):
        out_ref[pl.ds(pl.multiple_of((place_ref[2] ^ r) * rows, rows), rows), :] = ref[...]


def join_rows(place, pieces):
    rows, lanes = pieces[0].shape
    return kernel_call(
        join_kernel,
        out_shape=shape_of((rows * len(pieces), lanes), pieces[0].dtype),
        in_specs=[in_smem] + [in_vmem] * len(pieces),
        out_specs=in_vmem,
        name="join_rows",
    )(place, *pieces)


def sides_of(place_ref, mine_ref, other_ref):
    mine, other = mine_ref[...].astype(f32), other_ref[...].astype(f32)
    first = place_ref[0] == 0
    return jnp.where(first, mine, other), jnp.where(first, other, mine)


def unpack_late_kernel(place_ref, mine_ref, other_ref, *out_refs):
    attn_in_ref, attn_out_ref, attn_mag_ref, out_in_ref, out_out_ref, out_mag_ref = out_refs
    left, right = sides_of(place_ref, mine_ref, other_ref)
    split = left.shape[1] - D
    for member in range(3):
        attn_in_ref[member] = left[member * RANK : (member + 1) * RANK, :D]
    for group in range(GROUP):
        attn_out_ref[group] = left[3 * RANK :, group * KVW : (group + 1) * KVW]
    side = right[:, D - split :]
    attn_out_ref[GROUP] = side[:RANK]
    attn_out_ref[GROUP + 1] = side[RANK : 2 * RANK]
    attn_mag_ref[...] = side[2 * RANK : 2 * RANK + GROUP + 2]
    mid = jnp.concatenate([left[:, D:], right[:, : D - split]], axis=1)
    out_in_ref[...] = mid[:RANK]
    for group in range(GROUP):
        lanes = slice(group * KVW, (group + 1) * KVW)
        out_out_ref[group] = mid[RANK : 2 * RANK, lanes]
        out_mag_ref[group : group + 1, :] = mid[2 * RANK : 2 * RANK + 1, lanes]


def unpack_early_kernel(place_ref, mine_ref, other_ref, in_ref, out_ref, mag_ref, down_in_ref, down_out_ref):
    half = D // 2
    for at, values in enumerate(sides_of(place_ref, mine_ref, other_ref)):
        lanes = slice(at * half, (at + 1) * half)
        for member in range(2):
            in_ref[member, :, lanes] = values[member * RANK : (member + 1) * RANK]
        down_out_ref[:, lanes] = values[2 * RANK : 3 * RANK]
        for part in range(3):
            start = part * D + at * half
            width = min(half, FF - start)
            if width <= 0:
                continue
            block = values[64 * (1 + part) : 64 * (2 + part), :width]
            to = slice(start, start + width)
            for member in range(2):
                out_ref[member, :, to] = block[member * RANK : (member + 1) * RANK]
            down_in_ref[:, to] = block[2 * RANK : 3 * RANK]
            mag_ref[:, to] = block[3 * RANK : 3 * RANK + 2]


def unpack(kernel, place, halves, shapes, name):
    return kernel_call(
        kernel,
        out_shape=tuple(shape_of(shape) for shape in shapes),
        in_specs=[in_smem, in_vmem, in_vmem],
        out_specs=(in_vmem,) * len(shapes),
        compiler_params=limits(24),
        name=name,
    )(place, *halves)


class Order:
    def __init__(self):
        self.last = None

    def __call__(self, *values):
        if self.last is not None:
            values = lax.optimization_barrier(tuple(values) + (self.last,))[:-1]
        return values[0] if len(values) == 1 else values

    def mark(self, value):
        self.last = value
        return value

    def pin(self, *values):
        values = self(*values)
        self.last = values[0] if isinstance(values, (tuple, list)) else values
        return values


def after(value, *others):
    return lax.optimization_barrier((value,) + others)[0]


class Links:
    def __init__(self, devices, blocks):
        self.devices = devices
        self.blocks = blocks
        self.chips = devices // 2
        self.index = lax.axis_index("dp")
        self.core = self.index % 2
        self.chip = self.index // 2
        self.block = lax.axis_index("blk")
        self.square = self.chips == 4
        self.place = jnp.stack([self.core, self.index, self.chip]).astype(jnp.int32)

    def swap(self, value, bits):
        return lax.ppermute(value, "dp", [(i, i ^ bits) for i in range(self.devices)])

    def split_swap(self, value, even_bits, odd_bits):
        return lax.ppermute(
            value, "dp", [(i, i ^ (odd_bits if i % 2 else even_bits)) for i in range(self.devices)]
        )

    def row_swap(self, value, bits):
        return lax.ppermute(value, "blk", [(i, i ^ bits) for i in range(self.blocks)])

    def row_shift(self, value, distance):
        pairs = [(i, i + distance) for i in range(self.blocks) if 0 <= i + distance < self.blocks]
        return lax.ppermute(value, "blk", pairs)

    def sides(self, value):
        return self.swap(value, 2), self.swap(value, 4)

    def across(self, side, other):
        return self.split_swap(jnp.where(self.core == 0, other, side), 2, 4)

    def total(self, value, order):
        part = value.shape[1] // 2
        value = value.astype(bf16)
        cut = lambda core: lax.dynamic_slice_in_dim(value, core * part, part, 1)
        sent = self.swap(cut(1 - self.core), 1)
        kept = cut(self.core)
        yield
        sent = order(sent)
        value = (kept.astype(f32) + sent.astype(f32)).astype(bf16)
        cuts = cut_rows(self.place, value, self.chips)
        order.mark(cuts[0])
        sent = [self.swap(cuts[r], 2 * r) for r in range(1, self.chips)]
        yield
        sent = order(*sent)
        value = order.mark(sum([cuts[0].astype(f32)] + [part.astype(f32) for part in sent]).astype(bf16))
        bits = 1
        while bits < self.blocks:
            sent = self.row_swap(value, bits)
            yield
            sent = order(sent)
            value = order.mark((value.astype(f32) + sent.astype(f32)).astype(bf16))
            bits *= 2
        sent = [self.swap(value, 2 * r) for r in range(1, self.chips)]
        yield
        sent = order(*sent)
        value = order.mark(join_rows(self.place, [value, *sent]))
        sent = self.swap(value, 1)
        yield
        sent = order(sent)
        yield value, sent

    def small_total(self, value, order):
        for swap, count in ((self.swap, self.devices), (self.row_swap, self.blocks)):
            bits = 1
            while bits < count:
                sent = swap(value, bits)
                yield
                sent = order(sent)
                value = order.mark(value + sent)
                bits *= 2
        yield value


def shards(
    block_input,
    out_cotangent,
    row_lengths,
    rope_positions,
    gain_attention,
    gain_feedforward,
    base_attention,
    base_output,
    base_feedforward,
    base_down,
    rank_in_attention,
    rank_out_attention,
    magnitude_attention,
    rank_in_output,
    rank_out_output,
    magnitude_output,
    rank_in_feedforward,
    rank_out_feedforward,
    magnitude_feedforward,
    rank_in_down,
    rank_out_down,
    magnitude_down,
    *,
    devices,
    blocks,
):
    links = Links(devices, blocks)
    order = Order()
    mark = order.mark
    index, core, chip, chips = links.index, links.core, links.chip, links.chips
    place = links.place
    partner = lambda value: links.swap(value, 1)
    rows_in = block_input[0]
    tokens = rows_in.shape[0]
    length = row_lengths[0]
    token_pos = links.block * tokens + jnp.arange(tokens, dtype=jnp.int32)
    fast = links.square and base_attention.shape[2] * devices == KVW and blocks == 4
    heads = jnp.arange(KV_HEADS, dtype=jnp.int32)
    heads = chip ^ heads if fast else heads
    scalars = jnp.stack([links.block.astype(jnp.int32), length])

    def columns_of(value, width):
        return lax.dynamic_slice_in_dim(value, index * width, width, value.ndim - 1)

    attn_cols, out_cols = base_attention.shape[2], base_output.shape[2]
    feed_cols, down_cols = base_feedforward.shape[2], base_down.shape[1]
    chip_cols = 2 * feed_cols
    attn_rank = columns_of(rank_out_attention, attn_cols)
    attn_mag = columns_of(magnitude_attention, attn_cols)
    attn_base = base_attention.transpose(0, 2, 1)
    attn_in_t = rank_in_attention.transpose(0, 2, 1)
    out_in_t = rank_in_output.T
    feed_in_t = rank_in_feedforward.transpose(0, 2, 1)
    down_in_t = rank_in_down.T

    def fold_out():
        return fold(
            order(base_output).transpose(0, 2, 1),
            out_in_t[None],
            columns_of(rank_out_output, out_cols),
            columns_of(magnitude_output, out_cols),
            0,
            False,
            "fold_o",
        )

    def fold_feed():
        return fold(
            order(base_feedforward).transpose(0, 2, 1),
            feed_in_t,
            columns_of(rank_out_feedforward, feed_cols),
            columns_of(magnitude_feedforward, feed_cols),
            0,
            True,
            "fold_feed",
        )

    def folded_down():
        return fold_down(
            order(base_down),
            down_in_t,
            columns_of(rank_out_down, down_cols),
            columns_of(magnitude_down, down_cols),
            chips,
        )

    def norm_in():
        values = order(rows_in).astype(f32)
        return (values * rms_inverse(values) * gain_attention).astype(bf16)

    frequency = rope_base ** (-(jnp.arange(HEAD // 2, dtype=f32) * 2.0) / HEAD)
    angles = rope_positions[0].astype(f32)[:, None] * frequency[None, :]
    cos_half, sin_half = jnp.cos(angles), jnp.sin(angles)
    cosine = jnp.concatenate([cos_half, cos_half], axis=-1)
    sine = jnp.concatenate([-sin_half, sin_half], axis=-1)
    tables = (cosine, sine)

    wheres = [jnp.stack([core, chip ^ r, chip, chip ^ 1, chip ^ 2]).astype(jnp.int32) for r in range(KV_HEADS)]

    settle = order.pin

    def project(where, first, second, roped, name, before=()):
        first, second = order(first, second)
        weights, out, token = head_step(where, first, second, normed, tables, roped, before, name)
        mark(token)
        return weights, out

    def send_kv(kv_blocks):
        kv_blocks.append(links.row_shift(kv_blocks[-1], 1))

    kv_fold = mark(
        fold(attn_base, attn_in_t, attn_rank[GROUP:], attn_mag[GROUP:], 1, True, "fold_kv", first=GROUP)
    )
    down_cut = lambda r: lax.dynamic_index_in_dim(down_fold, chip ^ r, 0, keepdims=False)
    spread = lambda value: lax.all_gather(value, "dp", axis=0)
    grad_out = jnp.where((token_pos < length)[:, None], out_cotangent[0], jnp.zeros((), bf16))
    grad_own = grad_out[None]
    chip_in_t = lax.dynamic_slice_in_dim(down_in_t, chip * chip_cols, chip_cols, 1)
    halves_in_t = jnp.stack(
        [lax.dynamic_slice_in_dim(chip_in_t, at * feed_cols, feed_cols, 1) for at in (core, 1 - core)]
    )
    feed_mag = lax.dynamic_slice_in_dim(magnitude_feedforward, chip * chip_cols, chip_cols, 1)
    if fast:
        kv_side, kv_other = links.sides(kv_fold)
        kv_partner = partner(kv_fold)
        q_fold = mark(fold(order(attn_base), attn_in_t, attn_rank[:GROUP], attn_mag[:GROUP], 0, False, "fold_q"))
        q_weights = spread(q_fold)
        kv_side, kv_other, kv_partner = settle(kv_side, kv_other, kv_partner)
        kv_across = links.across(kv_side, kv_other)
        kv_side_p, kv_other_p = partner(kv_side), partner(kv_other)
        o_fold = mark(fold_out())
        o_weights = spread(after(o_fold, q_fold))
        normed = mark(norm_in())
        kv_made = [
            project(wheres[0], kv_fold, kv_partner, 1, "head_kv"),
            project(wheres[1], kv_side, kv_side_p, 1, "head_kv"),
            project(wheres[2], kv_other, kv_other_p, 1, "head_kv"),
        ]
        kv_across = settle(kv_across)
        kv_across_p = partner(kv_across)
        kv_made.append(project(wheres[3], kv_across, kv_across_p, 1, "head_kv", [out for _, out in kv_made]))
        kv_own = kv_made[-1][1]
        kv_blocks = [kv_own]
        send_kv(kv_blocks)
        grad_own, halves_in_t, feed_mag = settle(grad_own, halves_in_t, feed_mag)
        feed_own = mark(fold_feed())
        kv_blocks[1] = settle(kv_blocks[1])
        send_kv(kv_blocks)
        down_fold, down_proj = folded_down()
        mark(down_proj)
        down_0, down_c1, down_c2, down_c3 = settle(*[down_cut(r) for r in range(4)])
        grad_all = spread(order(grad_out))
        kv_blocks[2] = settle(kv_blocks[2])
        send_kv(kv_blocks)
        queries = mark(query_project(order(normed), tables, q_weights))
        kv_blocks[3] = settle(kv_blocks[3])
        down_1, down_2, down_3 = links.swap(down_c1, 2), links.swap(down_c2, 4), links.swap(down_c3, 6)
        mixed, lse = attend(scalars, order(queries), kv_blocks)
        mark(lse)
        feed_partner = partner(order(feed_own))

        def feed_late():
            near = settle(down_1, down_2, down_3)
            pieces = []
            for piece in (down_0, *near):
                pieces += [piece, partner(piece)]
            return settle(*pieces)

    else:
        q_fold = fold(attn_base, attn_in_t, attn_rank[:GROUP], attn_mag[:GROUP], 0, False, "fold_q")
        q_weights, o_weights, normed = spread(q_fold), spread(fold_out()), norm_in()
        down_fold, down_proj = folded_down()
        feed_own = fold_feed()
        feed_partner = partner(feed_own)
        whole = lax.all_gather(kv_fold, "dp", axis=1, tiled=True).reshape(2, KV_HEADS, 2, HEAD // 2, WIDE)
        kv_made = []
        for j in range(KV_HEADS):
            before = [out for _, out in kv_made] if j == KV_HEADS - 1 else ()
            where = jnp.array([0, j, 0, 1, 2], jnp.int32)
            kv_made.append(project(where, whole[:, j, 0], whole[:, j, 1], 1, "head_kv", before))
        kv_own = kv_made[-1][1]
        kv_blocks = [kv_own]
        for _ in range(1, blocks):
            send_kv(kv_blocks)
        queries = query_project(normed, tables, q_weights)
        grad_all = spread(grad_out)
        mixed, lse = attend(scalars, queries, kv_blocks)
        down_pieces = []
        for r in range(chips):
            piece = links.swap(down_cut(r), 2 * r) if r else down_cut(r)
            down_pieces += [piece, partner(piece)]
    residual, normed_feed = output_project(order(mixed), o_weights, rows_in, gain_feedforward)
    mark(normed_feed)

    forward = lambda normed_group: settle(*feed_forward(order(normed_group), feed_own, feed_partner, tokens))
    aux = []

    def backward(members, kept):
        grads = grad_own if members == (None,) else grad_all
        kept = list(order(*kept)) if isinstance(kept, (tuple, list)) else [order(kept)]
        made = feed_back(place, grads, members, kept, feed_own, feed_partner, down_pieces, tokens)
        mark(made[0])
        count = len(members)
        return made[:count], made[count : 2 * count], made[2 * count :]

    mag_sums = []

    def adapters(members, normed_group, made, before):
        hidden, grad_gate, grad_up, ext, mags, down_aux = made[2]
        parts = feed_adapter(
            place, order(normed_group), grad_own if members == (None,) else grad_all, members, hidden, grad_gate,
            grad_up, ext, feed_in_t.reshape(2 * RANK, D), halves_in_t, before,
        )
        mark(parts[0])
        aux.append(down_aux)
        mag_sums.append(mags)
        return tuple(parts)

    if fast:
        side, other = links.sides(normed_feed)
        down_pieces = feed_late()
        own_made = backward((None,), normed_feed)
        side, other = settle(side, other)
        crossed = links.across(side, other)
        near = settle(jnp.concatenate([side, other]))
        near_kept = forward(near)
        sums = adapters((None,), normed_feed, own_made, None)
        crossed = settle(crossed)
        far_made = backward((3,), crossed)
        from_far = links.split_swap(far_made[0][0], 2, 4)
        near_made = backward((1, 2), near_kept)
        early_first = links.split_swap(near_made[0][0], 2, 4)
        from_far = settle(from_far)
        late_share = settle((near_made[0][1].astype(f32) + from_far.astype(f32)).astype(bf16))
        early_second = links.split_swap(late_share, 4, 2)
        down_mag_steps = links.small_total(own_made[2][4][4:5] + near_made[2][4][4:5] + far_made[2][4][4:5], order)
        next(down_mag_steps)
        sums = adapters((1, 2), near, near_made, sums)
        next(down_mag_steps)
        sums = adapters((3,), crossed, far_made, sums)
        next(down_mag_steps)
        early_first = settle(early_first)
        reduced = (own_made[0][0], early_first, early_second)
        shares_out = [own_made[1][0], *near_made[1], far_made[1][0]]
    else:
        sums, shares_grad, shares_out = None, [], []
        for r in range(chips):
            normed_group = links.swap(normed_feed, 2 * r) if r else normed_feed
            made = backward((r,), normed_group)
            sums = adapters((r,), normed_group, made, sums)
            shares_grad.append(made[0][0])
            shares_out.append(made[1][0])
        rest = sum(links.swap(shares_grad[r], 2 * r).astype(f32) for r in range(1, chips)).astype(bf16)
        reduced = (shares_grad[0], rest, jnp.zeros(rest.shape, bf16))
        down_mag_steps = links.small_total(sum(mags[4:5] for mags in mag_sums), order)
        next(down_mag_steps)
    feed_in, feed_products, down_in, down_products = sums
    mag_raw = sum(mag_sums)
    for _ in range(2):
        next(down_mag_steps)
    reduced = settle(*reduced)
    grad_residual, grad_ordered, out_mag_raw, out_ext, grad_mixed, delta = residual_back(
        reduced, residual, gain_feedforward, grad_out, rows_in, mixed, o_weights
    )
    mark(delta)

    def pack_early(down_mag_total):
        feed_mags = jnp.stack(
            [lax.dynamic_slice_in_dim(feed_mag, at * feed_cols, feed_cols, 1) for at in (core, 1 - core)]
        )
        if fast:
            early, down_grad_mag = feed_pack(
                place, feed_own, feed_partner, down_fold, *order(feed_products, mag_raw), feed_mags, feed_in, down_in,
                down_products, down_mag_total, magnitude_down[None], aux[0], down_proj, rank_out_down,
                share=1.0 / blocks,
            )
            return down_grad_mag, early
        finished = [
            finish_columns(weights, feed_products[half], mag_raw[half:4:2, :feed_cols], feed_mags[half])
            for half, weights in enumerate((feed_own, feed_partner))
        ]
        grad_mag, grad_out_part, grad_in_part = zip(*finished)
        columns = [
            jnp.concatenate([part.astype(bf16) for part in parts])
            for parts in zip(grad_out_part, down_in, grad_mag)
        ]
        columns = jnp.where(core == 0, jnp.concatenate(columns, axis=1), jnp.concatenate(columns[::-1], axis=1))
        full = lax.dynamic_update_slice(jnp.zeros((64, 3 * D), bf16), columns, (0, chip * chip_cols))
        down_aux = aux[0]
        down_inverse = (down_aux[RANK].astype(f32) + down_aux[RANK + 1].astype(f32))[None]
        down_grad_mag = down_mag_total / magnitude_down[None]
        down_out = factor * down_products * (magnitude_down[None] * down_inverse)
        own_turn = columns_of(-down_grad_mag * down_inverse, down_cols) * (factor / blocks)
        down_out = lax.dynamic_update_slice(
            down_out, columns_of(down_out, down_cols) + down_proj * own_turn, (0, index * down_cols)
        )
        own_wide = (columns_of(rank_out_down.astype(f32), down_cols) * own_turn).astype(bf16)
        down_norm_in = lax.dot_general(
            own_wide, down_fold[:, :chip_cols], (((1,), (2,)), ((), ())), preferred_element_type=f32
        ).reshape(RANK, FF)
        down_full = (full[2 * RANK : 3 * RANK, :FF].astype(f32) + down_norm_in).astype(bf16)
        full = lax.dynamic_update_slice(full, down_full, (2 * RANK, 0))
        top = jnp.concatenate([(feed_in + sum(grad_in_part)).astype(bf16), down_out.astype(bf16)])
        return down_grad_mag, jnp.concatenate(
            [jnp.pad(top, ((0, 16), (0, 0)))] + [full[:, i * D : (i + 1) * D] for i in range(3)]
        )

    grad_queries, grad_kvs = None, []

    def keys_back(distance):
        grad_queries_next, grad_kv = attend_back(
            scalars, order(queries), grad_mixed, lse, delta, kv_blocks[distance], grad_queries, distance
        )
        mark(grad_kv)
        return grad_queries_next, grad_kv

    def pass_down(passed, grad_kv):
        passed = order(passed)
        passed = settle((passed.astype(f32) + grad_kv.astype(f32)).astype(bf16))
        return links.row_shift(passed, -1)

    grad_queries, grad_kv = keys_back(blocks - 1)
    passed = links.row_shift(grad_kv, -1)
    held = None
    for distance in reversed(range(1, blocks - 1)):
        grad_queries, grad_kv = keys_back(distance)
        if held is not None:
            passed = pass_down(passed, held)
        held = grad_kv
    if fast:
        out_far = links.split_swap(order(shares_out[3]), 2, 4)
        out_first = links.split_swap(order(shares_out[1]), 2, 4)
    grad_queries, grad_kv = keys_back(0)
    out_grad_mag, out_out, out_in = output_adapter(
        order(grad_ordered), out_mag_raw, magnitude_output, o_weights, mixed, out_ext, out_in_t
    )
    mark(out_in)
    passed = pass_down(passed, held)
    if fast:
        out_far, out_first = settle(out_far, out_first)
        out_late = settle((shares_out[2].astype(f32) + out_far.astype(f32)).astype(bf16))
        out_second = links.split_swap(out_late, 4, 2)
        out_parts = [shares_out[0], out_first, out_second]
    else:
        out_parts = [shares_out[0]] + [links.swap(shares_out[r], 2 * r) for r in range(1, chips)]
    q_acc, q_in, q_out, q_grad_mag = query_back(
        order(grad_queries), queries, q_weights, cosine, sine, normed, attn_in_t[0], magnitude_attention[:GROUP]
    )
    mark(q_in)
    for down_mag_total in down_mag_steps:
        pass
    down_grad_mag, early = pack_early(down_mag_total)
    early_steps = links.total(settle(early), order)
    next(early_steps)
    passed, *out_parts = settle(passed, *out_parts)
    next(early_steps)
    input_grad, kv_in, kv_out, kv_grad_mag = key_back(
        heads, passed, grad_kv, kv_own, [weights for weights, _ in kv_made], cosine, sine, normed, rows_in,
        gain_attention, grad_residual, q_acc, attn_in_t[1:].reshape(2 * RANK, D), magnitude_attention[GROUP:],
    )
    mark(kv_in)
    rows = lambda *parts: jnp.concatenate([part.astype(bf16) for part in parts])
    late = jnp.concatenate(
        [
            rows(q_in, kv_in, q_out),
            rows(out_in, out_out, out_grad_mag, jnp.zeros((31, D), bf16)),
            rows(
                kv_out[:, :KVW],
                kv_out[:, KVW:],
                q_grad_mag.reshape(-1, KVW),
                kv_grad_mag.reshape(-1, KVW),
                jnp.zeros((26, KVW), bf16),
            ),
        ],
        axis=1,
    )
    late_steps = links.total(settle(late), order)
    late = early = None
    next(late_steps)
    block_out = settle((residual + sum(part.astype(f32) for part in out_parts)).astype(bf16))[None]
    while early is None:
        early = next(early_steps)
        if late is None:
            late = next(late_steps)
    early_shapes = ((2, RANK, D), (2, RANK, FF), (2, FF), (RANK, FF), (RANK, D))
    feed_in, feed_out, feed_mag, down_in, down_out = unpack(
        unpack_early_kernel, place, order(*early), early_shapes, "unpack_early"
    )
    mark(feed_mag)
    while late is None:
        late = next(late_steps)
    late_shapes = ((3, RANK, D), (GROUP + 2, RANK, KVW), (GROUP + 2, KVW), (RANK, D), (GROUP, RANK, KVW), (GROUP, KVW))
    attn_in, attn_out, attn_mag, out_in, out_out, out_mag = unpack(
        unpack_late_kernel, place, order(*late), late_shapes, "unpack_late"
    )
    return (
        block_out,
        input_grad[None],
        attn_in.transpose(0, 2, 1),
        attn_out,
        attn_mag,
        out_in.T,
        out_out,
        out_mag,
        feed_in.transpose(0, 2, 1),
        feed_out,
        feed_mag,
        down_in.T,
        down_out,
        down_grad_mag[0],
    )


def solution(mesh):
    split_tokens = P("dp", "blk", None)
    placed = (
        split_tokens,
        split_tokens,
        P("dp"),
        P("dp", "blk"),
        P(),
        P(),
        P(None, None, "dp"),
        P(None, None, "dp"),
        P(None, None, "dp"),
        P(None, "dp"),
    ) + (P(),) * 12
    return jax.shard_map(
        functools.partial(shards, devices=mesh.shape["dp"], blocks=mesh.shape["blk"]),
        mesh=mesh,
        in_specs=placed,
        out_specs=(split_tokens, split_tokens) + (P(),) * 12,
        check_vma=False,
    )
```

```python
import functools

import jax
import jax.numpy as jnp
from jax import lax
from jax.experimental import pallas as pl
from jax.experimental.pallas import tpu as pltpu
from jax.sharding import PartitionSpec as P

D = 2048
KV_HEADS = 4
HEAD = 128
FF = 5632
RANK = 16
GROUP = 4
KVW = 512

EXT = 128
WIDE = D + EXT
SLOTS = 3
INV_AT = 48
PROJ_AT = 64
AUX = 32

factor = 32.0 / RANK
rms_eps = 1e-05
rope_base = 10000.0
masked_score = -1e30
log2_e = 1.4426950408889634
score_scale = HEAD ** (-0.5)
f32 = jnp.float32
bf16 = jnp.bfloat16


def dot_nt(left, right):
    return lax.dot_general(left, right, (((1,), (1,)), ((), ())), preferred_element_type=f32)


def dot_nn(left, right):
    return lax.dot_general(left, right, (((1,), (0,)), ((), ())), preferred_element_type=f32)


def dot_tn(left, right):
    return lax.dot_general(left, right, (((0,), (0,)), ((), ())), preferred_element_type=f32)


def limits(mebibytes):
    return pltpu.CompilerParams(vmem_limit_bytes=mebibytes << 20)


def kernel_call(*args, in_specs=None, **options):
    if in_specs is not None:
        options["in_specs"] = in_specs
    call = pl.pallas_call(
        *args, cost_estimate=pl.CostEstimate(flops=0, transcendentals=0, bytes_accessed=0), **options
    )
    if in_specs is None:
        return call
    keep = lambda value, spec: pltpu.with_memory_space_constraint(value, pltpu.HBM) if spec is anywhere else value
    return lambda *operands: call(*[keep(value, spec) for value, spec in zip(operands, in_specs)])


anywhere = pl.BlockSpec(memory_space=pltpu.HBM)
in_vmem = pl.BlockSpec(memory_space=pltpu.VMEM)
in_smem = pl.BlockSpec(memory_space=pltpu.SMEM)


def shape_of(shape, dtype=f32):
    return jax.ShapeDtypeStruct(shape, dtype)


def split_low(value):
    high = value.astype(bf16)
    return high, (value - high.astype(f32)).astype(bf16)


def iota(shape, dim):
    return lax.broadcasted_iota(jnp.int32, shape, dim)


def lanes_at(start):
    return pl.ds(pl.multiple_of(start, HEAD), HEAD)


def fold_kernel(weight_ref, rank_in_ref, rank_out_ref, mag_ref, out_ref, column_ref, *, first_slot, moving):
    slot = first_slot + (pl.program_id(0) if moving else 0)
    rows = weight_ref.shape[1]

    def placed_at(start):
        spot = iota((RANK, EXT), 1) == iota((RANK, EXT), 0) + start
        return jnp.where(spot, 1.0, 0.0).astype(bf16)

    @pl.when(pl.program_id(1) == 0)
    def _():
        column_ref[0] = dot_tn(rank_out_ref[0], placed_at(0))
        column_ref[1] = dot_tn(rank_out_ref[0], placed_at(RANK * slot))
        mags = jnp.broadcast_to(mag_ref[0], (8, mag_ref.shape[2]))
        one = jnp.where(iota((8, EXT), 0) == 0, 1.0, 0.0)
        column_ref[2] = lax.dot_general(
            mags, one, (((0,), (0,)), ((), ())), precision=lax.Precision.HIGHEST, preferred_element_type=f32
        )

    own = pl.ds(pl.multiple_of(pl.program_id(1) * rows, 16), rows)
    doubled = (factor * column_ref[0, own, :RANK]).astype(bf16)
    merged = weight_ref[0].astype(f32) + dot_nn(doubled, rank_in_ref[0])
    inverse = 1.0 / jnp.sqrt(jnp.sum(merged * merged, axis=1, keepdims=True))
    scale = column_ref[2, own, :1] * inverse
    folded = (merged * scale).astype(bf16)
    out_ref[0, :, :D] = folded
    ext = column_ref[1, own, :] * (factor * scale)
    for index, part in enumerate(split_low(dot_nt(folded, rank_in_ref[0]))):
        ext = ext + dot_nn(part, placed_at(PROJ_AT + RANK * index))
    lane = iota(ext.shape, 1)
    for index, part in enumerate(split_low(inverse)):
        ext = ext + jnp.where(lane == INV_AT + index, part.astype(f32), 0.0)
    out_ref[0, :, D:] = ext.astype(bf16)


def fold(weights, rank_in_t, rank_out, magnitude, rank_first, moving, name, first=0):
    members, columns = magnitude.shape
    pieces = 4 if columns % 64 == 0 and columns > 256 else 1
    rows = columns // pieces
    rank_block = (lambda b, c: (b + rank_first, 0, 0)) if moving else (lambda b, c: (rank_first, 0, 0))
    return kernel_call(
        functools.partial(fold_kernel, first_slot=rank_first, moving=moving),
        out_shape=shape_of((members, columns, WIDE), bf16),
        grid=(members, pieces),
        in_specs=[
            pl.BlockSpec((1, rows, D), lambda b, c: (b + first, c, 0)),
            pl.BlockSpec((1, RANK, D), rank_block),
            pl.BlockSpec((1, RANK, columns), lambda b, c: (b, 0, 0)),
            pl.BlockSpec((1, 1, columns), lambda b, c: (b, 0, 0)),
        ],
        out_specs=pl.BlockSpec((1, rows, WIDE), lambda b, c: (b, c, 0)),
        scratch_shapes=[pltpu.VMEM((3, columns, EXT), f32)],
        compiler_params=limits(32),
        name=name,
    )(weights, rank_in_t, rank_out, magnitude[:, None, :])


def fold_down_kernel(weight_ref, rank_in_ref, rank_out_ref, mag_ref, out_ref, proj_ref, merged_ref, *, chips):
    rows = weight_ref.shape[0] // chips
    total = 0.0
    doubled = (factor * rank_out_ref[...].astype(f32)).astype(bf16)
    for part in range(chips):
        span = slice(part * rows, (part + 1) * rows)
        merged = weight_ref[span, :].astype(f32) + dot_tn(rank_in_ref[:, span], doubled)
        merged_ref[span, :] = merged
        total = total + jnp.sum(merged * merged, axis=0, keepdims=True)
    inverse = 1.0 / jnp.sqrt(total)
    scale = mag_ref[...] * inverse
    high, low = split_low(inverse)
    row = iota((AUX - RANK, scale.shape[1]), 0)
    tail = jnp.where(row == 0, high.astype(f32), jnp.where(row == 1, low.astype(f32), 0.0))
    aux = jnp.concatenate([doubled.astype(f32) * scale, tail], axis=0).astype(bf16)
    proj = 0.0
    for part in range(chips):
        span = slice(part * rows, (part + 1) * rows)
        folded = (merged_ref[span, :] * scale).astype(bf16)
        out_ref[part, :rows, :] = folded
        out_ref[part, rows:, :] = aux
        proj = proj + dot_nn(rank_in_ref[:, span], folded)
    proj_ref[...] = proj


def fold_down(weights, rank_in_t, rank_out, magnitude, chips):
    inputs, columns = weights.shape
    return kernel_call(
        functools.partial(fold_down_kernel, chips=chips),
        out_shape=(shape_of((chips, inputs // chips + AUX, columns), bf16), shape_of((RANK, columns))),
        scratch_shapes=[pltpu.VMEM((inputs, columns), f32)],
        compiler_params=limits(32),
        name="fold_down",
    )(weights, rank_in_t, rank_out, magnitude[None])


def head_kernel(scalar_ref, first_ref, second_ref, input_ref, cos_ref, sin_ref, *refs, roped):
    before_refs, (weight_ref, out_ref, token_ref) = refs[:-3], refs[-3:]
    members, half = first_ref.shape[0], first_ref.shape[1]
    for member in range(members):
        for order, ref in ((scalar_ref[0], first_ref), (1 - scalar_ref[0], second_ref)):
            weight_ref[pl.ds(pl.multiple_of((2 * member + order) * half, half), half), :] = ref[member]
    wide = members * HEAD
    for index, ref in enumerate(before_refs):
        out_ref[:, pl.ds(pl.multiple_of(scalar_ref[2 + index] * wide, wide), wide)] = ref[...]
    raw = dot_nt(input_ref[...], weight_ref[:, :D])
    for member in range(members):
        part = raw[:, member * HEAD : (member + 1) * HEAD]
        if member < roped:
            part = part * cos_ref[...] + pltpu.roll(part, HEAD // 2, 1) * sin_ref[...]
        start = (scalar_ref[1] * wide if before_refs else 0) + member * HEAD
        out_ref[:, lanes_at(start)] = part.astype(bf16)
    token_ref[...] = jnp.zeros(token_ref.shape, f32)


def head_step(scalars, first, second, inputs, tables, roped, before, name):
    members, half, _ = first.shape
    tokens = inputs.shape[0]
    wide = members * HEAD
    return kernel_call(
        functools.partial(head_kernel, roped=roped),
        out_shape=(
            shape_of((wide, WIDE), bf16),
            shape_of((tokens, (1 + len(before)) * wide), bf16),
            shape_of((8, HEAD)),
        ),
        in_specs=[in_smem] + [in_vmem] * (5 + len(before)),
        out_specs=(in_vmem,) * 3,
        compiler_params=limits(24),
        name=name,
    )(scalars, first, second, inputs, *tables, *before)


def head_copies(weight_ref, head, out_ref, semaphores, first=0):
    devices, members, part = weight_ref.shape[:3]
    parts = devices // KV_HEADS
    copies = []
    for at in range(parts):
        for member in range(members):
            copies.append(
                pltpu.make_async_copy(
                    weight_ref.at[parts * head + at, member],
                    out_ref.at[pl.ds((parts * member + at) * part, part), :],
                    semaphores.at[first + len(copies)],
                )
            )
    return copies


def head_scratch(weights):
    each = weights.shape[0] // KV_HEADS * weights.shape[1]
    return [
        pltpu.VMEM((KV_HEADS, weights.shape[1] * HEAD, WIDE), bf16),
        pltpu.SemaphoreType.DMA((KV_HEADS * each,)),
    ]


def all_head_copies(weight_ref, out_ref, semaphores):
    each = weight_ref.shape[0] // KV_HEADS * weight_ref.shape[1]
    return [head_copies(weight_ref, head, out_ref.at[head], semaphores, head * each) for head in range(KV_HEADS)]


def next_head(copies, head):
    if head == 0:
        for copy in copies[0] + copies[1]:
            copy.start()
    elif head + 1 < len(copies):
        for copy in copies[head + 1]:
            copy.start()
    for copy in copies[head]:
        copy.wait()


def query_kernel(input_ref, cos_ref, sin_ref, weight_hbm, out_ref, weight_ref, semaphores):
    copies = all_head_copies(weight_hbm, weight_ref, semaphores)
    for head in range(KV_HEADS):
        next_head(copies, head)
        raw = dot_nt(input_ref[...], weight_ref[head, :, :D])
        for group in range(GROUP):
            part = raw[:, group * HEAD : (group + 1) * HEAD]
            part = part * cos_ref[...] + pltpu.roll(part, HEAD // 2, 1) * sin_ref[...]
            start = (head * GROUP + group) * HEAD
            out_ref[:, start : start + HEAD] = part.astype(bf16)


def query_project(inputs, tables, weights):
    return kernel_call(
        query_kernel,
        out_shape=shape_of((inputs.shape[0], D), bf16),
        in_specs=[in_vmem] * 3 + [anywhere],
        out_specs=in_vmem,
        scratch_shapes=head_scratch(weights),
        compiler_params=limits(24),
        name="query_project",
    )(inputs, *tables, weights)


def masked_scores(keys, queries, key_first, length, causal):
    tokens, lanes = keys.shape[0], queries.shape[0]
    scores = dot_nt(keys, queries)
    key_pos = key_first + iota((tokens, 1), 0)
    scores = scores + jnp.where(key_pos < length, 0.0, masked_score)
    if causal:
        allowed = iota((tokens, lanes), 0) <= (iota((tokens, lanes), 1) & (tokens - 1))
        scores = jnp.where(allowed, scores, masked_score)
    return scores


def attend_kernel(scalar_ref, query_ref, *refs, steps):
    kv_refs = refs[:steps]
    mixed_ref, lse_ref, stacked_ref, max_ref, sum_ref, accum_ref = refs[steps:]
    head = pl.program_id(0)
    tokens = query_ref.shape[0]
    block_index, length = scalar_ref[0], scalar_ref[1]
    scale = score_scale * log2_e
    for group in range(GROUP):
        stacked_ref[group * tokens : (group + 1) * tokens, :] = query_ref[:, group * HEAD : (group + 1) * HEAD]

    for distance in range(steps):

        def step(distance=distance):
            keys = kv_refs[distance][:, :HEAD]
            values = kv_refs[distance][:, HEAD:]
            key_first = (block_index - distance) * tokens
            scores = masked_scores(keys, stacked_ref[...], key_first, length, distance == 0)
            block_max = jnp.max(scores, axis=0, keepdims=True)
            new_max = block_max if distance == 0 else jnp.maximum(max_ref[...], block_max)
            terms = jnp.exp2((scores - new_max) * scale)
            added = jnp.sum(terms, axis=0, keepdims=True)
            product = dot_tn(values, terms.astype(bf16))
            if distance == 0:
                sum_ref[...] = added
                accum_ref[...] = product
            else:
                fade = jnp.exp2((max_ref[...] - new_max) * scale)
                sum_ref[...] = sum_ref[...] * fade + added
                accum_ref[...] = accum_ref[...] * fade + product
            max_ref[...] = new_max

        if distance == 0:
            step()
        else:
            pl.when(block_index >= distance)(step)
    mixed = accum_ref[...] / sum_ref[...]
    for group in range(GROUP):
        part = mixed[:, group * tokens : (group + 1) * tokens]
        mixed_ref[:, lanes_at(group * KVW + head * HEAD)] = part.T.astype(bf16)
    lse_ref[0] = max_ref[...] * scale + jnp.log(sum_ref[...]) * log2_e


def attend(scalars, queries, kv_blocks):
    tokens = queries.shape[0]
    steps = len(kv_blocks)
    lanes = GROUP * tokens
    return kernel_call(
        functools.partial(attend_kernel, steps=steps),
        out_shape=(shape_of((tokens, D), bf16), shape_of((KV_HEADS, 1, lanes))),
        grid_spec=pltpu.PrefetchScalarGridSpec(
            num_scalar_prefetch=1,
            grid=(KV_HEADS,),
            in_specs=[pl.BlockSpec((tokens, GROUP * HEAD), lambda j, s: (0, j))]
            + [pl.BlockSpec((tokens, 2 * HEAD), lambda j, s: (0, j))] * steps,
            out_specs=(
                pl.BlockSpec((tokens, D), lambda j, s: (0, 0)),
                pl.BlockSpec((1, 1, lanes), lambda j, s: (j, 0, 0)),
            ),
            scratch_shapes=[
                pltpu.VMEM((lanes, HEAD), bf16),
                pltpu.VMEM((1, lanes), f32),
                pltpu.VMEM((1, lanes), f32),
                pltpu.VMEM((HEAD, lanes), f32),
            ],
        ),
        compiler_params=limits(40),
        name="attend",
    )(scalars, queries, *kv_blocks)


def attend_back_kernel(scalar_ref, query_ref, grad_ref, lse_ref, delta_ref, kv_ref, *refs, distance, chained):
    if chained:
        before_ref, grad_query_ref, grad_kv_ref, stacked_ref, stacked_grad_ref = refs
    else:
        grad_query_ref, grad_kv_ref, stacked_ref, stacked_grad_ref = refs
    head = pl.program_id(0)
    tokens = query_ref.shape[0]
    block_index, length = scalar_ref[0], scalar_ref[1]
    active = (block_index >= distance) & (block_index * tokens < length)

    @pl.when(active)
    def _():
        for group in range(GROUP):
            rows = slice(group * tokens, (group + 1) * tokens)
            stacked_ref[rows, :] = query_ref[:, group * HEAD : (group + 1) * HEAD]
            stacked_grad_ref[rows, :] = grad_ref[:, lanes_at(group * KVW + head * HEAD)]
        keys = kv_ref[:, :HEAD]
        values = kv_ref[:, HEAD:]
        key_first = (block_index - distance) * tokens
        scores = masked_scores(keys, stacked_ref[...], key_first, length, distance == 0)
        probs = jnp.exp2(scores * (score_scale * log2_e) - lse_ref[0])
        grad_probs = dot_nt(values, stacked_grad_ref[...])
        grad_scores = (probs * (grad_probs - delta_ref[0])).astype(bf16)
        grad_values = dot_nn(probs.astype(bf16), stacked_grad_ref[...])
        grad_keys = dot_nn(grad_scores, stacked_ref[...]) * score_scale
        grad_queries = dot_tn(grad_scores, keys) * score_scale
        for group in range(GROUP):
            lanes = slice(group * HEAD, (group + 1) * HEAD)
            part = grad_queries[group * tokens : (group + 1) * tokens, :]
            if chained:
                part = part + before_ref[:, lanes]
            grad_query_ref[:, lanes] = part
        grad_kv_ref[:, :HEAD] = grad_keys.astype(grad_kv_ref.dtype)
        grad_kv_ref[:, HEAD:] = grad_values.astype(grad_kv_ref.dtype)

    @pl.when(jnp.logical_not(active))
    def _():
        grad_query_ref[...] = before_ref[...] if chained else jnp.zeros(grad_query_ref.shape, f32)
        grad_kv_ref[...] = jnp.zeros(grad_kv_ref.shape, grad_kv_ref.dtype)


def attend_back(scalars, queries, grad_mixed, lse, delta, kv_block, before, distance):
    tokens = queries.shape[0]
    lanes = GROUP * tokens
    row = pl.BlockSpec((1, 1, lanes), lambda j, s: (j, 0, 0))
    per_query = pl.BlockSpec((tokens, GROUP * HEAD), lambda j, s: (0, j))
    per_key = pl.BlockSpec((tokens, 2 * HEAD), lambda j, s: (0, j))
    chained = before is not None
    operands = [scalars, queries, grad_mixed, lse, delta, kv_block]
    specs = [per_query, pl.BlockSpec((tokens, D), lambda j, s: (0, 0)), row, row, per_key]
    if chained:
        operands += [before]
        specs += [per_query]
    return kernel_call(
        functools.partial(attend_back_kernel, distance=distance, chained=chained),
        out_shape=(shape_of((tokens, D)), shape_of((tokens, 2 * KVW), f32 if distance == 0 else bf16)),
        grid_spec=pltpu.PrefetchScalarGridSpec(
            num_scalar_prefetch=1,
            grid=(KV_HEADS,),
            in_specs=specs,
            out_specs=(per_query, per_key),
            scratch_shapes=[pltpu.VMEM((lanes, HEAD), bf16), pltpu.VMEM((lanes, HEAD), bf16)],
        ),
        input_output_aliases={6: 0} if chained else {},
        compiler_params=limits(40),
        name=f"attend_back_{distance}",
    )(*operands)


def rms_inverse(values):
    return lax.rsqrt(jnp.mean(values * values, axis=-1, keepdims=True) + rms_eps)


def rms_back(values, inverse, gain, grad):
    scaled = grad * gain
    return inverse * (scaled - values * (inverse * inverse * jnp.mean(scaled * values, axis=-1, keepdims=True)))


def output_kernel(mixed_ref, input_ref, gain_ref, weight_hbm, residual_ref, normed_ref, weight_ref, semaphores):
    copies = all_head_copies(weight_hbm, weight_ref, semaphores)
    for head in range(KV_HEADS):
        next_head(copies, head)
        value = dot_nt(mixed_ref[...], weight_ref[head, :, :D])
        for group in range(GROUP):
            start = group * KVW + head * HEAD
            lanes = slice(start, start + HEAD)
            residual_ref[:, lanes] = input_ref[:, lanes].astype(f32) + value[:, group * HEAD : (group + 1) * HEAD]
    values = residual_ref[...]
    normed_ref[...] = (values * rms_inverse(values) * gain_ref[...]).astype(bf16)


def output_project(mixed, weights, inputs, gain):
    tokens = mixed.shape[0]
    return kernel_call(
        output_kernel,
        out_shape=(shape_of((tokens, D)), shape_of((tokens, D), bf16)),
        in_specs=[in_vmem] * 3 + [anywhere],
        out_specs=(in_vmem,) * 2,
        scratch_shapes=head_scratch(weights),
        compiler_params=limits(28),
        name="output_project",
    )(mixed, inputs, gain[None], weights)


class Copies:
    def __init__(self, semaphores):
        self.semaphores = semaphores
        self.made = []

    def __call__(self, source, target):
        copy = pltpu.make_async_copy(source, target, self.semaphores.at[len(self.made)])
        self.made.append(copy)
        return copy

    def started(self, source, target):
        copy = self(source, target)
        copy.start()
        return copy


def feed_forward_kernel(normed_ref, own_ref, partner_ref, gate_hbm, up_hbm, weight_ref, value_ref, semaphores, *, block):
    copies = Copies(semaphores)
    pairs = [(half, member) for half in range(2) for member in range(2)]
    fetches = [
        copies((own_ref, partner_ref)[half].at[member], weight_ref.at[2 * half + member]) for half, member in pairs
    ]
    fetches[0].start()
    fetches[1].start()
    stores = []
    for half, member in pairs:
        at = 2 * half + member
        fetches[at].wait()
        if at + 2 < 4:
            fetches[at + 2].start()
        for start in range(0, normed_ref.shape[0], block):
            rows = slice(start, start + block)
            value_ref[at, rows, :] = dot_nt(normed_ref[rows, :], weight_ref[at, :, :D])
        stores.append(copies.started(value_ref.at[at], (gate_hbm, up_hbm)[member].at[half]))
    for store in stores:
        store.wait()


def feed_forward(normed, own, partner, block):
    tokens = normed.shape[0]
    columns = own.shape[1]
    return kernel_call(
        functools.partial(feed_forward_kernel, block=block),
        out_shape=(shape_of((2, tokens, columns)), shape_of((2, tokens, columns))),
        in_specs=[in_vmem, anywhere, anywhere],
        out_specs=(anywhere,) * 2,
        scratch_shapes=[
            pltpu.VMEM((4, columns, WIDE), bf16),
            pltpu.VMEM((4, tokens, columns), f32),
            pltpu.SemaphoreType.DMA((8,)),
        ],
        compiler_params=limits(28),
        name="feed_forward",
    )(normed, own, partner)


NEAR = ("first", "last")


def near_turn(place_ref, r):
    return place_ref[0] ^ NEAR.index(r)


def grad_copies(copies, place_ref, grad_hbm, grad_ref, chips, block):
    return [
        copies(
            grad_hbm.at[
                0 if r is None else place_ref[2] ^ (1 + near_turn(place_ref, r) if r in NEAR else r)
            ],
            grad_ref.at[pl.ds(turn * block, block), :]
        )
        for turn, r in enumerate(chips)
    ]


MAGS = 8


def feed_back_kernel(place_ref, grad_hbm, own_ref, partner_ref, *refs, block, devices, chips, fused):
    kept, refs = refs[: 2 - fused], refs[2 - fused :]
    piece_refs, refs = refs[:devices], refs[devices:]
    count = len(chips)
    share_hbm, down_hbm, refs = refs[:count], refs[count : 2 * count], refs[2 * count :]
    hidden_hbm, grad_gate_hbm, grad_up_hbm, ext_ref, mag_ref, aux_ref, refs = *refs[:6], refs[6:]
    weight_ref, down_weight_ref, grad_ref, share_ref, made_ref, value_ref, semaphores = refs
    core = place_ref[0]
    columns = own_ref.shape[1]
    width = piece_refs[0].shape[1]
    copies = Copies(semaphores)
    fetches = grad_copies(copies, place_ref, grad_hbm, grad_ref, chips, block)
    for i, ref in enumerate(piece_refs):
        lanes = pl.ds(pl.multiple_of((place_ref[1] ^ i) * width, width), width)
        fetches.append(copies(ref, down_weight_ref.at[:, lanes]))
    if not fused:
        start = pl.multiple_of(near_turn(place_ref, chips[0]) * block, block)
        for at in range(2):
            fetches.append(copies(kept[at].at[:, pl.ds(start, block), :], value_ref.at[at]))
    weight_fetches = [copies(ref, weight_ref.at[half]) for half, ref in enumerate((own_ref, partner_ref))]
    if fused:
        weight_fetches[0].start()
    for fetch in fetches:
        fetch.start()
    mag_ref[...] = jnp.zeros(mag_ref.shape, f32)
    if fused:
        weight_fetches[0].wait()
        value_ref[0, 0] = dot_nt(kept[0][...], weight_ref[0, 0, :, :D])
        value_ref[1, 0] = dot_nt(kept[0][...], weight_ref[0, 1, :, :D])
    else:
        weight_fetches[0].start()
    for fetch in fetches:
        fetch.wait()
    weight_fetches[1].start()
    aux_ref[...] = down_weight_ref[2 * columns :, :]
    stores = []
    for turn in range(count):
        rows = slice(turn * block, (turn + 1) * block)
        grad = grad_ref[rows, :]
        share, down = None, None
        for half in range(2):
            order = core if half == 0 else 1 - core
            down_rows = pl.ds(pl.multiple_of(order * columns, 16), columns)
            if fused and half:
                weight_fetches[1].wait()
                value_ref[0, 1] = dot_nt(kept[0][...], weight_ref[1, 0, :, :D])
                value_ref[1, 1] = dot_nt(kept[0][...], weight_ref[1, 1, :, :D])
            gate, up = value_ref[0, half, rows, :], value_ref[1, half, rows, :]
            grad_hidden = dot_nt(grad, down_weight_ref[down_rows, :])
            sigma = 1.0 / (1.0 + jnp.exp(-gate))
            silu = gate * sigma
            hidden = (silu * up).astype(bf16)
            grad_gate = grad_hidden * up * (sigma + silu * (1.0 - sigma))
            grad_up = grad_hidden * silu
            mag_ref[half : half + 1, :columns] += jnp.sum(grad_gate * gate, axis=0, keepdims=True)
            mag_ref[2 + half : 3 + half, :columns] += jnp.sum(grad_up * up, axis=0, keepdims=True)
            grad_gate, grad_up = grad_gate.astype(bf16), grad_up.astype(bf16)
            for at, (value, ref) in enumerate(((hidden, hidden_hbm), (grad_gate, grad_gate_hbm), (grad_up, grad_up_hbm))):
                made_ref[at, half, rows, :] = value
                stores.append(copies.started(made_ref.at[at, half, rows, :], ref.at[half, rows, :]))
            part = dot_nn(hidden, down_weight_ref[down_rows, :])
            down = part if down is None else down + part
            if turn == 0 and not fused:
                weight_fetches[half].wait()
            part = dot_nn(grad_gate, weight_ref[half, 0]) + dot_nn(grad_up, weight_ref[half, 1])
            share = part if share is None else share + part
        share_ref[0, rows, :] = share[:, :D].astype(bf16)
        share_ref[1, rows, :] = down.astype(bf16)
        ext_ref[rows, :EXT] = share[:, D:].astype(bf16)
        small = dot_nt(grad, down_weight_ref[2 * columns :, :])
        ext_ref[rows, EXT : EXT + AUX] = small.astype(bf16)
        mag_ref[4:5, :] += jnp.sum(grad.astype(f32) * down, axis=0, keepdims=True)
    for at in range(count):
        turn = at ^ core if count == 2 else at
        rows = pl.ds(pl.multiple_of(turn * block, block), block)
        stores.append(copies.started(share_ref.at[0, rows, :], share_hbm[at]))
        stores.append(copies.started(share_ref.at[1, rows, :], down_hbm[at]))
    for store in stores:
        store.wait()


def feed_back(place, grads, chips, kept, own, partner, pieces, block):
    fused = int(len(kept) == 1)
    count = len(chips)
    tokens = count * block
    columns = own.shape[1]
    devices = len(pieces)
    return kernel_call(
        functools.partial(feed_back_kernel, block=block, devices=devices, chips=chips, fused=fused),
        out_shape=(shape_of((block, D), bf16),) * (2 * count)
        + (
            shape_of((2, tokens, columns), bf16),
            shape_of((2, tokens, columns), bf16),
            shape_of((2, tokens, columns), bf16),
            shape_of((tokens, 2 * EXT), bf16),
            shape_of((MAGS, D)),
            shape_of((AUX, D), bf16),
        ),
        in_specs=[in_smem] + [anywhere] * 3 + ([in_vmem] if fused else [anywhere] * 2) + [anywhere] * devices,
        out_specs=(anywhere,) * (3 + 2 * count) + (in_vmem,) * 3,
        scratch_shapes=[
            pltpu.VMEM((2, 2, columns, WIDE), bf16),
            pltpu.VMEM((2 * columns + AUX, D), bf16),
            pltpu.VMEM((tokens, D), bf16),
            pltpu.VMEM((2, tokens, D), bf16),
            pltpu.VMEM((3, 2, tokens, columns), bf16),
            pltpu.VMEM((2, 2, tokens, columns), f32),
            pltpu.SemaphoreType.DMA((4 + devices + 9 * count,)),
        ],
        compiler_params=limits(54),
        name="feed_back",
    )(place, grads, own, partner, *kept, *pieces)


def feed_adapter_kernel(
    place_ref, normed_hbm, grad_hbm, hidden_hbm, grad_gate_hbm, grad_up_hbm, ext_ref, rank_in_ref, down_in_ref, *refs,
    chips, block, before,
):
    before_refs, refs = refs[: 4 * before], refs[4 * before :]
    in_ref, out_ref, down_rank_in_ref, down_out_ref, grad_ref, normed_ref, made_ref, semaphores = refs
    copies = Copies(semaphores)
    start = near_turn(place_ref, chips[0]) * block if chips[0] in NEAR else 0
    normed_fetch = copies.started(normed_hbm.at[pl.ds(pl.multiple_of(start, block), block), :], normed_ref)
    fetches = [
        copies.started(ref, made_ref.at[at]) for at, ref in enumerate((hidden_hbm, grad_gate_hbm, grad_up_hbm))
    ]
    for fetch in grad_copies(copies, place_ref, grad_hbm, grad_ref, chips, block):
        fetch.start()
        fetches.append(fetch)

    def put(ref, index, value, at):
        ref[index] = value + before_refs[at][index] if before else value

    normed_fetch.wait()
    normed = normed_ref[...]
    small = dot_nt(rank_in_ref[...], normed).astype(bf16)
    ext = ext_ref[...].T
    put(in_ref, ..., dot_nn(ext[: 2 * RANK], normed), 0)
    for fetch in fetches:
        fetch.wait()
    down_small = 0.0
    for half in range(2):
        put(out_ref, (half, slice(0, RANK)), dot_nn(small[:RANK], made_ref[1, half]), 1)
        put(out_ref, (half, slice(RANK, 2 * RANK)), dot_nn(small[RANK:], made_ref[2, half]), 1)
        down_small = down_small + dot_nt(down_in_ref[half], made_ref[0, half])
        put(down_rank_in_ref, half, dot_nn(ext[EXT : EXT + RANK], made_ref[0, half]), 2)
    put(down_out_ref, ..., dot_nn(down_small.astype(bf16), grad_ref[...]), 3)


def feed_adapter(place, normed, grads, chips, hidden, grad_gate, grad_up, ext, rank_in_t, down_in_t, before):
    columns = hidden.shape[2]
    return kernel_call(
        functools.partial(
            feed_adapter_kernel, chips=chips, block=hidden.shape[1], before=int(before is not None)
        ),
        out_shape=(
            shape_of((2 * RANK, D)),
            shape_of((2, 2 * RANK, columns)),
            shape_of((2, RANK, columns)),
            shape_of((RANK, D)),
        ),
        in_specs=[in_smem] + [anywhere] * 5 + [in_vmem] * (3 + 4 * (before is not None)),
        out_specs=(in_vmem,) * 4,
        scratch_shapes=[
            pltpu.VMEM((hidden.shape[1], D), bf16),
            pltpu.VMEM((hidden.shape[1], D), bf16),
            pltpu.VMEM((3,) + hidden.shape, bf16),
            pltpu.SemaphoreType.DMA((5,)),
        ],
        compiler_params=limits(28),
        name="feed_adapter",
    )(place, normed, grads, hidden, grad_gate, grad_up, ext, rank_in_t, down_in_t, *(before or ()))


def adapter_columns(products, mag_raw, mag, weights, slot):
    ext = weights[:, D:].astype(f32).T
    inverse = ext[INV_AT : INV_AT + 1] + ext[INV_AT + 1 : INV_AT + 2]
    proj = ext[PROJ_AT : PROJ_AT + RANK] + ext[PROJ_AT + RANK : PROJ_AT + 2 * RANK]
    grad_mag = mag_raw / mag
    grad_out = factor * (products * (mag * inverse) - proj * (grad_mag * inverse))
    turned = ext[RANK * slot : RANK * (slot + 1)] * (-grad_mag / mag)
    return grad_mag, grad_out, dot_nn(turned.astype(bf16), weights[:, :D])


def finish_kernel(weight_ref, products_ref, mag_raw_ref, mag_ref, grad_mag_ref, grad_out_ref, grad_in_ref):
    for slot in range(2):
        grad_mag, grad_out, grad_in = adapter_columns(
            products_ref[slot * RANK : (slot + 1) * RANK],
            mag_raw_ref[slot : slot + 1],
            mag_ref[slot : slot + 1],
            weight_ref[slot],
            slot,
        )
        grad_mag_ref[slot : slot + 1] = grad_mag
        grad_out_ref[slot * RANK : (slot + 1) * RANK] = grad_out
        grad_in_ref[slot * RANK : (slot + 1) * RANK] = grad_in


def finish_columns(weights, products, mag_raw, mag):
    columns = weights.shape[1]
    return kernel_call(
        finish_kernel,
        out_shape=(shape_of((2, columns)), shape_of((2 * RANK, columns)), shape_of((2 * RANK, D))),
        compiler_params=limits(40),
        name="feed_finish",
    )(weights, products, mag_raw, mag)


def feed_pack_kernel(
    place_ref, own_hbm, partner_hbm, fold_hbm, products_ref, mag_raw_ref, mag_ref, in_ref, down_in_ref,
    down_products_ref, down_total_ref, down_mag_ref, down_aux_ref, down_proj_ref, down_rank_ref,
    kept_ref, given_ref, down_grad_ref, out_ref, weight_ref, fold_ref, full_ref, semaphores, *, share,
):
    copies = Copies(semaphores)
    fold_fetch = copies(fold_hbm, fold_ref)
    fetches = [
        copies.started((own_hbm, partner_hbm)[half].at[slot], weight_ref.at[half, slot])
        for half in range(2)
        for slot in range(2)
    ]
    columns = own_hbm.shape[1]
    chips, rows = fold_ref.shape[0], 2 * columns
    core, index, chip = place_ref[0], place_ref[1], place_ref[2]
    width = fold_ref.shape[2]
    full_ref[...] = jnp.zeros(full_ref.shape, f32)
    down_grad_ref[...] = down_total_ref[...] / down_mag_ref[...]
    inverse = down_aux_ref[RANK : RANK + 1].astype(f32) + down_aux_ref[RANK + 1 : RANK + 2].astype(f32)
    down_out = factor * down_products_ref[...] * (down_mag_ref[...] * inverse)
    turn = down_grad_ref[...] * inverse * (-factor * share)
    full_ref[:1, :D] = turn
    full_ref[RANK : 2 * RANK, :D] = down_out
    own = pl.ds(pl.multiple_of(index * width, width), width)
    own_turn = full_ref[:1, own]
    full_ref[RANK : 2 * RANK, own] += down_proj_ref[...] * own_turn
    out_ref[2 * RANK : 3 * RANK] = full_ref[RANK : 2 * RANK, :D].astype(bf16)
    out_ref[3 * RANK : 4 * RANK] = jnp.zeros((RANK, D), bf16)
    own_wide = (down_rank_ref[:, own].astype(f32) * own_turn).astype(bf16)
    full_ref[: 2 * RANK, :D] = jnp.zeros((2 * RANK, D), f32)
    fetches[0].wait()
    fold_fetch.start()
    parts = []
    ins = [in_ref[slot * RANK : (slot + 1) * RANK] for slot in range(2)]
    for half in range(2):
        outs, mags = [], []
        for slot in range(2):
            at = 2 * half + slot
            if at:
                fetches[at].wait()
            grad_mag, grad_out, grad_in = adapter_columns(
                products_ref[half, slot * RANK : (slot + 1) * RANK],
                mag_raw_ref[half + 2 * slot : half + 2 * slot + 1, :columns],
                mag_ref[half, slot : slot + 1],
                weight_ref[half, slot],
                slot,
            )
            outs.append(grad_out)
            mags.append(grad_mag)
            ins[slot] = ins[slot] + grad_in
        row = iota((RANK, columns), 0)
        tail = jnp.where(row == 0, mags[0], jnp.where(row == 1, mags[1], 0.0))
        parts.append(jnp.concatenate([*outs, down_in_ref[half], tail], axis=0))
    first, second = jnp.where(core == 0, parts[0], parts[1]), jnp.where(core == 0, parts[1], parts[0])
    full_ref[:, pl.ds(pl.multiple_of(chip * rows, HEAD), rows)] = jnp.concatenate([first, second], axis=1)
    for slot in range(2):
        out_ref[slot * RANK : (slot + 1) * RANK] = ins[slot].astype(bf16)
    fold_fetch.wait()
    for part in range(chips):
        lanes = slice(part * rows, (part + 1) * rows)
        full_ref[2 * RANK : 3 * RANK, lanes] += dot_nt(own_wide, fold_ref[part, :rows])
    for part in range(3):
        out_ref[64 * (1 + part) : 64 * (2 + part)] = full_ref[:, part * D : (part + 1) * D].astype(bf16)
    give_halves(place_ref, out_ref, kept_ref, given_ref)


def feed_pack(place, own, partner, fold_down, *rest, share):
    return kernel_call(
        functools.partial(feed_pack_kernel, share=share),
        out_shape=(shape_of((256, D // 2), bf16), shape_of((256, D // 2), bf16), shape_of((1, D))),
        in_specs=[in_smem] + [anywhere] * 3 + [in_vmem] * 11,
        out_specs=(in_vmem,) * 3,
        scratch_shapes=[
            pltpu.VMEM((256, D), bf16),
            pltpu.VMEM((2,) + own.shape, bf16),
            pltpu.VMEM(fold_down.shape, bf16),
            pltpu.VMEM((64, 3 * D), f32),
            pltpu.SemaphoreType.DMA((5,)),
        ],
        compiler_params=limits(40),
        name="feed_pack",
    )(place, own, partner, fold_down, *rest)


def output_adapter_kernel(
    grad_ref, mag_raw_ref, mag_ref, mixed_ref, ext_ref, rank_in_ref, weight_hbm,
    grad_mag_ref, grad_out_ref, grad_in_ref, weight_ref, semaphores,
):
    copies = all_head_copies(weight_hbm, weight_ref, semaphores)
    small = dot_nt(rank_in_ref[...], mixed_ref[...]).astype(bf16)
    grad_in_total = dot_nn(ext_ref[...].T[:RANK], mixed_ref[...])
    wide = GROUP * HEAD
    for head in range(KV_HEADS):
        next_head(copies, head)
        lanes = slice(head * wide, (head + 1) * wide)
        place = slice(head * HEAD, (head + 1) * HEAD)
        mag = jnp.concatenate([mag_ref[group : group + 1, place] for group in range(GROUP)], axis=1)
        grad_mag, grad_out, grad_in = adapter_columns(
            dot_nn(small, grad_ref[:, lanes]), mag_raw_ref[:, lanes], mag, weight_ref[head], 0
        )
        for group in range(GROUP):
            own = slice(group * HEAD, (group + 1) * HEAD)
            at = slice(group * KVW + head * HEAD, group * KVW + (head + 1) * HEAD)
            grad_mag_ref[:, at] = grad_mag[:, own]
            grad_out_ref[:, at] = grad_out[:, own]
        grad_in_total = grad_in_total + grad_in
    grad_in_ref[...] = grad_in_total


def output_adapter(grads, mag_raw, mag, weights, mixed, ext, rank_in_t):
    return kernel_call(
        output_adapter_kernel,
        out_shape=(shape_of((1, D)), shape_of((RANK, D)), shape_of((RANK, D))),
        in_specs=[in_vmem] * 6 + [anywhere],
        out_specs=(in_vmem,) * 3,
        scratch_shapes=head_scratch(weights),
        compiler_params=limits(28),
        name="output_adapter",
    )(grads, mag_raw, mag, mixed, ext, rank_in_t, weights)


def residual_back_kernel(
    first_ref, second_ref, third_ref, residual_ref, gain_ref, cotangent_ref, input_ref, mixed_ref, weight_hbm,
    grad_ref, ordered_ref, mag_ref, ext_ref, grad_mixed_ref, delta_ref, weight_ref, semaphores, column_ref,
):
    tokens = residual_ref.shape[0]
    copies = all_head_copies(weight_hbm, weight_ref, semaphores)
    for head in range(KV_HEADS):
        for copy in copies[head]:
            copy.start()
    normed_grad = first_ref[...].astype(f32) + second_ref[...].astype(f32) + third_ref[...].astype(f32)
    values = residual_ref[...]
    grad_ref[...] = cotangent_ref[...].astype(f32) + rms_back(
        values, rms_inverse(values), gain_ref[...], normed_grad
    )
    wide = GROUP * HEAD
    total = None
    for head in range(KV_HEADS):
        for group in range(GROUP):
            start = group * KVW + head * HEAD
            lanes = slice(start, start + HEAD)
            own = slice(head * wide + group * HEAD, head * wide + (group + 1) * HEAD)
            grad = grad_ref[:, lanes]
            ordered_ref[:, own] = grad.astype(bf16)
            value = residual_ref[:, lanes] - input_ref[:, lanes].astype(f32)
            mag_ref[:, own] = jnp.sum(grad * value, axis=0, keepdims=True)
        for copy in copies[head]:
            copy.wait()
        part = dot_nn(ordered_ref[:, head * wide : (head + 1) * wide], weight_ref[head])
        total = part if total is None else total + part
    ext_ref[...] = total[:, D:].astype(bf16)
    grad_mixed_ref[...] = total[:, :D].astype(bf16)
    for head in range(KV_HEADS):
        for group in range(GROUP):
            start = group * KVW + head * HEAD
            lanes = slice(start, start + HEAD)
            both = grad_mixed_ref[:, lanes].astype(f32) * mixed_ref[:, lanes].astype(f32)
            column_ref[:, head * GROUP + group : head * GROUP + group + 1] = jnp.sum(both, axis=1, keepdims=True)
    rows = column_ref[...].T
    for head in range(KV_HEADS):
        for group in range(GROUP):
            at = head * GROUP + group
            delta_ref[head, :, group * tokens : (group + 1) * tokens] = rows[at : at + 1]


def residual_back(shares, residual, gain, cotangent, inputs, mixed, weights):
    tokens = residual.shape[0]
    lanes = GROUP * tokens
    return kernel_call(
        residual_back_kernel,
        out_shape=(
            shape_of((tokens, D)),
            shape_of((tokens, D), bf16),
            shape_of((1, D)),
            shape_of((tokens, EXT), bf16),
            shape_of((tokens, D), bf16),
            shape_of((KV_HEADS, 1, lanes)),
        ),
        in_specs=[in_vmem] * 8 + [anywhere],
        out_specs=(in_vmem,) * 6,
        scratch_shapes=head_scratch(weights) + [pltpu.VMEM((tokens, HEAD), f32)],
        compiler_params=limits(40),
        name="residual_back",
    )(*shares, residual, gain[None], cotangent, inputs, mixed, weights)


def turn_back(values, cosine, sine):
    return values * cosine - pltpu.roll(values, HEAD // 2, 1) * sine


def query_back_kernel(
    grad_ref, query_ref, cos_ref, sin_ref, normed_ref, rank_in_ref, mag_ref, weight_hbm,
    accum_ref, grad_in_ref, out_ref, grad_mag_ref, turned_ref, weight_ref, semaphores,
):
    copies = all_head_copies(weight_hbm, weight_ref, semaphores)
    wide = GROUP * HEAD
    small = dot_nt(rank_in_ref[...], normed_ref[...]).astype(bf16)
    total, grad_in_total = None, None
    for head in range(KV_HEADS):
        mags = []
        for group in range(GROUP):
            lanes = slice(head * wide + group * HEAD, head * wide + (group + 1) * HEAD)
            grad = turn_back(grad_ref[:, lanes], cos_ref[...], sin_ref[...])
            raw = turn_back(query_ref[:, lanes].astype(f32), cos_ref[...], sin_ref[...])
            mags.append(jnp.sum(grad * raw, axis=0, keepdims=True))
            turned_ref[:, lanes] = grad.astype(bf16)
        turned = turned_ref[:, head * wide : (head + 1) * wide]
        next_head(copies, head)
        part = dot_nn(turned, weight_ref[head])
        total = part if total is None else total + part
        place = slice(head * HEAD, (head + 1) * HEAD)
        mag = jnp.concatenate([mag_ref[group : group + 1, place] for group in range(GROUP)], axis=1)
        grad_mag, grad_out, grad_in = adapter_columns(
            dot_nn(small, turned), jnp.concatenate(mags, axis=1), mag, weight_ref[head], 0
        )
        grad_in_total = grad_in if grad_in_total is None else grad_in_total + grad_in
        for group in range(GROUP):
            own = slice(group * HEAD, (group + 1) * HEAD)
            at = slice(group * KVW + head * HEAD, group * KVW + (head + 1) * HEAD)
            grad_mag_ref[:, at] = grad_mag[:, own]
            out_ref[:, at] = grad_out[:, own]
    accum_ref[...] = total
    grad_in_ref[...] = grad_in_total + dot_nn(total[:, D:].astype(bf16).T[:RANK], normed_ref[...])


def query_back(grads, queries, weights, cosine, sine, normed, rank_in_t, mag):
    tokens = normed.shape[0]
    return kernel_call(
        query_back_kernel,
        out_shape=(
            shape_of((tokens, WIDE)),
            shape_of((RANK, D)),
            shape_of((RANK, D)),
            shape_of((1, D)),
        ),
        in_specs=[in_vmem] * 7 + [anywhere],
        out_specs=(in_vmem,) * 4,
        scratch_shapes=[pltpu.VMEM((tokens, D), bf16)] + head_scratch(weights),
        compiler_params=limits(40),
        name="query_back",
    )(grads, queries, cosine, sine, normed, rank_in_t, mag, weights)


def give_halves(place_ref, value_ref, kept_ref, given_ref):
    half = value_ref.shape[1] // 2
    left, right = value_ref[:, :half].astype(bf16), value_ref[:, half:].astype(bf16)
    first = place_ref[0] == 0
    kept_ref[...] = jnp.where(first, left, right)
    given_ref[...] = jnp.where(first, right, left)


def key_back_kernel(
    heads_ref, sent_ref, grad_ref, kv_ref, cos_ref, sin_ref, normed_ref, input_ref, gain_ref, residual_hbm,
    before_hbm, rank_in_ref, mag_ref, place_ref, q_in_ref, q_out_ref, q_mag_ref, out_in_ref, out_out_ref, out_mag_ref,
    *refs,
):
    weight_hbm = refs[:KV_HEADS]
    input_grad_ref, kept_ref, given_ref, late_ref, out_ref, grad_mag_ref, turned_ref = refs[KV_HEADS : KV_HEADS + 7]
    weight_refs, before_ref, residual_ref, semaphores = refs[KV_HEADS + 7 :]
    copies = Copies(semaphores)
    fetches = [copies.started(ref, weight_refs.at[slot]) for slot, ref in enumerate(weight_hbm)]
    before_fetch = copies.started(before_hbm, before_ref)
    residual_fetch = copies.started(residual_hbm, residual_ref)
    small = dot_nt(rank_in_ref[...], normed_ref[...]).astype(bf16)
    total = None
    near = 2 * HEAD
    grad_ins = [None, None]
    for slot in range(KV_HEADS):
        place = heads_ref[slot] * HEAD
        mags = []
        for part in range(2):
            lanes = lanes_at(2 * place + part * HEAD)
            grad = grad_ref[:, lanes] + sent_ref[:, lanes].astype(f32)
            raw = kv_ref[:, lanes].astype(f32)
            if part == 0:
                grad = turn_back(grad, cos_ref[...], sin_ref[...])
                raw = turn_back(raw, cos_ref[...], sin_ref[...])
            mags.append(jnp.sum(grad * raw, axis=0, keepdims=True))
            turned_ref[:, slot * near + part * HEAD : slot * near + (part + 1) * HEAD] = grad.astype(bf16)
        fetches[slot].wait()
        part = dot_nn(turned_ref[:, slot * near : (slot + 1) * near], weight_refs[slot])
        total = part if total is None else total + part
        for part in range(2):
            lanes = slice(slot * near + part * HEAD, slot * near + (part + 1) * HEAD)
            grad_mag, grad_out, grad_in = adapter_columns(
                dot_nn(small[part * RANK : (part + 1) * RANK], turned_ref[:, lanes]),
                mags[part],
                mag_ref[part : part + 1, lanes_at(place)],
                weight_refs[slot, part * HEAD : (part + 1) * HEAD, :],
                1 + part,
            )
            grad_mag_ref[:, lanes_at(part * KVW + place)] = grad_mag
            out_ref[:, lanes_at(part * KVW + place)] = grad_out
            grad_ins[part] = grad_in if grad_ins[part] is None else grad_ins[part] + grad_in
    before_fetch.wait()
    total = total + before_ref[...]
    residual_fetch.wait()
    ext = total[:, D:].astype(bf16).T
    late_ref[:RANK, :D] = q_in_ref[...]
    for part in range(2):
        late_ref[(1 + part) * RANK : (2 + part) * RANK, :D] = grad_ins[part] + dot_nn(
            ext[(1 + part) * RANK : (2 + part) * RANK], normed_ref[...]
        )
    late_ref[3 * RANK :, :D] = q_out_ref[...]
    late_ref[:RANK, D : 2 * D] = out_in_ref[...]
    late_ref[RANK : 2 * RANK, D : 2 * D] = out_out_ref[...]
    late_ref[2 * RANK :, D : 2 * D] = jnp.where(iota((2 * RANK, D), 0) == 0, out_mag_ref[...], 0.0)
    row = iota((2 * RANK, KVW), 0)
    side = jnp.zeros((2 * RANK, KVW), f32)
    for at in range(GROUP):
        side = jnp.where(row == at, q_mag_ref[:, at * KVW : (at + 1) * KVW], side)
    for part in range(2):
        lanes = slice(part * KVW, (part + 1) * KVW)
        late_ref[part * RANK : (part + 1) * RANK, 2 * D :] = out_ref[:, lanes]
        side = jnp.where(row == GROUP + part, grad_mag_ref[:, lanes], side)
    late_ref[2 * RANK :, 2 * D :] = side
    give_halves(place_ref, late_ref, kept_ref, given_ref)
    values = input_ref[...].astype(f32)
    back = rms_back(values, rms_inverse(values), gain_ref[...], total[:, :D])
    input_grad_ref[...] = (residual_ref[...] + back).astype(bf16)


def key_back(
    heads, sent, grads, kv, weights, cosine, sine, normed, inputs, gain, grad_residual, before, rank_in_t, mag, place,
    *others
):
    tokens = normed.shape[0]
    wide = 2 * D + KVW
    return kernel_call(
        key_back_kernel,
        out_shape=(
            shape_of((tokens, D), bf16),
            shape_of((4 * RANK, wide // 2), bf16),
            shape_of((4 * RANK, wide // 2), bf16),
        ),
        in_specs=[in_smem] + [in_vmem] * 8 + [anywhere] * 2 + [in_vmem] * 2 + [in_smem] + [in_vmem] * 6
        + [anywhere] * KV_HEADS,
        out_specs=(in_vmem,) * 3,
        scratch_shapes=[
            pltpu.VMEM((4 * RANK, wide), f32),
            pltpu.VMEM((RANK, 2 * KVW), f32),
            pltpu.VMEM((1, 2 * KVW), f32),
            pltpu.VMEM((tokens, 2 * KVW), bf16),
            pltpu.VMEM((KV_HEADS, 2 * HEAD, WIDE), bf16),
            pltpu.VMEM((tokens, WIDE), f32),
            pltpu.VMEM((tokens, D), f32),
            pltpu.SemaphoreType.DMA((KV_HEADS + 2,)),
        ],
        compiler_params=limits(40),
        name="key_back",
    )(
        heads, sent, grads, kv, cosine, sine, normed, inputs, gain[None], grad_residual,
        before, rank_in_t, mag, place, *others, *weights,
    )


def cut_kernel(place_ref, mine_ref, other_ref, *refs):
    out_refs, total_ref = refs[:-1], refs[-1]
    rows = out_refs[0].shape[0]
    total_ref[...] = (mine_ref[...].astype(f32) + other_ref[...].astype(f32)).astype(bf16)
    for r, ref in enumerate(out_refs):
        ref[...] = total_ref[pl.ds(pl.multiple_of((place_ref[2] ^ r) * rows, rows), rows), :]


def cut_rows(place, mine, other, chips):
    shape = shape_of((mine.shape[0] // chips, mine.shape[1]), bf16)
    return kernel_call(
        cut_kernel,
        out_shape=(shape,) * chips,
        in_specs=[in_smem, in_vmem, in_vmem],
        out_specs=(in_vmem,) * chips,
        scratch_shapes=[pltpu.VMEM(mine.shape, bf16)],
        name="cut_rows",
    )(place, mine, other)


def join_kernel(place_ref, *refs):
    piece_refs, out_ref = refs[:-1], refs[-1]
    rows = piece_refs[0].shape[0]
    for r, ref in enumerate(piece_refs):
        out_ref[pl.ds(pl.multiple_of((place_ref[2] ^ r) * rows, rows), rows), :] = ref[...]


def join_rows(place, pieces):
    rows, lanes = pieces[0].shape
    return kernel_call(
        join_kernel,
        out_shape=shape_of((rows * len(pieces), lanes), pieces[0].dtype),
        in_specs=[in_smem] + [in_vmem] * len(pieces),
        out_specs=in_vmem,
        name="join_rows",
    )(place, *pieces)


def sides_of(place_ref, mine_ref, other_ref):
    mine, other = mine_ref[...].astype(f32), other_ref[...].astype(f32)
    first = place_ref[0] == 0
    return jnp.where(first, mine, other), jnp.where(first, other, mine)


def unpack_late_kernel(place_ref, mine_ref, other_ref, *out_refs):
    attn_in_ref, attn_out_ref, attn_mag_ref, out_in_ref, out_out_ref, out_mag_ref = out_refs
    left, right = sides_of(place_ref, mine_ref, other_ref)
    split = left.shape[1] - D
    for member in range(3):
        attn_in_ref[member] = left[member * RANK : (member + 1) * RANK, :D]
    for group in range(GROUP):
        attn_out_ref[group] = left[3 * RANK :, group * KVW : (group + 1) * KVW]
    side = right[:, D - split :]
    attn_out_ref[GROUP] = side[:RANK]
    attn_out_ref[GROUP + 1] = side[RANK : 2 * RANK]
    attn_mag_ref[...] = side[2 * RANK : 2 * RANK + GROUP + 2]
    mid = jnp.concatenate([left[:, D:], right[:, : D - split]], axis=1)
    out_in_ref[...] = mid[:RANK]
    for group in range(GROUP):
        lanes = slice(group * KVW, (group + 1) * KVW)
        out_out_ref[group] = mid[RANK : 2 * RANK, lanes]
        out_mag_ref[group : group + 1, :] = mid[2 * RANK : 2 * RANK + 1, lanes]


def unpack_early_kernel(place_ref, mine_ref, other_ref, in_ref, out_ref, mag_ref, down_in_ref, down_out_ref):
    half = D // 2
    for at, values in enumerate(sides_of(place_ref, mine_ref, other_ref)):
        lanes = slice(at * half, (at + 1) * half)
        for member in range(2):
            in_ref[member, :, lanes] = values[member * RANK : (member + 1) * RANK]
        down_out_ref[:, lanes] = values[2 * RANK : 3 * RANK]
        for part in range(3):
            start = part * D + at * half
            width = min(half, FF - start)
            if width <= 0:
                continue
            block = values[64 * (1 + part) : 64 * (2 + part), :width]
            to = slice(start, start + width)
            for member in range(2):
                out_ref[member, :, to] = block[member * RANK : (member + 1) * RANK]
            down_in_ref[:, to] = block[2 * RANK : 3 * RANK]
            mag_ref[:, to] = block[3 * RANK : 3 * RANK + 2]


def unpack(kernel, place, halves, shapes, name):
    return kernel_call(
        kernel,
        out_shape=tuple(shape_of(shape) for shape in shapes),
        in_specs=[in_smem, in_vmem, in_vmem],
        out_specs=(in_vmem,) * len(shapes),
        compiler_params=limits(24),
        name=name,
    )(place, *halves)


class Order:
    def __init__(self):
        self.last = None

    def __call__(self, *values):
        if self.last is not None:
            values = lax.optimization_barrier(tuple(values) + (self.last,))[:-1]
        return values[0] if len(values) == 1 else values

    def mark(self, value):
        self.last = value
        return value

    def pin(self, *values):
        values = self(*values)
        self.last = values[0] if isinstance(values, (tuple, list)) else values
        return values


def after(value, *others):
    return lax.optimization_barrier((value,) + others)[0]


class Links:
    def __init__(self, devices, blocks):
        self.devices = devices
        self.blocks = blocks
        self.chips = devices // 2
        self.index = lax.axis_index("dp")
        self.core = self.index % 2
        self.chip = self.index // 2
        self.block = lax.axis_index("blk")
        self.square = self.chips == 4
        self.place = jnp.stack([self.core, self.index, self.chip]).astype(jnp.int32)

    def swap(self, value, bits):
        return lax.ppermute(value, "dp", [(i, i ^ bits) for i in range(self.devices)])

    def split_swap(self, value, even_bits, odd_bits):
        return lax.ppermute(
            value, "dp", [(i, i ^ (odd_bits if i % 2 else even_bits)) for i in range(self.devices)]
        )

    def row_swap(self, value, bits):
        return lax.ppermute(value, "blk", [(i, i ^ bits) for i in range(self.blocks)])

    def row_shift(self, value, distance):
        pairs = [(i, i + distance) for i in range(self.blocks) if 0 <= i + distance < self.blocks]
        return lax.ppermute(value, "blk", pairs)

    def sides(self, value):
        return self.swap(value, 2), self.swap(value, 4)

    def across(self, side, other):
        return self.split_swap(jnp.where(self.core == 0, other, side), 2, 4)

    def total(self, kept, given, order):
        sent = self.swap(given, 1)
        yield
        sent = order(sent)
        cuts = cut_rows(self.place, kept, sent, self.chips)
        order.mark(cuts[0])
        sent = [self.swap(cuts[r], 2 * r) for r in range(1, self.chips)]
        yield
        sent = order(*sent)
        value = order.mark(sum([cuts[0].astype(f32)] + [part.astype(f32) for part in sent]).astype(bf16))
        bits = 1
        while bits < self.blocks:
            sent = self.row_swap(value, bits)
            yield
            sent = order(sent)
            value = order.mark((value.astype(f32) + sent.astype(f32)).astype(bf16))
            bits *= 2
        sent = [self.swap(value, 2 * r) for r in range(1, self.chips)]
        yield
        sent = order(*sent)
        value = order.mark(join_rows(self.place, [value, *sent]))
        sent = self.swap(value, 1)
        yield
        sent = order(sent)
        yield value, sent

    def small_total(self, value, order):
        for swap, count in ((self.swap, self.devices), (self.row_swap, self.blocks)):
            bits = 1
            while bits < count:
                sent = swap(value, bits)
                yield
                sent = order(sent)
                value = order.mark(value + sent)
                bits *= 2
        yield value


def shards(
    block_input,
    out_cotangent,
    row_lengths,
    rope_positions,
    gain_attention,
    gain_feedforward,
    base_attention,
    base_output,
    base_feedforward,
    base_down,
    rank_in_attention,
    rank_out_attention,
    magnitude_attention,
    rank_in_output,
    rank_out_output,
    magnitude_output,
    rank_in_feedforward,
    rank_out_feedforward,
    magnitude_feedforward,
    rank_in_down,
    rank_out_down,
    magnitude_down,
    *,
    devices,
    blocks,
):
    links = Links(devices, blocks)
    order = Order()
    mark = order.mark
    index, core, chip, chips = links.index, links.core, links.chip, links.chips
    place = links.place
    partner = lambda value: links.swap(value, 1)
    rows_in = block_input[0]
    tokens = rows_in.shape[0]
    length = row_lengths[0]
    token_pos = links.block * tokens + jnp.arange(tokens, dtype=jnp.int32)
    fast = links.square and base_attention.shape[2] * devices == KVW and blocks == 4
    heads = jnp.arange(KV_HEADS, dtype=jnp.int32)
    heads = chip ^ heads if fast else heads
    scalars = jnp.stack([links.block.astype(jnp.int32), length])

    def columns_of(value, width):
        return lax.dynamic_slice_in_dim(value, index * width, width, value.ndim - 1)

    attn_cols, out_cols = base_attention.shape[2], base_output.shape[2]
    feed_cols, down_cols = base_feedforward.shape[2], base_down.shape[1]
    chip_cols = 2 * feed_cols
    attn_rank = columns_of(rank_out_attention, attn_cols)
    attn_mag = columns_of(magnitude_attention, attn_cols)
    attn_base = base_attention.transpose(0, 2, 1)
    attn_in_t = rank_in_attention.transpose(0, 2, 1)
    out_in_t = rank_in_output.T
    feed_in_t = rank_in_feedforward.transpose(0, 2, 1)
    down_in_t = rank_in_down.T

    def fold_out():
        return fold(
            order(base_output).transpose(0, 2, 1),
            out_in_t[None],
            columns_of(rank_out_output, out_cols),
            columns_of(magnitude_output, out_cols),
            0,
            False,
            "fold_o",
        )

    def fold_feed():
        return fold(
            order(base_feedforward).transpose(0, 2, 1),
            feed_in_t,
            columns_of(rank_out_feedforward, feed_cols),
            columns_of(magnitude_feedforward, feed_cols),
            0,
            True,
            "fold_feed",
        )

    def folded_down():
        return fold_down(
            order(base_down),
            down_in_t,
            columns_of(rank_out_down, down_cols),
            columns_of(magnitude_down, down_cols),
            chips,
        )

    def norm_in():
        values = order(rows_in).astype(f32)
        return (values * rms_inverse(values) * gain_attention).astype(bf16)

    frequency = rope_base ** (-(jnp.arange(HEAD // 2, dtype=f32) * 2.0) / HEAD)
    angles = rope_positions[0].astype(f32)[:, None] * frequency[None, :]
    cos_half, sin_half = jnp.cos(angles), jnp.sin(angles)
    cosine = jnp.concatenate([cos_half, cos_half], axis=-1)
    sine = jnp.concatenate([-sin_half, sin_half], axis=-1)
    tables = (cosine, sine)

    wheres = [jnp.stack([core, chip ^ r, chip, chip ^ 1, chip ^ 2]).astype(jnp.int32) for r in range(KV_HEADS)]

    settle = order.pin

    def project(where, first, second, roped, name, before=()):
        first, second = order(first, second)
        weights, out, token = head_step(where, first, second, normed, tables, roped, before, name)
        mark(token)
        return weights, out

    def send_kv(kv_blocks):
        kv_blocks.append(links.row_shift(kv_blocks[-1], 1))

    kv_fold = mark(
        fold(attn_base, attn_in_t, attn_rank[GROUP:], attn_mag[GROUP:], 1, True, "fold_kv", first=GROUP)
    )
    down_cut = lambda r: lax.dynamic_index_in_dim(down_fold, chip ^ r, 0, keepdims=False)
    spread = lambda value: lax.all_gather(value, "dp", axis=0)
    grad_out = jnp.where((token_pos < length)[:, None], out_cotangent[0], jnp.zeros((), bf16))
    grad_own = grad_out[None]
    chip_in_t = lax.dynamic_slice_in_dim(down_in_t, chip * chip_cols, chip_cols, 1)
    halves_in_t = jnp.stack(
        [lax.dynamic_slice_in_dim(chip_in_t, at * feed_cols, feed_cols, 1) for at in (core, 1 - core)]
    )
    feed_mag = lax.dynamic_slice_in_dim(magnitude_feedforward, chip * chip_cols, chip_cols, 1)
    if fast:
        kv_side, kv_other = links.sides(kv_fold)
        kv_partner = partner(kv_fold)
        q_fold = mark(fold(order(attn_base), attn_in_t, attn_rank[:GROUP], attn_mag[:GROUP], 0, False, "fold_q"))
        q_weights = spread(q_fold)
        kv_side, kv_other, kv_partner = settle(kv_side, kv_other, kv_partner)
        kv_across = links.across(kv_side, kv_other)
        kv_side_p, kv_other_p = partner(kv_side), partner(kv_other)
        o_fold = mark(fold_out())
        o_weights = spread(after(o_fold, q_fold))
        normed = mark(norm_in())
        kv_made = [
            project(wheres[0], kv_fold, kv_partner, 1, "head_kv"),
            project(wheres[1], kv_side, kv_side_p, 1, "head_kv"),
            project(wheres[2], kv_other, kv_other_p, 1, "head_kv"),
        ]
        kv_across = settle(kv_across)
        kv_across_p = partner(kv_across)
        kv_made.append(project(wheres[3], kv_across, kv_across_p, 1, "head_kv", [out for _, out in kv_made]))
        kv_own = kv_made[-1][1]
        kv_blocks = [kv_own]
        send_kv(kv_blocks)
        grad_own, halves_in_t, feed_mag = settle(grad_own, halves_in_t, feed_mag)
        feed_own = mark(fold_feed())
        kv_blocks[1] = settle(kv_blocks[1])
        send_kv(kv_blocks)
        down_fold, down_proj = folded_down()
        mark(down_proj)
        down_0, down_c1, down_c2, down_c3 = settle(*[down_cut(r) for r in range(4)])
        grad_all = lax.all_gather(
            order(grad_out), "dp", axis=0, axis_index_groups=[[2 * c + k for c in range(chips)] for k in range(2)]
        )
        kv_blocks[2] = settle(kv_blocks[2])
        send_kv(kv_blocks)
        queries = mark(query_project(order(normed), tables, q_weights))
        kv_blocks[3] = settle(kv_blocks[3])
        down_1, down_2, down_3 = links.swap(down_c1, 2), links.swap(down_c2, 4), links.swap(down_c3, 6)
        mixed, lse = attend(scalars, order(queries), kv_blocks)
        mark(lse)
        feed_partner = partner(order(feed_own))

        def feed_late():
            near = settle(down_1, down_2, down_3)
            pieces = []
            for piece in (down_0, *near):
                pieces += [piece, partner(piece)]
            return settle(*pieces)

    else:
        q_fold = fold(attn_base, attn_in_t, attn_rank[:GROUP], attn_mag[:GROUP], 0, False, "fold_q")
        q_weights, o_weights, normed = spread(q_fold), spread(fold_out()), norm_in()
        down_fold, down_proj = folded_down()
        feed_own = fold_feed()
        feed_partner = partner(feed_own)
        whole = lax.all_gather(kv_fold, "dp", axis=1, tiled=True).reshape(2, KV_HEADS, 2, HEAD // 2, WIDE)
        kv_made = []
        for j in range(KV_HEADS):
            before = [out for _, out in kv_made] if j == KV_HEADS - 1 else ()
            where = jnp.array([0, j, 0, 1, 2], jnp.int32)
            kv_made.append(project(where, whole[:, j, 0], whole[:, j, 1], 1, "head_kv", before))
        kv_own = kv_made[-1][1]
        kv_blocks = [kv_own]
        for _ in range(1, blocks):
            send_kv(kv_blocks)
        queries = query_project(normed, tables, q_weights)
        grad_all = lax.all_gather(
            grad_out, "dp", axis=0, axis_index_groups=[[2 * c + k for c in range(chips)] for k in range(2)]
        )
        mixed, lse = attend(scalars, queries, kv_blocks)
        down_pieces = []
        for r in range(chips):
            piece = links.swap(down_cut(r), 2 * r) if r else down_cut(r)
            down_pieces += [piece, partner(piece)]
    residual, normed_feed = output_project(order(mixed), o_weights, rows_in, gain_feedforward)
    mark(normed_feed)

    forward = lambda normed_group: settle(*feed_forward(order(normed_group), feed_own, feed_partner, tokens))
    aux = []

    def backward(members, kept):
        grads = grad_own if members == (None,) else grad_all
        kept = list(order(*kept)) if isinstance(kept, (tuple, list)) else [order(kept)]
        made = feed_back(place, grads, members, kept, feed_own, feed_partner, down_pieces, tokens)
        mark(made[0])
        count = len(members)
        return made[:count], made[count : 2 * count], made[2 * count :]

    mag_sums = []

    def adapters(members, normed_group, made, before):
        hidden, grad_gate, grad_up, ext, mags, down_aux = made[2]
        parts = feed_adapter(
            place, order(normed_group), grad_own if members == (None,) else grad_all, members, hidden, grad_gate,
            grad_up, ext, feed_in_t.reshape(2 * RANK, D), halves_in_t, before,
        )
        mark(parts[0])
        aux.append(down_aux)
        mag_sums.append(mags)
        return tuple(parts)

    if fast:
        side, other = links.sides(normed_feed)
        down_pieces = feed_late()
        own_made = backward((None,), normed_feed)
        side, other = settle(side, other)
        crossed = links.across(side, other)
        near = settle(jnp.concatenate([side, other]))
        near_kept = forward(near)
        sums = adapters((None,), normed_feed, own_made, None)
        crossed = settle(crossed)
        far_made = backward((3,), crossed)
        from_far = links.split_swap(far_made[0][0], 2, 4)
        first_made = backward(("first",), near_kept)
        early_first = links.split_swap(first_made[0][0], 2, 4)
        last_made = backward(("last",), near_kept)
        from_far = settle(from_far)
        late_share = settle((last_made[0][0].astype(f32) + from_far.astype(f32)).astype(bf16))
        early_second = links.split_swap(late_share, 4, 2)
        down_mag_steps = links.small_total(sum(made[2][4][4:5] for made in (own_made, first_made, last_made, far_made)), order)
        next(down_mag_steps)
        sums = adapters(("first",), near, first_made, sums)
        next(down_mag_steps)
        sums = adapters(("last",), near, last_made, sums)
        early_first = settle(early_first)
        reduced = (own_made[0][0], early_first, early_second)
        shares_out = [own_made[1][0], first_made[1][0], last_made[1][0], far_made[1][0]]
    else:
        sums, shares_grad, shares_out = None, [], []
        for r in range(chips):
            normed_group = links.swap(normed_feed, 2 * r) if r else normed_feed
            made = backward((r,), normed_group)
            sums = adapters((r,), normed_group, made, sums)
            shares_grad.append(made[0][0])
            shares_out.append(made[1][0])
        rest = sum(links.swap(shares_grad[r], 2 * r).astype(f32) for r in range(1, chips)).astype(bf16)
        reduced = (shares_grad[0], rest, jnp.zeros(rest.shape, bf16))
        down_mag_steps = links.small_total(sum(mags[4:5] for mags in mag_sums), order)
        next(down_mag_steps)
    reduced = settle(*reduced)
    grad_residual, grad_ordered, out_mag_raw, out_ext, grad_mixed, delta = residual_back(
        reduced, residual, gain_feedforward, grad_out, rows_in, mixed, o_weights
    )
    mark(delta)
    next(down_mag_steps)
    def pack_early(down_mag_total):
        feed_mags = jnp.stack(
            [lax.dynamic_slice_in_dim(feed_mag, at * feed_cols, feed_cols, 1) for at in (core, 1 - core)]
        )
        if fast:
            *early, down_grad_mag = feed_pack(
                place, feed_own, feed_partner, down_fold, *order(feed_products, mag_raw), feed_mags, feed_in, down_in,
                down_products, down_mag_total, magnitude_down[None], aux[0], down_proj, rank_out_down,
                share=1.0 / blocks,
            )
            return down_grad_mag, early
        finished = [
            finish_columns(weights, feed_products[half], mag_raw[half:4:2, :feed_cols], feed_mags[half])
            for half, weights in enumerate((feed_own, feed_partner))
        ]
        grad_mag, grad_out_part, grad_in_part = zip(*finished)
        columns = [
            jnp.concatenate([part.astype(bf16) for part in parts])
            for parts in zip(grad_out_part, down_in, grad_mag)
        ]
        columns = jnp.where(core == 0, jnp.concatenate(columns, axis=1), jnp.concatenate(columns[::-1], axis=1))
        full = lax.dynamic_update_slice(jnp.zeros((64, 3 * D), bf16), columns, (0, chip * chip_cols))
        down_aux = aux[0]
        down_inverse = (down_aux[RANK].astype(f32) + down_aux[RANK + 1].astype(f32))[None]
        down_grad_mag = down_mag_total / magnitude_down[None]
        down_out = factor * down_products * (magnitude_down[None] * down_inverse)
        own_turn = columns_of(-down_grad_mag * down_inverse, down_cols) * (factor / blocks)
        down_out = lax.dynamic_update_slice(
            down_out, columns_of(down_out, down_cols) + down_proj * own_turn, (0, index * down_cols)
        )
        own_wide = (columns_of(rank_out_down.astype(f32), down_cols) * own_turn).astype(bf16)
        down_norm_in = lax.dot_general(
            own_wide, down_fold[:, :chip_cols], (((1,), (2,)), ((), ())), preferred_element_type=f32
        ).reshape(RANK, FF)
        down_full = (full[2 * RANK : 3 * RANK, :FF].astype(f32) + down_norm_in).astype(bf16)
        full = lax.dynamic_update_slice(full, down_full, (2 * RANK, 0))
        top = jnp.concatenate([(feed_in + sum(grad_in_part)).astype(bf16), down_out.astype(bf16)])
        whole = jnp.concatenate(
            [jnp.pad(top, ((0, 16), (0, 0)))] + [full[:, i * D : (i + 1) * D] for i in range(3)]
        )
        left, right = whole[:, : D // 2], whole[:, D // 2 :]
        return down_grad_mag, (jnp.where(core == 0, left, right), jnp.where(core == 0, right, left))

    grad_queries, grad_kvs = None, []

    def keys_back(distance):
        grad_queries_next, grad_kv = attend_back(
            scalars, order(queries), grad_mixed, lse, delta, kv_blocks[distance], grad_queries, distance
        )
        mark(grad_kv)
        return grad_queries_next, grad_kv

    def pass_down(passed, grad_kv):
        passed = order(passed)
        passed = settle((passed.astype(f32) + grad_kv.astype(f32)).astype(bf16))
        return links.row_shift(passed, -1)

    grad_queries, grad_kv = keys_back(blocks - 1)
    passed = links.row_shift(grad_kv, -1)
    if fast:
        sums = adapters((3,), crossed, far_made, sums)
    feed_in, feed_products, down_in, down_products = sums
    mag_raw = sum(mag_sums)
    next(down_mag_steps)
    held = None
    for distance in reversed(range(1, blocks - 1)):
        grad_queries, grad_kv = keys_back(distance)
        if held is not None:
            passed = pass_down(passed, held)
        held = grad_kv
    if fast:
        out_far = links.split_swap(order(shares_out[3]), 2, 4)
        out_first = links.split_swap(order(shares_out[1]), 2, 4)
    next(down_mag_steps)
    grad_queries, grad_kv = keys_back(0)
    for down_mag_total in down_mag_steps:
        pass
    down_grad_mag, early = pack_early(down_mag_total)
    mark(down_grad_mag)
    early_steps = links.total(*early, order)
    next(early_steps)
    passed = pass_down(passed, held)
    out_grad_mag, out_out, out_in = output_adapter(
        order(grad_ordered), out_mag_raw, magnitude_output, o_weights, mixed, out_ext, out_in_t
    )
    mark(out_in)
    if fast:
        next(early_steps)
        out_far, out_first = settle(out_far, out_first)
        out_late = settle((shares_out[2].astype(f32) + out_far.astype(f32)).astype(bf16))
        out_second = links.split_swap(out_late, 4, 2)
        out_parts = [shares_out[0], out_first, out_second]
    else:
        out_parts = [shares_out[0]] + [links.swap(shares_out[r], 2 * r) for r in range(1, chips)]
    q_acc, q_in, q_out, q_grad_mag = query_back(
        order(grad_queries), queries, q_weights, cosine, sine, normed, attn_in_t[0], magnitude_attention[:GROUP]
    )
    mark(q_in)
    if fast:
        next(early_steps)
    passed = settle(passed)
    input_grad, *late = key_back(
        heads, passed, grad_kv, kv_own, [weights for weights, _ in kv_made], cosine, sine, normed, rows_in,
        gain_attention, grad_residual, q_acc, attn_in_t[1:].reshape(2 * RANK, D), magnitude_attention[GROUP:],
        place, q_in, q_out, q_grad_mag, out_in, out_out, out_grad_mag,
    )
    mark(late[0])
    late_steps = links.total(*late, order)
    next(late_steps)
    out_parts = settle(*out_parts)
    late = early = None
    next(late_steps)
    block_out = settle((residual + sum(part.astype(f32) for part in out_parts)).astype(bf16))[None]
    while early is None:
        early = next(early_steps)
        if late is None:
            late = next(late_steps)
    early_shapes = ((2, RANK, D), (2, RANK, FF), (2, FF), (RANK, FF), (RANK, D))
    feed_in, feed_out, feed_mag, down_in, down_out = unpack(
        unpack_early_kernel, place, order(*early), early_shapes, "unpack_early"
    )
    mark(feed_mag)
    while late is None:
        late = next(late_steps)
    late_shapes = ((3, RANK, D), (GROUP + 2, RANK, KVW), (GROUP + 2, KVW), (RANK, D), (GROUP, RANK, KVW), (GROUP, KVW))
    attn_in, attn_out, attn_mag, out_in, out_out, out_mag = unpack(
        unpack_late_kernel, place, order(*late), late_shapes, "unpack_late"
    )
    return (
        block_out,
        input_grad[None],
        attn_in.transpose(0, 2, 1),
        attn_out,
        attn_mag,
        out_in.T,
        out_out,
        out_mag,
        feed_in.transpose(0, 2, 1),
        feed_out,
        feed_mag,
        down_in.T,
        down_out,
        down_grad_mag[0],
    )


def solution(mesh):
    split_tokens = P("dp", "blk", None)
    placed = (
        split_tokens,
        split_tokens,
        P("dp"),
        P("dp", "blk"),
        P(),
        P(),
        P(None, None, "dp"),
        P(None, None, "dp"),
        P(None, None, "dp"),
        P(None, "dp"),
    ) + (P(),) * 12
    return jax.shard_map(
        functools.partial(shards, devices=mesh.shape["dp"], blocks=mesh.shape["blk"]),
        mesh=mesh,
        in_specs=placed,
        out_specs=(split_tokens, split_tokens) + (P(),) * 12,
        check_vma=False,
    )
```

```python
import functools

import jax
import jax.numpy as jnp
from jax import lax
from jax.experimental import pallas as pl
from jax.experimental.pallas import tpu as pltpu
from jax.sharding import PartitionSpec as P

D = 2048
KV_HEADS = 4
HEAD = 128
FF = 5632
RANK = 16
GROUP = 4
KVW = 512

EXT = 128
WIDE = D + EXT
SLOTS = 3
INV_AT = 48
PROJ_AT = 64
AUX = 32

factor = 32.0 / RANK
rms_eps = 1e-05
rope_base = 10000.0
masked_score = -1e30
log2_e = 1.4426950408889634
score_scale = HEAD ** (-0.5)
f32 = jnp.float32
bf16 = jnp.bfloat16


def dot_nt(left, right):
    return lax.dot_general(left, right, (((1,), (1,)), ((), ())), preferred_element_type=f32)


def dot_nn(left, right):
    return lax.dot_general(left, right, (((1,), (0,)), ((), ())), preferred_element_type=f32)


def dot_tn(left, right):
    return lax.dot_general(left, right, (((0,), (0,)), ((), ())), preferred_element_type=f32)


def limits(mebibytes):
    return pltpu.CompilerParams(vmem_limit_bytes=mebibytes << 20)


def kernel_call(*args, in_specs=None, **options):
    if in_specs is not None:
        options["in_specs"] = in_specs
    call = pl.pallas_call(
        *args, cost_estimate=pl.CostEstimate(flops=0, transcendentals=0, bytes_accessed=0), **options
    )
    if in_specs is None:
        return call
    keep = lambda value, spec: pltpu.with_memory_space_constraint(value, pltpu.HBM) if spec is anywhere else value
    return lambda *operands: call(*[keep(value, spec) for value, spec in zip(operands, in_specs)])


anywhere = pl.BlockSpec(memory_space=pltpu.HBM)
in_vmem = pl.BlockSpec(memory_space=pltpu.VMEM)
in_smem = pl.BlockSpec(memory_space=pltpu.SMEM)


def shape_of(shape, dtype=f32):
    return jax.ShapeDtypeStruct(shape, dtype)


def split_low(value):
    high = value.astype(bf16)
    return high, (value - high.astype(f32)).astype(bf16)


def iota(shape, dim):
    return lax.broadcasted_iota(jnp.int32, shape, dim)


def lanes_at(start):
    return pl.ds(pl.multiple_of(start, HEAD), HEAD)


def fold_kernel(weight_ref, rank_in_ref, rank_out_ref, mag_ref, out_ref, column_ref, *, first_slot, moving):
    slot = first_slot + (pl.program_id(0) if moving else 0)
    rows = weight_ref.shape[1]

    def placed_at(start):
        spot = iota((RANK, EXT), 1) == iota((RANK, EXT), 0) + start
        return jnp.where(spot, 1.0, 0.0).astype(bf16)

    @pl.when(pl.program_id(1) == 0)
    def _():
        column_ref[0] = dot_tn(rank_out_ref[0], placed_at(0))
        column_ref[1] = dot_tn(rank_out_ref[0], placed_at(RANK * slot))
        mags = jnp.broadcast_to(mag_ref[0], (8, mag_ref.shape[2]))
        one = jnp.where(iota((8, EXT), 0) == 0, 1.0, 0.0)
        column_ref[2] = lax.dot_general(
            mags, one, (((0,), (0,)), ((), ())), precision=lax.Precision.HIGHEST, preferred_element_type=f32
        )

    own = pl.ds(pl.multiple_of(pl.program_id(1) * rows, 16), rows)
    doubled = (factor * column_ref[0, own, :RANK]).astype(bf16)
    merged = weight_ref[0].astype(f32) + dot_nn(doubled, rank_in_ref[0])
    inverse = 1.0 / jnp.sqrt(jnp.sum(merged * merged, axis=1, keepdims=True))
    scale = column_ref[2, own, :1] * inverse
    folded = (merged * scale).astype(bf16)
    out_ref[0, :, :D] = folded
    ext = column_ref[1, own, :] * (factor * scale)
    for index, part in enumerate(split_low(dot_nt(folded, rank_in_ref[0]))):
        ext = ext + dot_nn(part, placed_at(PROJ_AT + RANK * index))
    lane = iota(ext.shape, 1)
    for index, part in enumerate(split_low(inverse)):
        ext = ext + jnp.where(lane == INV_AT + index, part.astype(f32), 0.0)
    out_ref[0, :, D:] = ext.astype(bf16)


def fold(weights, rank_in_t, rank_out, magnitude, rank_first, moving, name, first=0):
    members, columns = magnitude.shape
    pieces = 4 if columns % 64 == 0 and columns > 256 else 1
    rows = columns // pieces
    rank_block = (lambda b, c: (b + rank_first, 0, 0)) if moving else (lambda b, c: (rank_first, 0, 0))
    return kernel_call(
        functools.partial(fold_kernel, first_slot=rank_first, moving=moving),
        out_shape=shape_of((members, columns, WIDE), bf16),
        grid=(members, pieces),
        in_specs=[
            pl.BlockSpec((1, rows, D), lambda b, c: (b + first, c, 0)),
            pl.BlockSpec((1, RANK, D), rank_block),
            pl.BlockSpec((1, RANK, columns), lambda b, c: (b, 0, 0)),
            pl.BlockSpec((1, 1, columns), lambda b, c: (b, 0, 0)),
        ],
        out_specs=pl.BlockSpec((1, rows, WIDE), lambda b, c: (b, c, 0)),
        scratch_shapes=[pltpu.VMEM((3, columns, EXT), f32)],
        compiler_params=limits(32),
        name=name,
    )(weights, rank_in_t, rank_out, magnitude[:, None, :])


def fold_down_kernel(weight_ref, rank_in_ref, rank_out_ref, mag_ref, out_ref, proj_ref, merged_ref, *, chips):
    rows = weight_ref.shape[0] // chips
    total = 0.0
    doubled = (factor * rank_out_ref[...].astype(f32)).astype(bf16)
    for part in range(chips):
        span = slice(part * rows, (part + 1) * rows)
        merged = weight_ref[span, :].astype(f32) + dot_tn(rank_in_ref[:, span], doubled)
        merged_ref[span, :] = merged
        total = total + jnp.sum(merged * merged, axis=0, keepdims=True)
    inverse = 1.0 / jnp.sqrt(total)
    scale = mag_ref[...] * inverse
    high, low = split_low(inverse)
    row = iota((AUX - RANK, scale.shape[1]), 0)
    tail = jnp.where(row == 0, high.astype(f32), jnp.where(row == 1, low.astype(f32), 0.0))
    aux = jnp.concatenate([doubled.astype(f32) * scale, tail], axis=0).astype(bf16)
    proj = 0.0
    for part in range(chips):
        span = slice(part * rows, (part + 1) * rows)
        folded = (merged_ref[span, :] * scale).astype(bf16)
        out_ref[part, :rows, :] = folded
        out_ref[part, rows:, :] = aux
        proj = proj + dot_nn(rank_in_ref[:, span], folded)
    proj_ref[...] = proj


def fold_down(weights, rank_in_t, rank_out, magnitude, chips):
    inputs, columns = weights.shape
    return kernel_call(
        functools.partial(fold_down_kernel, chips=chips),
        out_shape=(shape_of((chips, inputs // chips + AUX, columns), bf16), shape_of((RANK, columns))),
        scratch_shapes=[pltpu.VMEM((inputs, columns), f32)],
        compiler_params=limits(32),
        name="fold_down",
    )(weights, rank_in_t, rank_out, magnitude[None])


def head_kernel(scalar_ref, first_ref, second_ref, input_ref, cos_ref, sin_ref, *refs, roped):
    before_refs, (weight_ref, out_ref, token_ref) = refs[:-3], refs[-3:]
    members, half = first_ref.shape[0], first_ref.shape[1]
    for member in range(members):
        for order, ref in ((scalar_ref[0], first_ref), (1 - scalar_ref[0], second_ref)):
            weight_ref[pl.ds(pl.multiple_of((2 * member + order) * half, half), half), :] = ref[member]
    wide = members * HEAD
    for index, ref in enumerate(before_refs):
        out_ref[:, pl.ds(pl.multiple_of(scalar_ref[2 + index] * wide, wide), wide)] = ref[...]
    raw = dot_nt(input_ref[...], weight_ref[:, :D])
    for member in range(members):
        part = raw[:, member * HEAD : (member + 1) * HEAD]
        if member < roped:
            part = part * cos_ref[...] + pltpu.roll(part, HEAD // 2, 1) * sin_ref[...]
        start = (scalar_ref[1] * wide if before_refs else 0) + member * HEAD
        out_ref[:, lanes_at(start)] = part.astype(bf16)
    token_ref[...] = jnp.zeros(token_ref.shape, f32)


def head_step(scalars, first, second, inputs, tables, roped, before, name):
    members, half, _ = first.shape
    tokens = inputs.shape[0]
    wide = members * HEAD
    return kernel_call(
        functools.partial(head_kernel, roped=roped),
        out_shape=(
            shape_of((wide, WIDE), bf16),
            shape_of((tokens, (1 + len(before)) * wide), bf16),
            shape_of((8, HEAD)),
        ),
        in_specs=[in_smem] + [in_vmem] * (5 + len(before)),
        out_specs=(in_vmem,) * 3,
        compiler_params=limits(24),
        name=name,
    )(scalars, first, second, inputs, *tables, *before)


def head_copies(weight_ref, head, out_ref, semaphores, first=0):
    devices, members, part = weight_ref.shape[:3]
    parts = devices // KV_HEADS
    copies = []
    for at in range(parts):
        for member in range(members):
            copies.append(
                pltpu.make_async_copy(
                    weight_ref.at[parts * head + at, member],
                    out_ref.at[pl.ds((parts * member + at) * part, part), :],
                    semaphores.at[first + len(copies)],
                )
            )
    return copies


def head_scratch(weights):
    each = weights.shape[0] // KV_HEADS * weights.shape[1]
    return [
        pltpu.VMEM((KV_HEADS, weights.shape[1] * HEAD, WIDE), bf16),
        pltpu.SemaphoreType.DMA((KV_HEADS * each,)),
    ]


def all_head_copies(weight_ref, out_ref, semaphores):
    each = weight_ref.shape[0] // KV_HEADS * weight_ref.shape[1]
    return [head_copies(weight_ref, head, out_ref.at[head], semaphores, head * each) for head in range(KV_HEADS)]


def next_head(copies, head):
    if head == 0:
        for copy in copies[0] + copies[1]:
            copy.start()
    elif head + 1 < len(copies):
        for copy in copies[head + 1]:
            copy.start()
    for copy in copies[head]:
        copy.wait()


def query_kernel(input_ref, cos_ref, sin_ref, weight_hbm, out_ref, weight_ref, semaphores):
    copies = all_head_copies(weight_hbm, weight_ref, semaphores)
    for head in range(KV_HEADS):
        next_head(copies, head)
        raw = dot_nt(input_ref[...], weight_ref[head, :, :D])
        for group in range(GROUP):
            part = raw[:, group * HEAD : (group + 1) * HEAD]
            part = part * cos_ref[...] + pltpu.roll(part, HEAD // 2, 1) * sin_ref[...]
            start = (head * GROUP + group) * HEAD
            out_ref[:, start : start + HEAD] = part.astype(bf16)


def query_project(inputs, tables, weights):
    return kernel_call(
        query_kernel,
        out_shape=shape_of((inputs.shape[0], D), bf16),
        in_specs=[in_vmem] * 3 + [anywhere],
        out_specs=in_vmem,
        scratch_shapes=head_scratch(weights),
        compiler_params=limits(24),
        name="query_project",
    )(inputs, *tables, weights)


def masked_scores(keys, queries, key_first, length, causal):
    tokens, lanes = keys.shape[0], queries.shape[0]
    scores = dot_nt(keys, queries)
    key_pos = key_first + iota((tokens, 1), 0)
    scores = scores + jnp.where(key_pos < length, 0.0, masked_score)
    if causal:
        allowed = iota((tokens, lanes), 0) <= (iota((tokens, lanes), 1) & (tokens - 1))
        scores = jnp.where(allowed, scores, masked_score)
    return scores


def attend_kernel(scalar_ref, query_ref, *refs, steps):
    kv_refs = refs[:steps]
    mixed_ref, lse_ref, stacked_ref, max_ref, sum_ref, accum_ref = refs[steps:]
    head = pl.program_id(0)
    tokens = query_ref.shape[0]
    block_index, length = scalar_ref[0], scalar_ref[1]
    scale = score_scale * log2_e
    for group in range(GROUP):
        stacked_ref[group * tokens : (group + 1) * tokens, :] = query_ref[:, group * HEAD : (group + 1) * HEAD]

    for distance in range(steps):

        def step(distance=distance):
            keys = kv_refs[distance][:, :HEAD]
            values = kv_refs[distance][:, HEAD:]
            key_first = (block_index - distance) * tokens
            scores = masked_scores(keys, stacked_ref[...], key_first, length, distance == 0)
            block_max = jnp.max(scores, axis=0, keepdims=True)
            new_max = block_max if distance == 0 else jnp.maximum(max_ref[...], block_max)
            terms = jnp.exp2((scores - new_max) * scale)
            added = jnp.sum(terms, axis=0, keepdims=True)
            product = dot_tn(values, terms.astype(bf16))
            if distance == 0:
                sum_ref[...] = added
                accum_ref[...] = product
            else:
                fade = jnp.exp2((max_ref[...] - new_max) * scale)
                sum_ref[...] = sum_ref[...] * fade + added
                accum_ref[...] = accum_ref[...] * fade + product
            max_ref[...] = new_max

        if distance == 0:
            step()
        else:
            pl.when(block_index >= distance)(step)
    mixed = accum_ref[...] / sum_ref[...]
    for group in range(GROUP):
        part = mixed[:, group * tokens : (group + 1) * tokens]
        mixed_ref[:, lanes_at(group * KVW + head * HEAD)] = part.T.astype(bf16)
    lse_ref[0] = max_ref[...] * scale + jnp.log(sum_ref[...]) * log2_e


def attend(scalars, queries, kv_blocks):
    tokens = queries.shape[0]
    steps = len(kv_blocks)
    lanes = GROUP * tokens
    return kernel_call(
        functools.partial(attend_kernel, steps=steps),
        out_shape=(shape_of((tokens, D), bf16), shape_of((KV_HEADS, 1, lanes))),
        grid_spec=pltpu.PrefetchScalarGridSpec(
            num_scalar_prefetch=1,
            grid=(KV_HEADS,),
            in_specs=[pl.BlockSpec((tokens, GROUP * HEAD), lambda j, s: (0, j))]
            + [pl.BlockSpec((tokens, 2 * HEAD), lambda j, s: (0, j))] * steps,
            out_specs=(
                pl.BlockSpec((tokens, D), lambda j, s: (0, 0)),
                pl.BlockSpec((1, 1, lanes), lambda j, s: (j, 0, 0)),
            ),
            scratch_shapes=[
                pltpu.VMEM((lanes, HEAD), bf16),
                pltpu.VMEM((1, lanes), f32),
                pltpu.VMEM((1, lanes), f32),
                pltpu.VMEM((HEAD, lanes), f32),
            ],
        ),
        compiler_params=limits(40),
        name="attend",
    )(scalars, queries, *kv_blocks)


def attend_back_kernel(scalar_ref, query_ref, grad_ref, lse_ref, delta_ref, kv_ref, *refs, distance, chained):
    if chained:
        before_ref, grad_query_ref, grad_kv_ref, stacked_ref, stacked_grad_ref = refs
    else:
        grad_query_ref, grad_kv_ref, stacked_ref, stacked_grad_ref = refs
    head = pl.program_id(0)
    tokens = query_ref.shape[0]
    block_index, length = scalar_ref[0], scalar_ref[1]
    active = (block_index >= distance) & (block_index * tokens < length)

    @pl.when(active)
    def _():
        for group in range(GROUP):
            rows = slice(group * tokens, (group + 1) * tokens)
            stacked_ref[rows, :] = query_ref[:, group * HEAD : (group + 1) * HEAD]
            stacked_grad_ref[rows, :] = grad_ref[:, lanes_at(group * KVW + head * HEAD)]
        keys = kv_ref[:, :HEAD]
        values = kv_ref[:, HEAD:]
        key_first = (block_index - distance) * tokens
        scores = masked_scores(keys, stacked_ref[...], key_first, length, distance == 0)
        probs = jnp.exp2(scores * (score_scale * log2_e) - lse_ref[0])
        grad_probs = dot_nt(values, stacked_grad_ref[...])
        grad_scores = (probs * (grad_probs - delta_ref[0])).astype(bf16)
        grad_values = dot_nn(probs.astype(bf16), stacked_grad_ref[...])
        grad_keys = dot_nn(grad_scores, stacked_ref[...]) * score_scale
        grad_queries = dot_tn(grad_scores, keys) * score_scale
        for group in range(GROUP):
            lanes = slice(group * HEAD, (group + 1) * HEAD)
            part = grad_queries[group * tokens : (group + 1) * tokens, :]
            if chained:
                part = part + before_ref[:, lanes]
            grad_query_ref[:, lanes] = part
        grad_kv_ref[:, :HEAD] = grad_keys.astype(grad_kv_ref.dtype)
        grad_kv_ref[:, HEAD:] = grad_values.astype(grad_kv_ref.dtype)

    @pl.when(jnp.logical_not(active))
    def _():
        grad_query_ref[...] = before_ref[...] if chained else jnp.zeros(grad_query_ref.shape, f32)
        grad_kv_ref[...] = jnp.zeros(grad_kv_ref.shape, grad_kv_ref.dtype)


def attend_back(scalars, queries, grad_mixed, lse, delta, kv_block, before, distance):
    tokens = queries.shape[0]
    lanes = GROUP * tokens
    row = pl.BlockSpec((1, 1, lanes), lambda j, s: (j, 0, 0))
    per_query = pl.BlockSpec((tokens, GROUP * HEAD), lambda j, s: (0, j))
    per_key = pl.BlockSpec((tokens, 2 * HEAD), lambda j, s: (0, j))
    chained = before is not None
    operands = [scalars, queries, grad_mixed, lse, delta, kv_block]
    specs = [per_query, pl.BlockSpec((tokens, D), lambda j, s: (0, 0)), row, row, per_key]
    if chained:
        operands += [before]
        specs += [per_query]
    return kernel_call(
        functools.partial(attend_back_kernel, distance=distance, chained=chained),
        out_shape=(shape_of((tokens, D)), shape_of((tokens, 2 * KVW), f32 if distance == 0 else bf16)),
        grid_spec=pltpu.PrefetchScalarGridSpec(
            num_scalar_prefetch=1,
            grid=(KV_HEADS,),
            in_specs=specs,
            out_specs=(per_query, per_key),
            scratch_shapes=[pltpu.VMEM((lanes, HEAD), bf16), pltpu.VMEM((lanes, HEAD), bf16)],
        ),
        input_output_aliases={6: 0} if chained else {},
        compiler_params=limits(40),
        name=f"attend_back_{distance}",
    )(*operands)


def rms_inverse(values):
    return lax.rsqrt(jnp.mean(values * values, axis=-1, keepdims=True) + rms_eps)


def rms_back(values, inverse, gain, grad):
    scaled = grad * gain
    return inverse * (scaled - values * (inverse * inverse * jnp.mean(scaled * values, axis=-1, keepdims=True)))


def output_kernel(mixed_ref, input_ref, gain_ref, weight_hbm, residual_ref, normed_ref, weight_ref, semaphores):
    copies = all_head_copies(weight_hbm, weight_ref, semaphores)
    for head in range(KV_HEADS):
        next_head(copies, head)
        value = dot_nt(mixed_ref[...], weight_ref[head, :, :D])
        for group in range(GROUP):
            start = group * KVW + head * HEAD
            lanes = slice(start, start + HEAD)
            residual_ref[:, lanes] = input_ref[:, lanes].astype(f32) + value[:, group * HEAD : (group + 1) * HEAD]
    values = residual_ref[...]
    normed_ref[...] = (values * rms_inverse(values) * gain_ref[...]).astype(bf16)


def output_project(mixed, weights, inputs, gain):
    tokens = mixed.shape[0]
    return kernel_call(
        output_kernel,
        out_shape=(shape_of((tokens, D)), shape_of((tokens, D), bf16)),
        in_specs=[in_vmem] * 3 + [anywhere],
        out_specs=(in_vmem,) * 2,
        scratch_shapes=head_scratch(weights),
        compiler_params=limits(28),
        name="output_project",
    )(mixed, inputs, gain[None], weights)


class Copies:
    def __init__(self, semaphores):
        self.semaphores = semaphores
        self.made = []

    def __call__(self, source, target):
        copy = pltpu.make_async_copy(source, target, self.semaphores.at[len(self.made)])
        self.made.append(copy)
        return copy

    def started(self, source, target):
        copy = self(source, target)
        copy.start()
        return copy


def feed_forward_kernel(normed_ref, own_ref, partner_ref, gate_hbm, up_hbm, weight_ref, value_ref, semaphores, *, block):
    copies = Copies(semaphores)
    pairs = [(half, member) for half in range(2) for member in range(2)]
    fetches = [
        copies((own_ref, partner_ref)[half].at[member], weight_ref.at[2 * half + member]) for half, member in pairs
    ]
    fetches[0].start()
    fetches[1].start()
    stores = []
    for half, member in pairs:
        at = 2 * half + member
        fetches[at].wait()
        if at + 2 < 4:
            fetches[at + 2].start()
        for start in range(0, normed_ref.shape[0], block):
            rows = slice(start, start + block)
            value_ref[at, rows, :] = dot_nt(normed_ref[rows, :], weight_ref[at, :, :D])
        stores.append(copies.started(value_ref.at[at], (gate_hbm, up_hbm)[member].at[half]))
    for store in stores:
        store.wait()


def feed_forward(normed, own, partner, block):
    tokens = normed.shape[0]
    columns = own.shape[1]
    return kernel_call(
        functools.partial(feed_forward_kernel, block=block),
        out_shape=(shape_of((2, tokens, columns)), shape_of((2, tokens, columns))),
        in_specs=[in_vmem, anywhere, anywhere],
        out_specs=(anywhere,) * 2,
        scratch_shapes=[
            pltpu.VMEM((4, columns, WIDE), bf16),
            pltpu.VMEM((4, tokens, columns), f32),
            pltpu.SemaphoreType.DMA((8,)),
        ],
        compiler_params=limits(28),
        name="feed_forward",
    )(normed, own, partner)


NEAR = ("first", "last")


def near_turn(place_ref, r):
    return place_ref[0] ^ NEAR.index(r)


def grad_copies(copies, place_ref, grad_hbm, grad_ref, chips, block):
    return [
        copies(
            grad_hbm.at[
                0 if r is None else place_ref[2] ^ (1 + near_turn(place_ref, r) if r in NEAR else r)
            ],
            grad_ref.at[pl.ds(turn * block, block), :]
        )
        for turn, r in enumerate(chips)
    ]


MAGS = 8


def feed_back_kernel(place_ref, grad_hbm, own_ref, partner_ref, *refs, block, devices, chips, fused):
    kept, refs = refs[: 2 - fused], refs[2 - fused :]
    piece_refs, refs = refs[:devices], refs[devices:]
    count = len(chips)
    share_hbm, down_hbm, refs = refs[:count], refs[count : 2 * count], refs[2 * count :]
    hidden_hbm, grad_gate_hbm, grad_up_hbm, ext_ref, mag_ref, aux_ref, refs = *refs[:6], refs[6:]
    weight_ref, down_weight_ref, grad_ref, share_ref, made_ref, value_ref, semaphores = refs
    core = place_ref[0]
    columns = own_ref.shape[1]
    width = piece_refs[0].shape[1]
    copies = Copies(semaphores)
    fetches = grad_copies(copies, place_ref, grad_hbm, grad_ref, chips, block)
    for i, ref in enumerate(piece_refs):
        lanes = pl.ds(pl.multiple_of((place_ref[1] ^ i) * width, width), width)
        fetches.append(copies(ref, down_weight_ref.at[:, lanes]))
    if not fused:
        start = pl.multiple_of(near_turn(place_ref, chips[0]) * block, block)
        for at in range(2):
            fetches.append(copies(kept[at].at[:, pl.ds(start, block), :], value_ref.at[at]))
    weight_fetches = [copies(ref, weight_ref.at[half]) for half, ref in enumerate((own_ref, partner_ref))]
    if fused:
        weight_fetches[0].start()
    for fetch in fetches:
        fetch.start()
    mag_ref[...] = jnp.zeros(mag_ref.shape, f32)
    if fused:
        weight_fetches[0].wait()
        value_ref[0, 0] = dot_nt(kept[0][...], weight_ref[0, 0, :, :D])
        value_ref[1, 0] = dot_nt(kept[0][...], weight_ref[0, 1, :, :D])
    else:
        weight_fetches[0].start()
    for fetch in fetches:
        fetch.wait()
    weight_fetches[1].start()
    aux_ref[...] = down_weight_ref[2 * columns :, :]
    stores = []
    for turn in range(count):
        rows = slice(turn * block, (turn + 1) * block)
        grad = grad_ref[rows, :]
        share, down = None, None
        for half in range(2):
            order = core if half == 0 else 1 - core
            down_rows = pl.ds(pl.multiple_of(order * columns, 16), columns)
            if fused and half:
                weight_fetches[1].wait()
                value_ref[0, 1] = dot_nt(kept[0][...], weight_ref[1, 0, :, :D])
                value_ref[1, 1] = dot_nt(kept[0][...], weight_ref[1, 1, :, :D])
            gate, up = value_ref[0, half, rows, :], value_ref[1, half, rows, :]
            grad_hidden = dot_nt(grad, down_weight_ref[down_rows, :])
            sigma = 1.0 / (1.0 + jnp.exp(-gate))
            silu = gate * sigma
            hidden = (silu * up).astype(bf16)
            grad_gate = grad_hidden * up * (sigma + silu * (1.0 - sigma))
            grad_up = grad_hidden * silu
            mag_ref[half : half + 1, :columns] += jnp.sum(grad_gate * gate, axis=0, keepdims=True)
            mag_ref[2 + half : 3 + half, :columns] += jnp.sum(grad_up * up, axis=0, keepdims=True)
            grad_gate, grad_up = grad_gate.astype(bf16), grad_up.astype(bf16)
            for at, (value, ref) in enumerate(((hidden, hidden_hbm), (grad_gate, grad_gate_hbm), (grad_up, grad_up_hbm))):
                made_ref[at, half, rows, :] = value
                stores.append(copies.started(made_ref.at[at, half, rows, :], ref.at[half, rows, :]))
            part = dot_nn(hidden, down_weight_ref[down_rows, :])
            down = part if down is None else down + part
            if turn == 0 and not fused:
                weight_fetches[half].wait()
            part = dot_nn(grad_gate, weight_ref[half, 0]) + dot_nn(grad_up, weight_ref[half, 1])
            share = part if share is None else share + part
        share_ref[0, rows, :] = share[:, :D].astype(bf16)
        share_ref[1, rows, :] = down.astype(bf16)
        ext_ref[rows, :EXT] = share[:, D:].astype(bf16)
        small = dot_nt(grad, down_weight_ref[2 * columns :, :])
        ext_ref[rows, EXT : EXT + AUX] = small.astype(bf16)
        mag_ref[4:5, :] += jnp.sum(grad.astype(f32) * down, axis=0, keepdims=True)
    for at in range(count):
        turn = at ^ core if count == 2 else at
        rows = pl.ds(pl.multiple_of(turn * block, block), block)
        stores.append(copies.started(share_ref.at[0, rows, :], share_hbm[at]))
        stores.append(copies.started(share_ref.at[1, rows, :], down_hbm[at]))
    for store in stores:
        store.wait()


def feed_back(place, grads, chips, kept, own, partner, pieces, block):
    fused = int(len(kept) == 1)
    count = len(chips)
    tokens = count * block
    columns = own.shape[1]
    devices = len(pieces)
    return kernel_call(
        functools.partial(feed_back_kernel, block=block, devices=devices, chips=chips, fused=fused),
        out_shape=(shape_of((block, D), bf16),) * (2 * count)
        + (
            shape_of((2, tokens, columns), bf16),
            shape_of((2, tokens, columns), bf16),
            shape_of((2, tokens, columns), bf16),
            shape_of((tokens, 2 * EXT), bf16),
            shape_of((MAGS, D)),
            shape_of((AUX, D), bf16),
        ),
        in_specs=[in_smem] + [anywhere] * 3 + ([in_vmem] if fused else [anywhere] * 2) + [anywhere] * devices,
        out_specs=(anywhere,) * (3 + 2 * count) + (in_vmem,) * 3,
        scratch_shapes=[
            pltpu.VMEM((2, 2, columns, WIDE), bf16),
            pltpu.VMEM((2 * columns + AUX, D), bf16),
            pltpu.VMEM((tokens, D), bf16),
            pltpu.VMEM((2, tokens, D), bf16),
            pltpu.VMEM((3, 2, tokens, columns), bf16),
            pltpu.VMEM((2, 2, tokens, columns), f32),
            pltpu.SemaphoreType.DMA((4 + devices + 9 * count,)),
        ],
        compiler_params=limits(54),
        name="feed_back",
    )(place, grads, own, partner, *kept, *pieces)


def feed_adapter_kernel(
    place_ref, normed_hbm, grad_hbm, hidden_hbm, grad_gate_hbm, grad_up_hbm, ext_ref, rank_in_ref, down_in_ref, *refs,
    chips, block, before,
):
    before_refs, refs = refs[: 4 * before], refs[4 * before :]
    in_ref, out_ref, down_rank_in_ref, down_out_ref, grad_ref, normed_ref, made_ref, semaphores = refs
    copies = Copies(semaphores)
    start = near_turn(place_ref, chips[0]) * block if chips[0] in NEAR else 0
    normed_fetch = copies.started(normed_hbm.at[pl.ds(pl.multiple_of(start, block), block), :], normed_ref)
    fetches = [
        copies.started(ref, made_ref.at[at]) for at, ref in enumerate((hidden_hbm, grad_gate_hbm, grad_up_hbm))
    ]
    for fetch in grad_copies(copies, place_ref, grad_hbm, grad_ref, chips, block):
        fetch.start()
        fetches.append(fetch)

    def put(ref, index, value, at):
        ref[index] = value + before_refs[at][index] if before else value

    normed_fetch.wait()
    normed = normed_ref[...]
    small = dot_nt(rank_in_ref[...], normed).astype(bf16)
    ext = ext_ref[...].T
    put(in_ref, ..., dot_nn(ext[: 2 * RANK], normed), 0)
    for fetch in fetches:
        fetch.wait()
    down_small = 0.0
    for half in range(2):
        put(out_ref, (half, slice(0, RANK)), dot_nn(small[:RANK], made_ref[1, half]), 1)
        put(out_ref, (half, slice(RANK, 2 * RANK)), dot_nn(small[RANK:], made_ref[2, half]), 1)
        down_small = down_small + dot_nt(down_in_ref[half], made_ref[0, half])
        put(down_rank_in_ref, half, dot_nn(ext[EXT : EXT + RANK], made_ref[0, half]), 2)
    put(down_out_ref, ..., dot_nn(down_small.astype(bf16), grad_ref[...]), 3)


def feed_adapter(place, normed, grads, chips, hidden, grad_gate, grad_up, ext, rank_in_t, down_in_t, before):
    columns = hidden.shape[2]
    return kernel_call(
        functools.partial(
            feed_adapter_kernel, chips=chips, block=hidden.shape[1], before=int(before is not None)
        ),
        out_shape=(
            shape_of((2 * RANK, D)),
            shape_of((2, 2 * RANK, columns)),
            shape_of((2, RANK, columns)),
            shape_of((RANK, D)),
        ),
        in_specs=[in_smem] + [anywhere] * 5 + [in_vmem] * (3 + 4 * (before is not None)),
        out_specs=(in_vmem,) * 4,
        scratch_shapes=[
            pltpu.VMEM((hidden.shape[1], D), bf16),
            pltpu.VMEM((hidden.shape[1], D), bf16),
            pltpu.VMEM((3,) + hidden.shape, bf16),
            pltpu.SemaphoreType.DMA((5,)),
        ],
        compiler_params=limits(28),
        name="feed_adapter",
    )(place, normed, grads, hidden, grad_gate, grad_up, ext, rank_in_t, down_in_t, *(before or ()))


def adapter_columns(products, mag_raw, mag, weights, slot):
    ext = weights[:, D:].astype(f32).T
    inverse = ext[INV_AT : INV_AT + 1] + ext[INV_AT + 1 : INV_AT + 2]
    proj = ext[PROJ_AT : PROJ_AT + RANK] + ext[PROJ_AT + RANK : PROJ_AT + 2 * RANK]
    grad_mag = mag_raw / mag
    grad_out = factor * (products * (mag * inverse) - proj * (grad_mag * inverse))
    turned = ext[RANK * slot : RANK * (slot + 1)] * (-grad_mag / mag)
    return grad_mag, grad_out, dot_nn(turned.astype(bf16), weights[:, :D])


def finish_kernel(weight_ref, products_ref, mag_raw_ref, mag_ref, grad_mag_ref, grad_out_ref, grad_in_ref):
    for slot in range(2):
        grad_mag, grad_out, grad_in = adapter_columns(
            products_ref[slot * RANK : (slot + 1) * RANK],
            mag_raw_ref[slot : slot + 1],
            mag_ref[slot : slot + 1],
            weight_ref[slot],
            slot,
        )
        grad_mag_ref[slot : slot + 1] = grad_mag
        grad_out_ref[slot * RANK : (slot + 1) * RANK] = grad_out
        grad_in_ref[slot * RANK : (slot + 1) * RANK] = grad_in


def finish_columns(weights, products, mag_raw, mag):
    columns = weights.shape[1]
    return kernel_call(
        finish_kernel,
        out_shape=(shape_of((2, columns)), shape_of((2 * RANK, columns)), shape_of((2 * RANK, D))),
        compiler_params=limits(40),
        name="feed_finish",
    )(weights, products, mag_raw, mag)


def feed_pack_kernel(
    place_ref, own_hbm, partner_hbm, fold_hbm, products_ref, mag_raw_ref, mag_ref, in_ref, down_in_ref,
    down_products_ref, down_total_ref, down_mag_ref, down_aux_ref, down_proj_ref, down_rank_ref,
    kept_ref, given_ref, down_grad_ref, out_ref, weight_ref, fold_ref, full_ref, semaphores, *, share,
):
    copies = Copies(semaphores)
    fold_fetch = copies(fold_hbm, fold_ref)
    fetches = [
        copies.started((own_hbm, partner_hbm)[half].at[slot], weight_ref.at[half, slot])
        for half in range(2)
        for slot in range(2)
    ]
    columns = own_hbm.shape[1]
    chips, rows = fold_ref.shape[0], 2 * columns
    core, index, chip = place_ref[0], place_ref[1], place_ref[2]
    width = fold_ref.shape[2]
    full_ref[...] = jnp.zeros(full_ref.shape, f32)
    down_grad_ref[...] = down_total_ref[...] / down_mag_ref[...]
    inverse = down_aux_ref[RANK : RANK + 1].astype(f32) + down_aux_ref[RANK + 1 : RANK + 2].astype(f32)
    down_out = factor * down_products_ref[...] * (down_mag_ref[...] * inverse)
    turn = down_grad_ref[...] * inverse * (-factor * share)
    full_ref[:1, :D] = turn
    full_ref[RANK : 2 * RANK, :D] = down_out
    own = pl.ds(pl.multiple_of(index * width, width), width)
    own_turn = full_ref[:1, own]
    full_ref[RANK : 2 * RANK, own] += down_proj_ref[...] * own_turn
    out_ref[2 * RANK : 3 * RANK] = full_ref[RANK : 2 * RANK, :D].astype(bf16)
    out_ref[3 * RANK : 4 * RANK] = jnp.zeros((RANK, D), bf16)
    own_wide = (down_rank_ref[:, own].astype(f32) * own_turn).astype(bf16)
    full_ref[: 2 * RANK, :D] = jnp.zeros((2 * RANK, D), f32)
    fetches[0].wait()
    fold_fetch.start()
    parts = []
    ins = [in_ref[slot * RANK : (slot + 1) * RANK] for slot in range(2)]
    for half in range(2):
        outs, mags = [], []
        for slot in range(2):
            at = 2 * half + slot
            if at:
                fetches[at].wait()
            grad_mag, grad_out, grad_in = adapter_columns(
                products_ref[half, slot * RANK : (slot + 1) * RANK],
                mag_raw_ref[half + 2 * slot : half + 2 * slot + 1, :columns],
                mag_ref[half, slot : slot + 1],
                weight_ref[half, slot],
                slot,
            )
            outs.append(grad_out)
            mags.append(grad_mag)
            ins[slot] = ins[slot] + grad_in
        row = iota((RANK, columns), 0)
        tail = jnp.where(row == 0, mags[0], jnp.where(row == 1, mags[1], 0.0))
        parts.append(jnp.concatenate([*outs, down_in_ref[half], tail], axis=0))
    first, second = jnp.where(core == 0, parts[0], parts[1]), jnp.where(core == 0, parts[1], parts[0])
    full_ref[:, pl.ds(pl.multiple_of(chip * rows, HEAD), rows)] = jnp.concatenate([first, second], axis=1)
    for slot in range(2):
        out_ref[slot * RANK : (slot + 1) * RANK] = ins[slot].astype(bf16)
    fold_fetch.wait()
    for part in range(chips):
        lanes = slice(part * rows, (part + 1) * rows)
        full_ref[2 * RANK : 3 * RANK, lanes] += dot_nt(own_wide, fold_ref[part, :rows])
    for part in range(3):
        out_ref[64 * (1 + part) : 64 * (2 + part)] = full_ref[:, part * D : (part + 1) * D].astype(bf16)
    give_halves(place_ref, out_ref, kept_ref, given_ref)


def feed_pack(place, own, partner, fold_down, *rest, share):
    return kernel_call(
        functools.partial(feed_pack_kernel, share=share),
        out_shape=(shape_of((256, D // 2), bf16), shape_of((256, D // 2), bf16), shape_of((1, D))),
        in_specs=[in_smem] + [anywhere] * 3 + [in_vmem] * 11,
        out_specs=(in_vmem,) * 3,
        scratch_shapes=[
            pltpu.VMEM((256, D), bf16),
            pltpu.VMEM((2,) + own.shape, bf16),
            pltpu.VMEM(fold_down.shape, bf16),
            pltpu.VMEM((64, 3 * D), f32),
            pltpu.SemaphoreType.DMA((5,)),
        ],
        compiler_params=limits(40),
        name="feed_pack",
    )(place, own, partner, fold_down, *rest)


def output_adapter_kernel(
    grad_ref, mag_raw_ref, mag_ref, mixed_ref, ext_ref, rank_in_ref, weight_hbm,
    grad_mag_ref, grad_out_ref, grad_in_ref, weight_ref, semaphores,
):
    copies = all_head_copies(weight_hbm, weight_ref, semaphores)
    small = dot_nt(rank_in_ref[...], mixed_ref[...]).astype(bf16)
    grad_in_total = dot_nn(ext_ref[...].T[:RANK], mixed_ref[...])
    wide = GROUP * HEAD
    for head in range(KV_HEADS):
        next_head(copies, head)
        lanes = slice(head * wide, (head + 1) * wide)
        place = slice(head * HEAD, (head + 1) * HEAD)
        mag = jnp.concatenate([mag_ref[group : group + 1, place] for group in range(GROUP)], axis=1)
        grad_mag, grad_out, grad_in = adapter_columns(
            dot_nn(small, grad_ref[:, lanes]), mag_raw_ref[:, lanes], mag, weight_ref[head], 0
        )
        for group in range(GROUP):
            own = slice(group * HEAD, (group + 1) * HEAD)
            at = slice(group * KVW + head * HEAD, group * KVW + (head + 1) * HEAD)
            grad_mag_ref[:, at] = grad_mag[:, own]
            grad_out_ref[:, at] = grad_out[:, own]
        grad_in_total = grad_in_total + grad_in
    grad_in_ref[...] = grad_in_total


def output_adapter(grads, mag_raw, mag, weights, mixed, ext, rank_in_t):
    return kernel_call(
        output_adapter_kernel,
        out_shape=(shape_of((1, D)), shape_of((RANK, D)), shape_of((RANK, D))),
        in_specs=[in_vmem] * 6 + [anywhere],
        out_specs=(in_vmem,) * 3,
        scratch_shapes=head_scratch(weights),
        compiler_params=limits(28),
        name="output_adapter",
    )(grads, mag_raw, mag, mixed, ext, rank_in_t, weights)


def residual_back_kernel(
    first_ref, second_ref, third_ref, residual_ref, gain_ref, cotangent_ref, input_ref, mixed_ref, weight_hbm,
    grad_ref, ordered_ref, mag_ref, ext_ref, grad_mixed_ref, delta_ref, weight_ref, semaphores, column_ref,
):
    tokens = residual_ref.shape[0]
    copies = all_head_copies(weight_hbm, weight_ref, semaphores)
    for head in range(KV_HEADS):
        for copy in copies[head]:
            copy.start()
    normed_grad = first_ref[...].astype(f32) + second_ref[...].astype(f32) + third_ref[...].astype(f32)
    values = residual_ref[...]
    grad_ref[...] = cotangent_ref[...].astype(f32) + rms_back(
        values, rms_inverse(values), gain_ref[...], normed_grad
    )
    wide = GROUP * HEAD
    total = None
    for head in range(KV_HEADS):
        for group in range(GROUP):
            start = group * KVW + head * HEAD
            lanes = slice(start, start + HEAD)
            own = slice(head * wide + group * HEAD, head * wide + (group + 1) * HEAD)
            grad = grad_ref[:, lanes]
            ordered_ref[:, own] = grad.astype(bf16)
            value = residual_ref[:, lanes] - input_ref[:, lanes].astype(f32)
            mag_ref[:, own] = jnp.sum(grad * value, axis=0, keepdims=True)
        for copy in copies[head]:
            copy.wait()
        part = dot_nn(ordered_ref[:, head * wide : (head + 1) * wide], weight_ref[head])
        total = part if total is None else total + part
    ext_ref[...] = total[:, D:].astype(bf16)
    grad_mixed_ref[...] = total[:, :D].astype(bf16)
    for head in range(KV_HEADS):
        for group in range(GROUP):
            start = group * KVW + head * HEAD
            lanes = slice(start, start + HEAD)
            both = grad_mixed_ref[:, lanes].astype(f32) * mixed_ref[:, lanes].astype(f32)
            column_ref[:, head * GROUP + group : head * GROUP + group + 1] = jnp.sum(both, axis=1, keepdims=True)
    rows = column_ref[...].T
    for head in range(KV_HEADS):
        for group in range(GROUP):
            at = head * GROUP + group
            delta_ref[head, :, group * tokens : (group + 1) * tokens] = rows[at : at + 1]


def residual_back(shares, residual, gain, cotangent, inputs, mixed, weights):
    tokens = residual.shape[0]
    lanes = GROUP * tokens
    return kernel_call(
        residual_back_kernel,
        out_shape=(
            shape_of((tokens, D)),
            shape_of((tokens, D), bf16),
            shape_of((1, D)),
            shape_of((tokens, EXT), bf16),
            shape_of((tokens, D), bf16),
            shape_of((KV_HEADS, 1, lanes)),
        ),
        in_specs=[in_vmem] * 8 + [anywhere],
        out_specs=(in_vmem,) * 6,
        scratch_shapes=head_scratch(weights) + [pltpu.VMEM((tokens, HEAD), f32)],
        compiler_params=limits(40),
        name="residual_back",
    )(*shares, residual, gain[None], cotangent, inputs, mixed, weights)


def turn_back(values, cosine, sine):
    return values * cosine - pltpu.roll(values, HEAD // 2, 1) * sine


def query_back_kernel(
    grad_ref, query_ref, cos_ref, sin_ref, normed_ref, rank_in_ref, mag_ref, weight_hbm,
    accum_ref, grad_in_ref, out_ref, grad_mag_ref, turned_ref, weight_ref, semaphores,
):
    copies = all_head_copies(weight_hbm, weight_ref, semaphores)
    wide = GROUP * HEAD
    small = dot_nt(rank_in_ref[...], normed_ref[...]).astype(bf16)
    total, grad_in_total = None, None
    for head in range(KV_HEADS):
        mags = []
        for group in range(GROUP):
            lanes = slice(head * wide + group * HEAD, head * wide + (group + 1) * HEAD)
            grad = turn_back(grad_ref[:, lanes], cos_ref[...], sin_ref[...])
            raw = turn_back(query_ref[:, lanes].astype(f32), cos_ref[...], sin_ref[...])
            mags.append(jnp.sum(grad * raw, axis=0, keepdims=True))
            turned_ref[:, lanes] = grad.astype(bf16)
        turned = turned_ref[:, head * wide : (head + 1) * wide]
        next_head(copies, head)
        part = dot_nn(turned, weight_ref[head])
        total = part if total is None else total + part
        place = slice(head * HEAD, (head + 1) * HEAD)
        mag = jnp.concatenate([mag_ref[group : group + 1, place] for group in range(GROUP)], axis=1)
        grad_mag, grad_out, grad_in = adapter_columns(
            dot_nn(small, turned), jnp.concatenate(mags, axis=1), mag, weight_ref[head], 0
        )
        grad_in_total = grad_in if grad_in_total is None else grad_in_total + grad_in
        for group in range(GROUP):
            own = slice(group * HEAD, (group + 1) * HEAD)
            at = slice(group * KVW + head * HEAD, group * KVW + (head + 1) * HEAD)
            grad_mag_ref[:, at] = grad_mag[:, own]
            out_ref[:, at] = grad_out[:, own]
    accum_ref[...] = total
    grad_in_ref[...] = grad_in_total + dot_nn(total[:, D:].astype(bf16).T[:RANK], normed_ref[...])


def query_back(grads, queries, weights, cosine, sine, normed, rank_in_t, mag):
    tokens = normed.shape[0]
    return kernel_call(
        query_back_kernel,
        out_shape=(
            shape_of((tokens, WIDE)),
            shape_of((RANK, D)),
            shape_of((RANK, D)),
            shape_of((1, D)),
        ),
        in_specs=[in_vmem] * 7 + [anywhere],
        out_specs=(in_vmem,) * 4,
        scratch_shapes=[pltpu.VMEM((tokens, D), bf16)] + head_scratch(weights),
        compiler_params=limits(40),
        name="query_back",
    )(grads, queries, cosine, sine, normed, rank_in_t, mag, weights)


def give_halves(place_ref, value_ref, kept_ref, given_ref):
    half = value_ref.shape[1] // 2
    left, right = value_ref[:, :half].astype(bf16), value_ref[:, half:].astype(bf16)
    first = place_ref[0] == 0
    kept_ref[...] = jnp.where(first, left, right)
    given_ref[...] = jnp.where(first, right, left)


def key_back_kernel(
    heads_ref, sent_ref, grad_ref, kv_ref, cos_ref, sin_ref, normed_ref, input_ref, gain_ref, residual_hbm,
    before_hbm, rank_in_ref, mag_ref, place_ref, q_in_ref, q_out_ref, q_mag_ref, out_in_ref, out_out_ref, out_mag_ref,
    *refs,
):
    weight_hbm = refs[:KV_HEADS]
    input_grad_ref, kept_ref, given_ref, late_ref, out_ref, grad_mag_ref, turned_ref = refs[KV_HEADS : KV_HEADS + 7]
    weight_refs, before_ref, residual_ref, semaphores = refs[KV_HEADS + 7 :]
    copies = Copies(semaphores)
    fetches = [copies.started(ref, weight_refs.at[slot]) for slot, ref in enumerate(weight_hbm)]
    before_fetch = copies.started(before_hbm, before_ref)
    residual_fetch = copies.started(residual_hbm, residual_ref)
    small = dot_nt(rank_in_ref[...], normed_ref[...]).astype(bf16)
    total = None
    near = 2 * HEAD
    grad_ins = [None, None]
    for slot in range(KV_HEADS):
        place = heads_ref[slot] * HEAD
        mags = []
        for part in range(2):
            lanes = lanes_at(2 * place + part * HEAD)
            grad = grad_ref[:, lanes] + sent_ref[:, lanes].astype(f32)
            raw = kv_ref[:, lanes].astype(f32)
            if part == 0:
                grad = turn_back(grad, cos_ref[...], sin_ref[...])
                raw = turn_back(raw, cos_ref[...], sin_ref[...])
            mags.append(jnp.sum(grad * raw, axis=0, keepdims=True))
            turned_ref[:, slot * near + part * HEAD : slot * near + (part + 1) * HEAD] = grad.astype(bf16)
        fetches[slot].wait()
        part = dot_nn(turned_ref[:, slot * near : (slot + 1) * near], weight_refs[slot])
        total = part if total is None else total + part
        for part in range(2):
            lanes = slice(slot * near + part * HEAD, slot * near + (part + 1) * HEAD)
            grad_mag, grad_out, grad_in = adapter_columns(
                dot_nn(small[part * RANK : (part + 1) * RANK], turned_ref[:, lanes]),
                mags[part],
                mag_ref[part : part + 1, lanes_at(place)],
                weight_refs[slot, part * HEAD : (part + 1) * HEAD, :],
                1 + part,
            )
            grad_mag_ref[:, lanes_at(part * KVW + place)] = grad_mag
            out_ref[:, lanes_at(part * KVW + place)] = grad_out
            grad_ins[part] = grad_in if grad_ins[part] is None else grad_ins[part] + grad_in
    before_fetch.wait()
    total = total + before_ref[...]
    residual_fetch.wait()
    ext = total[:, D:].astype(bf16).T
    late_ref[:RANK, :D] = q_in_ref[...]
    for part in range(2):
        late_ref[(1 + part) * RANK : (2 + part) * RANK, :D] = grad_ins[part] + dot_nn(
            ext[(1 + part) * RANK : (2 + part) * RANK], normed_ref[...]
        )
    late_ref[3 * RANK :, :D] = q_out_ref[...]
    late_ref[:RANK, D : 2 * D] = out_in_ref[...]
    late_ref[RANK : 2 * RANK, D : 2 * D] = out_out_ref[...]
    late_ref[2 * RANK :, D : 2 * D] = jnp.where(iota((2 * RANK, D), 0) == 0, out_mag_ref[...], 0.0)
    row = iota((2 * RANK, KVW), 0)
    side = jnp.zeros((2 * RANK, KVW), f32)
    for at in range(GROUP):
        side = jnp.where(row == at, q_mag_ref[:, at * KVW : (at + 1) * KVW], side)
    for part in range(2):
        lanes = slice(part * KVW, (part + 1) * KVW)
        late_ref[part * RANK : (part + 1) * RANK, 2 * D :] = out_ref[:, lanes]
        side = jnp.where(row == GROUP + part, grad_mag_ref[:, lanes], side)
    late_ref[2 * RANK :, 2 * D :] = side
    give_halves(place_ref, late_ref, kept_ref, given_ref)
    values = input_ref[...].astype(f32)
    back = rms_back(values, rms_inverse(values), gain_ref[...], total[:, :D])
    input_grad_ref[...] = (residual_ref[...] + back).astype(bf16)


def key_back(
    heads, sent, grads, kv, weights, cosine, sine, normed, inputs, gain, grad_residual, before, rank_in_t, mag, place,
    *others
):
    tokens = normed.shape[0]
    wide = 2 * D + KVW
    return kernel_call(
        key_back_kernel,
        out_shape=(
            shape_of((tokens, D), bf16),
            shape_of((4 * RANK, wide // 2), bf16),
            shape_of((4 * RANK, wide // 2), bf16),
        ),
        in_specs=[in_smem] + [in_vmem] * 8 + [anywhere] * 2 + [in_vmem] * 2 + [in_smem] + [in_vmem] * 6
        + [anywhere] * KV_HEADS,
        out_specs=(in_vmem,) * 3,
        scratch_shapes=[
            pltpu.VMEM((4 * RANK, wide), f32),
            pltpu.VMEM((RANK, 2 * KVW), f32),
            pltpu.VMEM((1, 2 * KVW), f32),
            pltpu.VMEM((tokens, 2 * KVW), bf16),
            pltpu.VMEM((KV_HEADS, 2 * HEAD, WIDE), bf16),
            pltpu.VMEM((tokens, WIDE), f32),
            pltpu.VMEM((tokens, D), f32),
            pltpu.SemaphoreType.DMA((KV_HEADS + 2,)),
        ],
        compiler_params=limits(40),
        name="key_back",
    )(
        heads, sent, grads, kv, cosine, sine, normed, inputs, gain[None], grad_residual,
        before, rank_in_t, mag, place, *others, *weights,
    )


def cut_kernel(place_ref, mine_ref, other_ref, *refs):
    out_refs, total_ref = refs[:-1], refs[-1]
    rows = out_refs[0].shape[0]
    total_ref[...] = (mine_ref[...].astype(f32) + other_ref[...].astype(f32)).astype(bf16)
    for r, ref in enumerate(out_refs):
        ref[...] = total_ref[pl.ds(pl.multiple_of((place_ref[2] ^ r) * rows, rows), rows), :]


def cut_rows(place, mine, other, chips):
    shape = shape_of((mine.shape[0] // chips, mine.shape[1]), bf16)
    return kernel_call(
        cut_kernel,
        out_shape=(shape,) * chips,
        in_specs=[in_smem, in_vmem, in_vmem],
        out_specs=(in_vmem,) * chips,
        scratch_shapes=[pltpu.VMEM(mine.shape, bf16)],
        name="cut_rows",
    )(place, mine, other)


def join_kernel(place_ref, *refs):
    piece_refs, out_ref = refs[:-1], refs[-1]
    rows = piece_refs[0].shape[0]
    for r, ref in enumerate(piece_refs):
        out_ref[pl.ds(pl.multiple_of((place_ref[2] ^ r) * rows, rows), rows), :] = ref[...]


def join_rows(place, pieces):
    rows, lanes = pieces[0].shape
    return kernel_call(
        join_kernel,
        out_shape=shape_of((rows * len(pieces), lanes), pieces[0].dtype),
        in_specs=[in_smem] + [in_vmem] * len(pieces),
        out_specs=in_vmem,
        name="join_rows",
    )(place, *pieces)


def sides_of(place_ref, mine_ref, other_ref):
    mine, other = mine_ref[...].astype(f32), other_ref[...].astype(f32)
    first = place_ref[0] == 0
    return jnp.where(first, mine, other), jnp.where(first, other, mine)


def unpack_late_kernel(place_ref, mine_ref, other_ref, *out_refs):
    attn_in_ref, attn_out_ref, attn_mag_ref, out_in_ref, out_out_ref, out_mag_ref = out_refs
    left, right = sides_of(place_ref, mine_ref, other_ref)
    split = left.shape[1] - D
    for member in range(3):
        attn_in_ref[member] = left[member * RANK : (member + 1) * RANK, :D]
    for group in range(GROUP):
        attn_out_ref[group] = left[3 * RANK :, group * KVW : (group + 1) * KVW]
    side = right[:, D - split :]
    attn_out_ref[GROUP] = side[:RANK]
    attn_out_ref[GROUP + 1] = side[RANK : 2 * RANK]
    attn_mag_ref[...] = side[2 * RANK : 2 * RANK + GROUP + 2]
    mid = jnp.concatenate([left[:, D:], right[:, : D - split]], axis=1)
    out_in_ref[...] = mid[:RANK]
    for group in range(GROUP):
        lanes = slice(group * KVW, (group + 1) * KVW)
        out_out_ref[group] = mid[RANK : 2 * RANK, lanes]
        out_mag_ref[group : group + 1, :] = mid[2 * RANK : 2 * RANK + 1, lanes]


def unpack_early_kernel(place_ref, mine_ref, other_ref, in_ref, out_ref, mag_ref, down_in_ref, down_out_ref):
    half = D // 2
    for at, values in enumerate(sides_of(place_ref, mine_ref, other_ref)):
        lanes = slice(at * half, (at + 1) * half)
        for member in range(2):
            in_ref[member, :, lanes] = values[member * RANK : (member + 1) * RANK]
        down_out_ref[:, lanes] = values[2 * RANK : 3 * RANK]
        for part in range(3):
            start = part * D + at * half
            width = min(half, FF - start)
            if width <= 0:
                continue
            block = values[64 * (1 + part) : 64 * (2 + part), :width]
            to = slice(start, start + width)
            for member in range(2):
                out_ref[member, :, to] = block[member * RANK : (member + 1) * RANK]
            down_in_ref[:, to] = block[2 * RANK : 3 * RANK]
            mag_ref[:, to] = block[3 * RANK : 3 * RANK + 2]


def unpack(kernel, place, halves, shapes, name):
    return kernel_call(
        kernel,
        out_shape=tuple(shape_of(shape) for shape in shapes),
        in_specs=[in_smem, in_vmem, in_vmem],
        out_specs=(in_vmem,) * len(shapes),
        compiler_params=limits(24),
        name=name,
    )(place, *halves)


class Order:
    def __init__(self):
        self.last = None

    def __call__(self, *values):
        if self.last is not None:
            values = lax.optimization_barrier(tuple(values) + (self.last,))[:-1]
        return values[0] if len(values) == 1 else values

    def mark(self, value):
        self.last = value
        return value

    def pin(self, *values):
        values = self(*values)
        self.last = values[0] if isinstance(values, (tuple, list)) else values
        return values


def after(value, *others):
    return lax.optimization_barrier((value,) + others)[0]


class Links:
    def __init__(self, devices, blocks):
        self.devices = devices
        self.blocks = blocks
        self.chips = devices // 2
        self.index = lax.axis_index("dp")
        self.core = self.index % 2
        self.chip = self.index // 2
        self.block = lax.axis_index("blk")
        self.square = self.chips == 4
        self.place = jnp.stack([self.core, self.index, self.chip]).astype(jnp.int32)

    def swap(self, value, bits):
        return lax.ppermute(value, "dp", [(i, i ^ bits) for i in range(self.devices)])

    def split_swap(self, value, even_bits, odd_bits):
        return lax.ppermute(
            value, "dp", [(i, i ^ (odd_bits if i % 2 else even_bits)) for i in range(self.devices)]
        )

    def row_swap(self, value, bits):
        return lax.ppermute(value, "blk", [(i, i ^ bits) for i in range(self.blocks)])

    def row_shift(self, value, distance):
        pairs = [(i, i + distance) for i in range(self.blocks) if 0 <= i + distance < self.blocks]
        return lax.ppermute(value, "blk", pairs)

    def sides(self, value):
        return self.swap(value, 2), self.swap(value, 4)

    def across(self, side, other):
        return self.split_swap(jnp.where(self.core == 0, other, side), 2, 4)

    def total(self, kept, given, order):
        sent = self.swap(given, 1)
        yield
        sent = order(sent)
        cuts = cut_rows(self.place, kept, sent, self.chips)
        order.mark(cuts[0])
        sent = [self.swap(cuts[r], 2 * r) for r in range(1, self.chips)]
        yield
        sent = order(*sent)
        value = order.mark(sum([cuts[0].astype(f32)] + [part.astype(f32) for part in sent]).astype(bf16))
        bits = 1
        while bits < self.blocks:
            sent = self.row_swap(value, bits)
            yield
            sent = order(sent)
            value = order.mark((value.astype(f32) + sent.astype(f32)).astype(bf16))
            bits *= 2
        sent = [self.swap(value, 2 * r) for r in range(1, self.chips)]
        yield
        sent = order(*sent)
        value = order.mark(join_rows(self.place, [value, *sent]))
        sent = self.swap(value, 1)
        yield
        sent = order(sent)
        yield value, sent

    def small_total(self, value, order):
        for swap, count in ((self.swap, self.devices), (self.row_swap, self.blocks)):
            bits = 1
            while bits < count:
                sent = swap(value, bits)
                yield
                sent = order(sent)
                value = order.mark(value + sent)
                bits *= 2
        yield value


def shards(
    block_input,
    out_cotangent,
    row_lengths,
    rope_positions,
    gain_attention,
    gain_feedforward,
    base_attention,
    base_output,
    base_feedforward,
    base_down,
    rank_in_attention,
    rank_out_attention,
    magnitude_attention,
    rank_in_output,
    rank_out_output,
    magnitude_output,
    rank_in_feedforward,
    rank_out_feedforward,
    magnitude_feedforward,
    rank_in_down,
    rank_out_down,
    magnitude_down,
    *,
    devices,
    blocks,
):
    links = Links(devices, blocks)
    order = Order()
    mark = order.mark
    index, core, chip, chips = links.index, links.core, links.chip, links.chips
    place = links.place
    partner = lambda value: links.swap(value, 1)
    rows_in = block_input[0]
    tokens = rows_in.shape[0]
    length = row_lengths[0]
    token_pos = links.block * tokens + jnp.arange(tokens, dtype=jnp.int32)
    fast = links.square and base_attention.shape[2] * devices == KVW and blocks == 4
    heads = jnp.arange(KV_HEADS, dtype=jnp.int32)
    heads = chip ^ heads if fast else heads
    scalars = jnp.stack([links.block.astype(jnp.int32), length])

    def columns_of(value, width):
        return lax.dynamic_slice_in_dim(value, index * width, width, value.ndim - 1)

    attn_cols, out_cols = base_attention.shape[2], base_output.shape[2]
    feed_cols, down_cols = base_feedforward.shape[2], base_down.shape[1]
    chip_cols = 2 * feed_cols
    attn_rank = columns_of(rank_out_attention, attn_cols)
    attn_mag = columns_of(magnitude_attention, attn_cols)
    attn_base = base_attention.transpose(0, 2, 1)
    attn_in_t = rank_in_attention.transpose(0, 2, 1)
    out_in_t = rank_in_output.T
    feed_in_t = rank_in_feedforward.transpose(0, 2, 1)
    down_in_t = rank_in_down.T

    def fold_out():
        return fold(
            order(base_output).transpose(0, 2, 1),
            out_in_t[None],
            columns_of(rank_out_output, out_cols),
            columns_of(magnitude_output, out_cols),
            0,
            False,
            "fold_o",
        )

    def fold_feed():
        return fold(
            order(base_feedforward).transpose(0, 2, 1),
            feed_in_t,
            columns_of(rank_out_feedforward, feed_cols),
            columns_of(magnitude_feedforward, feed_cols),
            0,
            True,
            "fold_feed",
        )

    def folded_down():
        return fold_down(
            order(base_down),
            down_in_t,
            columns_of(rank_out_down, down_cols),
            columns_of(magnitude_down, down_cols),
            chips,
        )

    def norm_in():
        values = order(rows_in).astype(f32)
        return (values * rms_inverse(values) * gain_attention).astype(bf16)

    frequency = rope_base ** (-(jnp.arange(HEAD // 2, dtype=f32) * 2.0) / HEAD)
    angles = rope_positions[0].astype(f32)[:, None] * frequency[None, :]
    cos_half, sin_half = jnp.cos(angles), jnp.sin(angles)
    cosine = jnp.concatenate([cos_half, cos_half], axis=-1)
    sine = jnp.concatenate([-sin_half, sin_half], axis=-1)
    tables = (cosine, sine)

    wheres = [jnp.stack([core, chip ^ r, chip, chip ^ 1, chip ^ 2]).astype(jnp.int32) for r in range(KV_HEADS)]

    settle = order.pin

    def project(where, first, second, roped, name, before=()):
        first, second = order(first, second)
        weights, out, token = head_step(where, first, second, normed, tables, roped, before, name)
        mark(token)
        return weights, out

    def send_kv(kv_blocks):
        kv_blocks.append(links.row_shift(kv_blocks[-1], 1))

    kv_fold = mark(
        fold(attn_base, attn_in_t, attn_rank[GROUP:], attn_mag[GROUP:], 1, True, "fold_kv", first=GROUP)
    )
    down_cut = lambda r: lax.dynamic_index_in_dim(down_fold, chip ^ r, 0, keepdims=False)
    spread = lambda value: lax.all_gather(value, "dp", axis=0)
    grad_out = jnp.where((token_pos < length)[:, None], out_cotangent[0], jnp.zeros((), bf16))
    grad_own = grad_out[None]
    chip_in_t = lax.dynamic_slice_in_dim(down_in_t, chip * chip_cols, chip_cols, 1)
    halves_in_t = jnp.stack(
        [lax.dynamic_slice_in_dim(chip_in_t, at * feed_cols, feed_cols, 1) for at in (core, 1 - core)]
    )
    feed_mag = lax.dynamic_slice_in_dim(magnitude_feedforward, chip * chip_cols, chip_cols, 1)
    if fast:
        kv_side, kv_other = links.sides(kv_fold)
        kv_partner = partner(kv_fold)
        q_fold = mark(fold(order(attn_base), attn_in_t, attn_rank[:GROUP], attn_mag[:GROUP], 0, False, "fold_q"))
        q_weights = spread(q_fold)
        kv_side, kv_other, kv_partner = settle(kv_side, kv_other, kv_partner)
        kv_across = links.across(kv_side, kv_other)
        kv_side_p, kv_other_p = partner(kv_side), partner(kv_other)
        o_fold = mark(fold_out())
        o_weights = spread(after(o_fold, q_fold))
        normed = mark(norm_in())
        kv_made = [
            project(wheres[0], kv_fold, kv_partner, 1, "head_kv"),
            project(wheres[1], kv_side, kv_side_p, 1, "head_kv"),
            project(wheres[2], kv_other, kv_other_p, 1, "head_kv"),
        ]
        kv_across = settle(kv_across)
        kv_across_p = partner(kv_across)
        kv_made.append(project(wheres[3], kv_across, kv_across_p, 1, "head_kv", [out for _, out in kv_made]))
        kv_own = kv_made[-1][1]
        kv_blocks = [kv_own]
        send_kv(kv_blocks)
        grad_own, halves_in_t, feed_mag = settle(grad_own, halves_in_t, feed_mag)
        feed_own = mark(fold_feed())
        kv_blocks[1] = settle(kv_blocks[1])
        send_kv(kv_blocks)
        down_fold, down_proj = folded_down()
        mark(down_proj)
        down_0, down_c1, down_c2, down_c3 = settle(*[down_cut(r) for r in range(4)])
        grad_all = lax.all_gather(
            order(grad_out), "dp", axis=0, axis_index_groups=[[2 * c + k for c in range(chips)] for k in range(2)]
        )
        kv_blocks[2] = settle(kv_blocks[2])
        send_kv(kv_blocks)
        queries = mark(query_project(order(normed), tables, q_weights))
        kv_blocks[3] = settle(kv_blocks[3])
        down_1, down_2, down_3 = links.swap(down_c1, 2), links.swap(down_c2, 4), links.swap(down_c3, 6)
        mixed, lse = attend(scalars, order(queries), kv_blocks)
        mark(lse)
        feed_partner = partner(order(feed_own))

        def feed_late():
            near = settle(down_1, down_2, down_3)
            pieces = []
            for piece in (down_0, *near):
                pieces += [piece, partner(piece)]
            return settle(*pieces)

    else:
        q_fold = fold(attn_base, attn_in_t, attn_rank[:GROUP], attn_mag[:GROUP], 0, False, "fold_q")
        q_weights, o_weights, normed = spread(q_fold), spread(fold_out()), norm_in()
        down_fold, down_proj = folded_down()
        feed_own = fold_feed()
        feed_partner = partner(feed_own)
        whole = lax.all_gather(kv_fold, "dp", axis=1, tiled=True).reshape(2, KV_HEADS, 2, HEAD // 2, WIDE)
        kv_made = []
        for j in range(KV_HEADS):
            before = [out for _, out in kv_made] if j == KV_HEADS - 1 else ()
            where = jnp.array([0, j, 0, 1, 2], jnp.int32)
            kv_made.append(project(where, whole[:, j, 0], whole[:, j, 1], 1, "head_kv", before))
        kv_own = kv_made[-1][1]
        kv_blocks = [kv_own]
        for _ in range(1, blocks):
            send_kv(kv_blocks)
        queries = query_project(normed, tables, q_weights)
        grad_all = lax.all_gather(
            grad_out, "dp", axis=0, axis_index_groups=[[2 * c + k for c in range(chips)] for k in range(2)]
        )
        mixed, lse = attend(scalars, queries, kv_blocks)
        down_pieces = []
        for r in range(chips):
            piece = links.swap(down_cut(r), 2 * r) if r else down_cut(r)
            down_pieces += [piece, partner(piece)]
    residual, normed_feed = output_project(order(mixed), o_weights, rows_in, gain_feedforward)
    mark(normed_feed)

    forward = lambda normed_group: settle(*feed_forward(order(normed_group), feed_own, feed_partner, tokens))
    aux = []

    def backward(members, kept):
        grads = grad_own if members == (None,) else grad_all
        kept = list(order(*kept)) if isinstance(kept, (tuple, list)) else [order(kept)]
        made = feed_back(place, grads, members, kept, feed_own, feed_partner, down_pieces, tokens)
        mark(made[0])
        count = len(members)
        return made[:count], made[count : 2 * count], made[2 * count :]

    mag_sums = []

    def adapters(members, normed_group, made, before):
        hidden, grad_gate, grad_up, ext, mags, down_aux = made[2]
        parts = feed_adapter(
            place, order(normed_group), grad_own if members == (None,) else grad_all, members, hidden, grad_gate,
            grad_up, ext, feed_in_t.reshape(2 * RANK, D), halves_in_t, before,
        )
        mark(parts[0])
        aux.append(down_aux)
        mag_sums.append(mags)
        return tuple(parts)

    if fast:
        side, other = links.sides(normed_feed)
        down_pieces = feed_late()
        own_made = backward((None,), normed_feed)
        side, other = settle(side, other)
        crossed = links.across(side, other)
        near = settle(jnp.concatenate([side, other]))
        near_kept = forward(near)
        sums = adapters((None,), normed_feed, own_made, None)
        crossed = settle(crossed)
        far_made = backward((3,), crossed)
        from_far = links.split_swap(far_made[0][0], 2, 4)
        first_made = backward(("first",), near_kept)
        early_first = links.split_swap(first_made[0][0], 2, 4)
        last_made = backward(("last",), near_kept)
        from_far = settle(from_far)
        late_share = settle((last_made[0][0].astype(f32) + from_far.astype(f32)).astype(bf16))
        early_second = links.split_swap(late_share, 4, 2)
        down_mag_steps = links.small_total(sum(made[2][4][4:5] for made in (own_made, first_made, last_made, far_made)), order)
        next(down_mag_steps)
        sums = adapters(("first",), near, first_made, sums)
        next(down_mag_steps)
        sums = adapters(("last",), near, last_made, sums)
        early_first = settle(early_first)
        reduced = (own_made[0][0], early_first, early_second)
        shares_out = [own_made[1][0], first_made[1][0], last_made[1][0], far_made[1][0]]
    else:
        sums, shares_grad, shares_out = None, [], []
        for r in range(chips):
            normed_group = links.swap(normed_feed, 2 * r) if r else normed_feed
            made = backward((r,), normed_group)
            sums = adapters((r,), normed_group, made, sums)
            shares_grad.append(made[0][0])
            shares_out.append(made[1][0])
        rest = sum(links.swap(shares_grad[r], 2 * r).astype(f32) for r in range(1, chips)).astype(bf16)
        reduced = (shares_grad[0], rest, jnp.zeros(rest.shape, bf16))
        down_mag_steps = links.small_total(sum(mags[4:5] for mags in mag_sums), order)
        next(down_mag_steps)
    reduced = settle(*reduced)
    grad_residual, grad_ordered, out_mag_raw, out_ext, grad_mixed, delta = residual_back(
        reduced, residual, gain_feedforward, grad_out, rows_in, mixed, o_weights
    )
    mark(delta)
    next(down_mag_steps)
    def pack_early(down_mag_total):
        feed_mags = jnp.stack(
            [lax.dynamic_slice_in_dim(feed_mag, at * feed_cols, feed_cols, 1) for at in (core, 1 - core)]
        )
        if fast:
            *early, down_grad_mag = feed_pack(
                place, feed_own, feed_partner, down_fold, *order(feed_products, mag_raw), feed_mags, feed_in, down_in,
                down_products, down_mag_total, magnitude_down[None], aux[0], down_proj, rank_out_down,
                share=1.0 / blocks,
            )
            return down_grad_mag, early
        finished = [
            finish_columns(weights, feed_products[half], mag_raw[half:4:2, :feed_cols], feed_mags[half])
            for half, weights in enumerate((feed_own, feed_partner))
        ]
        grad_mag, grad_out_part, grad_in_part = zip(*finished)
        columns = [
            jnp.concatenate([part.astype(bf16) for part in parts])
            for parts in zip(grad_out_part, down_in, grad_mag)
        ]
        columns = jnp.where(core == 0, jnp.concatenate(columns, axis=1), jnp.concatenate(columns[::-1], axis=1))
        full = lax.dynamic_update_slice(jnp.zeros((64, 3 * D), bf16), columns, (0, chip * chip_cols))
        down_aux = aux[0]
        down_inverse = (down_aux[RANK].astype(f32) + down_aux[RANK + 1].astype(f32))[None]
        down_grad_mag = down_mag_total / magnitude_down[None]
        down_out = factor * down_products * (magnitude_down[None] * down_inverse)
        own_turn = columns_of(-down_grad_mag * down_inverse, down_cols) * (factor / blocks)
        down_out = lax.dynamic_update_slice(
            down_out, columns_of(down_out, down_cols) + down_proj * own_turn, (0, index * down_cols)
        )
        own_wide = (columns_of(rank_out_down.astype(f32), down_cols) * own_turn).astype(bf16)
        down_norm_in = lax.dot_general(
            own_wide, down_fold[:, :chip_cols], (((1,), (2,)), ((), ())), preferred_element_type=f32
        ).reshape(RANK, FF)
        down_full = (full[2 * RANK : 3 * RANK, :FF].astype(f32) + down_norm_in).astype(bf16)
        full = lax.dynamic_update_slice(full, down_full, (2 * RANK, 0))
        top = jnp.concatenate([(feed_in + sum(grad_in_part)).astype(bf16), down_out.astype(bf16)])
        whole = jnp.concatenate(
            [jnp.pad(top, ((0, 16), (0, 0)))] + [full[:, i * D : (i + 1) * D] for i in range(3)]
        )
        left, right = whole[:, : D // 2], whole[:, D // 2 :]
        return down_grad_mag, (jnp.where(core == 0, left, right), jnp.where(core == 0, right, left))

    grad_queries, grad_kvs = None, []

    def keys_back(distance):
        grad_queries_next, grad_kv = attend_back(
            scalars, order(queries), grad_mixed, lse, delta, kv_blocks[distance], grad_queries, distance
        )
        mark(grad_kv)
        return grad_queries_next, grad_kv

    def pass_down(passed, grad_kv):
        passed = order(passed)
        passed = settle((passed.astype(f32) + grad_kv.astype(f32)).astype(bf16))
        return links.row_shift(passed, -1)

    grad_queries, grad_kv = keys_back(blocks - 1)
    passed = links.row_shift(grad_kv, -1)
    next(down_mag_steps)
    held = None
    for distance in reversed(range(1, blocks - 1)):
        grad_queries, grad_kv = keys_back(distance)
        if held is not None:
            passed = pass_down(passed, held)
        held = grad_kv
    if fast:
        out_far = links.split_swap(order(shares_out[3]), 2, 4)
        out_first = links.split_swap(order(shares_out[1]), 2, 4)
    next(down_mag_steps)
    grad_queries, grad_kv = keys_back(0)
    if fast:
        sums = adapters((3,), crossed, far_made, sums)
    feed_in, feed_products, down_in, down_products = sums
    mag_raw = sum(mag_sums)
    for down_mag_total in down_mag_steps:
        pass
    down_grad_mag, early = pack_early(down_mag_total)
    mark(down_grad_mag)
    early_steps = links.total(*early, order)
    next(early_steps)
    passed = pass_down(passed, held)
    out_grad_mag, out_out, out_in = output_adapter(
        order(grad_ordered), out_mag_raw, magnitude_output, o_weights, mixed, out_ext, out_in_t
    )
    mark(out_in)
    if fast:
        next(early_steps)
        out_far, out_first = settle(out_far, out_first)
        out_late = settle((shares_out[2].astype(f32) + out_far.astype(f32)).astype(bf16))
        out_second = links.split_swap(out_late, 4, 2)
        out_parts = [shares_out[0], out_first, out_second]
    else:
        out_parts = [shares_out[0]] + [links.swap(shares_out[r], 2 * r) for r in range(1, chips)]
    q_acc, q_in, q_out, q_grad_mag = query_back(
        order(grad_queries), queries, q_weights, cosine, sine, normed, attn_in_t[0], magnitude_attention[:GROUP]
    )
    mark(q_in)
    if fast:
        next(early_steps)
    passed = settle(passed)
    input_grad, *late = key_back(
        heads, passed, grad_kv, kv_own, [weights for weights, _ in kv_made], cosine, sine, normed, rows_in,
        gain_attention, grad_residual, q_acc, attn_in_t[1:].reshape(2 * RANK, D), magnitude_attention[GROUP:],
        place, q_in, q_out, q_grad_mag, out_in, out_out, out_grad_mag,
    )
    mark(late[0])
    late_steps = links.total(*late, order)
    next(late_steps)
    out_parts = settle(*out_parts)
    late = early = None
    next(late_steps)
    block_out = settle((residual + sum(part.astype(f32) for part in out_parts)).astype(bf16))[None]
    while early is None:
        early = next(early_steps)
        if late is None:
            late = next(late_steps)
    early_shapes = ((2, RANK, D), (2, RANK, FF), (2, FF), (RANK, FF), (RANK, D))
    feed_in, feed_out, feed_mag, down_in, down_out = unpack(
        unpack_early_kernel, place, order(*early), early_shapes, "unpack_early"
    )
    mark(feed_mag)
    while late is None:
        late = next(late_steps)
    late_shapes = ((3, RANK, D), (GROUP + 2, RANK, KVW), (GROUP + 2, KVW), (RANK, D), (GROUP, RANK, KVW), (GROUP, KVW))
    attn_in, attn_out, attn_mag, out_in, out_out, out_mag = unpack(
        unpack_late_kernel, place, order(*late), late_shapes, "unpack_late"
    )
    return (
        block_out,
        input_grad[None],
        attn_in.transpose(0, 2, 1),
        attn_out,
        attn_mag,
        out_in.T,
        out_out,
        out_mag,
        feed_in.transpose(0, 2, 1),
        feed_out,
        feed_mag,
        down_in.T,
        down_out,
        down_grad_mag[0],
    )


def solution(mesh):
    split_tokens = P("dp", "blk", None)
    placed = (
        split_tokens,
        split_tokens,
        P("dp"),
        P("dp", "blk"),
        P(),
        P(),
        P(None, None, "dp"),
        P(None, None, "dp"),
        P(None, None, "dp"),
        P(None, "dp"),
    ) + (P(),) * 12
    return jax.shard_map(
        functools.partial(shards, devices=mesh.shape["dp"], blocks=mesh.shape["blk"]),
        mesh=mesh,
        in_specs=placed,
        out_specs=(split_tokens, split_tokens) + (P(),) * 12,
        check_vma=False,
    )
```

```python
import functools

import jax
import jax.numpy as jnp
from jax import lax
from jax.experimental import pallas as pl
from jax.experimental.pallas import tpu as pltpu
from jax.sharding import PartitionSpec as P

D = 2048
KV_HEADS = 4
HEAD = 128
FF = 5632
RANK = 16
GROUP = 4
KVW = 512

EXT = 128
WIDE = D + EXT
SLOTS = 3
INV_AT = 48
PROJ_AT = 64
AUX = 32

factor = 32.0 / RANK
rms_eps = 1e-05
rope_base = 10000.0
masked_score = -1e30
log2_e = 1.4426950408889634
score_scale = HEAD ** (-0.5)
f32 = jnp.float32
bf16 = jnp.bfloat16


def dot_nt(left, right):
    return lax.dot_general(left, right, (((1,), (1,)), ((), ())), preferred_element_type=f32)


def dot_nn(left, right):
    return lax.dot_general(left, right, (((1,), (0,)), ((), ())), preferred_element_type=f32)


def dot_tn(left, right):
    return lax.dot_general(left, right, (((0,), (0,)), ((), ())), preferred_element_type=f32)


def limits(mebibytes):
    return pltpu.CompilerParams(vmem_limit_bytes=mebibytes << 20)


def kernel_call(*args, in_specs=None, **options):
    if in_specs is not None:
        options["in_specs"] = in_specs
    call = pl.pallas_call(
        *args, cost_estimate=pl.CostEstimate(flops=0, transcendentals=0, bytes_accessed=0), **options
    )
    if in_specs is None:
        return call
    keep = lambda value, spec: pltpu.with_memory_space_constraint(value, pltpu.HBM) if spec is anywhere else value
    return lambda *operands: call(*[keep(value, spec) for value, spec in zip(operands, in_specs)])


anywhere = pl.BlockSpec(memory_space=pltpu.HBM)
in_vmem = pl.BlockSpec(memory_space=pltpu.VMEM)
in_smem = pl.BlockSpec(memory_space=pltpu.SMEM)


def shape_of(shape, dtype=f32):
    return jax.ShapeDtypeStruct(shape, dtype)


def split_low(value):
    high = value.astype(bf16)
    return high, (value - high.astype(f32)).astype(bf16)


def iota(shape, dim):
    return lax.broadcasted_iota(jnp.int32, shape, dim)


def lanes_at(start):
    return pl.ds(pl.multiple_of(start, HEAD), HEAD)


def fold_kernel(weight_ref, rank_in_ref, rank_out_ref, mag_ref, out_ref, column_ref, *, first_slot, moving):
    slot = first_slot + (pl.program_id(0) if moving else 0)
    rows = weight_ref.shape[1]

    def placed_at(start):
        spot = iota((RANK, EXT), 1) == iota((RANK, EXT), 0) + start
        return jnp.where(spot, 1.0, 0.0).astype(bf16)

    @pl.when(pl.program_id(1) == 0)
    def _():
        column_ref[0] = dot_tn(rank_out_ref[0], placed_at(0))
        column_ref[1] = dot_tn(rank_out_ref[0], placed_at(RANK * slot))
        mags = jnp.broadcast_to(mag_ref[0], (8, mag_ref.shape[2]))
        one = jnp.where(iota((8, EXT), 0) == 0, 1.0, 0.0)
        column_ref[2] = lax.dot_general(
            mags, one, (((0,), (0,)), ((), ())), precision=lax.Precision.HIGHEST, preferred_element_type=f32
        )

    own = pl.ds(pl.multiple_of(pl.program_id(1) * rows, 16), rows)
    doubled = (factor * column_ref[0, own, :RANK]).astype(bf16)
    merged = weight_ref[0].astype(f32) + dot_nn(doubled, rank_in_ref[0])
    inverse = 1.0 / jnp.sqrt(jnp.sum(merged * merged, axis=1, keepdims=True))
    scale = column_ref[2, own, :1] * inverse
    folded = (merged * scale).astype(bf16)
    out_ref[0, :, :D] = folded
    ext = column_ref[1, own, :] * (factor * scale)
    for index, part in enumerate(split_low(dot_nt(folded, rank_in_ref[0]))):
        ext = ext + dot_nn(part, placed_at(PROJ_AT + RANK * index))
    lane = iota(ext.shape, 1)
    for index, part in enumerate(split_low(inverse)):
        ext = ext + jnp.where(lane == INV_AT + index, part.astype(f32), 0.0)
    out_ref[0, :, D:] = ext.astype(bf16)


def fold(weights, rank_in_t, rank_out, magnitude, rank_first, moving, name, first=0):
    members, columns = magnitude.shape
    pieces = 4 if columns % 64 == 0 and columns > 256 else 1
    rows = columns // pieces
    rank_block = (lambda b, c: (b + rank_first, 0, 0)) if moving else (lambda b, c: (rank_first, 0, 0))
    return kernel_call(
        functools.partial(fold_kernel, first_slot=rank_first, moving=moving),
        out_shape=shape_of((members, columns, WIDE), bf16),
        grid=(members, pieces),
        in_specs=[
            pl.BlockSpec((1, rows, D), lambda b, c: (b + first, c, 0)),
            pl.BlockSpec((1, RANK, D), rank_block),
            pl.BlockSpec((1, RANK, columns), lambda b, c: (b, 0, 0)),
            pl.BlockSpec((1, 1, columns), lambda b, c: (b, 0, 0)),
        ],
        out_specs=pl.BlockSpec((1, rows, WIDE), lambda b, c: (b, c, 0)),
        scratch_shapes=[pltpu.VMEM((3, columns, EXT), f32)],
        compiler_params=limits(32),
        name=name,
    )(weights, rank_in_t, rank_out, magnitude[:, None, :])


def fold_down_kernel(weight_ref, rank_in_ref, rank_out_ref, mag_ref, out_ref, proj_ref, merged_ref, *, chips):
    rows = weight_ref.shape[0] // chips
    total = 0.0
    doubled = (factor * rank_out_ref[...].astype(f32)).astype(bf16)
    for part in range(chips):
        span = slice(part * rows, (part + 1) * rows)
        merged = weight_ref[span, :].astype(f32) + dot_tn(rank_in_ref[:, span], doubled)
        merged_ref[span, :] = merged
        total = total + jnp.sum(merged * merged, axis=0, keepdims=True)
    inverse = 1.0 / jnp.sqrt(total)
    scale = mag_ref[...] * inverse
    high, low = split_low(inverse)
    row = iota((AUX - RANK, scale.shape[1]), 0)
    tail = jnp.where(row == 0, high.astype(f32), jnp.where(row == 1, low.astype(f32), 0.0))
    aux = jnp.concatenate([doubled.astype(f32) * scale, tail], axis=0).astype(bf16)
    proj = 0.0
    for part in range(chips):
        span = slice(part * rows, (part + 1) * rows)
        folded = (merged_ref[span, :] * scale).astype(bf16)
        out_ref[part, :rows, :] = folded
        out_ref[part, rows:, :] = aux
        proj = proj + dot_nn(rank_in_ref[:, span], folded)
    proj_ref[...] = proj


def fold_down(weights, rank_in_t, rank_out, magnitude, chips):
    inputs, columns = weights.shape
    return kernel_call(
        functools.partial(fold_down_kernel, chips=chips),
        out_shape=(shape_of((chips, inputs // chips + AUX, columns), bf16), shape_of((RANK, columns))),
        scratch_shapes=[pltpu.VMEM((inputs, columns), f32)],
        compiler_params=limits(32),
        name="fold_down",
    )(weights, rank_in_t, rank_out, magnitude[None])


def head_kernel(scalar_ref, first_ref, second_ref, input_ref, cos_ref, sin_ref, *refs, roped):
    before_refs, (weight_ref, out_ref, token_ref) = refs[:-3], refs[-3:]
    members, half = first_ref.shape[0], first_ref.shape[1]
    for member in range(members):
        for order, ref in ((scalar_ref[0], first_ref), (1 - scalar_ref[0], second_ref)):
            weight_ref[pl.ds(pl.multiple_of((2 * member + order) * half, half), half), :] = ref[member]
    wide = members * HEAD
    for index, ref in enumerate(before_refs):
        out_ref[:, pl.ds(pl.multiple_of(scalar_ref[2 + index] * wide, wide), wide)] = ref[...]
    raw = dot_nt(input_ref[...], weight_ref[:, :D])
    for member in range(members):
        part = raw[:, member * HEAD : (member + 1) * HEAD]
        if member < roped:
            part = part * cos_ref[...] + pltpu.roll(part, HEAD // 2, 1) * sin_ref[...]
        start = (scalar_ref[1] * wide if before_refs else 0) + member * HEAD
        out_ref[:, lanes_at(start)] = part.astype(bf16)
    token_ref[...] = jnp.zeros(token_ref.shape, f32)


def head_step(scalars, first, second, inputs, tables, roped, before, name):
    members, half, _ = first.shape
    tokens = inputs.shape[0]
    wide = members * HEAD
    return kernel_call(
        functools.partial(head_kernel, roped=roped),
        out_shape=(
            shape_of((wide, WIDE), bf16),
            shape_of((tokens, (1 + len(before)) * wide), bf16),
            shape_of((8, HEAD)),
        ),
        in_specs=[in_smem] + [in_vmem] * (5 + len(before)),
        out_specs=(in_vmem,) * 3,
        compiler_params=limits(24),
        name=name,
    )(scalars, first, second, inputs, *tables, *before)


def head_copies(weight_ref, head, out_ref, semaphores, first=0):
    devices, members, part = weight_ref.shape[:3]
    parts = devices // KV_HEADS
    copies = []
    for at in range(parts):
        for member in range(members):
            copies.append(
                pltpu.make_async_copy(
                    weight_ref.at[parts * head + at, member],
                    out_ref.at[pl.ds((parts * member + at) * part, part), :],
                    semaphores.at[first + len(copies)],
                )
            )
    return copies


def head_scratch(weights):
    each = weights.shape[0] // KV_HEADS * weights.shape[1]
    return [
        pltpu.VMEM((KV_HEADS, weights.shape[1] * HEAD, WIDE), bf16),
        pltpu.SemaphoreType.DMA((KV_HEADS * each,)),
    ]


def all_head_copies(weight_ref, out_ref, semaphores):
    each = weight_ref.shape[0] // KV_HEADS * weight_ref.shape[1]
    return [head_copies(weight_ref, head, out_ref.at[head], semaphores, head * each) for head in range(KV_HEADS)]


def next_head(copies, head):
    if head == 0:
        for copy in copies[0] + copies[1]:
            copy.start()
    elif head + 1 < len(copies):
        for copy in copies[head + 1]:
            copy.start()
    for copy in copies[head]:
        copy.wait()


def query_kernel(input_ref, cos_ref, sin_ref, weight_hbm, out_ref, weight_ref, semaphores):
    copies = all_head_copies(weight_hbm, weight_ref, semaphores)
    for head in range(KV_HEADS):
        next_head(copies, head)
        raw = dot_nt(input_ref[...], weight_ref[head, :, :D])
        for group in range(GROUP):
            part = raw[:, group * HEAD : (group + 1) * HEAD]
            part = part * cos_ref[...] + pltpu.roll(part, HEAD // 2, 1) * sin_ref[...]
            start = (head * GROUP + group) * HEAD
            out_ref[:, start : start + HEAD] = part.astype(bf16)


def query_project(inputs, tables, weights):
    return kernel_call(
        query_kernel,
        out_shape=shape_of((inputs.shape[0], D), bf16),
        in_specs=[in_vmem] * 3 + [anywhere],
        out_specs=in_vmem,
        scratch_shapes=head_scratch(weights),
        compiler_params=limits(24),
        name="query_project",
    )(inputs, *tables, weights)


def masked_scores(keys, queries, key_first, length, causal):
    tokens, lanes = keys.shape[0], queries.shape[0]
    scores = dot_nt(keys, queries)
    key_pos = key_first + iota((tokens, 1), 0)
    scores = scores + jnp.where(key_pos < length, 0.0, masked_score)
    if causal:
        allowed = iota((tokens, lanes), 0) <= (iota((tokens, lanes), 1) & (tokens - 1))
        scores = jnp.where(allowed, scores, masked_score)
    return scores


def attend_kernel(scalar_ref, query_ref, *refs, steps):
    kv_refs = refs[:steps]
    mixed_ref, lse_ref, stacked_ref, max_ref, sum_ref, accum_ref = refs[steps:]
    head = pl.program_id(0)
    tokens = query_ref.shape[0]
    block_index, length = scalar_ref[0], scalar_ref[1]
    scale = score_scale * log2_e
    for group in range(GROUP):
        stacked_ref[group * tokens : (group + 1) * tokens, :] = query_ref[:, group * HEAD : (group + 1) * HEAD]

    for distance in range(steps):

        def step(distance=distance):
            keys = kv_refs[distance][:, :HEAD]
            values = kv_refs[distance][:, HEAD:]
            key_first = (block_index - distance) * tokens
            scores = masked_scores(keys, stacked_ref[...], key_first, length, distance == 0)
            block_max = jnp.max(scores, axis=0, keepdims=True)
            new_max = block_max if distance == 0 else jnp.maximum(max_ref[...], block_max)
            terms = jnp.exp2((scores - new_max) * scale)
            added = jnp.sum(terms, axis=0, keepdims=True)
            product = dot_tn(values, terms.astype(bf16))
            if distance == 0:
                sum_ref[...] = added
                accum_ref[...] = product
            else:
                fade = jnp.exp2((max_ref[...] - new_max) * scale)
                sum_ref[...] = sum_ref[...] * fade + added
                accum_ref[...] = accum_ref[...] * fade + product
            max_ref[...] = new_max

        if distance == 0:
            step()
        else:
            pl.when(block_index >= distance)(step)
    mixed = accum_ref[...] / sum_ref[...]
    for group in range(GROUP):
        part = mixed[:, group * tokens : (group + 1) * tokens]
        mixed_ref[:, lanes_at(group * KVW + head * HEAD)] = part.T.astype(bf16)
    lse_ref[0] = max_ref[...] * scale + jnp.log(sum_ref[...]) * log2_e


def attend(scalars, queries, kv_blocks):
    tokens = queries.shape[0]
    steps = len(kv_blocks)
    lanes = GROUP * tokens
    return kernel_call(
        functools.partial(attend_kernel, steps=steps),
        out_shape=(shape_of((tokens, D), bf16), shape_of((KV_HEADS, 1, lanes))),
        grid_spec=pltpu.PrefetchScalarGridSpec(
            num_scalar_prefetch=1,
            grid=(KV_HEADS,),
            in_specs=[pl.BlockSpec((tokens, GROUP * HEAD), lambda j, s: (0, j))]
            + [pl.BlockSpec((tokens, 2 * HEAD), lambda j, s: (0, j))] * steps,
            out_specs=(
                pl.BlockSpec((tokens, D), lambda j, s: (0, 0)),
                pl.BlockSpec((1, 1, lanes), lambda j, s: (j, 0, 0)),
            ),
            scratch_shapes=[
                pltpu.VMEM((lanes, HEAD), bf16),
                pltpu.VMEM((1, lanes), f32),
                pltpu.VMEM((1, lanes), f32),
                pltpu.VMEM((HEAD, lanes), f32),
            ],
        ),
        compiler_params=limits(40),
        name="attend",
    )(scalars, queries, *kv_blocks)


def attend_back_kernel(scalar_ref, query_ref, grad_ref, lse_ref, delta_ref, kv_ref, *refs, distance, chained):
    if chained:
        before_ref, grad_query_ref, grad_kv_ref, stacked_ref, stacked_grad_ref = refs
    else:
        grad_query_ref, grad_kv_ref, stacked_ref, stacked_grad_ref = refs
    head = pl.program_id(0)
    tokens = query_ref.shape[0]
    block_index, length = scalar_ref[0], scalar_ref[1]
    active = (block_index >= distance) & (block_index * tokens < length)

    @pl.when(active)
    def _():
        for group in range(GROUP):
            rows = slice(group * tokens, (group + 1) * tokens)
            stacked_ref[rows, :] = query_ref[:, group * HEAD : (group + 1) * HEAD]
            stacked_grad_ref[rows, :] = grad_ref[:, lanes_at(group * KVW + head * HEAD)]
        keys = kv_ref[:, :HEAD]
        values = kv_ref[:, HEAD:]
        key_first = (block_index - distance) * tokens
        scores = masked_scores(keys, stacked_ref[...], key_first, length, distance == 0)
        probs = jnp.exp2(scores * (score_scale * log2_e) - lse_ref[0])
        grad_probs = dot_nt(values, stacked_grad_ref[...])
        grad_scores = (probs * (grad_probs - delta_ref[0])).astype(bf16)
        grad_values = dot_nn(probs.astype(bf16), stacked_grad_ref[...])
        grad_keys = dot_nn(grad_scores, stacked_ref[...]) * score_scale
        grad_queries = dot_tn(grad_scores, keys) * score_scale
        for group in range(GROUP):
            lanes = slice(group * HEAD, (group + 1) * HEAD)
            part = grad_queries[group * tokens : (group + 1) * tokens, :]
            if chained:
                part = part + before_ref[:, lanes]
            grad_query_ref[:, lanes] = part
        grad_kv_ref[:, :HEAD] = grad_keys.astype(grad_kv_ref.dtype)
        grad_kv_ref[:, HEAD:] = grad_values.astype(grad_kv_ref.dtype)

    @pl.when(jnp.logical_not(active))
    def _():
        grad_query_ref[...] = before_ref[...] if chained else jnp.zeros(grad_query_ref.shape, f32)
        grad_kv_ref[...] = jnp.zeros(grad_kv_ref.shape, grad_kv_ref.dtype)


def attend_back(scalars, queries, grad_mixed, lse, delta, kv_block, before, distance):
    tokens = queries.shape[0]
    lanes = GROUP * tokens
    row = pl.BlockSpec((1, 1, lanes), lambda j, s: (j, 0, 0))
    per_query = pl.BlockSpec((tokens, GROUP * HEAD), lambda j, s: (0, j))
    per_key = pl.BlockSpec((tokens, 2 * HEAD), lambda j, s: (0, j))
    chained = before is not None
    operands = [scalars, queries, grad_mixed, lse, delta, kv_block]
    specs = [per_query, pl.BlockSpec((tokens, D), lambda j, s: (0, 0)), row, row, per_key]
    if chained:
        operands += [before]
        specs += [per_query]
    return kernel_call(
        functools.partial(attend_back_kernel, distance=distance, chained=chained),
        out_shape=(shape_of((tokens, D)), shape_of((tokens, 2 * KVW), f32 if distance == 0 else bf16)),
        grid_spec=pltpu.PrefetchScalarGridSpec(
            num_scalar_prefetch=1,
            grid=(KV_HEADS,),
            in_specs=specs,
            out_specs=(per_query, per_key),
            scratch_shapes=[pltpu.VMEM((lanes, HEAD), bf16), pltpu.VMEM((lanes, HEAD), bf16)],
        ),
        input_output_aliases={6: 0} if chained else {},
        compiler_params=limits(40),
        name=f"attend_back_{distance}",
    )(*operands)


def rms_inverse(values):
    return lax.rsqrt(jnp.mean(values * values, axis=-1, keepdims=True) + rms_eps)


def rms_back(values, inverse, gain, grad):
    scaled = grad * gain
    return inverse * (scaled - values * (inverse * inverse * jnp.mean(scaled * values, axis=-1, keepdims=True)))


def output_kernel(mixed_ref, input_ref, gain_ref, weight_hbm, residual_ref, normed_ref, weight_ref, semaphores):
    copies = all_head_copies(weight_hbm, weight_ref, semaphores)
    for head in range(KV_HEADS):
        next_head(copies, head)
        value = dot_nt(mixed_ref[...], weight_ref[head, :, :D])
        for group in range(GROUP):
            start = group * KVW + head * HEAD
            lanes = slice(start, start + HEAD)
            residual_ref[:, lanes] = input_ref[:, lanes].astype(f32) + value[:, group * HEAD : (group + 1) * HEAD]
    values = residual_ref[...]
    normed_ref[...] = (values * rms_inverse(values) * gain_ref[...]).astype(bf16)


def output_project(mixed, weights, inputs, gain):
    tokens = mixed.shape[0]
    return kernel_call(
        output_kernel,
        out_shape=(shape_of((tokens, D)), shape_of((tokens, D), bf16)),
        in_specs=[in_vmem] * 3 + [anywhere],
        out_specs=(in_vmem,) * 2,
        scratch_shapes=head_scratch(weights),
        compiler_params=limits(28),
        name="output_project",
    )(mixed, inputs, gain[None], weights)


class Copies:
    def __init__(self, semaphores):
        self.semaphores = semaphores
        self.made = []

    def __call__(self, source, target):
        copy = pltpu.make_async_copy(source, target, self.semaphores.at[len(self.made)])
        self.made.append(copy)
        return copy

    def started(self, source, target):
        copy = self(source, target)
        copy.start()
        return copy


def feed_forward_kernel(normed_ref, own_ref, partner_ref, gate_hbm, up_hbm, weight_ref, value_ref, semaphores, *, block):
    copies = Copies(semaphores)
    pairs = [(half, member) for half in range(2) for member in range(2)]
    fetches = [
        copies((own_ref, partner_ref)[half].at[member], weight_ref.at[2 * half + member]) for half, member in pairs
    ]
    fetches[0].start()
    fetches[1].start()
    stores = []
    for half, member in pairs:
        at = 2 * half + member
        fetches[at].wait()
        if at + 2 < 4:
            fetches[at + 2].start()
        for start in range(0, normed_ref.shape[0], block):
            rows = slice(start, start + block)
            value_ref[at, rows, :] = dot_nt(normed_ref[rows, :], weight_ref[at, :, :D])
        stores.append(copies.started(value_ref.at[at], (gate_hbm, up_hbm)[member].at[half]))
    for store in stores:
        store.wait()


def feed_forward(normed, own, partner, block):
    tokens = normed.shape[0]
    columns = own.shape[1]
    return kernel_call(
        functools.partial(feed_forward_kernel, block=block),
        out_shape=(shape_of((2, tokens, columns)), shape_of((2, tokens, columns))),
        in_specs=[in_vmem, anywhere, anywhere],
        out_specs=(anywhere,) * 2,
        scratch_shapes=[
            pltpu.VMEM((4, columns, WIDE), bf16),
            pltpu.VMEM((4, tokens, columns), f32),
            pltpu.SemaphoreType.DMA((8,)),
        ],
        compiler_params=limits(28),
        name="feed_forward",
    )(normed, own, partner)


NEAR = ("first", "last")


def near_turn(place_ref, r):
    return place_ref[0] ^ NEAR.index(r)


def grad_copies(copies, place_ref, grad_hbm, grad_ref, chips, block):
    return [
        copies(
            grad_hbm.at[
                0 if r is None else place_ref[2] ^ (1 + near_turn(place_ref, r) if r in NEAR else r)
            ],
            grad_ref.at[pl.ds(turn * block, block), :]
        )
        for turn, r in enumerate(chips)
    ]


MAGS = 8


def feed_back_kernel(place_ref, grad_hbm, own_ref, partner_ref, *refs, block, devices, chips, fused):
    kept, refs = refs[: 2 - fused], refs[2 - fused :]
    piece_refs, refs = refs[:devices], refs[devices:]
    count = len(chips)
    share_hbm, down_hbm, refs = refs[:count], refs[count : 2 * count], refs[2 * count :]
    hidden_hbm, grad_gate_hbm, grad_up_hbm, ext_ref, mag_ref, aux_ref, refs = *refs[:6], refs[6:]
    weight_ref, down_weight_ref, grad_ref, share_ref, made_ref, value_ref, semaphores = refs
    core = place_ref[0]
    columns = own_ref.shape[1]
    width = piece_refs[0].shape[1]
    copies = Copies(semaphores)
    fetches = grad_copies(copies, place_ref, grad_hbm, grad_ref, chips, block)
    for i, ref in enumerate(piece_refs):
        lanes = pl.ds(pl.multiple_of((place_ref[1] ^ i) * width, width), width)
        fetches.append(copies(ref, down_weight_ref.at[:, lanes]))
    if not fused:
        start = pl.multiple_of(near_turn(place_ref, chips[0]) * block, block)
        for at in range(2):
            fetches.append(copies(kept[at].at[:, pl.ds(start, block), :], value_ref.at[at]))
    weight_fetches = [copies(ref, weight_ref.at[half]) for half, ref in enumerate((own_ref, partner_ref))]
    if fused:
        weight_fetches[0].start()
    for fetch in fetches:
        fetch.start()
    mag_ref[...] = jnp.zeros(mag_ref.shape, f32)
    if fused:
        weight_fetches[0].wait()
        value_ref[0, 0] = dot_nt(kept[0][...], weight_ref[0, 0, :, :D])
        value_ref[1, 0] = dot_nt(kept[0][...], weight_ref[0, 1, :, :D])
    else:
        weight_fetches[0].start()
    for fetch in fetches:
        fetch.wait()
    weight_fetches[1].start()
    aux_ref[...] = down_weight_ref[2 * columns :, :]
    stores = []
    for turn in range(count):
        rows = slice(turn * block, (turn + 1) * block)
        grad = grad_ref[rows, :]
        share, down = None, None
        for half in range(2):
            order = core if half == 0 else 1 - core
            down_rows = pl.ds(pl.multiple_of(order * columns, 16), columns)
            if fused and half:
                weight_fetches[1].wait()
                value_ref[0, 1] = dot_nt(kept[0][...], weight_ref[1, 0, :, :D])
                value_ref[1, 1] = dot_nt(kept[0][...], weight_ref[1, 1, :, :D])
            gate, up = value_ref[0, half, rows, :], value_ref[1, half, rows, :]
            grad_hidden = dot_nt(grad, down_weight_ref[down_rows, :])
            sigma = 1.0 / (1.0 + jnp.exp(-gate))
            silu = gate * sigma
            hidden = (silu * up).astype(bf16)
            grad_gate = grad_hidden * up * (sigma + silu * (1.0 - sigma))
            grad_up = grad_hidden * silu
            mag_ref[half : half + 1, :columns] += jnp.sum(grad_gate * gate, axis=0, keepdims=True)
            mag_ref[2 + half : 3 + half, :columns] += jnp.sum(grad_up * up, axis=0, keepdims=True)
            grad_gate, grad_up = grad_gate.astype(bf16), grad_up.astype(bf16)
            for at, (value, ref) in enumerate(((hidden, hidden_hbm), (grad_gate, grad_gate_hbm), (grad_up, grad_up_hbm))):
                made_ref[at, half, rows, :] = value
                stores.append(copies.started(made_ref.at[at, half, rows, :], ref.at[half, rows, :]))
            part = dot_nn(hidden, down_weight_ref[down_rows, :])
            down = part if down is None else down + part
            if turn == 0 and not fused:
                weight_fetches[half].wait()
            part = dot_nn(grad_gate, weight_ref[half, 0]) + dot_nn(grad_up, weight_ref[half, 1])
            share = part if share is None else share + part
        share_ref[0, rows, :] = share[:, :D].astype(bf16)
        share_ref[1, rows, :] = down.astype(bf16)
        ext_ref[rows, :EXT] = share[:, D:].astype(bf16)
        small = dot_nt(grad, down_weight_ref[2 * columns :, :])
        ext_ref[rows, EXT : EXT + AUX] = small.astype(bf16)
        mag_ref[4:5, :] += jnp.sum(grad.astype(f32) * down, axis=0, keepdims=True)
    for at in range(count):
        turn = at ^ core if count == 2 else at
        rows = pl.ds(pl.multiple_of(turn * block, block), block)
        stores.append(copies.started(share_ref.at[0, rows, :], share_hbm[at]))
        stores.append(copies.started(share_ref.at[1, rows, :], down_hbm[at]))
    for store in stores:
        store.wait()


def feed_back(place, grads, chips, kept, own, partner, pieces, block):
    fused = int(len(kept) == 1)
    count = len(chips)
    tokens = count * block
    columns = own.shape[1]
    devices = len(pieces)
    return kernel_call(
        functools.partial(feed_back_kernel, block=block, devices=devices, chips=chips, fused=fused),
        out_shape=(shape_of((block, D), bf16),) * (2 * count)
        + (
            shape_of((2, tokens, columns), bf16),
            shape_of((2, tokens, columns), bf16),
            shape_of((2, tokens, columns), bf16),
            shape_of((tokens, 2 * EXT), bf16),
            shape_of((MAGS, D)),
            shape_of((AUX, D), bf16),
        ),
        in_specs=[in_smem] + [anywhere] * 3 + ([in_vmem] if fused else [anywhere] * 2) + [anywhere] * devices,
        out_specs=(anywhere,) * (3 + 2 * count) + (in_vmem,) * 3,
        scratch_shapes=[
            pltpu.VMEM((2, 2, columns, WIDE), bf16),
            pltpu.VMEM((2 * columns + AUX, D), bf16),
            pltpu.VMEM((tokens, D), bf16),
            pltpu.VMEM((2, tokens, D), bf16),
            pltpu.VMEM((3, 2, tokens, columns), bf16),
            pltpu.VMEM((2, 2, tokens, columns), f32),
            pltpu.SemaphoreType.DMA((4 + devices + 9 * count,)),
        ],
        compiler_params=limits(54),
        name="feed_back",
    )(place, grads, own, partner, *kept, *pieces)


def feed_adapter_kernel(
    place_ref, normed_hbm, grad_hbm, hidden_hbm, grad_gate_hbm, grad_up_hbm, ext_ref, rank_in_ref, down_in_ref, *refs,
    chips, block, before,
):
    before_refs, refs = refs[: 4 * before], refs[4 * before :]
    in_ref, out_ref, down_rank_in_ref, down_out_ref, grad_ref, normed_ref, made_ref, semaphores = refs
    copies = Copies(semaphores)
    start = near_turn(place_ref, chips[0]) * block if chips[0] in NEAR else 0
    normed_fetch = copies.started(normed_hbm.at[pl.ds(pl.multiple_of(start, block), block), :], normed_ref)
    fetches = [
        copies.started(ref, made_ref.at[at]) for at, ref in enumerate((hidden_hbm, grad_gate_hbm, grad_up_hbm))
    ]
    for fetch in grad_copies(copies, place_ref, grad_hbm, grad_ref, chips, block):
        fetch.start()
        fetches.append(fetch)

    def put(ref, index, value, at):
        ref[index] = value + before_refs[at][index] if before else value

    normed_fetch.wait()
    normed = normed_ref[...]
    small = dot_nt(rank_in_ref[...], normed).astype(bf16)
    ext = ext_ref[...].T
    put(in_ref, ..., dot_nn(ext[: 2 * RANK], normed), 0)
    for fetch in fetches:
        fetch.wait()
    down_small = 0.0
    for half in range(2):
        put(out_ref, (half, slice(0, RANK)), dot_nn(small[:RANK], made_ref[1, half]), 1)
        put(out_ref, (half, slice(RANK, 2 * RANK)), dot_nn(small[RANK:], made_ref[2, half]), 1)
        down_small = down_small + dot_nt(down_in_ref[half], made_ref[0, half])
        put(down_rank_in_ref, half, dot_nn(ext[EXT : EXT + RANK], made_ref[0, half]), 2)
    put(down_out_ref, ..., dot_nn(down_small.astype(bf16), grad_ref[...]), 3)


def feed_adapter(place, normed, grads, chips, hidden, grad_gate, grad_up, ext, rank_in_t, down_in_t, before):
    columns = hidden.shape[2]
    return kernel_call(
        functools.partial(
            feed_adapter_kernel, chips=chips, block=hidden.shape[1], before=int(before is not None)
        ),
        out_shape=(
            shape_of((2 * RANK, D)),
            shape_of((2, 2 * RANK, columns)),
            shape_of((2, RANK, columns)),
            shape_of((RANK, D)),
        ),
        in_specs=[in_smem] + [anywhere] * 5 + [in_vmem] * (3 + 4 * (before is not None)),
        out_specs=(in_vmem,) * 4,
        scratch_shapes=[
            pltpu.VMEM((hidden.shape[1], D), bf16),
            pltpu.VMEM((hidden.shape[1], D), bf16),
            pltpu.VMEM((3,) + hidden.shape, bf16),
            pltpu.SemaphoreType.DMA((5,)),
        ],
        compiler_params=limits(28),
        name="feed_adapter",
    )(place, normed, grads, hidden, grad_gate, grad_up, ext, rank_in_t, down_in_t, *(before or ()))


def adapter_columns(products, mag_raw, mag, weights, slot):
    ext = weights[:, D:].astype(f32).T
    inverse = ext[INV_AT : INV_AT + 1] + ext[INV_AT + 1 : INV_AT + 2]
    proj = ext[PROJ_AT : PROJ_AT + RANK] + ext[PROJ_AT + RANK : PROJ_AT + 2 * RANK]
    grad_mag = mag_raw / mag
    grad_out = factor * (products * (mag * inverse) - proj * (grad_mag * inverse))
    turned = ext[RANK * slot : RANK * (slot + 1)] * (-grad_mag / mag)
    return grad_mag, grad_out, dot_nn(turned.astype(bf16), weights[:, :D])


def finish_kernel(weight_ref, products_ref, mag_raw_ref, mag_ref, grad_mag_ref, grad_out_ref, grad_in_ref):
    for slot in range(2):
        grad_mag, grad_out, grad_in = adapter_columns(
            products_ref[slot * RANK : (slot + 1) * RANK],
            mag_raw_ref[slot : slot + 1],
            mag_ref[slot : slot + 1],
            weight_ref[slot],
            slot,
        )
        grad_mag_ref[slot : slot + 1] = grad_mag
        grad_out_ref[slot * RANK : (slot + 1) * RANK] = grad_out
        grad_in_ref[slot * RANK : (slot + 1) * RANK] = grad_in


def finish_columns(weights, products, mag_raw, mag):
    columns = weights.shape[1]
    return kernel_call(
        finish_kernel,
        out_shape=(shape_of((2, columns)), shape_of((2 * RANK, columns)), shape_of((2 * RANK, D))),
        compiler_params=limits(40),
        name="feed_finish",
    )(weights, products, mag_raw, mag)


def feed_pack_kernel(
    place_ref, own_hbm, partner_hbm, fold_hbm, products_ref, mag_raw_ref, mag_ref, in_ref, down_in_ref,
    down_products_ref, down_total_ref, down_mag_ref, down_aux_ref, down_proj_ref, down_rank_ref,
    kept_ref, given_ref, down_grad_ref, out_ref, weight_ref, fold_ref, full_ref, semaphores, *, share,
):
    copies = Copies(semaphores)
    fold_fetch = copies(fold_hbm, fold_ref)
    fetches = [
        copies.started((own_hbm, partner_hbm)[half].at[slot], weight_ref.at[half, slot])
        for half in range(2)
        for slot in range(2)
    ]
    columns = own_hbm.shape[1]
    chips, rows = fold_ref.shape[0], 2 * columns
    core, index, chip = place_ref[0], place_ref[1], place_ref[2]
    width = fold_ref.shape[2]
    full_ref[...] = jnp.zeros(full_ref.shape, f32)
    down_grad_ref[...] = down_total_ref[...] / down_mag_ref[...]
    inverse = down_aux_ref[RANK : RANK + 1].astype(f32) + down_aux_ref[RANK + 1 : RANK + 2].astype(f32)
    down_out = factor * down_products_ref[...] * (down_mag_ref[...] * inverse)
    turn = down_grad_ref[...] * inverse * (-factor * share)
    full_ref[:1, :D] = turn
    full_ref[RANK : 2 * RANK, :D] = down_out
    own = pl.ds(pl.multiple_of(index * width, width), width)
    own_turn = full_ref[:1, own]
    full_ref[RANK : 2 * RANK, own] += down_proj_ref[...] * own_turn
    out_ref[2 * RANK : 3 * RANK] = full_ref[RANK : 2 * RANK, :D].astype(bf16)
    out_ref[3 * RANK : 4 * RANK] = jnp.zeros((RANK, D), bf16)
    own_wide = (down_rank_ref[:, own].astype(f32) * own_turn).astype(bf16)
    full_ref[: 2 * RANK, :D] = jnp.zeros((2 * RANK, D), f32)
    fetches[0].wait()
    fold_fetch.start()
    parts = []
    ins = [in_ref[slot * RANK : (slot + 1) * RANK] for slot in range(2)]
    for half in range(2):
        outs, mags = [], []
        for slot in range(2):
            at = 2 * half + slot
            if at:
                fetches[at].wait()
            grad_mag, grad_out, grad_in = adapter_columns(
                products_ref[half, slot * RANK : (slot + 1) * RANK],
                mag_raw_ref[half + 2 * slot : half + 2 * slot + 1, :columns],
                mag_ref[half, slot : slot + 1],
                weight_ref[half, slot],
                slot,
            )
            outs.append(grad_out)
            mags.append(grad_mag)
            ins[slot] = ins[slot] + grad_in
        row = iota((RANK, columns), 0)
        tail = jnp.where(row == 0, mags[0], jnp.where(row == 1, mags[1], 0.0))
        parts.append(jnp.concatenate([*outs, down_in_ref[half], tail], axis=0))
    first, second = jnp.where(core == 0, parts[0], parts[1]), jnp.where(core == 0, parts[1], parts[0])
    full_ref[:, pl.ds(pl.multiple_of(chip * rows, HEAD), rows)] = jnp.concatenate([first, second], axis=1)
    for slot in range(2):
        out_ref[slot * RANK : (slot + 1) * RANK] = ins[slot].astype(bf16)
    fold_fetch.wait()
    for part in range(chips):
        lanes = slice(part * rows, (part + 1) * rows)
        full_ref[2 * RANK : 3 * RANK, lanes] += dot_nt(own_wide, fold_ref[part, :rows])
    for part in range(3):
        out_ref[64 * (1 + part) : 64 * (2 + part)] = full_ref[:, part * D : (part + 1) * D].astype(bf16)
    give_halves(place_ref, out_ref, kept_ref, given_ref)


def feed_pack(place, own, partner, fold_down, *rest, share):
    return kernel_call(
        functools.partial(feed_pack_kernel, share=share),
        out_shape=(shape_of((256, D // 2), bf16), shape_of((256, D // 2), bf16), shape_of((1, D))),
        in_specs=[in_smem] + [anywhere] * 3 + [in_vmem] * 11,
        out_specs=(in_vmem,) * 3,
        scratch_shapes=[
            pltpu.VMEM((256, D), bf16),
            pltpu.VMEM((2,) + own.shape, bf16),
            pltpu.VMEM(fold_down.shape, bf16),
            pltpu.VMEM((64, 3 * D), f32),
            pltpu.SemaphoreType.DMA((5,)),
        ],
        compiler_params=limits(40),
        name="feed_pack",
    )(place, own, partner, fold_down, *rest)


def output_adapter_kernel(
    grad_ref, mag_raw_ref, mag_ref, mixed_ref, ext_ref, rank_in_ref, weight_hbm,
    grad_mag_ref, grad_out_ref, grad_in_ref, weight_ref, semaphores,
):
    copies = all_head_copies(weight_hbm, weight_ref, semaphores)
    small = dot_nt(rank_in_ref[...], mixed_ref[...]).astype(bf16)
    grad_in_total = dot_nn(ext_ref[...].T[:RANK], mixed_ref[...])
    wide = GROUP * HEAD
    for head in range(KV_HEADS):
        next_head(copies, head)
        lanes = slice(head * wide, (head + 1) * wide)
        place = slice(head * HEAD, (head + 1) * HEAD)
        mag = jnp.concatenate([mag_ref[group : group + 1, place] for group in range(GROUP)], axis=1)
        grad_mag, grad_out, grad_in = adapter_columns(
            dot_nn(small, grad_ref[:, lanes]), mag_raw_ref[:, lanes], mag, weight_ref[head], 0
        )
        for group in range(GROUP):
            own = slice(group * HEAD, (group + 1) * HEAD)
            at = slice(group * KVW + head * HEAD, group * KVW + (head + 1) * HEAD)
            grad_mag_ref[:, at] = grad_mag[:, own]
            grad_out_ref[:, at] = grad_out[:, own]
        grad_in_total = grad_in_total + grad_in
    grad_in_ref[...] = grad_in_total


def output_adapter(grads, mag_raw, mag, weights, mixed, ext, rank_in_t):
    return kernel_call(
        output_adapter_kernel,
        out_shape=(shape_of((1, D)), shape_of((RANK, D)), shape_of((RANK, D))),
        in_specs=[in_vmem] * 6 + [anywhere],
        out_specs=(in_vmem,) * 3,
        scratch_shapes=head_scratch(weights),
        compiler_params=limits(28),
        name="output_adapter",
    )(grads, mag_raw, mag, mixed, ext, rank_in_t, weights)


def residual_back_kernel(
    first_ref, second_ref, third_ref, residual_ref, gain_ref, cotangent_ref, input_ref, mixed_ref, weight_hbm,
    grad_ref, ordered_ref, mag_ref, ext_ref, grad_mixed_ref, delta_ref, weight_ref, semaphores, column_ref,
):
    tokens = residual_ref.shape[0]
    copies = all_head_copies(weight_hbm, weight_ref, semaphores)
    for head in range(KV_HEADS):
        for copy in copies[head]:
            copy.start()
    normed_grad = first_ref[...].astype(f32) + second_ref[...].astype(f32) + third_ref[...].astype(f32)
    values = residual_ref[...]
    grad_ref[...] = cotangent_ref[...].astype(f32) + rms_back(
        values, rms_inverse(values), gain_ref[...], normed_grad
    )
    wide = GROUP * HEAD
    total = None
    for head in range(KV_HEADS):
        for group in range(GROUP):
            start = group * KVW + head * HEAD
            lanes = slice(start, start + HEAD)
            own = slice(head * wide + group * HEAD, head * wide + (group + 1) * HEAD)
            grad = grad_ref[:, lanes]
            ordered_ref[:, own] = grad.astype(bf16)
            value = residual_ref[:, lanes] - input_ref[:, lanes].astype(f32)
            mag_ref[:, own] = jnp.sum(grad * value, axis=0, keepdims=True)
        for copy in copies[head]:
            copy.wait()
        part = dot_nn(ordered_ref[:, head * wide : (head + 1) * wide], weight_ref[head])
        total = part if total is None else total + part
    ext_ref[...] = total[:, D:].astype(bf16)
    grad_mixed_ref[...] = total[:, :D].astype(bf16)
    for head in range(KV_HEADS):
        for group in range(GROUP):
            start = group * KVW + head * HEAD
            lanes = slice(start, start + HEAD)
            both = grad_mixed_ref[:, lanes].astype(f32) * mixed_ref[:, lanes].astype(f32)
            column_ref[:, head * GROUP + group : head * GROUP + group + 1] = jnp.sum(both, axis=1, keepdims=True)
    rows = column_ref[...].T
    for head in range(KV_HEADS):
        for group in range(GROUP):
            at = head * GROUP + group
            delta_ref[head, :, group * tokens : (group + 1) * tokens] = rows[at : at + 1]


def residual_back(shares, residual, gain, cotangent, inputs, mixed, weights):
    tokens = residual.shape[0]
    lanes = GROUP * tokens
    return kernel_call(
        residual_back_kernel,
        out_shape=(
            shape_of((tokens, D)),
            shape_of((tokens, D), bf16),
            shape_of((1, D)),
            shape_of((tokens, EXT), bf16),
            shape_of((tokens, D), bf16),
            shape_of((KV_HEADS, 1, lanes)),
        ),
        in_specs=[in_vmem] * 8 + [anywhere],
        out_specs=(in_vmem,) * 6,
        scratch_shapes=head_scratch(weights) + [pltpu.VMEM((tokens, HEAD), f32)],
        compiler_params=limits(40),
        name="residual_back",
    )(*shares, residual, gain[None], cotangent, inputs, mixed, weights)


def turn_back(values, cosine, sine):
    return values * cosine - pltpu.roll(values, HEAD // 2, 1) * sine


def query_back_kernel(
    grad_ref, query_ref, cos_ref, sin_ref, normed_ref, rank_in_ref, mag_ref, weight_hbm,
    accum_ref, grad_in_ref, out_ref, grad_mag_ref, turned_ref, weight_ref, semaphores,
):
    copies = all_head_copies(weight_hbm, weight_ref, semaphores)
    wide = GROUP * HEAD
    small = dot_nt(rank_in_ref[...], normed_ref[...]).astype(bf16)
    total, grad_in_total = None, None
    for head in range(KV_HEADS):
        mags = []
        for group in range(GROUP):
            lanes = slice(head * wide + group * HEAD, head * wide + (group + 1) * HEAD)
            grad = turn_back(grad_ref[:, lanes], cos_ref[...], sin_ref[...])
            raw = turn_back(query_ref[:, lanes].astype(f32), cos_ref[...], sin_ref[...])
            mags.append(jnp.sum(grad * raw, axis=0, keepdims=True))
            turned_ref[:, lanes] = grad.astype(bf16)
        turned = turned_ref[:, head * wide : (head + 1) * wide]
        next_head(copies, head)
        part = dot_nn(turned, weight_ref[head])
        total = part if total is None else total + part
        place = slice(head * HEAD, (head + 1) * HEAD)
        mag = jnp.concatenate([mag_ref[group : group + 1, place] for group in range(GROUP)], axis=1)
        grad_mag, grad_out, grad_in = adapter_columns(
            dot_nn(small, turned), jnp.concatenate(mags, axis=1), mag, weight_ref[head], 0
        )
        grad_in_total = grad_in if grad_in_total is None else grad_in_total + grad_in
        for group in range(GROUP):
            own = slice(group * HEAD, (group + 1) * HEAD)
            at = slice(group * KVW + head * HEAD, group * KVW + (head + 1) * HEAD)
            grad_mag_ref[:, at] = grad_mag[:, own]
            out_ref[:, at] = grad_out[:, own]
    accum_ref[...] = total
    grad_in_ref[...] = grad_in_total + dot_nn(total[:, D:].astype(bf16).T[:RANK], normed_ref[...])


def query_back(grads, queries, weights, cosine, sine, normed, rank_in_t, mag):
    tokens = normed.shape[0]
    return kernel_call(
        query_back_kernel,
        out_shape=(
            shape_of((tokens, WIDE)),
            shape_of((RANK, D)),
            shape_of((RANK, D)),
            shape_of((1, D)),
        ),
        in_specs=[in_vmem] * 7 + [anywhere],
        out_specs=(in_vmem,) * 4,
        scratch_shapes=[pltpu.VMEM((tokens, D), bf16)] + head_scratch(weights),
        compiler_params=limits(40),
        name="query_back",
    )(grads, queries, cosine, sine, normed, rank_in_t, mag, weights)


def give_halves(place_ref, value_ref, kept_ref, given_ref):
    half = value_ref.shape[1] // 2
    left, right = value_ref[:, :half].astype(bf16), value_ref[:, half:].astype(bf16)
    first = place_ref[0] == 0
    kept_ref[...] = jnp.where(first, left, right)
    given_ref[...] = jnp.where(first, right, left)


def key_back_kernel(
    heads_ref, sent_ref, grad_ref, kv_ref, cos_ref, sin_ref, normed_ref, input_ref, gain_ref, residual_hbm,
    before_hbm, rank_in_ref, mag_ref, place_ref, q_in_ref, q_out_ref, q_mag_ref, out_in_ref, out_out_ref, out_mag_ref,
    *refs,
):
    weight_hbm = refs[:KV_HEADS]
    input_grad_ref, kept_ref, given_ref, late_ref, out_ref, grad_mag_ref, turned_ref = refs[KV_HEADS : KV_HEADS + 7]
    weight_refs, before_ref, residual_ref, semaphores = refs[KV_HEADS + 7 :]
    copies = Copies(semaphores)
    fetches = [copies.started(ref, weight_refs.at[slot]) for slot, ref in enumerate(weight_hbm)]
    before_fetch = copies.started(before_hbm, before_ref)
    residual_fetch = copies.started(residual_hbm, residual_ref)
    small = dot_nt(rank_in_ref[...], normed_ref[...]).astype(bf16)
    total = None
    near = 2 * HEAD
    grad_ins = [None, None]
    for slot in range(KV_HEADS):
        place = heads_ref[slot] * HEAD
        mags = []
        for part in range(2):
            lanes = lanes_at(2 * place + part * HEAD)
            grad = grad_ref[:, lanes] + sent_ref[:, lanes].astype(f32)
            raw = kv_ref[:, lanes].astype(f32)
            if part == 0:
                grad = turn_back(grad, cos_ref[...], sin_ref[...])
                raw = turn_back(raw, cos_ref[...], sin_ref[...])
            mags.append(jnp.sum(grad * raw, axis=0, keepdims=True))
            turned_ref[:, slot * near + part * HEAD : slot * near + (part + 1) * HEAD] = grad.astype(bf16)
        fetches[slot].wait()
        part = dot_nn(turned_ref[:, slot * near : (slot + 1) * near], weight_refs[slot])
        total = part if total is None else total + part
        for part in range(2):
            lanes = slice(slot * near + part * HEAD, slot * near + (part + 1) * HEAD)
            grad_mag, grad_out, grad_in = adapter_columns(
                dot_nn(small[part * RANK : (part + 1) * RANK], turned_ref[:, lanes]),
                mags[part],
                mag_ref[part : part + 1, lanes_at(place)],
                weight_refs[slot, part * HEAD : (part + 1) * HEAD, :],
                1 + part,
            )
            grad_mag_ref[:, lanes_at(part * KVW + place)] = grad_mag
            out_ref[:, lanes_at(part * KVW + place)] = grad_out
            grad_ins[part] = grad_in if grad_ins[part] is None else grad_ins[part] + grad_in
    before_fetch.wait()
    total = total + before_ref[...]
    residual_fetch.wait()
    ext = total[:, D:].astype(bf16).T
    late_ref[:RANK, :D] = q_in_ref[...]
    for part in range(2):
        late_ref[(1 + part) * RANK : (2 + part) * RANK, :D] = grad_ins[part] + dot_nn(
            ext[(1 + part) * RANK : (2 + part) * RANK], normed_ref[...]
        )
    late_ref[3 * RANK :, :D] = q_out_ref[...]
    late_ref[:RANK, D : 2 * D] = out_in_ref[...]
    late_ref[RANK : 2 * RANK, D : 2 * D] = out_out_ref[...]
    late_ref[2 * RANK :, D : 2 * D] = jnp.where(iota((2 * RANK, D), 0) == 0, out_mag_ref[...], 0.0)
    row = iota((2 * RANK, KVW), 0)
    side = jnp.zeros((2 * RANK, KVW), f32)
    for at in range(GROUP):
        side = jnp.where(row == at, q_mag_ref[:, at * KVW : (at + 1) * KVW], side)
    for part in range(2):
        lanes = slice(part * KVW, (part + 1) * KVW)
        late_ref[part * RANK : (part + 1) * RANK, 2 * D :] = out_ref[:, lanes]
        side = jnp.where(row == GROUP + part, grad_mag_ref[:, lanes], side)
    late_ref[2 * RANK :, 2 * D :] = side
    give_halves(place_ref, late_ref, kept_ref, given_ref)
    values = input_ref[...].astype(f32)
    back = rms_back(values, rms_inverse(values), gain_ref[...], total[:, :D])
    input_grad_ref[...] = (residual_ref[...] + back).astype(bf16)


def key_back(
    heads, sent, grads, kv, weights, cosine, sine, normed, inputs, gain, grad_residual, before, rank_in_t, mag, place,
    *others
):
    tokens = normed.shape[0]
    wide = 2 * D + KVW
    return kernel_call(
        key_back_kernel,
        out_shape=(
            shape_of((tokens, D), bf16),
            shape_of((4 * RANK, wide // 2), bf16),
            shape_of((4 * RANK, wide // 2), bf16),
        ),
        in_specs=[in_smem] + [in_vmem] * 8 + [anywhere] * 2 + [in_vmem] * 2 + [in_smem] + [in_vmem] * 6
        + [anywhere] * KV_HEADS,
        out_specs=(in_vmem,) * 3,
        scratch_shapes=[
            pltpu.VMEM((4 * RANK, wide), f32),
            pltpu.VMEM((RANK, 2 * KVW), f32),
            pltpu.VMEM((1, 2 * KVW), f32),
            pltpu.VMEM((tokens, 2 * KVW), bf16),
            pltpu.VMEM((KV_HEADS, 2 * HEAD, WIDE), bf16),
            pltpu.VMEM((tokens, WIDE), f32),
            pltpu.VMEM((tokens, D), f32),
            pltpu.SemaphoreType.DMA((KV_HEADS + 2,)),
        ],
        compiler_params=limits(40),
        name="key_back",
    )(
        heads, sent, grads, kv, cosine, sine, normed, inputs, gain[None], grad_residual,
        before, rank_in_t, mag, place, *others, *weights,
    )


def cut_kernel(place_ref, mine_ref, other_ref, *refs):
    out_refs, total_ref = refs[:-1], refs[-1]
    rows = out_refs[0].shape[0]
    total_ref[...] = (mine_ref[...].astype(f32) + other_ref[...].astype(f32)).astype(bf16)
    for r, ref in enumerate(out_refs):
        ref[...] = total_ref[pl.ds(pl.multiple_of((place_ref[2] ^ r) * rows, rows), rows), :]


def cut_rows(place, mine, other, chips):
    shape = shape_of((mine.shape[0] // chips, mine.shape[1]), bf16)
    return kernel_call(
        cut_kernel,
        out_shape=(shape,) * chips,
        in_specs=[in_smem, in_vmem, in_vmem],
        out_specs=(in_vmem,) * chips,
        scratch_shapes=[pltpu.VMEM(mine.shape, bf16)],
        name="cut_rows",
    )(place, mine, other)


def join_kernel(place_ref, *refs):
    piece_refs, out_ref = refs[:-1], refs[-1]
    rows = piece_refs[0].shape[0]
    for r, ref in enumerate(piece_refs):
        out_ref[pl.ds(pl.multiple_of((place_ref[2] ^ r) * rows, rows), rows), :] = ref[...]


def join_rows(place, pieces):
    rows, lanes = pieces[0].shape
    return kernel_call(
        join_kernel,
        out_shape=shape_of((rows * len(pieces), lanes), pieces[0].dtype),
        in_specs=[in_smem] + [in_vmem] * len(pieces),
        out_specs=in_vmem,
        name="join_rows",
    )(place, *pieces)


def sides_of(place_ref, mine_ref, other_ref):
    mine, other = mine_ref[...].astype(f32), other_ref[...].astype(f32)
    first = place_ref[0] == 0
    return jnp.where(first, mine, other), jnp.where(first, other, mine)


def unpack_late_kernel(place_ref, mine_ref, other_ref, *out_refs):
    attn_in_ref, attn_out_ref, attn_mag_ref, out_in_ref, out_out_ref, out_mag_ref = out_refs
    left, right = sides_of(place_ref, mine_ref, other_ref)
    split = left.shape[1] - D
    for member in range(3):
        attn_in_ref[member] = left[member * RANK : (member + 1) * RANK, :D]
    for group in range(GROUP):
        attn_out_ref[group] = left[3 * RANK :, group * KVW : (group + 1) * KVW]
    side = right[:, D - split :]
    attn_out_ref[GROUP] = side[:RANK]
    attn_out_ref[GROUP + 1] = side[RANK : 2 * RANK]
    attn_mag_ref[...] = side[2 * RANK : 2 * RANK + GROUP + 2]
    mid = jnp.concatenate([left[:, D:], right[:, : D - split]], axis=1)
    out_in_ref[...] = mid[:RANK]
    for group in range(GROUP):
        lanes = slice(group * KVW, (group + 1) * KVW)
        out_out_ref[group] = mid[RANK : 2 * RANK, lanes]
        out_mag_ref[group : group + 1, :] = mid[2 * RANK : 2 * RANK + 1, lanes]


def unpack_early_kernel(place_ref, mine_ref, other_ref, in_ref, out_ref, mag_ref, down_in_ref, down_out_ref):
    half = D // 2
    for at, values in enumerate(sides_of(place_ref, mine_ref, other_ref)):
        lanes = slice(at * half, (at + 1) * half)
        for member in range(2):
            in_ref[member, :, lanes] = values[member * RANK : (member + 1) * RANK]
        down_out_ref[:, lanes] = values[2 * RANK : 3 * RANK]
        for part in range(3):
            start = part * D + at * half
            width = min(half, FF - start)
            if width <= 0:
                continue
            block = values[64 * (1 + part) : 64 * (2 + part), :width]
            to = slice(start, start + width)
            for member in range(2):
                out_ref[member, :, to] = block[member * RANK : (member + 1) * RANK]
            down_in_ref[:, to] = block[2 * RANK : 3 * RANK]
            mag_ref[:, to] = block[3 * RANK : 3 * RANK + 2]


def unpack(kernel, place, halves, shapes, name):
    return kernel_call(
        kernel,
        out_shape=tuple(shape_of(shape) for shape in shapes),
        in_specs=[in_smem, in_vmem, in_vmem],
        out_specs=(in_vmem,) * len(shapes),
        compiler_params=limits(24),
        name=name,
    )(place, *halves)


class Order:
    def __init__(self):
        self.last = None

    def __call__(self, *values):
        if self.last is not None:
            values = lax.optimization_barrier(tuple(values) + (self.last,))[:-1]
        return values[0] if len(values) == 1 else values

    def mark(self, value):
        self.last = value
        return value

    def pin(self, *values):
        values = self(*values)
        self.last = values[0] if isinstance(values, (tuple, list)) else values
        return values


def after(value, *others):
    return lax.optimization_barrier((value,) + others)[0]


class Links:
    def __init__(self, devices, blocks):
        self.devices = devices
        self.blocks = blocks
        self.chips = devices // 2
        self.index = lax.axis_index("dp")
        self.core = self.index % 2
        self.chip = self.index // 2
        self.block = lax.axis_index("blk")
        self.square = self.chips == 4
        self.place = jnp.stack([self.core, self.index, self.chip]).astype(jnp.int32)

    def swap(self, value, bits):
        return lax.ppermute(value, "dp", [(i, i ^ bits) for i in range(self.devices)])

    def split_swap(self, value, even_bits, odd_bits):
        return lax.ppermute(
            value, "dp", [(i, i ^ (odd_bits if i % 2 else even_bits)) for i in range(self.devices)]
        )

    def row_swap(self, value, bits):
        return lax.ppermute(value, "blk", [(i, i ^ bits) for i in range(self.blocks)])

    def row_shift(self, value, distance):
        pairs = [(i, i + distance) for i in range(self.blocks) if 0 <= i + distance < self.blocks]
        return lax.ppermute(value, "blk", pairs)

    def sides(self, value):
        return self.swap(value, 2), self.swap(value, 4)

    def across(self, side, other):
        return self.split_swap(jnp.where(self.core == 0, other, side), 2, 4)

    def total(self, kept, given, order):
        sent = self.swap(given, 1)
        yield
        sent = order(sent)
        cuts = cut_rows(self.place, kept, sent, self.chips)
        order.mark(cuts[0])
        sent = [self.swap(cuts[r], 2 * r) for r in range(1, self.chips)]
        yield
        sent = order(*sent)
        value = order.mark(sum([cuts[0].astype(f32)] + [part.astype(f32) for part in sent]).astype(bf16))
        bits = 1
        while bits < self.blocks:
            sent = self.row_swap(value, bits)
            yield
            sent = order(sent)
            value = order.mark((value.astype(f32) + sent.astype(f32)).astype(bf16))
            bits *= 2
        sent = [self.swap(value, 2 * r) for r in range(1, self.chips)]
        yield
        sent = order(*sent)
        value = order.mark(join_rows(self.place, [value, *sent]))
        sent = self.swap(value, 1)
        yield
        sent = order(sent)
        yield value, sent

    def small_total(self, value, order):
        for swap, count in ((self.swap, self.devices), (self.row_swap, self.blocks)):
            bits = 1
            while bits < count:
                sent = swap(value, bits)
                yield
                sent = order(sent)
                value = order.mark(value + sent)
                bits *= 2
        yield value


def shards(
    block_input,
    out_cotangent,
    row_lengths,
    rope_positions,
    gain_attention,
    gain_feedforward,
    base_attention,
    base_output,
    base_feedforward,
    base_down,
    rank_in_attention,
    rank_out_attention,
    magnitude_attention,
    rank_in_output,
    rank_out_output,
    magnitude_output,
    rank_in_feedforward,
    rank_out_feedforward,
    magnitude_feedforward,
    rank_in_down,
    rank_out_down,
    magnitude_down,
    *,
    devices,
    blocks,
):
    links = Links(devices, blocks)
    order = Order()
    mark = order.mark
    index, core, chip, chips = links.index, links.core, links.chip, links.chips
    place = links.place
    partner = lambda value: links.swap(value, 1)
    rows_in = block_input[0]
    tokens = rows_in.shape[0]
    length = row_lengths[0]
    token_pos = links.block * tokens + jnp.arange(tokens, dtype=jnp.int32)
    fast = links.square and base_attention.shape[2] * devices == KVW and blocks == 4
    heads = jnp.arange(KV_HEADS, dtype=jnp.int32)
    heads = chip ^ heads if fast else heads
    scalars = jnp.stack([links.block.astype(jnp.int32), length])

    def columns_of(value, width):
        return lax.dynamic_slice_in_dim(value, index * width, width, value.ndim - 1)

    attn_cols, out_cols = base_attention.shape[2], base_output.shape[2]
    feed_cols, down_cols = base_feedforward.shape[2], base_down.shape[1]
    chip_cols = 2 * feed_cols
    attn_rank = columns_of(rank_out_attention, attn_cols)
    attn_mag = columns_of(magnitude_attention, attn_cols)
    attn_base = base_attention.transpose(0, 2, 1)
    attn_in_t = rank_in_attention.transpose(0, 2, 1)
    out_in_t = rank_in_output.T
    feed_in_t = rank_in_feedforward.transpose(0, 2, 1)
    down_in_t = rank_in_down.T

    def fold_out():
        return fold(
            order(base_output).transpose(0, 2, 1),
            out_in_t[None],
            columns_of(rank_out_output, out_cols),
            columns_of(magnitude_output, out_cols),
            0,
            False,
            "fold_o",
        )

    def fold_feed():
        return fold(
            order(base_feedforward).transpose(0, 2, 1),
            feed_in_t,
            columns_of(rank_out_feedforward, feed_cols),
            columns_of(magnitude_feedforward, feed_cols),
            0,
            True,
            "fold_feed",
        )

    def folded_down():
        return fold_down(
            order(base_down),
            down_in_t,
            columns_of(rank_out_down, down_cols),
            columns_of(magnitude_down, down_cols),
            chips,
        )

    def norm_in():
        values = order(rows_in).astype(f32)
        return (values * rms_inverse(values) * gain_attention).astype(bf16)

    frequency = rope_base ** (-(jnp.arange(HEAD // 2, dtype=f32) * 2.0) / HEAD)
    angles = rope_positions[0].astype(f32)[:, None] * frequency[None, :]
    cos_half, sin_half = jnp.cos(angles), jnp.sin(angles)
    cosine = jnp.concatenate([cos_half, cos_half], axis=-1)
    sine = jnp.concatenate([-sin_half, sin_half], axis=-1)
    tables = (cosine, sine)

    wheres = [jnp.stack([core, chip ^ r, chip, chip ^ 1, chip ^ 2]).astype(jnp.int32) for r in range(KV_HEADS)]

    settle = order.pin

    def project(where, first, second, roped, name, before=()):
        first, second = order(first, second)
        weights, out, token = head_step(where, first, second, normed, tables, roped, before, name)
        mark(token)
        return weights, out

    def send_kv(kv_blocks):
        kv_blocks.append(links.row_shift(kv_blocks[-1], 1))

    kv_fold = mark(
        fold(attn_base, attn_in_t, attn_rank[GROUP:], attn_mag[GROUP:], 1, True, "fold_kv", first=GROUP)
    )
    down_cut = lambda r: lax.dynamic_index_in_dim(down_fold, chip ^ r, 0, keepdims=False)
    spread = lambda value: lax.all_gather(value, "dp", axis=0)
    grad_out = jnp.where((token_pos < length)[:, None], out_cotangent[0], jnp.zeros((), bf16))
    grad_own = grad_out[None]
    chip_in_t = lax.dynamic_slice_in_dim(down_in_t, chip * chip_cols, chip_cols, 1)
    halves_in_t = jnp.stack(
        [lax.dynamic_slice_in_dim(chip_in_t, at * feed_cols, feed_cols, 1) for at in (core, 1 - core)]
    )
    feed_mag = lax.dynamic_slice_in_dim(magnitude_feedforward, chip * chip_cols, chip_cols, 1)
    if fast:
        kv_side, kv_other = links.sides(kv_fold)
        kv_partner = partner(kv_fold)
        q_fold = mark(fold(order(attn_base), attn_in_t, attn_rank[:GROUP], attn_mag[:GROUP], 0, False, "fold_q"))
        q_weights = spread(q_fold)
        kv_side, kv_other, kv_partner = settle(kv_side, kv_other, kv_partner)
        kv_across = links.across(kv_side, kv_other)
        kv_side_p, kv_other_p = partner(kv_side), partner(kv_other)
        o_fold = mark(fold_out())
        o_weights = spread(after(o_fold, q_fold))
        normed = mark(norm_in())
        kv_made = [
            project(wheres[0], kv_fold, kv_partner, 1, "head_kv"),
            project(wheres[1], kv_side, kv_side_p, 1, "head_kv"),
            project(wheres[2], kv_other, kv_other_p, 1, "head_kv"),
        ]
        kv_across = settle(kv_across)
        kv_across_p = partner(kv_across)
        kv_made.append(project(wheres[3], kv_across, kv_across_p, 1, "head_kv", [out for _, out in kv_made]))
        kv_own = kv_made[-1][1]
        kv_blocks = [kv_own]
        send_kv(kv_blocks)
        grad_own, halves_in_t, feed_mag = settle(grad_own, halves_in_t, feed_mag)
        feed_own = mark(fold_feed())
        kv_blocks[1] = settle(kv_blocks[1])
        send_kv(kv_blocks)
        down_fold, down_proj = folded_down()
        mark(down_proj)
        down_0, down_c1, down_c2, down_c3 = settle(*[down_cut(r) for r in range(4)])
        grad_all = lax.all_gather(
            order(grad_out), "dp", axis=0, axis_index_groups=[[2 * c + k for c in range(chips)] for k in range(2)]
        )
        kv_blocks[2] = settle(kv_blocks[2])
        send_kv(kv_blocks)
        queries = mark(query_project(order(normed), tables, q_weights))
        kv_blocks[3] = settle(kv_blocks[3])
        down_1, down_2, down_3 = links.swap(down_c1, 2), links.swap(down_c2, 4), links.swap(down_c3, 6)
        mixed, lse = attend(scalars, order(queries), kv_blocks)
        mark(lse)
        feed_partner = partner(order(feed_own))

        def feed_late():
            near = settle(down_1, down_2, down_3)
            pieces = []
            for piece in (down_0, *near):
                pieces += [piece, partner(piece)]
            return settle(*pieces)

    else:
        q_fold = fold(attn_base, attn_in_t, attn_rank[:GROUP], attn_mag[:GROUP], 0, False, "fold_q")
        q_weights, o_weights, normed = spread(q_fold), spread(fold_out()), norm_in()
        down_fold, down_proj = folded_down()
        feed_own = fold_feed()
        feed_partner = partner(feed_own)
        whole = lax.all_gather(kv_fold, "dp", axis=1, tiled=True).reshape(2, KV_HEADS, 2, HEAD // 2, WIDE)
        kv_made = []
        for j in range(KV_HEADS):
            before = [out for _, out in kv_made] if j == KV_HEADS - 1 else ()
            where = jnp.array([0, j, 0, 1, 2], jnp.int32)
            kv_made.append(project(where, whole[:, j, 0], whole[:, j, 1], 1, "head_kv", before))
        kv_own = kv_made[-1][1]
        kv_blocks = [kv_own]
        for _ in range(1, blocks):
            send_kv(kv_blocks)
        queries = query_project(normed, tables, q_weights)
        grad_all = lax.all_gather(
            grad_out, "dp", axis=0, axis_index_groups=[[2 * c + k for c in range(chips)] for k in range(2)]
        )
        mixed, lse = attend(scalars, queries, kv_blocks)
        down_pieces = []
        for r in range(chips):
            piece = links.swap(down_cut(r), 2 * r) if r else down_cut(r)
            down_pieces += [piece, partner(piece)]
    residual, normed_feed = output_project(order(mixed), o_weights, rows_in, gain_feedforward)
    mark(normed_feed)

    forward = lambda normed_group: settle(*feed_forward(order(normed_group), feed_own, feed_partner, tokens))
    aux = []

    def backward(members, kept):
        grads = grad_own if members == (None,) else grad_all
        kept = list(order(*kept)) if isinstance(kept, (tuple, list)) else [order(kept)]
        made = feed_back(place, grads, members, kept, feed_own, feed_partner, down_pieces, tokens)
        mark(made[0])
        count = len(members)
        return made[:count], made[count : 2 * count], made[2 * count :]

    mag_sums = []

    def adapters(members, normed_group, made, before):
        hidden, grad_gate, grad_up, ext, mags, down_aux = made[2]
        parts = feed_adapter(
            place, order(normed_group), grad_own if members == (None,) else grad_all, members, hidden, grad_gate,
            grad_up, ext, feed_in_t.reshape(2 * RANK, D), halves_in_t, before,
        )
        mark(parts[0])
        aux.append(down_aux)
        mag_sums.append(mags)
        return tuple(parts)

    if fast:
        side, other = links.sides(normed_feed)
        down_pieces = feed_late()
        own_made = backward((None,), normed_feed)
        side, other = settle(side, other)
        crossed = links.across(side, other)
        near = settle(jnp.concatenate([side, other]))
        near_kept = forward(near)
        sums = adapters((None,), normed_feed, own_made, None)
        crossed = settle(crossed)
        far_made = backward((3,), crossed)
        from_far = links.split_swap(far_made[0][0], 2, 4)
        first_made = backward(("first",), near_kept)
        early_first = links.split_swap(first_made[0][0], 2, 4)
        last_made = backward(("last",), near_kept)
        from_far = settle(from_far)
        late_share = settle((last_made[0][0].astype(f32) + from_far.astype(f32)).astype(bf16))
        early_second = links.split_swap(late_share, 4, 2)
        down_mag_steps = links.small_total(sum(made[2][4][4:5] for made in (own_made, first_made, last_made, far_made)), order)
        next(down_mag_steps)
        sums = adapters(("first",), near, first_made, sums)
        next(down_mag_steps)
        sums = adapters(("last",), near, last_made, sums)
        early_first = settle(early_first)
        reduced = (own_made[0][0], early_first, early_second)
        shares_out = [own_made[1][0], first_made[1][0], last_made[1][0], far_made[1][0]]
    else:
        sums, shares_grad, shares_out = None, [], []
        for r in range(chips):
            normed_group = links.swap(normed_feed, 2 * r) if r else normed_feed
            made = backward((r,), normed_group)
            sums = adapters((r,), normed_group, made, sums)
            shares_grad.append(made[0][0])
            shares_out.append(made[1][0])
        rest = sum(links.swap(shares_grad[r], 2 * r).astype(f32) for r in range(1, chips)).astype(bf16)
        reduced = (shares_grad[0], rest, jnp.zeros(rest.shape, bf16))
        down_mag_steps = links.small_total(sum(mags[4:5] for mags in mag_sums), order)
        next(down_mag_steps)
    reduced = settle(*reduced)
    grad_residual, grad_ordered, out_mag_raw, out_ext, grad_mixed, delta = residual_back(
        reduced, residual, gain_feedforward, grad_out, rows_in, mixed, o_weights
    )
    mark(delta)
    next(down_mag_steps)
    def pack_early(down_mag_total):
        feed_mags = jnp.stack(
            [lax.dynamic_slice_in_dim(feed_mag, at * feed_cols, feed_cols, 1) for at in (core, 1 - core)]
        )
        if fast:
            *early, down_grad_mag = feed_pack(
                place, feed_own, feed_partner, down_fold, *order(feed_products, mag_raw), feed_mags, feed_in, down_in,
                down_products, down_mag_total, magnitude_down[None], aux[0], down_proj, rank_out_down,
                share=1.0 / blocks,
            )
            return down_grad_mag, early
        finished = [
            finish_columns(weights, feed_products[half], mag_raw[half:4:2, :feed_cols], feed_mags[half])
            for half, weights in enumerate((feed_own, feed_partner))
        ]
        grad_mag, grad_out_part, grad_in_part = zip(*finished)
        columns = [
            jnp.concatenate([part.astype(bf16) for part in parts])
            for parts in zip(grad_out_part, down_in, grad_mag)
        ]
        columns = jnp.where(core == 0, jnp.concatenate(columns, axis=1), jnp.concatenate(columns[::-1], axis=1))
        full = lax.dynamic_update_slice(jnp.zeros((64, 3 * D), bf16), columns, (0, chip * chip_cols))
        down_aux = aux[0]
        down_inverse = (down_aux[RANK].astype(f32) + down_aux[RANK + 1].astype(f32))[None]
        down_grad_mag = down_mag_total / magnitude_down[None]
        down_out = factor * down_products * (magnitude_down[None] * down_inverse)
        own_turn = columns_of(-down_grad_mag * down_inverse, down_cols) * (factor / blocks)
        down_out = lax.dynamic_update_slice(
            down_out, columns_of(down_out, down_cols) + down_proj * own_turn, (0, index * down_cols)
        )
        own_wide = (columns_of(rank_out_down.astype(f32), down_cols) * own_turn).astype(bf16)
        down_norm_in = lax.dot_general(
            own_wide, down_fold[:, :chip_cols], (((1,), (2,)), ((), ())), preferred_element_type=f32
        ).reshape(RANK, FF)
        down_full = (full[2 * RANK : 3 * RANK, :FF].astype(f32) + down_norm_in).astype(bf16)
        full = lax.dynamic_update_slice(full, down_full, (2 * RANK, 0))
        top = jnp.concatenate([(feed_in + sum(grad_in_part)).astype(bf16), down_out.astype(bf16)])
        whole = jnp.concatenate(
            [jnp.pad(top, ((0, 16), (0, 0)))] + [full[:, i * D : (i + 1) * D] for i in range(3)]
        )
        left, right = whole[:, : D // 2], whole[:, D // 2 :]
        return down_grad_mag, (jnp.where(core == 0, left, right), jnp.where(core == 0, right, left))

    grad_queries, grad_kvs = None, []

    def keys_back(distance):
        grad_queries_next, grad_kv = attend_back(
            scalars, order(queries), grad_mixed, lse, delta, kv_blocks[distance], grad_queries, distance
        )
        mark(grad_kv)
        return grad_queries_next, grad_kv

    def pass_down(passed, grad_kv):
        passed = order(passed)
        passed = settle((passed.astype(f32) + grad_kv.astype(f32)).astype(bf16))
        return links.row_shift(passed, -1)

    grad_queries, grad_kv = keys_back(blocks - 1)
    passed = links.row_shift(grad_kv, -1)
    next(down_mag_steps)
    held = None
    for distance in reversed(range(1, blocks - 1)):
        grad_queries, grad_kv = keys_back(distance)
        if held is not None:
            passed = pass_down(passed, held)
        held = grad_kv
    if fast:
        out_far = links.split_swap(order(shares_out[3]), 2, 4)
        out_first = links.split_swap(order(shares_out[1]), 2, 4)
    next(down_mag_steps)
    grad_queries, grad_kv = keys_back(0)
    if fast:
        sums = adapters((3,), crossed, far_made, sums)
    feed_in, feed_products, down_in, down_products = sums
    mag_raw = sum(mag_sums)
    for down_mag_total in down_mag_steps:
        pass
    down_grad_mag, early = pack_early(down_mag_total)
    mark(down_grad_mag)
    early_steps = links.total(*early, order)
    next(early_steps)
    passed = pass_down(passed, held)
    out_grad_mag, out_out, out_in = output_adapter(
        order(grad_ordered), out_mag_raw, magnitude_output, o_weights, mixed, out_ext, out_in_t
    )
    mark(out_in)
    if fast:
        next(early_steps)
        out_far, out_first = settle(out_far, out_first)
        out_late = settle((shares_out[2].astype(f32) + out_far.astype(f32)).astype(bf16))
        out_second = links.split_swap(out_late, 4, 2)
        out_parts = [shares_out[0], out_first, out_second]
    else:
        out_parts = [shares_out[0]] + [links.swap(shares_out[r], 2 * r) for r in range(1, chips)]
    q_acc, q_in, q_out, q_grad_mag = query_back(
        order(grad_queries), queries, q_weights, cosine, sine, normed, attn_in_t[0], magnitude_attention[:GROUP]
    )
    mark(q_in)
    if fast:
        next(early_steps)
    passed = settle(passed)
    input_grad, *late = key_back(
        heads, passed, grad_kv, kv_own, [weights for weights, _ in kv_made], cosine, sine, normed, rows_in,
        gain_attention, grad_residual, q_acc, attn_in_t[1:].reshape(2 * RANK, D), magnitude_attention[GROUP:],
        place, q_in, q_out, q_grad_mag, out_in, out_out, out_grad_mag,
    )
    mark(late[0])
    late_steps = links.total(*late, order)
    next(late_steps)
    out_parts = settle(*out_parts)
    late = early = None
    next(late_steps)
    out_parts = settle(*out_parts)
    block_out = settle((residual + sum(part.astype(f32) for part in out_parts)).astype(bf16))[None]
    while early is None:
        early = next(early_steps)
        if late is None:
            late = next(late_steps)
    early_shapes = ((2, RANK, D), (2, RANK, FF), (2, FF), (RANK, FF), (RANK, D))
    feed_in, feed_out, feed_mag, down_in, down_out = unpack(
        unpack_early_kernel, place, order(*early), early_shapes, "unpack_early"
    )
    mark(feed_mag)
    while late is None:
        late = next(late_steps)
    late_shapes = ((3, RANK, D), (GROUP + 2, RANK, KVW), (GROUP + 2, KVW), (RANK, D), (GROUP, RANK, KVW), (GROUP, KVW))
    attn_in, attn_out, attn_mag, out_in, out_out, out_mag = unpack(
        unpack_late_kernel, place, order(*late), late_shapes, "unpack_late"
    )
    return (
        block_out,
        input_grad[None],
        attn_in.transpose(0, 2, 1),
        attn_out,
        attn_mag,
        out_in.T,
        out_out,
        out_mag,
        feed_in.transpose(0, 2, 1),
        feed_out,
        feed_mag,
        down_in.T,
        down_out,
        down_grad_mag[0],
    )


def solution(mesh):
    split_tokens = P("dp", "blk", None)
    placed = (
        split_tokens,
        split_tokens,
        P("dp"),
        P("dp", "blk"),
        P(),
        P(),
        P(None, None, "dp"),
        P(None, None, "dp"),
        P(None, None, "dp"),
        P(None, "dp"),
    ) + (P(),) * 12
    return jax.shard_map(
        functools.partial(shards, devices=mesh.shape["dp"], blocks=mesh.shape["blk"]),
        mesh=mesh,
        in_specs=placed,
        out_specs=(split_tokens, split_tokens) + (P(),) * 12,
        check_vma=False,
    )
```
